32 devices in a mesh: fsdp: 8 (over z, x), tensor: 4 (over y, core).
Axes of the slice: x: 2, y: 2, z: 4, core: 2. Of those that a mesh axis runs over, the one named last changes fastest.
Arguments:
- tokens: bfloat16 [16384, 1024], P(('fsdp', 'tensor')), may hold values from -6 to 6
- cotangent: bfloat16 [16384, 1024], P(('fsdp', 'tensor')), may hold values from -6 to 6
- pic_starts: int32 [8, 4], P('fsdp'), may hold values from 0 to 1792, as said below
- w_qkv: bfloat16 [1024, 3, 1024], P('fsdp', None, 'tensor'), may hold values from -0.1875 to 0.1875
- qv_bias: float32 [2, 1024], replicated, may hold values from -3 to 3
- w_out: bfloat16 [1024, 1024], P('tensor', 'fsdp'), may hold values from -0.75 to 0.75
- out_bias: float32 [1024], replicated, may hold values from -3 to 3
- ln1_gain: float32 [1024], replicated, may hold values from 0.5 to 1.5
- ln1_bias: float32 [1024], replicated, may hold values from -1.2 to 1.2
- w_fc1: bfloat16 [1024, 4096], P('fsdp', 'tensor'), may hold values from -0.1875 to 0.1875
- fc1_bias: float32 [4096], replicated, may hold values from -10 to 10
- w_fc2: bfloat16 [4096, 1024], P('tensor', 'fsdp'), may hold values from -0.125 to 0.125
- fc2_bias: float32 [1024], replicated, may hold values from -6 to 6
- ln2_gain: float32 [1024], replicated, may hold values from 0.1 to 1.9
- ln2_bias: float32 [1024], replicated, may hold values from -1.2 to 1.2
Outputs:
- output: float32 [16384, 1024], P(('fsdp', 'tensor'))
- grad_tokens: float32 [16384, 1024], P(('fsdp', 'tensor'))
- grad_w_qkv: float32 [1024, 3, 1024], P('fsdp', None, 'tensor')
- grad_qv_bias: float32 [2, 1024], replicated
- grad_w_out: float32 [1024, 1024], P('tensor', 'fsdp')
- grad_out_bias: float32 [1024], replicated
- grad_ln1_gain: float32 [1024], replicated
- grad_ln1_bias: float32 [1024], replicated
- grad_w_fc1: float32 [1024, 4096], P('fsdp', 'tensor')
- grad_fc1_bias: float32 [4096], replicated
- grad_w_fc2: float32 [4096, 1024], P('tensor', 'fsdp')
- grad_fc2_bias: float32 [1024], replicated
- grad_ln2_gain: float32 [1024], replicated
- grad_ln2_bias: float32 [1024], replicated
The draws below stay inside these ranges and needn't reach their ends.
Inputs may be any that keep to these rules, and one draw needn't show every extreme that they name: `pic_starts`: picture pieces of a sequence do not intersect: piece k starts between k * 512 and k * 512 + 256 and covers 256 tokens.
All inputs are finite; a program needn't handle non-finite values.
Results may differ from the reference program's by a relative error of at most 0.011.
Values may be sent and summed in bfloat16 or wider, within the bound.
A program may use at most 192 MiB of HBM per device.

```python
import jax
import jax.numpy as jnp
from jax import lax

D = 1024
H = 16
HD = 64
FF = 4096
LEN = 2048
SLOT = 512
PIC = 256
NPIC = 4
SEQS = 8
TOKENS = 16384
N_TENSOR = 4


def draw_pic_starts(key, part):
    offsets = jax.random.randint(key, (SEQS, NPIC), 0, SLOT - PIC + 1, dtype=jnp.int32)
    starts = jnp.arange(NPIC, dtype=jnp.int32)[None, :] * SLOT + offsets
    starts = starts.at[0, 0].set(0)
    starts = starts.at[SEQS - 1, NPIC - 1].set(LEN - PIC)
    return starts.astype(jnp.int32)


def strengthened(drawn, stream_key, source, target, parts, factor):
    def block_of(axis_at):
        return (jnp.arange(drawn.shape[axis_at]) // (drawn.shape[axis_at] // parts)).reshape((-1,) + (1,) * (drawn.ndim - 1 - axis_at))

    one_side = jax.random.permutation(stream_key, parts)[block_of(target)]
    far = (block_of(target) + parts // 2) % parts
    return jnp.where((block_of(source) == one_side) | (block_of(source) == far), factor * drawn, drawn)


def steps_of(rng, extent, cuts, low, top_value):
    factor_of, own = 1.0, jax.random.fold_in(rng, 6)
    for position, blocks in cuts:
        draws = jnp.exp(jax.random.uniform(jax.random.fold_in(own, position), (blocks,), jnp.float32, low / len(cuts), top_value / len(cuts)))
        factor_of = factor_of * jnp.repeat(draws, extent[position] // blocks).reshape([-1 if axis == position else 1 for axis in range(len(extent))])
    return factor_of


def normal_values(stream_key, extent, scale, bound, split=(), held_as=jnp.bfloat16):
    drawn = jax.random.normal(stream_key, extent, jnp.float32) * scale
    if len(split) > 0:
        drawn = steps_of(stream_key, extent, split, -0.22, 0.18) * drawn
    return jnp.clip(drawn, min=-bound, max=bound).astype(held_as)


def bell_draw_with(key, extent, scale, limit, shards, heavy, held_as=jnp.bfloat16):
    entries = scale * jax.random.normal(key, extent, jnp.float32)
    if shards:
        entries = entries * steps_of(key, extent, shards, -0.22, 0.18)
    return jnp.clip(strengthened(entries, jax.random.fold_in(key, 3), *heavy), -limit, limit).astype(held_as)


def setup_inputs(seed: int = 0) -> dict:
    key_of = jax.random.split(jax.random.key(seed), 16)
    return {
        "tokens": bell_draw_with(key_of[0], (TOKENS, D), 1.0, 6.0, ((0, 32),), (0, 1, 32, 2.75)),
        "cotangent": bell_draw_with(key_of[1], (TOKENS, D), 1.0, 6.0, ((0, 32),), (0, 1, 32, 2.75)),
        "pic_starts": draw_pic_starts(jax.random.fold_in(key_of[15], 71), 0),
        "w_qkv": normal_values(key_of[3], (D, 3, D), D ** -0.5, 0.1875, ((0, 8), (2, 4))),
        "qv_bias": normal_values(key_of[4], (2, D), 0.5, 3.0, (), jnp.float32),
        "w_out": normal_values(key_of[5], (D, D), (D // 16) ** -0.5, 0.75, ((0, 4), (1, 8))),
        "out_bias": normal_values(key_of[6], (D,), 0.5, 3.0, (), jnp.float32),
        "ln1_gain": jnp.clip(1.0 + 0.1 * jax.random.normal(key_of[7], (D,), jnp.float32), 0.5, 1.5),
        "ln1_bias": normal_values(key_of[8], (D,), 0.2, 1.2, (), jnp.float32),
        "w_fc1": normal_values(key_of[9], (D, FF), D ** -0.5, 0.1875, ((0, 8), (1, 4))),
        "fc1_bias": normal_values(key_of[10], (FF,), 2.5, 10.0, (), jnp.float32),
        "w_fc2": normal_values(key_of[11], (FF, D), (FF // 2) ** -0.5, 0.125, ((0, 4), (1, 8))),
        "fc2_bias": normal_values(key_of[12], (D,), 1.0, 6.0, (), jnp.float32),
        "ln2_gain": jnp.clip(1.0 + 0.18 * jax.random.normal(key_of[13], (D,), jnp.float32), 0.1, 1.9),
        "ln2_bias": normal_values(key_of[14], (D,), 0.2, 1.2, (), jnp.float32),
    }


NORM_EPSILON = 1e-05
MASKED_SCORE = -1e+30
HIGHEST = lax.Precision.HIGHEST

@jax.custom_vjp
def low(v):
    return lax.optimization_barrier(v.astype(jnp.bfloat16)).astype(jnp.float32)

@jax.custom_vjp
def low_back(v):
    return v

def low_keep(v):
    return (low(v), None)

def low_pass(kept, grad):
    return (grad,)

def back_keep(v):
    return (v, None)

def back_low(kept, grad):
    return (low(grad),)
low.defvjp(low_keep, low_pass)
low_back.defvjp(back_keep, back_low)

def normalize(values, gain_row, bias_row):
    average = lax.optimization_barrier(jnp.mean(values, axis=-1, keepdims=True))
    centered = values - average
    variance = lax.optimization_barrier(jnp.mean(centered * centered, axis=-1, keepdims=True))
    return centered * lax.rsqrt(variance + NORM_EPSILON) * gain_row + bias_row

def piece_labels(starts):
    positions = jnp.arange(LEN, dtype=jnp.int32)
    inside = (positions[None, :] >= starts[:, None]) & (positions[None, :] < starts[:, None] + PIC)
    labels = jnp.arange(1, NPIC + 1, dtype=jnp.int32)
    return lax.optimization_barrier(jnp.sum(jnp.where(inside, labels[:, None], 0), axis=0)).astype(jnp.int32)

def layer(inputs, starts, w_qkv, qv_bias, w_out, out_bias, ln1_gain, ln1_bias, w_fc1, fc1_bias, w_fc2, fc2_bias, ln2_gain, ln2_bias):
    head_width = D // N_TENSOR
    hidden_width = FF // N_TENSOR
    head_count = H // N_TENSOR
    score_scale = HD ** (-0.5)
    positions = jnp.arange(LEN, dtype=jnp.int32)
    labels = piece_labels(starts)
    permitted = (positions[None, :] <= positions[:, None]) | (labels[:, None] == labels[None, :]) & (labels[:, None] > 0)
    normed_one = low(normalize(inputs, ln1_gain, ln1_bias))
    attn_total = jnp.zeros((LEN, D), jnp.float32)
    for member in range(N_TENSOR):
        first_col = member * head_width
        weight_block = w_qkv[:, :, first_col:first_col + head_width].reshape(D, 3 * head_width)
        projected = jnp.dot(normed_one, weight_block, precision=HIGHEST, preferred_element_type=jnp.float32).reshape(LEN, 3, head_width)
        queries = low_back(low(projected[:, 0] + qv_bias[0, first_col:first_col + head_width])).reshape(LEN, head_count, HD)
        key_rows = low_back(low(projected[:, 1])).reshape(LEN, head_count, HD)
        values = low_back(low(projected[:, 2] + qv_bias[1, first_col:first_col + head_width])).reshape(LEN, head_count, HD)
        scores = jnp.einsum('qhd,khd->hqk', queries, key_rows, precision=HIGHEST) * score_scale
        scores = low_back(jnp.where(permitted[None], scores, MASKED_SCORE))
        probability = low(jax.nn.softmax(scores, axis=-1))
        attended = jnp.einsum('hqk,khd->qhd', probability, values, precision=HIGHEST).reshape(LEN, head_width)
        attended = low_back(low(attended))
        attn_total = attn_total + jnp.dot(attended, w_out[first_col:first_col + head_width], precision=HIGHEST, preferred_element_type=jnp.float32)
    hidden_one = inputs + (low_back(attn_total) + out_bias)
    normed_two = low(normalize(hidden_one, ln2_gain, ln2_bias))
    ffn_total = jnp.zeros((LEN, D), jnp.float32)
    for member in range(N_TENSOR):
        first_col = member * hidden_width
        pre_act = jnp.dot(normed_two, w_fc1[:, first_col:first_col + hidden_width], precision=HIGHEST, preferred_element_type=jnp.float32) + fc1_bias[first_col:first_col + hidden_width]
        activated = low(jax.nn.gelu(low_back(pre_act), approximate=True))
        ffn_total = ffn_total + jnp.dot(activated, w_fc2[first_col:first_col + hidden_width], precision=HIGHEST, preferred_element_type=jnp.float32)
    return hidden_one + (low_back(ffn_total) + fc2_bias)

def reference(tokens, cotangent, pic_starts, w_qkv, qv_bias, w_out, out_bias, ln1_gain, ln1_bias, w_fc1, fc1_bias, w_fc2, fc2_bias, ln2_gain, ln2_bias):
    weights = tuple((entry.astype(jnp.float32) for entry in (w_qkv, qv_bias, w_out, out_bias, ln1_gain, ln1_bias, w_fc1, fc1_bias, w_fc2, fc2_bias, ln2_gain, ln2_bias)))
    inputs = tokens.astype(jnp.float32).reshape(SEQS, LEN, D)
    upstream = cotangent.astype(jnp.float32).reshape(SEQS, LEN, D)

    def per_sequence(totals, sequence_items):
        seq_inputs, seq_upstream, starts = sequence_items

        def forward(seq_values, *params):
            return layer(seq_values, starts, *params)
        result, pullback = jax.vjp(forward, seq_inputs, *weights)
        gradients = pullback(seq_upstream)
        totals = jax.tree.map(lambda older, newer: older + newer, totals, tuple(gradients[1:]))
        return (totals, (result, gradients[0]))
    zero_grads = tuple((jnp.zeros_like(entry) for entry in weights))
    totals, (outputs, input_grads) = lax.scan(per_sequence, zero_grads, (inputs, upstream, pic_starts))
    return (outputs.reshape(TOKENS, D), input_grads.reshape(TOKENS, D), totals[0], totals[1], totals[2], totals[3], totals[4], totals[5], totals[6], totals[7], totals[8], totals[9], totals[10], totals[11])
```

```python
import functools
import math

import jax
import jax.numpy as jnp
from jax import lax
from jax.experimental import pallas as pl
from jax.experimental.pallas import tpu as pltpu
from jax.sharding import PartitionSpec as P

HD = 64
PIC = 256
F32 = jnp.float32
BF = jnp.bfloat16
NEG = -1e30
NORM_EPSILON = 1e-05
GELU_SCALE = math.sqrt(2.0 / math.pi)
GELU_CUBIC = 0.044715
VM = pltpu.MemorySpace.VMEM
SM = pltpu.MemorySpace.SMEM


def nn(a, b):
    return lax.dot_general(a, b, (((1,), (0,)), ((), ())), preferred_element_type=F32)


def nt(a, b):
    return lax.dot_general(a, b, (((1,), (1,)), ((), ())), preferred_element_type=F32)


def normalize(values):
    average = jnp.mean(values, axis=1, keepdims=True)
    centered = values - average
    inv_std = lax.rsqrt(jnp.mean(centered * centered, axis=1, keepdims=True) + NORM_EPSILON)
    return centered * inv_std, inv_std


def normalize_back(gradient, unit_rows, inv_std, gain_row):
    scaled = gradient * gain_row
    inner = (
        scaled
        - jnp.mean(scaled, axis=1, keepdims=True)
        - unit_rows * jnp.mean(scaled * unit_rows, axis=1, keepdims=True)
    )
    return inv_std * inner, jnp.sum(gradient * unit_rows, axis=0), jnp.sum(gradient, axis=0)


def attn_fwd_kernel(meta, q0,q1,q2,q3, att0,att1,att2,att3, lse_ref, kz, qT, vT, att):
    t=meta[0]
    B=q0.shape[0]; HW=q0.shape[1]//3; NH=HW//HD; NP=NH//2
    qs=(q0,q1,q2,q3); outs=(att0,att1,att2,att3)
    for j in range(4):
        b=t^j
        kz[b]=qs[j][:,HW:2*HW]
        qT[b]=(qs[j][:,:HW]*jnp.asarray(HD**-0.5,BF)).T
        vT[b]=qs[j][:,2*HW:].T
    rowk=lax.broadcasted_iota(jnp.int32,(B,B),0)
    colq=lax.broadcasted_iota(jnp.int32,(B,B),1)
    half=lax.broadcasted_iota(jnp.int32,(2*HD,B),0)<HD
    for i in range(4):
        ps=meta[1+i]-i*B
        jj=t^i
        def pair(p,_):
            kcol=pl.multiple_of(p*2*HD,2*HD)
            qp=qT[i,pl.ds(kcol,2*HD),:]
            zero=jnp.zeros_like(qp)
            qzs=(jnp.where(half,qp,zero),jnp.where(half,zero,qp))
            os=[]
            for hh in range(2):
                ss=[]; mx=None
                for m in range(i+1):
                    s=nn(kz[m,:,pl.ds(kcol,2*HD)],qzs[hh])
                    if m==i:
                        ok=(rowk<=colq)|((rowk>=ps)&(rowk<ps+PIC)&(colq>=ps)&(colq<ps+PIC))
                        s=jnp.where(ok,s,NEG)
                    sm=jnp.max(s,axis=0,keepdims=True)
                    mx=sm if mx is None else jnp.maximum(mx,sm)
                    ss.append(s)
                l=0.; acc=0.
                for m in range(i+1):
                    e=jnp.exp(ss[m]-mx)
                    l=l+jnp.sum(e,axis=0,keepdims=True)
                    acc=acc+nn(vT[m,pl.ds(kcol+hh*HD,HD),:],e.astype(BF))
                os.append(acc*(1.0/l))
                lse_ref[jj,pl.ds(p*2+hh,1),:]=mx+jnp.log(l)
            o=jnp.concatenate(os,axis=0).astype(BF)
            att[i,:,pl.ds(kcol,2*HD)]=o.T
            return 0
        lax.fori_loop(0,NP,pair,0)
    for j in range(4): outs[j][...]=att[t^j]

def attn_fwd(meta,qs):
    B=qs[0].shape[0]; HW=qs[0].shape[1]//3; NH=HW//HD
    vm=pl.BlockSpec(memory_space=pltpu.MemorySpace.VMEM)
    return pl.pallas_call(attn_fwd_kernel,name="attn_fwd",
        out_shape=[jax.ShapeDtypeStruct((B,HW),BF)]*4+[jax.ShapeDtypeStruct((4,NH,B),F32)],
        in_specs=[pl.BlockSpec(memory_space=pltpu.MemorySpace.SMEM)]+[vm]*4,
        out_specs=[vm]*5,
        scratch_shapes=[pltpu.VMEM((4,B,HW),BF),pltpu.VMEM((4,HW,B),BF),pltpu.VMEM((4,HW,B),BF),pltpu.VMEM((4,B,HW),BF)],
        compiler_params=pltpu.CompilerParams(vmem_limit_bytes=56<<20),
        cost_estimate=pl.CostEstimate(flops=8<<30,bytes_accessed=8<<20,transcendentals=0))(meta,*qs)

def attn_bwd_kernel(meta, *refs):
    qs=refs[0:4]; dos=refs[4:8]; ats=refs[8:12]; lse_ref=refs[12]
    outs=refs[13:17]
    qn,kn,vn,don,qT,kT,doT,dk,dv,dqT,dl=refs[17:]
    t=meta[0]
    B=qs[0].shape[0]; HW=qs[0].shape[1]//3; NH=HW//HD; NP=NH//2
    for j in range(4):
        b=t^j
        q=qs[j][:,:HW]*jnp.asarray(HD**-0.5,BF)
        k=qs[j][:,HW:2*HW]
        do=dos[j][...]
        qn[b]=q; kn[b]=k; vn[b]=qs[j][:,2*HW:]; don[b]=do
        qT[b]=q.T; kT[b]=k.T; doT[b]=do.T
        prod=(do.astype(F32)*ats[j][...].astype(F32)).T
        for h in range(NH):
            dl[b,h:h+1,:]=jnp.sum(prod[h*HD:(h+1)*HD],axis=0,keepdims=True)
    dk[...]=jnp.zeros_like(dk); dv[...]=jnp.zeros_like(dv)
    rowk=lax.broadcasted_iota(jnp.int32,(B,B),0)
    colq=lax.broadcasted_iota(jnp.int32,(B,B),1)
    hrow=lax.broadcasted_iota(jnp.int32,(2*HD,B),0)<HD
    hcol=lax.broadcasted_iota(jnp.int32,(B,2*HD),1)<HD
    for i in range(4):
        jj=t^i
        ps=meta[1+i]-i*B
        def pair(p,_):
            kcol=pl.multiple_of(p*2*HD,2*HD)
            def two(x,m):
                z=jnp.zeros_like(x)
                return (jnp.where(m,x,z),jnp.where(m,z,x))
            qTz=two(qT[i,pl.ds(kcol,2*HD),:],hrow)
            doTz=two(doT[i,pl.ds(kcol,2*HD),:],hrow)
            qz=two(qn[i,:,pl.ds(kcol,2*HD)],hcol)
            doz=two(don[i,:,pl.ds(kcol,2*HD)],hcol)
            lse=[lse_ref[jj,pl.ds(p*2+hh,1),:] for hh in range(2)]
            dlt=[dl[i,pl.ds(p*2+hh,1),:] for hh in range(2)]
            def blk(m,carry,diag):
                kb=kn[m,:,pl.ds(kcol,2*HD)]
                vb=vn[m,:,pl.ds(kcol,2*HD)]
                ktb=kT[m,pl.ds(kcol,2*HD),:]
                dvs=0.; dks=0.; new=[]
                for hh in range(2):
                    s=nn(kb,qTz[hh])
                    if diag:
                        ok=(rowk<=colq)|((rowk>=ps)&(rowk<ps+PIC)&(colq>=ps)&(colq<ps+PIC))
                        s=jnp.where(ok,s,NEG)
                    pr=jnp.exp(s-lse[hh])
                    dp=nn(vb,doTz[hh])
                    ds=(pr*(dp-dlt[hh])).astype(BF)
                    dvs=dvs+nn(pr.astype(BF),doz[hh])
                    dks=dks+nn(ds,qz[hh])
                    new.append(carry[hh]+nn(ktb[hh*HD:(hh+1)*HD],ds))
                dv[m,:,pl.ds(kcol,2*HD)]+=dvs
                dk[m,:,pl.ds(kcol,2*HD)]+=dks
                return tuple(new)
            c=tuple(jnp.zeros((HD,B),F32) for _ in range(2))
            c=blk(i,c,True)
            c=lax.fori_loop(0,i,lambda m,c: blk(m,c,False),c) if i>0 else c
            dqT[i,pl.ds(kcol,2*HD),:]=(jnp.concatenate(c,axis=0)*(HD**-0.5)).astype(BF)
            return 0
        lax.fori_loop(0,NP,pair,0)
    for j in range(4):
        b=t^j
        outs[j][:,:HW]=dqT[b].T
        outs[j][:,HW:2*HW]=dk[b].astype(BF)
        outs[j][:,2*HW:]=dv[b].astype(BF)

def attn_bwd(meta,qs,dos,ats,lse):
    B=qs[0].shape[0]; HW=qs[0].shape[1]//3; NH=HW//HD
    vm=pl.BlockSpec(memory_space=pltpu.MemorySpace.VMEM)
    V=pltpu.VMEM
    return pl.pallas_call(attn_bwd_kernel,name="attn_bwd",
        out_shape=[jax.ShapeDtypeStruct((B,3*HW),BF)]*4,
        in_specs=[pl.BlockSpec(memory_space=pltpu.MemorySpace.SMEM)]+[vm]*13,
        out_specs=[vm]*4,
        scratch_shapes=[V((4,B,HW),BF)]*4+[V((4,HW,B),BF)]*3+[V((4,B,HW),F32)]*2+[V((4,HW,B),BF),V((4,NH,B),F32)],
        compiler_params=pltpu.CompilerParams(vmem_limit_bytes=56<<20),
        cost_estimate=pl.CostEstimate(flops=20<<30,bytes_accessed=16<<20,transcendentals=0))(meta,*qs,*dos,*ats,lse)


def ffn_kernel(m_ref, g_ref, w1_ref, w2_ref, b_ref, act_ref, pg_ref, gn_ref, bg_ref, acc):
    n = pl.program_id(0)
    x = nn(m_ref[...], w1_ref[...]) + b_ref[...]
    hg = nn(g_ref[...], w2_ref[...])
    sq = x * x
    t = jnp.tanh(GELU_SCALE * (x + GELU_CUBIC * (sq * x)))
    half = 0.5 * (1.0 + t)
    act_ref[...] = (x * half).astype(BF)
    slope = half + (0.5 * GELU_SCALE) * x * (1.0 - t * t) * (1.0 + (3.0 * GELU_CUBIC) * sq)
    pg = (hg * slope).astype(BF)
    pg_ref[...] = pg
    bg_ref[...] = jnp.sum(pg.astype(F32), axis=0, keepdims=True)
    part = nt(pg, w1_ref[...])

    @pl.when(n == 0)
    def _():
        acc[...] = part

    @pl.when(n > 0)
    def _():
        acc[...] += part

    @pl.when(n == pl.num_programs(0) - 1)
    def _():
        gn_ref[...] = acc[...].astype(BF)


def ffn(m, g, w1, w2t, bias):
    rows, width = m.shape
    hid = w1.shape[1]
    tn = 256
    full = pl.BlockSpec((rows, width), lambda n: (0, 0))
    wblk = pl.BlockSpec((width, tn), lambda n: (0, n))
    hblk = pl.BlockSpec((rows, tn), lambda n: (0, n))
    vec = pl.BlockSpec((1, tn), lambda n: (0, n))
    return pl.pallas_call(
        ffn_kernel,
        name="ffn",
        grid=(hid // tn,),
        out_shape=[
            jax.ShapeDtypeStruct((rows, hid), BF),
            jax.ShapeDtypeStruct((rows, hid), BF),
            jax.ShapeDtypeStruct((rows, width), BF),
            jax.ShapeDtypeStruct((1, hid), F32),
        ],
        in_specs=[full, full, wblk, wblk, vec],
        out_specs=[hblk, hblk, full, vec],
        scratch_shapes=[pltpu.VMEM((rows, width), F32)],
        compiler_params=pltpu.CompilerParams(vmem_limit_bytes=40 << 20),
        cost_estimate=pl.CostEstimate(
            flops=6 * rows * width * hid, bytes_accessed=8 << 20, transcendentals=rows * hid
        ),
    )(m, g, w1, w2t, bias)


def wgrad_kernel(*refs):
    lhs, rhs, out, lhs_t = refs[0:4], refs[4:8], refs[8], refs[9]
    rows = lhs[0].shape[0]

    @pl.when(pl.program_id(0) == 0)
    def _():
        for j in range(4):
            lhs_t[:, j * rows : (j + 1) * rows] = lhs[j][...].T

    acc = nn(lhs_t[:, :rows], rhs[0][...])
    for j in range(1, 4):
        acc = acc + nn(lhs_t[:, j * rows : (j + 1) * rows], rhs[j][...])
    out[...] = acc.astype(BF)


def wgrad(lhs, rhs):
    rows, width = lhs[0].shape
    cols = rhs[0].shape[1]
    tn = 256
    return pl.pallas_call(
        wgrad_kernel,
        name="wgrad",
        grid=(cols // tn,),
        out_shape=jax.ShapeDtypeStruct((width, cols), BF),
        in_specs=[pl.BlockSpec((rows, width), lambda n: (0, 0))] * 4
        + [pl.BlockSpec((rows, tn), lambda n: (0, n))] * 4,
        out_specs=pl.BlockSpec((width, tn), lambda n: (0, n)),
        scratch_shapes=[pltpu.VMEM((width, 4 * rows), BF)],
        compiler_params=pltpu.CompilerParams(vmem_limit_bytes=40 << 20),
        cost_estimate=pl.CostEstimate(
            flops=8 * rows * width * cols, bytes_accessed=8 << 20, transcendentals=0
        ),
    )(*lhs, *rhs)


CORE = [(0, 1), (1, 0), (2, 3), (3, 2)]
FAR = [(0, 2), (2, 0), (1, 3), (3, 1)]


def swap_core(v):
    return lax.ppermute(v, "tensor", CORE)


def swap_far(v):
    return lax.ppermute(v, "tensor", FAR)


def after(value, *others):
    return lax.optimization_barrier((value,) + others)[0]


def gather_rows(v):
    far = swap_far(v)
    return (v, swap_core(v), far, swap_core(far))


def scatter_rows(parts):
    far = (parts[2].astype(F32) + swap_core(parts[3]).astype(F32)).astype(BF)
    near = parts[0].astype(F32) + swap_core(parts[1]).astype(F32)
    return near + swap_far(far).astype(F32)


def sum_all(v, count):
    v = v + swap_core(v)
    v = v + swap_far(v)
    step = 1
    while step < count:
        v = v + lax.ppermute(v, "fsdp", [(i, i ^ step) for i in range(count)])
        step *= 2
    return v


def body(
    tokens,
    cotangent,
    pic_starts,
    w_qkv,
    qv_bias,
    w_out,
    out_bias,
    ln1_gain,
    ln1_bias,
    w_fc1,
    fc1_bias,
    w_fc2,
    fc2_bias,
    ln2_gain,
    ln2_bias,
):
    rows, width = tokens.shape
    groups = lax.axis_size("tensor")
    shards = lax.axis_size("fsdp")
    head_width = w_qkv.shape[2]
    hidden_width = w_fc1.shape[1]
    fsdp_rows = w_qkv.shape[0]
    rank = lax.axis_index("tensor")
    meta = jnp.concatenate([rank.astype(jnp.int32)[None], pic_starts[0]])

    def gather_w(v):
        return lax.all_gather(v, "fsdp", axis=0, tiled=True)

    def scatter_w(v):
        return lax.psum_scatter(v, "fsdp", scatter_dimension=0, tiled=True)

    qkv_full = gather_w(w_qkv.reshape(fsdp_rows, 3 * head_width))
    out_t = gather_w(w_out.T)
    fc1_full = gather_w(w_fc1)
    fc2_t = gather_w(w_fc2.T)

    inputs = tokens.astype(F32)
    unit_one, inv_one = normalize(inputs)
    normed_one = (unit_one * ln1_gain + ln1_bias).astype(BF)
    one = gather_rows(normed_one)
    bias_part = lax.dynamic_slice_in_dim(qv_bias, rank * head_width, head_width, 1)
    qkv_bias = jnp.concatenate([bias_part[0], jnp.zeros_like(bias_part[0]), bias_part[1]])
    qkv = [(nn(one[j], qkv_full) + qkv_bias).astype(BF) for j in range(4)]
    up = gather_rows(after(cotangent, one[2]))
    *att, lse = attn_fwd(meta, qkv)
    attn_sum = scatter_rows([nt(att[j], out_t).astype(BF) for j in range(4)])
    hidden_one = inputs + attn_sum + out_bias
    unit_two, inv_two = normalize(hidden_one)
    normed_two = (unit_two * ln2_gain + ln2_bias).astype(BF)
    two = gather_rows(normed_two)
    bias_hidden = lax.dynamic_slice_in_dim(fc1_bias, rank * hidden_width, hidden_width, 0)
    hid = [ffn(two[j], up[j], fc1_full, fc2_t, bias_hidden[None]) for j in range(4)]
    activated = [h[0] for h in hid]
    pre_grad = [h[1] for h in hid]
    grad_normed_two = scatter_rows([h[2] for h in hid])
    fc1_local = (hid[0][3] + hid[1][3] + hid[2][3] + hid[3][3])[0]
    back_two, gain_two_grad, shift_two_grad = normalize_back(
        grad_normed_two, unit_two, inv_two, ln2_gain
    )
    grad_out = cotangent.astype(F32)
    grad_hidden_one = grad_out + back_two
    back = gather_rows(grad_hidden_one.astype(BF))

    fc2_grad = scatter_w(wgrad(up, activated))
    fc1_grad = scatter_w(wgrad(two, pre_grad))
    out_grad = scatter_w(wgrad(back, att))

    ffn_parts = [nt(activated[j], fc2_t).astype(BF) for j in range(4)]
    ffn_sum = scatter_rows([after(part, back[2]) for part in ffn_parts])
    output = hidden_one + ffn_sum + fc2_bias

    grad_att = [nn(back[j], out_t).astype(BF) for j in range(4)]
    qkv_grad = attn_bwd(meta, qkv, grad_att, att, lse)
    grad_normed_one = scatter_rows([nt(qkv_grad[j], qkv_full).astype(BF) for j in range(4)])
    back_one, gain_one_grad, shift_one_grad = normalize_back(
        grad_normed_one, unit_one, inv_one, ln1_gain
    )
    input_grad = grad_hidden_one + back_one
    qkv_wgrad = scatter_w(wgrad(one, qkv_grad))

    spread = jnp.zeros((groups, hidden_width), F32)
    fc1_spread = lax.dynamic_update_slice(spread, fc1_local[None], (rank, rank * 0))
    early = jnp.concatenate(
        [
            fc1_spread.reshape(-1),
            jnp.sum(grad_hidden_one, axis=0),
            jnp.sum(grad_out, axis=0),
            gain_two_grad,
            shift_two_grad,
        ]
    ).reshape(-1, 128)
    early = sum_all(early, shards).reshape(-1)
    qkv_sums = sum(jnp.sum(qkv_grad[j].astype(F32), axis=0) for j in range(4))
    qv_spread = lax.dynamic_update_slice(
        jnp.zeros((2, groups, head_width), F32),
        jnp.stack([qkv_sums[:head_width], qkv_sums[2 * head_width :]])[:, None],
        (rank * 0, rank, rank * 0),
    )
    late = jnp.concatenate([qv_spread.reshape(-1), gain_one_grad, shift_one_grad]).reshape(-1, 128)
    late = sum_all(late, shards).reshape(-1)
    hid_all = groups * hidden_width
    return (
        output,
        input_grad,
        qkv_wgrad.astype(F32).reshape(fsdp_rows, 3, head_width),
        late[: 2 * width].reshape(2, width),
        out_grad.astype(F32).T,
        early[hid_all : hid_all + width],
        late[2 * width : 3 * width],
        late[3 * width : 4 * width],
        fc1_grad.astype(F32),
        early[:hid_all],
        fc2_grad.astype(F32).T,
        early[hid_all + width : hid_all + 2 * width],
        early[hid_all + 2 * width : hid_all + 3 * width],
        early[hid_all + 3 * width : hid_all + 4 * width],
    )


def solution(mesh):
    return jax.shard_map(
        body,
        mesh=mesh,
        in_specs=(
            P(("fsdp", "tensor"), None),
            P(("fsdp", "tensor"), None),
            P("fsdp", None),
            P("fsdp", None, "tensor"),
            P(),
            P("tensor", "fsdp"),
            P(),
            P(),
            P(),
            P("fsdp", "tensor"),
            P(),
            P("tensor", "fsdp"),
            P(),
            P(),
            P(),
        ),
        out_specs=(
            P(("fsdp", "tensor"), None),
            P(("fsdp", "tensor"), None),
            P("fsdp", None, "tensor"),
            P(),
            P("tensor", "fsdp"),
            P(),
            P(),
            P(),
            P("fsdp", "tensor"),
            P(),
            P("tensor", "fsdp"),
            P(),
            P(),
            P(),
        ),
        check_vma=False,
    )
```

```python
import functools
import math

import jax
import jax.numpy as jnp
from jax import lax
from jax.experimental import pallas as pl
from jax.experimental.pallas import tpu as pltpu
from jax.sharding import PartitionSpec as P

HD = 64
PIC = 256
F32 = jnp.float32
BF = jnp.bfloat16
NEG = -1e30
NORM_EPSILON = 1e-05
GELU_SCALE = math.sqrt(2.0 / math.pi)
GELU_CUBIC = 0.044715
VM = pltpu.MemorySpace.VMEM
SM = pltpu.MemorySpace.SMEM


def nn(a, b):
    return lax.dot_general(a, b, (((1,), (0,)), ((), ())), preferred_element_type=F32)


def nt(a, b):
    return lax.dot_general(a, b, (((1,), (1,)), ((), ())), preferred_element_type=F32)


def normalize(values):
    average = jnp.mean(values, axis=1, keepdims=True)
    centered = values - average
    inv_std = lax.rsqrt(jnp.mean(centered * centered, axis=1, keepdims=True) + NORM_EPSILON)
    return centered * inv_std, inv_std


def normalize_back(gradient, unit_rows, inv_std, gain_row):
    scaled = gradient * gain_row
    inner = (
        scaled
        - jnp.mean(scaled, axis=1, keepdims=True)
        - unit_rows * jnp.mean(scaled * unit_rows, axis=1, keepdims=True)
    )
    return inv_std * inner, jnp.sum(gradient * unit_rows, axis=0), jnp.sum(gradient, axis=0)


def attn_fwd_kernel(meta, qs, att0,att1,att2,att3, lse_ref, kz, qT, vT, att):
    t=meta[0]
    B=qs.shape[1]; HW=qs.shape[2]//3; NH=HW//HD; NP=NH//2
    outs=(att0,att1,att2,att3)
    for j in range(4):
        b=t^j
        kz[b]=qs[j,:,HW:2*HW]
        qT[b]=(qs[j,:,:HW]*jnp.asarray(HD**-0.5,BF)).T
        vT[b]=qs[j,:,2*HW:].T
    rowk=lax.broadcasted_iota(jnp.int32,(B,B),0)
    colq=lax.broadcasted_iota(jnp.int32,(B,B),1)
    half=lax.broadcasted_iota(jnp.int32,(2*HD,B),0)<HD
    for i in range(4):
        ps=meta[1+i]-i*B
        jj=t^i
        def pair(p,_):
            kcol=pl.multiple_of(p*2*HD,2*HD)
            qp=qT[i,pl.ds(kcol,2*HD),:]
            zero=jnp.zeros_like(qp)
            qzs=(jnp.where(half,qp,zero),jnp.where(half,zero,qp))
            os=[]
            for hh in range(2):
                ss=[]; mx=None
                for m in range(i+1):
                    s=nn(kz[m,:,pl.ds(kcol,2*HD)],qzs[hh])
                    if m==i:
                        ok=(rowk<=colq)|((rowk>=ps)&(rowk<ps+PIC)&(colq>=ps)&(colq<ps+PIC))
                        s=jnp.where(ok,s,NEG)
                    sm=jnp.max(s,axis=0,keepdims=True)
                    mx=sm if mx is None else jnp.maximum(mx,sm)
                    ss.append(s)
                l=0.; acc=0.
                for m in range(i+1):
                    e=jnp.exp(ss[m]-mx)
                    l=l+jnp.sum(e,axis=0,keepdims=True)
                    acc=acc+nn(vT[m,pl.ds(kcol+hh*HD,HD),:],e.astype(BF))
                os.append(acc*(1.0/l))
                lse_ref[jj,pl.ds(p*2+hh,1),:]=mx+jnp.log(l)
            o=jnp.concatenate(os,axis=0).astype(BF)
            att[i,:,pl.ds(kcol,2*HD)]=o.T
            return 0
        lax.fori_loop(0,NP,pair,0)
    for j in range(4): outs[j][...]=att[t^j]

def attn_fwd(meta,qs):
    B=qs.shape[1]; HW=qs.shape[2]//3; NH=HW//HD
    vm=pl.BlockSpec(memory_space=pltpu.MemorySpace.VMEM)
    return pl.pallas_call(attn_fwd_kernel,name="attn_fwd",
        out_shape=[jax.ShapeDtypeStruct((B,HW),BF)]*4+[jax.ShapeDtypeStruct((4,NH,B),F32)],
        in_specs=[pl.BlockSpec(memory_space=pltpu.MemorySpace.SMEM)]+[vm],
        out_specs=[vm]*5,
        scratch_shapes=[pltpu.VMEM((4,B,HW),BF),pltpu.VMEM((4,HW,B),BF),pltpu.VMEM((4,HW,B),BF),pltpu.VMEM((4,B,HW),BF)],
        compiler_params=pltpu.CompilerParams(vmem_limit_bytes=56<<20),
        cost_estimate=pl.CostEstimate(flops=8<<30,bytes_accessed=8<<20,transcendentals=0))(meta,qs)

def attn_bwd_kernel(meta, *refs):
    qs=refs[0]; dos=refs[1:5]; ats=refs[5:9]; lse_ref=refs[9]
    outs=refs[10:14]
    qn,kn,vn,don,qT,kT,doT,dk,dv,dqT,dl=refs[14:]
    t=meta[0]
    B=qs.shape[1]; HW=qs.shape[2]//3; NH=HW//HD; NP=NH//2
    for j in range(4):
        b=t^j
        q=qs[j,:,:HW]*jnp.asarray(HD**-0.5,BF)
        k=qs[j,:,HW:2*HW]
        do=dos[j][...]
        qn[b]=q; kn[b]=k; vn[b]=qs[j,:,2*HW:]; don[b]=do
        qT[b]=q.T; kT[b]=k.T; doT[b]=do.T
        prod=(do.astype(F32)*ats[j][...].astype(F32)).T
        for h in range(NH):
            dl[b,h:h+1,:]=jnp.sum(prod[h*HD:(h+1)*HD],axis=0,keepdims=True)
    dk[...]=jnp.zeros_like(dk); dv[...]=jnp.zeros_like(dv)
    rowk=lax.broadcasted_iota(jnp.int32,(B,B),0)
    colq=lax.broadcasted_iota(jnp.int32,(B,B),1)
    hrow=lax.broadcasted_iota(jnp.int32,(2*HD,B),0)<HD
    hcol=lax.broadcasted_iota(jnp.int32,(B,2*HD),1)<HD
    for i in range(4):
        jj=t^i
        ps=meta[1+i]-i*B
        def pair(p,_):
            kcol=pl.multiple_of(p*2*HD,2*HD)
            def two(x,m):
                z=jnp.zeros_like(x)
                return (jnp.where(m,x,z),jnp.where(m,z,x))
            qTz=two(qT[i,pl.ds(kcol,2*HD),:],hrow)
            doTz=two(doT[i,pl.ds(kcol,2*HD),:],hrow)
            qz=two(qn[i,:,pl.ds(kcol,2*HD)],hcol)
            doz=two(don[i,:,pl.ds(kcol,2*HD)],hcol)
            lse=[lse_ref[jj,pl.ds(p*2+hh,1),:] for hh in range(2)]
            dlt=[dl[i,pl.ds(p*2+hh,1),:] for hh in range(2)]
            def blk(m,carry,diag):
                kb=kn[m,:,pl.ds(kcol,2*HD)]
                vb=vn[m,:,pl.ds(kcol,2*HD)]
                ktb=kT[m,pl.ds(kcol,2*HD),:]
                dvs=0.; dks=0.; new=[]
                for hh in range(2):
                    s=nn(kb,qTz[hh])
                    if diag:
                        ok=(rowk<=colq)|((rowk>=ps)&(rowk<ps+PIC)&(colq>=ps)&(colq<ps+PIC))
                        s=jnp.where(ok,s,NEG)
                    pr=jnp.exp(s-lse[hh])
                    dp=nn(vb,doTz[hh])
                    ds=(pr*(dp-dlt[hh])).astype(BF)
                    dvs=dvs+nn(pr.astype(BF),doz[hh])
                    dks=dks+nn(ds,qz[hh])
                    new.append(carry[hh]+nn(ktb[hh*HD:(hh+1)*HD],ds))
                dv[m,:,pl.ds(kcol,2*HD)]+=dvs
                dk[m,:,pl.ds(kcol,2*HD)]+=dks
                return tuple(new)
            c=tuple(jnp.zeros((HD,B),F32) for _ in range(2))
            c=blk(i,c,True)
            c=lax.fori_loop(0,i,lambda m,c: blk(m,c,False),c) if i>0 else c
            dqT[i,pl.ds(kcol,2*HD),:]=(jnp.concatenate(c,axis=0)*(HD**-0.5)).astype(BF)
            return 0
        lax.fori_loop(0,NP,pair,0)
    for j in range(4):
        b=t^j
        outs[j][:,:HW]=dqT[b].T
        outs[j][:,HW:2*HW]=dk[b].astype(BF)
        outs[j][:,2*HW:]=dv[b].astype(BF)

def attn_bwd(meta,qs,dos,ats,lse):
    B=qs.shape[1]; HW=qs.shape[2]//3; NH=HW//HD
    vm=pl.BlockSpec(memory_space=pltpu.MemorySpace.VMEM)
    V=pltpu.VMEM
    return pl.pallas_call(attn_bwd_kernel,name="attn_bwd",
        out_shape=[jax.ShapeDtypeStruct((B,3*HW),BF)]*4,
        in_specs=[pl.BlockSpec(memory_space=pltpu.MemorySpace.SMEM)]+[vm]*10,
        out_specs=[vm]*4,
        scratch_shapes=[V((4,B,HW),BF)]*4+[V((4,HW,B),BF)]*3+[V((4,B,HW),F32)]*2+[V((4,HW,B),BF),V((4,NH,B),F32)],
        compiler_params=pltpu.CompilerParams(vmem_limit_bytes=56<<20),
        cost_estimate=pl.CostEstimate(flops=20<<30,bytes_accessed=16<<20,transcendentals=0))(meta,qs,*dos,*ats,lse)


def ffn_kernel(m_ref, g_ref, w1_ref, w2_ref, b_ref, act_ref, pg_ref, gn_ref, bg_ref, acc):
    n = pl.program_id(0)
    x = nn(m_ref[...], w1_ref[...]) + b_ref[...]
    hg = nn(g_ref[...], w2_ref[...])
    sq = x * x
    t = jnp.tanh(GELU_SCALE * (x + GELU_CUBIC * (sq * x)))
    half = 0.5 * (1.0 + t)
    act_ref[...] = (x * half).astype(BF)
    slope = half + (0.5 * GELU_SCALE) * x * (1.0 - t * t) * (1.0 + (3.0 * GELU_CUBIC) * sq)
    pg = (hg * slope).astype(BF)
    pg_ref[...] = pg
    bg_ref[...] = jnp.sum(pg.astype(F32), axis=0, keepdims=True)
    part = nt(pg, w1_ref[...])

    @pl.when(n == 0)
    def _():
        acc[...] = part

    @pl.when(n > 0)
    def _():
        acc[...] += part

    @pl.when(n == pl.num_programs(0) - 1)
    def _():
        gn_ref[...] = acc[...].astype(BF)


def ffn(m, g, weights, bias):
    rows, width = m.shape
    hid = weights.shape[1] // 2
    tn = 256
    tiles = hid // tn
    full = pl.BlockSpec((rows, width), lambda n: (0, 0))
    w1blk = pl.BlockSpec((width, tn), lambda n: (0, n))
    w2blk = pl.BlockSpec((width, tn), lambda n: (0, n + tiles))
    hblk = pl.BlockSpec((rows, tn), lambda n: (0, n))
    vec = pl.BlockSpec((1, tn), lambda n: (0, n))
    return pl.pallas_call(
        ffn_kernel,
        name="ffn",
        grid=(hid // tn,),
        out_shape=[
            jax.ShapeDtypeStruct((rows, hid), BF),
            jax.ShapeDtypeStruct((rows, hid), BF),
            jax.ShapeDtypeStruct((rows, width), BF),
            jax.ShapeDtypeStruct((1, hid), F32),
        ],
        in_specs=[full, full, w1blk, w2blk, vec],
        out_specs=[hblk, hblk, full, vec],
        scratch_shapes=[pltpu.VMEM((rows, width), F32)],
        compiler_params=pltpu.CompilerParams(vmem_limit_bytes=40 << 20),
        cost_estimate=pl.CostEstimate(
            flops=6 * rows * width * hid, bytes_accessed=8 << 20, transcendentals=rows * hid
        ),
    )(m, g, weights, weights, bias)


def wgrad_kernel(*refs):
    lhs, rhs, out, lhs_t = refs[0:4], refs[4:8], refs[8], refs[9]
    rows = lhs[0].shape[0]

    @pl.when(pl.program_id(0) == 0)
    def _():
        for j in range(4):
            lhs_t[:, j * rows : (j + 1) * rows] = lhs[j][...].T

    acc = nn(lhs_t[:, :rows], rhs[0][...])
    for j in range(1, 4):
        acc = acc + nn(lhs_t[:, j * rows : (j + 1) * rows], rhs[j][...])
    out[...] = acc.astype(BF)


def wgrad(lhs, rhs):
    rows, width = lhs[0].shape
    cols = rhs[0].shape[1]
    tn = 256
    return pl.pallas_call(
        wgrad_kernel,
        name="wgrad",
        grid=(cols // tn,),
        out_shape=jax.ShapeDtypeStruct((width, cols), BF),
        in_specs=[pl.BlockSpec((rows, width), lambda n: (0, 0))] * 4
        + [pl.BlockSpec((rows, tn), lambda n: (0, n))] * 4,
        out_specs=pl.BlockSpec((width, tn), lambda n: (0, n)),
        scratch_shapes=[pltpu.VMEM((width, 4 * rows), BF)],
        compiler_params=pltpu.CompilerParams(vmem_limit_bytes=40 << 20),
        cost_estimate=pl.CostEstimate(
            flops=8 * rows * width * cols, bytes_accessed=8 << 20, transcendentals=0
        ),
    )(*lhs, *rhs)


MESH = pl.DeviceIdType.MESH


def remote(src, dst, send, recv, where):
    return pltpu.make_async_remote_copy(
        src_ref=src, dst_ref=dst, send_sem=send, recv_sem=recv, device_id=where, device_id_type=MESH
    )


def greet(peers):
    barrier = pltpu.get_barrier_semaphore()
    for peer in peers:
        pl.semaphore_signal(barrier, inc=1, device_id=peer, device_id_type=MESH)
    pl.semaphore_wait(barrier, len(peers))


def front_kernel(
    shards, chunks, tok, wq, wo, gain, bias, qvb,
    n_out, qkv_out, wq_out, wo_out,
    nv, wqv, wov, qv, ysend, yrecv, csend, crecv, fsend, frecv,
    zqs, zqr, xqs, xqr, zos, zor, xos, xor, osem,
):
    f = lax.axis_index("fsdp")
    t = lax.axis_index("tensor")
    rows, width = tok.shape
    head_width = wo.shape[1]
    step = rows // chunks
    far = {"fsdp": f, "tensor": t ^ 2}
    sib = {"fsdp": f, "tensor": t ^ 1}
    side = {"fsdp": f ^ 1, "tensor": t}
    lines = shards // 2
    alongs = [{"fsdp": f ^ (2 * d), "tensor": t} for d in range(1, lines)]
    greet([far, sib, side] + alongs)
    started = []

    def go(copy):
        copy.start()
        started.append(copy)
        return copy

    zq, zo, xq, xo = [], [], [], []
    for d in range(1, lines):
        zq.append(go(remote(wq, wqv.at[f], zqs.at[d], zqr.at[d], alongs[d - 1])))
    xq.append(go(remote(wq, wqv.at[f], xqs.at[0], xqr.at[0], side)))
    wqv[f] = wq[...]
    wov[f] = wo[...]
    ys, cs, fs = [], [], []
    for c in range(chunks):
        part = pl.ds(c * step, step)
        values = tok[part, :].astype(F32)
        unit, _ = normalize(values)
        nv[0, part, :] = (unit * gain[...] + bias[...]).astype(BF)
        ys.append(go(remote(nv.at[0, part], nv.at[2, part], ysend.at[c], yrecv.at[c], far)))
        cs.append(go(remote(nv.at[0, part], nv.at[1, part], csend.at[c], crecv.at[c], sib)))
    for d in range(1, lines):
        zo.append(go(remote(wo, wov.at[f], zos.at[d], zor.at[d], alongs[d - 1])))
    xo.append(go(remote(wo, wov.at[f], xos.at[0], xor.at[0], side)))

    def forward_far(c):
        part = pl.ds(c * step, step)
        ys[c].wait_recv()
        fs.append(go(remote(nv.at[2, part], nv.at[3, part], fsend.at[c], frecv.at[c], sib)))

    todo = list(range(chunks))
    for d in range(1, lines):
        zq[d - 1].wait_recv()
        xq.append(go(remote(wqv.at[f ^ (2 * d)], wqv.at[f ^ (2 * d)], xqs.at[d], xqr.at[d], side)))
        if len(todo) > 1:
            forward_far(todo.pop(0))
    for d in range(1, lines):
        zo[d - 1].wait_recv()
        xo.append(go(remote(wov.at[f ^ (2 * d)], wov.at[f ^ (2 * d)], xos.at[d], xor.at[d], side)))
    for c in cs:
        c.wait_recv()
    for d in range(lines):
        xq[d].wait_recv()
    outs = [pltpu.make_async_copy(wqv, wq_out, osem.at[0])]
    outs[0].start()
    weights = wqv[...].reshape(width, 3 * head_width)
    start = pl.multiple_of(t * head_width, head_width)
    qb = qvb[0:1, pl.ds(start, head_width)]
    vb = qvb[1:2, pl.ds(start, head_width)]
    full = jnp.concatenate([qb, jnp.zeros_like(qb), vb], axis=1)

    def project(j, _):
        qv[j] = (nn(nv[j], weights) + full).astype(BF)
        return 0

    lax.fori_loop(0, 2, project, 0)
    while todo:
        forward_far(todo.pop(0))
    lax.fori_loop(2, 3, project, 0)
    for c in fs:
        c.wait_recv()
    lax.fori_loop(3, 4, project, 0)
    outs.append(pltpu.make_async_copy(nv, n_out, osem.at[1]))
    outs.append(pltpu.make_async_copy(qv, qkv_out, osem.at[2]))
    outs[1].start()
    outs[2].start()
    for d in range(lines):
        xo[d].wait_recv()
    outs.append(pltpu.make_async_copy(wov, wo_out, osem.at[3]))
    outs[3].start()
    for c in started:
        c.wait_send()
    for c in outs:
        c.wait()


def front(shards, tokens, wq, wo, gain, bias, qv_bias):
    rows, width = tokens.shape
    per, head_width = wo.shape
    lines = shards // 2
    chunks = 4
    dma = pltpu.SemaphoreType.DMA
    vm = pl.BlockSpec(memory_space=VM)
    hbm = pl.BlockSpec(memory_space=pl.ANY)
    shapes = [
        (4, rows, width), (4, rows, 3 * head_width),
        (shards, per, 3 * head_width), (shards, per, head_width),
    ]
    return pl.pallas_call(
        functools.partial(front_kernel, shards, chunks),
        name="front",
        out_shape=[jax.ShapeDtypeStruct(s, BF) for s in shapes],
        in_specs=[vm] * 6,
        out_specs=[hbm] * 4,
        scratch_shapes=[
            pltpu.VMEM(shapes[0], BF), pltpu.VMEM(shapes[2], BF),
            pltpu.VMEM(shapes[3], BF), pltpu.VMEM(shapes[1], BF),
        ]
        + [dma((chunks,))] * 6
        + [dma((lines,))] * 8
        + [dma((4,))],
        compiler_params=pltpu.CompilerParams(
            collective_id=0, has_side_effects=True, vmem_limit_bytes=40 << 20
        ),
        cost_estimate=pl.CostEstimate(flops=8 << 30, bytes_accessed=90 << 20, transcendentals=0),
    )(tokens, wq, wo, gain, bias, qv_bias)


CORE = [(0, 1), (1, 0), (2, 3), (3, 2)]
FAR = [(0, 2), (2, 0), (1, 3), (3, 1)]


def swap_core(v):
    return lax.ppermute(v, "tensor", CORE)


def swap_far(v):
    return lax.ppermute(v, "tensor", FAR)


def after(value, *others):
    return lax.optimization_barrier((value,) + others)[0]


def gather_rows(v):
    far = swap_far(v)
    return (v, swap_core(v), far, swap_core(far))


def scatter_rows(parts):
    far = (parts[2].astype(F32) + swap_core(parts[3]).astype(F32)).astype(BF)
    near = parts[0].astype(F32) + swap_core(parts[1]).astype(F32)
    return near + swap_far(far).astype(F32)


def sum_all(v, count):
    v = v + swap_core(v)
    v = v + swap_far(v)
    step = 1
    while step < count:
        v = v + lax.ppermute(v, "fsdp", [(i, i ^ step) for i in range(count)])
        step *= 2
    return v


def body(
    tokens,
    cotangent,
    pic_starts,
    w_qkv,
    qv_bias,
    w_out,
    out_bias,
    ln1_gain,
    ln1_bias,
    w_fc1,
    fc1_bias,
    w_fc2,
    fc2_bias,
    ln2_gain,
    ln2_bias,
):
    rows, width = tokens.shape
    groups = lax.axis_size("tensor")
    shards = lax.axis_size("fsdp")
    head_width = w_qkv.shape[2]
    hidden_width = w_fc1.shape[1]
    fsdp_rows = w_qkv.shape[0]
    rank = lax.axis_index("tensor")
    meta = jnp.concatenate([rank.astype(jnp.int32)[None], pic_starts[0]])

    def gather_w(v):
        return lax.all_gather(v, "fsdp", axis=0, tiled=True)

    def scatter_w(v):
        return lax.psum_scatter(v, "fsdp", scatter_dimension=0, tiled=True)

    one, qkv, qkv_full, out_t = front(
        shards,
        tokens,
        w_qkv.reshape(fsdp_rows, 3 * head_width),
        w_out.T,
        ln1_gain[None],
        ln1_bias[None],
        qv_bias,
    )
    fc_own = after(jnp.concatenate([w_fc1, w_fc2.T], axis=1), qkv)
    fc_full = gather_w(fc_own)
    qkv_full = qkv_full.reshape(width, 3 * head_width)
    out_t = out_t.reshape(width, head_width)
    inputs = tokens.astype(F32)
    unit_one, inv_one = normalize(inputs)
    up_far = swap_far(after(cotangent, qkv))
    up = (cotangent, swap_core(cotangent), up_far, swap_core(up_far))
    *att, lse = attn_fwd(meta, qkv)
    parts = [nt(att[j], out_t).astype(BF) for j in range(4)]
    parts[3] = after(parts[3], up_far)
    attn_sum = scatter_rows(parts)
    hidden_one = inputs + attn_sum + out_bias
    unit_two, inv_two = normalize(hidden_one)
    normed_two = (unit_two * ln2_gain + ln2_bias).astype(BF)
    two = gather_rows(normed_two)
    bias_hidden = lax.dynamic_slice_in_dim(fc1_bias, rank * hidden_width, hidden_width, 0)
    hid = [ffn(two[j], up[j], fc_full, bias_hidden[None]) for j in range(4)]
    activated = [h[0] for h in hid]
    pre_grad = [h[1] for h in hid]
    grad_normed_two = scatter_rows([h[2] for h in hid])
    fc1_local = (hid[0][3] + hid[1][3] + hid[2][3] + hid[3][3])[0]
    back_two, gain_two_grad, shift_two_grad = normalize_back(
        grad_normed_two, unit_two, inv_two, ln2_gain
    )
    grad_out = cotangent.astype(F32)
    grad_hidden_one = grad_out + back_two
    back = gather_rows(grad_hidden_one.astype(BF))

    bulk = scatter_w(
        jnp.concatenate([wgrad(two, pre_grad), wgrad(up, activated), wgrad(back, att)], axis=1)
    )
    fc1_grad = bulk[:, :hidden_width]
    fc2_grad = bulk[:, hidden_width : 2 * hidden_width]
    out_grad = bulk[:, 2 * hidden_width :]

    ffn_parts = [nt(activated[j], fc_full[:, hidden_width:]).astype(BF) for j in range(4)]
    ffn_sum = scatter_rows([after(part, back[2]) for part in ffn_parts])
    output = hidden_one + ffn_sum + fc2_bias

    grad_att = [nn(back[j], out_t).astype(BF) for j in range(4)]
    qkv_grad = attn_bwd(meta, qkv, grad_att, att, lse)
    grad_normed_one = scatter_rows([nt(qkv_grad[j], qkv_full).astype(BF) for j in range(4)])
    back_one, gain_one_grad, shift_one_grad = normalize_back(
        grad_normed_one, unit_one, inv_one, ln1_gain
    )
    input_grad = grad_hidden_one + back_one
    qkv_wgrad = scatter_w(wgrad([one[j] for j in range(4)], qkv_grad))

    spread = jnp.zeros((groups, hidden_width), F32)
    fc1_spread = lax.dynamic_update_slice(spread, fc1_local[None], (rank, rank * 0))
    early = jnp.concatenate(
        [
            fc1_spread.reshape(-1),
            jnp.sum(grad_hidden_one, axis=0),
            jnp.sum(grad_out, axis=0),
            gain_two_grad,
            shift_two_grad,
        ]
    ).reshape(-1, 128)
    early = sum_all(early, shards).reshape(-1)
    qkv_sums = sum(jnp.sum(qkv_grad[j].astype(F32), axis=0) for j in range(4))
    qv_spread = lax.dynamic_update_slice(
        jnp.zeros((2, groups, head_width), F32),
        jnp.stack([qkv_sums[:head_width], qkv_sums[2 * head_width :]])[:, None],
        (rank * 0, rank, rank * 0),
    )
    late = jnp.concatenate([qv_spread.reshape(-1), gain_one_grad, shift_one_grad]).reshape(-1, 128)
    late = sum_all(late, shards).reshape(-1)
    hid_all = groups * hidden_width
    return (
        output,
        input_grad,
        qkv_wgrad.astype(F32).reshape(fsdp_rows, 3, head_width),
        late[: 2 * width].reshape(2, width),
        out_grad.astype(F32).T,
        early[hid_all : hid_all + width],
        late[2 * width : 3 * width],
        late[3 * width : 4 * width],
        fc1_grad.astype(F32),
        early[:hid_all],
        fc2_grad.astype(F32).T,
        early[hid_all + width : hid_all + 2 * width],
        early[hid_all + 2 * width : hid_all + 3 * width],
        early[hid_all + 3 * width : hid_all + 4 * width],
    )


def solution(mesh):
    return jax.shard_map(
        body,
        mesh=mesh,
        in_specs=(
            P(("fsdp", "tensor"), None),
            P(("fsdp", "tensor"), None),
            P("fsdp", None),
            P("fsdp", None, "tensor"),
            P(),
            P("tensor", "fsdp"),
            P(),
            P(),
            P(),
            P("fsdp", "tensor"),
            P(),
            P("tensor", "fsdp"),
            P(),
            P(),
            P(),
        ),
        out_specs=(
            P(("fsdp", "tensor"), None),
            P(("fsdp", "tensor"), None),
            P("fsdp", None, "tensor"),
            P(),
            P("tensor", "fsdp"),
            P(),
            P(),
            P(),
            P("fsdp", "tensor"),
            P(),
            P("tensor", "fsdp"),
            P(),
            P(),
            P(),
        ),
        check_vma=False,
    )
```

```python
import functools
import math

import jax
import jax.numpy as jnp
from jax import lax
from jax.experimental import pallas as pl
from jax.experimental.pallas import tpu as pltpu
from jax.sharding import PartitionSpec as P

HD = 64
PIC = 256
F32 = jnp.float32
BF = jnp.bfloat16
NEG = -1e30
NORM_EPSILON = 1e-05
GELU_SCALE = math.sqrt(2.0 / math.pi)
GELU_CUBIC = 0.044715
VM = pltpu.MemorySpace.VMEM
SM = pltpu.MemorySpace.SMEM


def nn(a, b):
    return lax.dot_general(a, b, (((1,), (0,)), ((), ())), preferred_element_type=F32)


def nt(a, b):
    return lax.dot_general(a, b, (((1,), (1,)), ((), ())), preferred_element_type=F32)


def normalize(values):
    average = jnp.mean(values, axis=1, keepdims=True)
    centered = values - average
    inv_std = lax.rsqrt(jnp.mean(centered * centered, axis=1, keepdims=True) + NORM_EPSILON)
    return centered * inv_std, inv_std


def normalize_back(gradient, unit_rows, inv_std, gain_row):
    scaled = gradient * gain_row
    inner = (
        scaled
        - jnp.mean(scaled, axis=1, keepdims=True)
        - unit_rows * jnp.mean(scaled * unit_rows, axis=1, keepdims=True)
    )
    return inv_std * inner, jnp.sum(gradient * unit_rows, axis=0), jnp.sum(gradient, axis=0)


def attn_fwd_kernel(meta, qs, out, lse_ref, kz, qT, vT, att):
    t=meta[0]
    B=qs.shape[1]; HW=qs.shape[2]//3; NH=HW//HD; NP=NH//2
    for j in range(4):
        b=t^j
        kz[b]=qs[j,:,HW:2*HW]
        qT[b]=(qs[j,:,:HW]*jnp.asarray(HD**-0.5,BF)).T
        vT[b]=qs[j,:,2*HW:].T
    rowk=lax.broadcasted_iota(jnp.int32,(B,B),0)
    colq=lax.broadcasted_iota(jnp.int32,(B,B),1)
    half=lax.broadcasted_iota(jnp.int32,(2*HD,B),0)<HD
    for i in range(4):
        ps=meta[1+i]-i*B
        jj=t^i
        def pair(p,_):
            kcol=pl.multiple_of(p*2*HD,2*HD)
            qp=qT[i,pl.ds(kcol,2*HD),:]
            zero=jnp.zeros_like(qp)
            qzs=(jnp.where(half,qp,zero),jnp.where(half,zero,qp))
            os=[]
            for hh in range(2):
                ss=[]; mx=None
                for m in range(i+1):
                    s=nn(kz[m,:,pl.ds(kcol,2*HD)],qzs[hh])
                    if m==i:
                        ok=(rowk<=colq)|((rowk>=ps)&(rowk<ps+PIC)&(colq>=ps)&(colq<ps+PIC))
                        s=jnp.where(ok,s,NEG)
                    sm=jnp.max(s,axis=0,keepdims=True)
                    mx=sm if mx is None else jnp.maximum(mx,sm)
                    ss.append(s)
                l=0.; acc=0.
                for m in range(i+1):
                    e=jnp.exp(ss[m]-mx)
                    l=l+jnp.sum(e,axis=0,keepdims=True)
                    acc=acc+nn(vT[m,pl.ds(kcol+hh*HD,HD),:],e.astype(BF))
                os.append(acc*(1.0/l))
                lse_ref[jj,pl.ds(p*2+hh,1),:]=mx+jnp.log(l)
            o=jnp.concatenate(os,axis=0).astype(BF)
            att[i,:,pl.ds(kcol,2*HD)]=o.T
            return 0
        lax.fori_loop(0,NP,pair,0)
    for j in range(4): out[j]=att[t^j]

def attn_fwd(meta,qs):
    B=qs.shape[1]; HW=qs.shape[2]//3; NH=HW//HD
    vm=pl.BlockSpec(memory_space=pltpu.MemorySpace.VMEM)
    return pl.pallas_call(attn_fwd_kernel,name="attn_fwd",
        out_shape=[jax.ShapeDtypeStruct((4,B,HW),BF)]+[jax.ShapeDtypeStruct((4,NH,B),F32)],
        in_specs=[pl.BlockSpec(memory_space=pltpu.MemorySpace.SMEM)]+[vm],
        out_specs=[vm]*2,
        scratch_shapes=[pltpu.VMEM((4,B,HW),BF),pltpu.VMEM((4,HW,B),BF),pltpu.VMEM((4,HW,B),BF),pltpu.VMEM((4,B,HW),BF)],
        compiler_params=pltpu.CompilerParams(vmem_limit_bytes=56<<20),
        cost_estimate=pl.CostEstimate(flops=8<<30,bytes_accessed=8<<20,transcendentals=0))(meta,qs)

def attn_bwd_kernel(meta, *refs):
    qs,dos,ats,lse_ref,out=refs[:5]
    qn,kn,vn,don,qT,kT,doT,dk,dv,dqT,dl=refs[5:]
    t=meta[0]
    B=qs.shape[1]; HW=qs.shape[2]//3; NH=HW//HD; NP=NH//2
    for j in range(4):
        b=t^j
        q=qs[j,:,:HW]*jnp.asarray(HD**-0.5,BF)
        k=qs[j,:,HW:2*HW]
        do=dos[j]
        qn[b]=q; kn[b]=k; vn[b]=qs[j,:,2*HW:]; don[b]=do
        qT[b]=q.T; kT[b]=k.T; doT[b]=do.T
        prod=(do.astype(F32)*ats[j].astype(F32)).T
        for h in range(NH):
            dl[b,h:h+1,:]=jnp.sum(prod[h*HD:(h+1)*HD],axis=0,keepdims=True)
    dk[...]=jnp.zeros_like(dk); dv[...]=jnp.zeros_like(dv)
    rowk=lax.broadcasted_iota(jnp.int32,(B,B),0)
    colq=lax.broadcasted_iota(jnp.int32,(B,B),1)
    hrow=lax.broadcasted_iota(jnp.int32,(2*HD,B),0)<HD
    hcol=lax.broadcasted_iota(jnp.int32,(B,2*HD),1)<HD
    for i in range(4):
        jj=t^i
        ps=meta[1+i]-i*B
        def pair(p,_):
            kcol=pl.multiple_of(p*2*HD,2*HD)
            def two(x,m):
                z=jnp.zeros_like(x)
                return (jnp.where(m,x,z),jnp.where(m,z,x))
            qTz=two(qT[i,pl.ds(kcol,2*HD),:],hrow)
            doTz=two(doT[i,pl.ds(kcol,2*HD),:],hrow)
            qz=two(qn[i,:,pl.ds(kcol,2*HD)],hcol)
            doz=two(don[i,:,pl.ds(kcol,2*HD)],hcol)
            lse=[lse_ref[jj,pl.ds(p*2+hh,1),:] for hh in range(2)]
            dlt=[dl[i,pl.ds(p*2+hh,1),:] for hh in range(2)]
            def blk(m,carry,diag):
                kb=kn[m,:,pl.ds(kcol,2*HD)]
                vb=vn[m,:,pl.ds(kcol,2*HD)]
                ktb=kT[m,pl.ds(kcol,2*HD),:]
                dvs=0.; dks=0.; new=[]
                for hh in range(2):
                    s=nn(kb,qTz[hh])
                    if diag:
                        ok=(rowk<=colq)|((rowk>=ps)&(rowk<ps+PIC)&(colq>=ps)&(colq<ps+PIC))
                        s=jnp.where(ok,s,NEG)
                    pr=jnp.exp(s-lse[hh])
                    dp=nn(vb,doTz[hh])
                    ds=(pr*(dp-dlt[hh])).astype(BF)
                    dvs=dvs+nn(pr.astype(BF),doz[hh])
                    dks=dks+nn(ds,qz[hh])
                    new.append(carry[hh]+nn(ktb[hh*HD:(hh+1)*HD],ds))
                dv[m,:,pl.ds(kcol,2*HD)]+=dvs
                dk[m,:,pl.ds(kcol,2*HD)]+=dks
                return tuple(new)
            c=tuple(jnp.zeros((HD,B),F32) for _ in range(2))
            c=blk(i,c,True)
            c=lax.fori_loop(0,i,lambda m,c: blk(m,c,False),c) if i>0 else c
            dqT[i,pl.ds(kcol,2*HD),:]=(jnp.concatenate(c,axis=0)*(HD**-0.5)).astype(BF)
            return 0
        lax.fori_loop(0,NP,pair,0)
    for j in range(4):
        b=t^j
        out[j,:,:HW]=dqT[b].T
        out[j,:,HW:2*HW]=dk[b].astype(BF)
        out[j,:,2*HW:]=dv[b].astype(BF)

def attn_bwd(meta,qs,dos,ats,lse):
    B=qs.shape[1]; HW=qs.shape[2]//3; NH=HW//HD
    vm=pl.BlockSpec(memory_space=pltpu.MemorySpace.VMEM)
    V=pltpu.VMEM
    return pl.pallas_call(attn_bwd_kernel,name="attn_bwd",
        out_shape=[jax.ShapeDtypeStruct((4,B,3*HW),BF)],
        in_specs=[pl.BlockSpec(memory_space=pltpu.MemorySpace.SMEM)]+[vm]*4,
        out_specs=[vm],
        scratch_shapes=[V((4,B,HW),BF)]*4+[V((4,HW,B),BF)]*3+[V((4,B,HW),F32)]*2+[V((4,HW,B),BF),V((4,NH,B),F32)],
        compiler_params=pltpu.CompilerParams(vmem_limit_bytes=56<<20),
        cost_estimate=pl.CostEstimate(flops=20<<30,bytes_accessed=16<<20,transcendentals=0))(meta,qs,dos,ats,lse)[0]


MESH = pl.DeviceIdType.MESH


def remote(src, dst, send, recv, where):
    return pltpu.make_async_remote_copy(
        src_ref=src, dst_ref=dst, send_sem=send, recv_sem=recv, device_id=where, device_id_type=MESH
    )


def greet(peers):
    barrier = pltpu.get_barrier_semaphore()
    for peer in peers:
        pl.semaphore_signal(barrier, inc=1, device_id=peer, device_id_type=MESH)
    pl.semaphore_wait(barrier, len(peers))


def front_kernel(
    shards, chunks, tok, wq, wo, gain, bias, qvb,
    n_out, qkv_out, wq_out, wo_out,
    nv, wqv, wov, qv, ysend, yrecv, csend, crecv, fsend, frecv,
    zqs, zqr, xqs, xqr, zos, zor, xos, xor, osem,
):
    f = lax.axis_index("fsdp")
    t = lax.axis_index("tensor")
    rows, width = tok.shape
    head_width = wo.shape[1]
    step = rows // chunks
    far = {"fsdp": f, "tensor": t ^ 2}
    sib = {"fsdp": f, "tensor": t ^ 1}
    side = {"fsdp": f ^ 1, "tensor": t}
    lines = shards // 2
    alongs = [{"fsdp": f ^ (2 * d), "tensor": t} for d in range(1, lines)]
    greet([far, sib, side] + alongs)
    started = []

    def go(copy):
        copy.start()
        started.append(copy)
        return copy

    zq, zo, xq, xo = [], [], [], []
    for d in range(1, lines):
        zq.append(go(remote(wq, wqv.at[f], zqs.at[d], zqr.at[d], alongs[d - 1])))
    xq.append(go(remote(wq, wqv.at[f], xqs.at[0], xqr.at[0], side)))
    wqv[f] = wq[...]
    wov[f] = wo[...]
    ys, cs, fs = [], [], []
    for c in range(chunks):
        part = pl.ds(c * step, step)
        values = tok[part, :].astype(F32)
        unit, _ = normalize(values)
        nv[0, part, :] = (unit * gain[...] + bias[...]).astype(BF)
        ys.append(go(remote(nv.at[0, part], nv.at[2, part], ysend.at[c], yrecv.at[c], far)))
        cs.append(go(remote(nv.at[0, part], nv.at[1, part], csend.at[c], crecv.at[c], sib)))
    for d in range(1, lines):
        zo.append(go(remote(wo, wov.at[f], zos.at[d], zor.at[d], alongs[d - 1])))
    xo.append(go(remote(wo, wov.at[f], xos.at[0], xor.at[0], side)))

    def forward_far(c):
        part = pl.ds(c * step, step)
        ys[c].wait_recv()
        fs.append(go(remote(nv.at[2, part], nv.at[3, part], fsend.at[c], frecv.at[c], sib)))

    todo = list(range(chunks))
    for d in range(1, lines):
        zq[d - 1].wait_recv()
        xq.append(go(remote(wqv.at[f ^ (2 * d)], wqv.at[f ^ (2 * d)], xqs.at[d], xqr.at[d], side)))
        if len(todo) > 1:
            forward_far(todo.pop(0))
    for d in range(1, lines):
        zo[d - 1].wait_recv()
        xo.append(go(remote(wov.at[f ^ (2 * d)], wov.at[f ^ (2 * d)], xos.at[d], xor.at[d], side)))
    for c in cs:
        c.wait_recv()
    for d in range(lines):
        xq[d].wait_recv()
    outs = [pltpu.make_async_copy(wqv, wq_out, osem.at[0])]
    outs[0].start()
    weights = wqv[...].reshape(width, 3 * head_width)
    start = pl.multiple_of(t * head_width, head_width)
    qb = qvb[0:1, pl.ds(start, head_width)]
    vb = qvb[1:2, pl.ds(start, head_width)]
    full = jnp.concatenate([qb, jnp.zeros_like(qb), vb], axis=1)

    def project(j, _):
        qv[j] = (nn(nv[j], weights) + full).astype(BF)
        return 0

    lax.fori_loop(0, 2, project, 0)
    while todo:
        forward_far(todo.pop(0))
    lax.fori_loop(2, 3, project, 0)
    for c in fs:
        c.wait_recv()
    lax.fori_loop(3, 4, project, 0)
    outs.append(pltpu.make_async_copy(nv, n_out, osem.at[1]))
    outs.append(pltpu.make_async_copy(qv, qkv_out, osem.at[2]))
    outs[1].start()
    outs[2].start()
    for d in range(lines):
        xo[d].wait_recv()
    outs.append(pltpu.make_async_copy(wov, wo_out, osem.at[3]))
    outs[3].start()
    for c in started:
        c.wait_send()
    for c in outs:
        c.wait()


def front(shards, tokens, wq, wo, gain, bias, qv_bias):
    rows, width = tokens.shape
    per, head_width = wo.shape
    lines = shards // 2
    chunks = 4
    dma = pltpu.SemaphoreType.DMA
    vm = pl.BlockSpec(memory_space=VM)
    hbm = pl.BlockSpec(memory_space=pl.ANY)
    shapes = [
        (4, rows, width), (4, rows, 3 * head_width),
        (shards, per, 3 * head_width), (shards, per, head_width),
    ]
    return pl.pallas_call(
        functools.partial(front_kernel, shards, chunks),
        name="front",
        out_shape=[jax.ShapeDtypeStruct(s, BF) for s in shapes],
        in_specs=[vm] * 6,
        out_specs=[hbm] * 4,
        scratch_shapes=[
            pltpu.VMEM(shapes[0], BF), pltpu.VMEM(shapes[2], BF),
            pltpu.VMEM(shapes[3], BF), pltpu.VMEM(shapes[1], BF),
        ]
        + [dma((chunks,))] * 6
        + [dma((lines,))] * 8
        + [dma((4,))],
        compiler_params=pltpu.CompilerParams(
            collective_id=0, has_side_effects=True, vmem_limit_bytes=40 << 20
        ),
        cost_estimate=pl.CostEstimate(flops=8 << 30, bytes_accessed=90 << 20, transcendentals=0),
    )(tokens, wq, wo, gain, bias, qv_bias)


def middle_kernel(
    shards, pre, chunks,
    att, out_t, tok, cot, up_far, own, *rest,
):
    shard_in = rest[: 1 + len(pre)]
    (
        gain, bias, out_bias, fc_bias,
        hid_out, ghid_out, back_out, grad_out, part_far, part_near, vec,
        wfc, wt, ot, upv, twov, actv, pgv, backv,
        s1, r1, a1, q1, near, hv, stage,
        s1s, s1r, y1s, y1r, c2s, c2r, y2s, y2r, f2s, f2r,
        s3s, s3r, y3s, y3r, c4s, c4r, y4s, y4r, f4s, f4r,
        s5s, s5r, ups, upr, lsem, zs, zr, xs, xr, osem, gsem,
    ) = rest[1 + len(pre):]
    f = lax.axis_index("fsdp")
    t = lax.axis_index("tensor")
    rows, width = tok.shape
    per = own.shape[0]
    hid = own.shape[1] // 2
    step = rows // chunks
    lines = shards // 2
    far = {"fsdp": f, "tensor": t ^ 2}
    sib = {"fsdp": f, "tensor": t ^ 1}
    side = {"fsdp": f ^ 1, "tensor": t}
    direct = [d for d in range(1, lines) if d not in pre]
    alongs = {d: {"fsdp": f ^ (2 * d), "tensor": t} for d in direct}
    greet([far, sib, side] + [alongs[d] for d in direct])
    sends = []

    def go(copy):
        copy.start()
        sends.append(copy)
        return copy

    def part(c):
        return pl.ds(c * step, step)

    halves = (pl.ds(0, hid), pl.ds(hid, hid))
    local = []
    for n, (src, slot) in enumerate(
        [(own, f), (shard_in[0], f ^ 1)] + [(shard_in[1 + i], f ^ (2 * d)) for i, d in enumerate(pre)]
    ):
        local.append(pltpu.make_async_copy(src, wfc.at[slot], lsem.at[n]))
    local.append(pltpu.make_async_copy(cot, upv.at[0], lsem.at[len(pre) + 2]))
    local.append(pltpu.make_async_copy(up_far, upv.at[2], lsem.at[len(pre) + 3]))
    for c in local:
        c.start()
    xf = {}
    zf = {}
    for h in range(2):
        for d in direct:
            zf[d, h] = go(
                remote(own.at[:, halves[h]], wfc.at[f, :, halves[h]], zs.at[h, d], zr.at[h, d], alongs[d])
            )

    def forward_pre(h):
        for i, d in enumerate(pre):
            slot = f ^ (2 * d)
            xf[d, h] = go(
                remote(
                    shard_in[1 + i].at[:, halves[h]], wfc.at[slot, :, halves[h]],
                    xs.at[h, d], xr.at[h, d], side,
                )
            )

    def forward_direct(h):
        for d in direct:
            zf[d, h].wait_recv()
            slot = f ^ (2 * d)
            xf[d, h] = go(
                remote(
                    wfc.at[slot, :, halves[h]], wfc.at[slot, :, halves[h]],
                    xs.at[h, d], xr.at[h, d], side,
                )
            )

    forward_pre(0)
    ot[...] = out_t[...].T
    first, second, third = [], [], []
    for c in range(chunks):
        s1[0, part(c), :] = nn(att[3, part(c), :], ot[...]).astype(BF)
        first.append(go(remote(s1.at[0, part(c)], r1.at[0, part(c)], s1s.at[0, c], s1r.at[0, c], sib)))
    for c in range(chunks):
        mine = nn(att[2, part(c), :], ot[...])
        first[c].wait_recv()
        a1[0, part(c), :] = (mine + r1[0, part(c), :].astype(F32)).astype(BF)
        second.append(go(remote(a1.at[0, part(c)], q1.at[0, part(c)], y1s.at[c], y1r.at[c], far)))
    for c in range(chunks):
        s1[1, part(c), :] = nn(att[1, part(c), :], ot[...]).astype(BF)
        third.append(go(remote(s1.at[1, part(c)], r1.at[1, part(c)], s1s.at[1, c], s1r.at[1, c], sib)))
    up_copies = [
        go(remote(cot, upv.at[1], ups.at[0], upr.at[0], sib)),
        go(remote(up_far, upv.at[3], ups.at[1], upr.at[1], sib)),
    ]
    for c in range(chunks):
        mine = nn(att[0, part(c), :], ot[...])
        third[c].wait_recv()
        near[part(c), :] = mine + r1[1, part(c), :].astype(F32)
    vec[...] = jnp.zeros_like(vec)
    forward_direct(0)
    forward_pre(1)
    ag_far, ag_sib = [], []
    for c in range(chunks):
        second[c].wait_recv()
        hidden = (
            tok[part(c), :].astype(F32)
            + near[part(c), :]
            + q1[0, part(c), :].astype(F32)
            + out_bias[...]
        )
        hv[part(c), :] = hidden
        unit, _ = normalize(hidden)
        twov[0, part(c), :] = (unit * gain[...] + bias[...]).astype(BF)
        ag_far.append(go(remote(twov.at[0, part(c)], twov.at[2, part(c)], y2s.at[c], y2r.at[c], far)))
        ag_sib.append(go(remote(twov.at[0, part(c)], twov.at[1, part(c)], c2s.at[c], c2r.at[c], sib)))
        if c == 0:
            forward_direct(1)
    outs = [pltpu.make_async_copy(hv, hid_out, osem.at[0])]
    outs[0].start()
    for c in local:
        c.wait()
    for h in range(2):
        xo = [xf[d, h] for d in pre] + [xf[d, h] for d in direct]
        for c in xo:
            c.wait_recv()

        def flip(s, _, h=h):
            wt[pl.ds(h * hid, hid), pl.ds(pl.multiple_of(s * per, per), per)] = wfc[s, :, halves[h]].T
            return 0

        if per % 128 == 0:
            lax.fori_loop(0, shards, flip, 0)
        else:
            wt[pl.ds(h * hid, hid), :] = wfc[:, :, halves[h]].reshape(width, hid).T
    for c in up_copies:
        c.wait_recv()
    for c in ag_sib:
        c.wait_recv()
    start = pl.multiple_of(t * hid, hid)
    tile = hid // 2

    def feed(j, at):
        block = pl.ds(pl.multiple_of(at * step, step), step)
        two = twov[j, block, :]
        up = upv[j, block, :]
        total = None
        for n in range(2):
            cols = pl.ds(n * tile, tile)
            x = nn(two, wfc[:, :, cols].reshape(width, tile))
            x = x + fc_bias[:, pl.ds(pl.multiple_of(start + n * tile, tile), tile)]
            hg = nn(up, wfc[:, :, pl.ds(hid + n * tile, tile)].reshape(width, tile))
            sq = x * x
            th = jnp.tanh(GELU_SCALE * (x + GELU_CUBIC * (sq * x)))
            half = 0.5 * (1.0 + th)
            actv[j, block, cols] = (x * half).astype(BF)
            slope = half + (0.5 * GELU_SCALE) * x * (1.0 - th * th) * (1.0 + (3.0 * GELU_CUBIC) * sq)
            pg = (hg * slope).astype(BF)
            pgv[j, block, cols] = pg
            vec[0:1, cols] += jnp.sum(pg.astype(F32), axis=0, keepdims=True)
            term = nn(pg, wt[cols, :])
            total = term if total is None else total + term
        return total

    def copies(c):
        block = pl.ds(pl.multiple_of(c * step, step), step)
        return (
            remote(twov.at[0, block], twov.at[2, block], y2s.at[c], y2r.at[c], far),
            remote(twov.at[2, block], twov.at[3, block], f2s.at[c], f2r.at[c], sib),
            remote(a1.at[1, block], q1.at[1, block], y3s.at[c], y3r.at[c], far),
        )

    def core_copy(k, c):
        block = pl.ds(pl.multiple_of(c * step, step), step)
        return remote(s1.at[2 + k, block], r1.at[2 + k, block], s3s.at[k, c], s3r.at[k, c], sib)

    def chunk(c, _):
        block = pl.ds(pl.multiple_of(c * step, step), step)
        got, fwd, send2 = copies(c)
        got.wait_recv()
        fwd.start()
        fwd.wait_recv()

        def pair(k, _):
            give = core_copy(k, c)

            def one(i, _):
                total = feed(3 - 2 * k - i, c)

                @pl.when(i == 0)
                def _():
                    s1[2 + k, block, :] = total.astype(BF)
                    give.start()

                @pl.when(i == 1)
                def _():
                    near[block, :] = total

                return 0

            lax.fori_loop(0, 2, one, 0)

            @pl.when(k == 0)
            def _():
                give.wait_recv()
                a1[1, block, :] = (near[block, :] + r1[2, block, :].astype(F32)).astype(BF)
                send2.start()

            return 0

        lax.fori_loop(0, 2, pair, 0)
        return 0

    lax.fori_loop(0, chunks, chunk, 0)
    b_far, b_sib = [], []
    for c in range(chunks):
        _, _, send2 = copies(c)
        core_copy(1, c).wait_recv()
        send2.wait_recv()
        gn = near[part(c), :] + r1[3, part(c), :].astype(F32) + q1[1, part(c), :].astype(F32)
        unit, inv = normalize(hv[part(c), :])
        back, g_sum, b_sum = normalize_back(gn, unit, inv, gain[...])
        cots = upv[0, part(c), :].astype(F32)
        ghid = cots + back
        near[part(c), :] = ghid
        backv[0, part(c), :] = ghid.astype(BF)
        b_far.append(go(remote(backv.at[0, part(c)], backv.at[2, part(c)], y4s.at[c], y4r.at[c], far)))
        b_sib.append(go(remote(backv.at[0, part(c)], backv.at[1, part(c)], c4s.at[c], c4r.at[c], sib)))
        vec[1:2, :] += g_sum[None]
        vec[2:3, :] += b_sum[None]
        vec[3:4, :] += jnp.sum(ghid, axis=0, keepdims=True)
        vec[4:5, :] += jnp.sum(cots, axis=0, keepdims=True)
    outs.append(pltpu.make_async_copy(near, ghid_out, osem.at[1]))
    outs[1].start()

    for c in range(chunks):
        first[c].wait_send()
        third[c].wait_send()
        core_copy(0, c).wait_send()
        core_copy(1, c).wait_send()
    for k, slot in ((0, 0), (1, 1)):
        def give(c, _, j=3 - 2 * k, slot=slot):
            block = pl.ds(pl.multiple_of(c * step, step), step)
            s1[slot, block, :] = nn(actv[j, block, :], wt[hid:, :]).astype(BF)
            return 0

        lax.fori_loop(0, chunks, give, 0)
        given = go(remote(s1.at[slot], r1.at[slot], s5s.at[slot], s5r.at[slot], sib))

        def keep(c, _, j=2 - 2 * k, slot=slot):
            block = pl.ds(pl.multiple_of(c * step, step), step)
            s1[2 + slot, block, :] = nn(actv[j, block, :], wt[hid:, :]).astype(BF)
            return 0

        lax.fori_loop(0, chunks, keep, 0)
        given.wait_recv()
        summed = s1.at[2 + slot]
        summed[...] = (summed[...].astype(F32) + r1[slot].astype(F32)).astype(BF)
        outs.append(pltpu.make_async_copy(summed, part_near if k else part_far, osem.at[2 + k]))
        outs[-1].start()

    span = 256
    for k, (left, right) in enumerate(((upv, actv), (twov, pgv))):
        def grad(n, _, k=k, left=left, right=right):
            cols = pl.ds(pl.multiple_of(n * span, span), span)
            acc = None
            for j in range(4):
                term = nn(left[j, :, cols].T, right[j])
                acc = term if acc is None else acc + term
            slot = lax.rem(n, 2)
            target = grad_out.at[cols, pl.ds((1 - k) * hid, hid)]
            copy = pltpu.make_async_copy(stage.at[slot], target, gsem.at[slot])

            if k == 0:
                @pl.when(n >= 2)
                def _():
                    copy.wait()
            else:
                copy.wait()
            stage[slot] = acc.astype(BF)
            copy.start()
            return 0

        lax.fori_loop(0, width // span, grad, 0)
    for slot in range(2):
        pltpu.make_async_copy(stage.at[slot], grad_out.at[pl.ds(0, span), pl.ds(0, hid)], gsem.at[slot]).wait()
    fwds = []
    for c in range(chunks):
        b_far[c].wait_recv()
        fwds.append(go(remote(backv.at[2, part(c)], backv.at[3, part(c)], f4s.at[c], f4r.at[c], sib)))
    for c in b_sib + fwds:
        c.wait_recv()
    outs.append(pltpu.make_async_copy(backv, back_out, osem.at[4]))
    outs[-1].start()
    for c in sends:
        if not any(c is other for other in first + third):
            c.wait_send()
    for c in range(chunks):
        _, fwd, send2 = copies(c)
        fwd.wait_send()
        send2.wait_send()
    for c in outs:
        c.wait()


def middle(shards, pre, att, out_t, tok, cot, up_far, own, shard_in, gain, bias, out_bias, fc_bias):
    rows, width = tok.shape
    per, hid2 = own.shape
    hid = hid2 // 2
    head_width = out_t.shape[1]
    lines = shards // 2
    chunks = 2
    step = rows // chunks
    dma = pltpu.SemaphoreType.DMA
    vm = pl.BlockSpec(memory_space=VM)
    hbm = pl.BlockSpec(memory_space=pl.ANY)
    full = (4, rows, width)
    one = (rows, width)
    V = pltpu.VMEM
    sems = [
        (2, chunks), (2, chunks), (chunks,), (chunks,), (chunks,), (chunks,),
        (chunks,), (chunks,), (chunks,), (chunks,),
        (2, chunks), (2, chunks), (chunks,), (chunks,), (chunks,), (chunks,),
        (chunks,), (chunks,), (chunks,), (chunks,),
        (2,), (2,), (2,), (2,), (len(pre) + 4,),
        (2, lines), (2, lines), (2, lines), (2, lines), (5,), (2,),
    ]
    return pl.pallas_call(
        functools.partial(middle_kernel, shards, pre, chunks),
        name="middle",
        out_shape=[
            jax.ShapeDtypeStruct(one, F32),
            jax.ShapeDtypeStruct(one, F32),
            jax.ShapeDtypeStruct(full, BF),
            jax.ShapeDtypeStruct((width, 2 * hid), BF),
            jax.ShapeDtypeStruct(one, BF),
            jax.ShapeDtypeStruct(one, BF),
            jax.ShapeDtypeStruct((8, width), F32),
        ],
        in_specs=[vm, vm, vm, hbm, hbm, hbm] + [hbm] * len(shard_in) + [vm] * 4,
        out_specs=[hbm] * 6 + [vm],
        scratch_shapes=[
            V((shards, per, 2 * hid), BF), V((2 * hid, width), BF), V((head_width, width), BF),
            V(full, BF), V(full, BF), V((4, rows, hid), BF), V((4, rows, hid), BF), V(full, BF),
            V(full, BF), V(full, BF), V((2, rows, width), BF), V((2, rows, width), BF),
            V(one, F32), V(one, F32), V((2, 256, hid), BF),
        ]
        + [dma(s) for s in sems],
        compiler_params=pltpu.CompilerParams(
            collective_id=1, has_side_effects=True, vmem_limit_bytes=60 << 20
        ),
        cost_estimate=pl.CostEstimate(flops=60 << 30, bytes_accessed=200 << 20, transcendentals=0),
    )(att, out_t, tok, cot, up_far, own, *shard_in, gain, bias, out_bias, fc_bias)


def last_kernel(
    shards, chunks,
    dqkv, weights, one_in, back_in, att_in, tok_in, ghid_in, vec, gain, bias,
    tok_out, w_out_ref, small_out,
    onev, backv, attv, tokv, ghidv, wt, s1, r1, a1, q1, near, grads, keep, rx, sz, rz, wsum,
    stats, lv, rv1, sv, rv2, gv,
    lsem, s1s, s1r, y1s, y1r, xs, xr, zs, zr, v1s, v1r, v2s, v2r, v3s, v3r, osem,
):
    f = lax.axis_index("fsdp")
    t = lax.axis_index("tensor")
    _, rows, width = onev.shape
    head_width = attv.shape[2]
    per = width // shards
    lines = shards // 2
    step = rows // chunks
    z = f // 2
    x = lax.rem(f, 2)
    far = {"fsdp": f, "tensor": t ^ 2}
    sib = {"fsdp": f, "tensor": t ^ 1}
    side = {"fsdp": f ^ 1, "tensor": t}
    mates = [{"fsdp": f, "tensor": t ^ j} for j in range(1, 4)]
    others = [{"fsdp": f ^ e, "tensor": t} for e in range(1, shards)]
    greet(mates + others)
    sends = []

    def go(copy):
        copy.start()
        sends.append(copy)
        return copy

    def part(c):
        return pl.ds(c * step, step)

    local = [
        pltpu.make_async_copy(src, dst, lsem.at[n])
        for n, (src, dst) in enumerate(
            [(one_in, onev), (back_in, backv), (att_in, attv), (tok_in, tokv), (ghid_in, ghidv)]
        )
    ]
    for c in local:
        c.start()
    wt[...] = weights[...].T
    stats[...] = jnp.zeros_like(stats)
    local[0].wait()

    def norm_grad(j, c):
        mine = dqkv[j, part(c), :]
        total = nn(mine, wt[...])
        stats[0:1, :width] += jnp.sum(total * onev[j, part(c), :].astype(F32), axis=0, keepdims=True)
        stats[1:2, :width] += jnp.sum(total, axis=0, keepdims=True)
        stats[2:3, : 3 * head_width] += jnp.sum(mine.astype(F32), axis=0, keepdims=True)
        return total

    first, second, third = [], [], []
    for c in range(chunks):
        s1[0, part(c), :] = norm_grad(3, c).astype(BF)
        first.append(go(remote(s1.at[0, part(c)], r1.at[0, part(c)], s1s.at[0, c], s1r.at[0, c], sib)))
    for c in range(chunks):
        mine = norm_grad(2, c)
        first[c].wait_recv()
        a1[part(c), :] = (mine + r1[0, part(c), :].astype(F32)).astype(BF)
        second.append(go(remote(a1.at[part(c)], q1.at[part(c)], y1s.at[c], y1r.at[c], far)))
    for c in local[1:]:
        c.wait()
    span = 256
    ratio = span // (2 * per)
    groups = width // span

    def row(block):
        return pl.ds(pl.multiple_of(block * per, per), per)

    def x_copy(d):
        mine = (z ^ d) * 2 + (1 - x)
        return remote(grads.at[row(mine)], rx.at[d], xs.at[d], xr.at[d], side)

    def z_copy(d):
        return remote(sz.at[d], rz.at[d], zs.at[d], zr.at[d], {"fsdp": f ^ (2 * d), "tensor": t})

    def block(i, _):
        near_group = groups - 1 - i
        group = near_group ^ (z // ratio)
        cols = pl.ds(pl.multiple_of(group * span, span), span)
        acc, acc_out = None, None
        for j in range(4):
            term = nn(onev[j, :, cols].T, dqkv[j])
            acc = term if acc is None else acc + term
            term = nn(backv[j, :, cols].T, attv[j])
            acc_out = term if acc_out is None else acc_out + term
        keep[cols, : 3 * head_width] = acc
        keep[cols, 3 * head_width :] = acc_out
        grads[cols, : 3 * head_width] = acc.astype(BF)
        grads[cols, 3 * head_width :] = acc_out.astype(BF)

        def send(e, _):
            x_copy(near_group * ratio + e).start()
            return 0

        lax.fori_loop(0, ratio, send, 0)
        return 0

    lax.fori_loop(0, groups, block, 0)
    for c in range(chunks):
        s1[1, part(c), :] = norm_grad(1, c).astype(BF)
        third.append(go(remote(s1.at[1, part(c)], r1.at[1, part(c)], s1s.at[1, c], s1r.at[1, c], sib)))
    for c in range(chunks):
        near[part(c), :] = norm_grad(0, c)
    bias_sum = stats[1:2, :width]
    gain_sum = (stats[0:1, :width] - bias[...] * bias_sum) / gain[...]
    slot = lax.broadcasted_iota(jnp.int32, (4, head_width), 0)
    lv[...] = jnp.zeros_like(lv)
    qsum = stats[2:3, :head_width]
    vsum = stats[2:3, 2 * head_width : 3 * head_width]
    for u in range(4):
        cols = pl.ds(u * head_width, head_width)
        lv[u, 0:4, :] = jnp.where(slot == t, vec[0:1, cols], 0.0)
        here = (t == u).astype(F32)
        lv[u, 4:5, :] = qsum * here
        lv[u, 5:6, :] = vsum * here
        lv[u, 6:7, :] = vec[3:4, cols]
        lv[u, 7:8, :] = vec[4:5, cols]
        lv[u, 8:9, :] = vec[1:2, cols]
        lv[u, 9:10, :] = vec[2:3, cols]
        lv[u, 10:11, :] = gain_sum[:, u * head_width : (u + 1) * head_width]
        lv[u, 11:12, :] = bias_sum[:, u * head_width : (u + 1) * head_width]
    level1 = [
        go(remote(lv.at[t ^ j], rv1.at[j], v1s.at[j], v1r.at[j], mates[j - 1])) for j in range(1, 4)
    ]

    def pass_on(i, _):
        d = lines - 1 - i
        x_copy(d).wait_recv()
        sz[d] = (keep[row((z ^ d) * 2 + x), :] + rx[d].astype(F32)).astype(BF)
        z_copy(d).start()
        return 0

    lax.fori_loop(0, (lines - 1) // 2, pass_on, 0)
    for c in level1:
        c.wait_recv()
    sv[...] = lv[t] + rv1[1] + rv1[2] + rv1[3]
    level2 = [
        go(remote(sv, rv2.at[e], v2s.at[e], v2r.at[e], others[e - 1])) for e in range(1, shards)
    ]
    for c in third:
        c.wait_recv()

    def finish(c):
        second[c].wait_recv()
        gn = near[part(c), :] + r1[1, part(c), :].astype(F32) + q1[part(c), :].astype(F32)
        unit, inv = normalize(tokv[part(c), :].astype(F32))
        scaled = gn * gain[...]
        inner = (
            scaled
            - jnp.mean(scaled, axis=1, keepdims=True)
            - unit * jnp.mean(scaled * unit, axis=1, keepdims=True)
        )
        ghidv[part(c), :] = ghidv[part(c), :] + inv * inner

    for c in range(chunks - 1):
        finish(c)
    lax.fori_loop((lines - 1) // 2, lines - 1, pass_on, 0)
    for c in level2:
        c.wait_recv()
    total = sv[...]
    for e in range(1, shards):
        total = total + rv2[e]
    gv[t] = total
    level3 = [
        go(remote(gv.at[t], gv.at[t], v3s.at[j], v3r.at[j], mates[j - 1])) for j in range(1, 4)
    ]
    finish(chunks - 1)
    outs = [pltpu.make_async_copy(ghidv, tok_out, osem.at[0])]
    outs[0].start()
    x_copy(0).wait_recv()
    wsum[...] = keep[row(f), :] + rx[0].astype(F32)

    def collect(i, _):
        d = lines - 1 - i
        z_copy(d).wait_recv()
        wsum[...] += rz[d].astype(F32)
        return 0

    lax.fori_loop(0, lines - 1, collect, 0)
    outs.append(pltpu.make_async_copy(wsum, w_out_ref, osem.at[1]))
    outs[1].start()
    for c in level3:
        c.wait_recv()
    outs.append(pltpu.make_async_copy(gv, small_out, osem.at[2]))
    outs[2].start()
    for c in sends:
        c.wait_send()

    def drain(d, _):
        x_copy(d).wait_send()

        @pl.when(d > 0)
        def _():
            z_copy(d).wait_send()

        return 0

    lax.fori_loop(0, lines, drain, 0)
    for c in outs:
        c.wait()


def last(shards, dqkv, weights, one, back, att, tok, ghid, vec, gain, bias):
    _, rows, width = one.shape
    head_width = att.shape[2]
    per = width // shards
    lines = shards // 2
    chunks = 2
    dma = pltpu.SemaphoreType.DMA
    vm = pl.BlockSpec(memory_space=VM)
    hbm = pl.BlockSpec(memory_space=pl.ANY)
    V = pltpu.VMEM
    sems = [
        (5,), (2, chunks), (2, chunks), (chunks,), (chunks,), (lines,), (lines,), (lines,), (lines,),
        (4,), (4,), (shards,), (shards,), (4,), (4,), (3,),
    ]
    return pl.pallas_call(
        functools.partial(last_kernel, shards, chunks),
        name="last",
        out_shape=[
            jax.ShapeDtypeStruct((rows, width), F32),
            jax.ShapeDtypeStruct((per, 4 * head_width), F32),
            jax.ShapeDtypeStruct((4, 16, head_width), F32),
        ],
        in_specs=[vm, vm, hbm, hbm, hbm, hbm, hbm, vm, vm, vm],
        out_specs=[hbm] * 3,
        scratch_shapes=[
            V((4, rows, width), BF), V((4, rows, width), BF), V((4, rows, head_width), BF),
            V((rows, width), BF), V((rows, width), F32), V((3 * head_width, width), BF),
            V((2, rows, width), BF), V((2, rows, width), BF), V((rows, width), BF), V((rows, width), BF),
            V((rows, width), F32), V((width, 4 * head_width), BF), V((width, 4 * head_width), F32),
            V((lines, per, 4 * head_width), BF), V((lines, per, 4 * head_width), BF),
            V((lines, per, 4 * head_width), BF), V((per, 4 * head_width), F32),
            V((8, width), F32), V((4, 16, head_width), F32), V((4, 16, head_width), F32),
            V((16, head_width), F32), V((shards, 16, head_width), F32), V((4, 16, head_width), F32),
        ]
        + [dma(s) for s in sems],
        compiler_params=pltpu.CompilerParams(
            collective_id=2, has_side_effects=True, vmem_limit_bytes=60 << 20
        ),
        cost_estimate=pl.CostEstimate(flops=30 << 30, bytes_accessed=100 << 20, transcendentals=0),
    )(dqkv, weights, one, back, att, tok, ghid, vec, gain, bias)


CORE = [(0, 1), (1, 0), (2, 3), (3, 2)]
FAR = [(0, 2), (2, 0), (1, 3), (3, 1)]


def swap_core(v):
    return lax.ppermute(v, "tensor", CORE)


def swap_far(v):
    return lax.ppermute(v, "tensor", FAR)


def after(value, *others):
    return lax.optimization_barrier((value,) + others)[0]


def body(
    tokens,
    cotangent,
    pic_starts,
    w_qkv,
    qv_bias,
    w_out,
    out_bias,
    ln1_gain,
    ln1_bias,
    w_fc1,
    fc1_bias,
    w_fc2,
    fc2_bias,
    ln2_gain,
    ln2_bias,
):
    rows, width = tokens.shape
    shards = lax.axis_size("fsdp")
    head_width = w_qkv.shape[2]
    hidden_width = w_fc1.shape[1]
    fsdp_rows = w_qkv.shape[0]
    rank = lax.axis_index("tensor")
    meta = jnp.concatenate([rank.astype(jnp.int32)[None], pic_starts[0]])

    def gather_w(v):
        return lax.all_gather(v, "fsdp", axis=0, tiled=True)

    def scatter_w(v):
        return lax.psum_scatter(v, "fsdp", scatter_dimension=0, tiled=True)

    one, qkv, qkv_full, out_t = front(
        shards,
        tokens,
        w_qkv.reshape(fsdp_rows, 3 * head_width),
        w_out.T,
        ln1_gain[None],
        ln1_bias[None],
        qv_bias,
    )
    fc_own = jnp.concatenate([w_fc1, w_fc2.T], axis=1)
    fc_sent = after(fc_own, qkv)
    pre = [d for d in (1, 2) if d < shards // 2]
    fc_in = [
        lax.ppermute(fc_sent, "fsdp", [(i, i ^ hop) for i in range(shards)])
        for hop in [1] + [2 * d for d in pre]
    ]
    qkv_full = qkv_full.reshape(width, 3 * head_width)
    out_t = out_t.reshape(width, head_width)
    up_far = swap_far(after(cotangent, qkv))
    att, lse = attn_fwd(meta, qkv)
    hidden_one, grad_hidden_one, back, bulk_grad, part_far, part_near, vec = middle(
        shards, pre, att, out_t, tokens, cotangent, up_far, fc_own, fc_in,
        ln2_gain[None], ln2_bias[None], out_bias[None], fc1_bias[None],
    )
    bulk = scatter_w(bulk_grad)
    fc1_grad = bulk[:, :hidden_width]
    fc2_grad = bulk[:, hidden_width:]
    ffn_sum = part_near.astype(F32) + swap_far(part_far).astype(F32)
    output = hidden_one + ffn_sum + fc2_bias

    grad_att = nn(back.reshape(4 * rows, width), out_t).astype(BF).reshape(4, rows, head_width)
    qkv_grad = attn_bwd(meta, qkv, grad_att, att, lse)
    input_grad, w_sums, small = last(
        shards, qkv_grad, qkv_full, one, back, att, tokens, grad_hidden_one, vec,
        ln1_gain[None], ln1_bias[None],
    )
    small = small.transpose(1, 0, 2).reshape(16, width)
    return (
        output,
        input_grad,
        w_sums[:, : 3 * head_width].reshape(fsdp_rows, 3, head_width),
        small[4:6],
        w_sums[:, 3 * head_width :].T,
        small[6],
        small[10],
        small[11],
        fc1_grad.astype(F32),
        small[0:4].reshape(-1),
        fc2_grad.astype(F32).T,
        small[7],
        small[8],
        small[9],
    )


def solution(mesh):
    return jax.shard_map(
        body,
        mesh=mesh,
        in_specs=(
            P(("fsdp", "tensor"), None),
            P(("fsdp", "tensor"), None),
            P("fsdp", None),
            P("fsdp", None, "tensor"),
            P(),
            P("tensor", "fsdp"),
            P(),
            P(),
            P(),
            P("fsdp", "tensor"),
            P(),
            P("tensor", "fsdp"),
            P(),
            P(),
            P(),
        ),
        out_specs=(
            P(("fsdp", "tensor"), None),
            P(("fsdp", "tensor"), None),
            P("fsdp", None, "tensor"),
            P(),
            P("tensor", "fsdp"),
            P(),
            P(),
            P(),
            P("fsdp", "tensor"),
            P(),
            P("tensor", "fsdp"),
            P(),
            P(),
            P(),
        ),
        check_vma=False,
    )
```

```python
import functools
import math

import jax
import jax.numpy as jnp
from jax import lax
from jax.experimental import pallas as pl
from jax.experimental.pallas import tpu as pltpu
from jax.sharding import PartitionSpec as P

HD = 64
PIC = 256
F32 = jnp.float32
BF = jnp.bfloat16
NEG = -1e30
NORM_EPSILON = 1e-05
GELU_SCALE = math.sqrt(2.0 / math.pi)
GELU_CUBIC = 0.044715
VM = pltpu.MemorySpace.VMEM
SM = pltpu.MemorySpace.SMEM
HB = pltpu.MemorySpace.HBM
PRE = (1, 2)


def nn(a, b):
    return lax.dot_general(a, b, (((1,), (0,)), ((), ())), preferred_element_type=F32)


def nt(a, b):
    return lax.dot_general(a, b, (((1,), (1,)), ((), ())), preferred_element_type=F32)


def normalize(values):
    average = jnp.mean(values, axis=1, keepdims=True)
    centered = values - average
    inv_std = lax.rsqrt(jnp.mean(centered * centered, axis=1, keepdims=True) + NORM_EPSILON)
    return centered * inv_std, inv_std


def normalize_back(gradient, unit_rows, inv_std, gain_row):
    scaled = gradient * gain_row
    inner = (
        scaled
        - jnp.mean(scaled, axis=1, keepdims=True)
        - unit_rows * jnp.mean(scaled * unit_rows, axis=1, keepdims=True)
    )
    return inv_std * inner, jnp.sum(gradient * unit_rows, axis=0), jnp.sum(gradient, axis=0)


def attn_bwd_kernel(meta, *refs):
    qs,dos,ats,lse_ref,out=refs[:5]
    qn,kn,vn,don,qT,kT,doT,dk,dv,dqT,dl=refs[5:]
    t=meta[0]
    B=qs.shape[1]; HW=qs.shape[2]//3; NH=HW//HD; NP=NH//2
    for j in range(4):
        b=t^j
        q=qs[j,:,:HW]*jnp.asarray(HD**-0.5,BF)
        k=qs[j,:,HW:2*HW]
        do=dos[j]
        qn[b]=q; kn[b]=k; vn[b]=qs[j,:,2*HW:]; don[b]=do
        qT[b]=q.T; kT[b]=k.T; doT[b]=do.T
        prod=(do.astype(F32)*ats[j].astype(F32)).T
        for h in range(NH):
            dl[b,h:h+1,:]=jnp.sum(prod[h*HD:(h+1)*HD],axis=0,keepdims=True)
    dk[...]=jnp.zeros_like(dk); dv[...]=jnp.zeros_like(dv)
    rowk=lax.broadcasted_iota(jnp.int32,(B,B),0)
    colq=lax.broadcasted_iota(jnp.int32,(B,B),1)
    hrow=lax.broadcasted_iota(jnp.int32,(2*HD,B),0)<HD
    hcol=lax.broadcasted_iota(jnp.int32,(B,2*HD),1)<HD
    for i in range(4):
        jj=t^i
        ps=meta[1+i]-i*B
        def pair(p,_):
            kcol=pl.multiple_of(p*2*HD,2*HD)
            def two(x,m):
                z=jnp.zeros_like(x)
                return (jnp.where(m,x,z),jnp.where(m,z,x))
            qTz=two(qT[i,pl.ds(kcol,2*HD),:],hrow)
            doTz=two(doT[i,pl.ds(kcol,2*HD),:],hrow)
            qz=two(qn[i,:,pl.ds(kcol,2*HD)],hcol)
            doz=two(don[i,:,pl.ds(kcol,2*HD)],hcol)
            lse=[lse_ref[jj,pl.ds(p*2+hh,1),:] for hh in range(2)]
            dlt=[dl[i,pl.ds(p*2+hh,1),:] for hh in range(2)]
            def blk(m,carry,diag):
                kb=kn[m,:,pl.ds(kcol,2*HD)]
                vb=vn[m,:,pl.ds(kcol,2*HD)]
                ktb=kT[m,pl.ds(kcol,2*HD),:]
                dvs=0.; dks=0.; new=[]
                for hh in range(2):
                    s=nn(kb,qTz[hh])
                    if diag:
                        ok=(rowk<=colq)|((rowk>=ps)&(rowk<ps+PIC)&(colq>=ps)&(colq<ps+PIC))
                        s=jnp.where(ok,s,NEG)
                    pr=jnp.exp(s-lse[hh])
                    dp=nn(vb,doTz[hh])
                    ds=(pr*(dp-dlt[hh])).astype(BF)
                    dvs=dvs+nn(pr.astype(BF),doz[hh])
                    dks=dks+nn(ds,qz[hh])
                    new.append(carry[hh]+nn(ktb[hh*HD:(hh+1)*HD],ds))
                dv[m,:,pl.ds(kcol,2*HD)]+=dvs
                dk[m,:,pl.ds(kcol,2*HD)]+=dks
                return tuple(new)
            c=tuple(jnp.zeros((HD,B),F32) for _ in range(2))
            c=blk(i,c,True)
            c=lax.fori_loop(0,i,lambda m,c: blk(m,c,False),c) if i>0 else c
            dqT[i,pl.ds(kcol,2*HD),:]=(jnp.concatenate(c,axis=0)*(HD**-0.5)).astype(BF)
            return 0
        lax.fori_loop(0,NP,pair,0)
    for j in range(4):
        b=t^j
        out[j,:,:HW]=dqT[b].T
        out[j,:,HW:2*HW]=dk[b].astype(BF)
        out[j,:,2*HW:]=dv[b].astype(BF)

def attn_bwd(meta,qs,dos,ats,lse):
    B=qs.shape[1]; HW=qs.shape[2]//3; NH=HW//HD
    vm=pl.BlockSpec(memory_space=pltpu.MemorySpace.VMEM)
    V=pltpu.VMEM
    return pl.pallas_call(attn_bwd_kernel,name="attn_bwd",
        out_shape=[jax.ShapeDtypeStruct((4,B,3*HW),BF)],
        in_specs=[pl.BlockSpec(memory_space=pltpu.MemorySpace.SMEM)]+[vm]*4,
        out_specs=[vm],
        scratch_shapes=[V((4,B,HW),BF)]*4+[V((4,HW,B),BF)]*3+[V((4,B,HW),F32)]*2+[V((4,HW,B),BF),V((4,NH,B),F32)],
        compiler_params=pltpu.CompilerParams(vmem_limit_bytes=56<<20),
        cost_estimate=pl.CostEstimate(flops=20<<30,bytes_accessed=16<<20,transcendentals=0))(meta,qs,dos,ats,lse)[0]


MESH = pl.DeviceIdType.MESH


def remote(src, dst, send, recv, where):
    return pltpu.make_async_remote_copy(
        src_ref=src, dst_ref=dst, send_sem=send, recv_sem=recv, device_id=where, device_id_type=MESH
    )


def greet(peers):
    barrier = pltpu.get_barrier_semaphore()
    for peer in peers:
        pl.semaphore_signal(barrier, inc=1, device_id=peer, device_id_type=MESH)
    pl.semaphore_wait(barrier, len(peers))


def head_kernel(
    shards, chunks,
    tok, wq, wo, w1, w2, gain, bias, qvb, starts, cot,
    n_out, qkv_out, wq_out, ot_out, fc_out, up_out, att_out, lse_out,
    nv, wqv, wov, otv, fcv, qv, kn, qT, vT, att, lsev,
    ysend, yrecv, csend, crecv, fsend, frecv, zqs, zqr, xqs, xqr, zos, zor, xos, xor,
    zfs, zfr, ups, upr, lsem, osem,
):
    f = lax.axis_index("fsdp")
    t = lax.axis_index("tensor")
    rows, width = tok.shape
    head_width, per = wo.shape
    hid = w1.shape[1]
    step = rows // chunks
    lines = shards // 2
    far = {"fsdp": f, "tensor": t ^ 2}
    sib = {"fsdp": f, "tensor": t ^ 1}
    side = {"fsdp": f ^ 1, "tensor": t}
    alongs = [{"fsdp": f ^ (2 * d), "tensor": t} for d in range(1, lines)]
    greet([far, sib, side] + alongs)
    sends = []

    def go(copy):
        copy.start()
        sends.append(copy)
        return copy

    zq, zo, xq, xo = [], [], [], []
    for d in range(1, lines):
        zq.append(go(remote(wq, wqv.at[f], zqs.at[d], zqr.at[d], alongs[d - 1])))
    xq.append(go(remote(wq, wqv.at[f], xqs.at[0], xqr.at[0], side)))
    ys, cs, fs = [], [], []
    for c in range(chunks):
        part = pl.ds(c * step, step)
        unit, _ = normalize(tok[part, :].astype(F32))
        nv[0, part, :] = (unit * gain[...] + bias[...]).astype(BF)
        ys.append(go(remote(nv.at[0, part], nv.at[2, part], ysend.at[c], yrecv.at[c], far)))
        cs.append(go(remote(nv.at[0, part], nv.at[1, part], csend.at[c], crecv.at[c], sib)))
    for d in range(1, lines):
        zo.append(go(remote(wo, wov.at[f], zos.at[d], zor.at[d], alongs[d - 1])))
    xo.append(go(remote(wo, wov.at[f], xos.at[0], xor.at[0], side)))
    wqv[f] = wq[...]
    wov[f] = wo[...]
    fcv[:, :hid] = w1[...]
    fcv[:, hid:] = w2[...].T
    local = [pltpu.make_async_copy(fcv, fc_out.at[f], lsem.at[0])]
    local[0].start()

    def forward_far(c):
        part = pl.ds(c * step, step)
        ys[c].wait_recv()
        fs.append(go(remote(nv.at[2, part], nv.at[3, part], fsend.at[c], frecv.at[c], sib)))

    todo = list(range(chunks))
    for d in range(1, lines):
        zq[d - 1].wait_recv()
        slot = f ^ (2 * d)
        xq.append(go(remote(wqv.at[slot], wqv.at[slot], xqs.at[d], xqr.at[d], side)))
        if len(todo) > 1:
            forward_far(todo.pop(0))
    for d in range(1, lines):
        zo[d - 1].wait_recv()
        slot = f ^ (2 * d)
        xo.append(go(remote(wov.at[slot], wov.at[slot], xos.at[d], xor.at[d], side)))
    fc = []
    for d in PRE:
        if d < lines:
            fc.append(go(remote(fcv, fc_out.at[f], zfs.at[d], zfr.at[d], alongs[d - 1])))
    for c in cs:
        c.wait_recv()
    for d in range(lines):
        xq[d].wait_recv()
    start = pl.multiple_of(t * head_width, head_width)
    adds = (qvb[0:1, pl.ds(start, head_width)], None, qvb[1:2, pl.ds(start, head_width)])

    def project(j, _):
        b = t ^ j
        for k in range(3):
            value = nn(nv[j], wqv[:, k].reshape(width, head_width))
            if adds[k] is not None:
                value = value + adds[k]
            value = value.astype(BF)
            qv[j, :, k * head_width : (k + 1) * head_width] = value
            if k == 0:
                qT[b] = (value * jnp.asarray(HD**-0.5, BF)).T
            elif k == 1:
                kn[b] = value
            else:
                vT[b] = value.T
        return 0

    lax.fori_loop(0, 2, project, 0)
    while todo:
        forward_far(todo.pop(0))
    up = go(remote(cot, up_out, ups.at[0], upr.at[0], far))
    for c in fs:
        c.wait_recv()
    lax.fori_loop(2, 4, project, 0)
    for d in range(lines):
        xo[d].wait_recv()
    fc.append(go(remote(fcv, fc_out.at[f], zfs.at[0], zfr.at[0], side)))
    if per % 128 == 0:
        def place(s, _):
            otv[:, pl.ds(pl.multiple_of(s * per, per), per)] = wov[s]
            return 0

        lax.fori_loop(0, shards, place, 0)
    else:
        for s in range(shards):
            otv[:, s * per : (s + 1) * per] = wov[s]
    outs = [
        pltpu.make_async_copy(src, dst, osem.at[n])
        for n, (src, dst) in enumerate([(nv, n_out), (qv, qkv_out), (wqv, wq_out), (otv, ot_out)])
    ]
    for c in outs:
        c.start()
    rowk = lax.broadcasted_iota(jnp.int32, (rows, rows), 0)
    colq = lax.broadcasted_iota(jnp.int32, (rows, rows), 1)
    half = lax.broadcasted_iota(jnp.int32, (2 * HD, rows), 0) < HD
    for i in range(4):
        at = starts[0, i] - i * rows

        def pair(p, _, i=i, at=at):
            col = pl.multiple_of(p * 2 * HD, 2 * HD)
            qp = qT[i, pl.ds(col, 2 * HD), :]
            zero = jnp.zeros_like(qp)
            masked = (jnp.where(half, qp, zero), jnp.where(half, zero, qp))
            found = []
            for hh in range(2):
                ss, top = [], None
                for m in range(i + 1):
                    s = nn(kn[m, :, pl.ds(col, 2 * HD)], masked[hh])
                    if m == i:
                        inside = (rowk >= at) & (rowk < at + PIC) & (colq >= at) & (colq < at + PIC)
                        s = jnp.where((rowk <= colq) | inside, s, NEG)
                    peak = jnp.max(s, axis=0, keepdims=True)
                    top = peak if top is None else jnp.maximum(top, peak)
                    ss.append(s)
                total, acc = 0.0, 0.0
                for m in range(i + 1):
                    e = jnp.exp(ss[m] - top)
                    total = total + jnp.sum(e, axis=0, keepdims=True)
                    acc = acc + nn(vT[m, pl.ds(col + hh * HD, HD), :], e.astype(BF))
                found.append(acc * (1.0 / total))
                lsev[t ^ i, pl.ds(p * 2 + hh, 1), :] = top + jnp.log(total)
            att[i, :, pl.ds(col, 2 * HD)] = jnp.concatenate(found, axis=0).astype(BF).T
            return 0

        lax.fori_loop(0, head_width // (2 * HD), pair, 0)
    outs += [pltpu.make_async_copy(att.at[t ^ j], att_out.at[j], osem.at[4 + j]) for j in range(4)]
    outs.append(pltpu.make_async_copy(lsev, lse_out, osem.at[8]))
    for c in outs[4:]:
        c.start()
    for c in fc + [up]:
        c.wait_recv()
    for c in sends:
        c.wait_send()
    for c in local + outs:
        c.wait()


def head(shards, tokens, wq, wo, w1, w2, gain, bias, qv_bias, starts, cot):
    rows, width = tokens.shape
    head_width, per = wo.shape
    hid = w1.shape[1]
    lines = shards // 2
    chunks = 4
    heads = head_width // HD
    dma = pltpu.SemaphoreType.DMA
    vm = pl.BlockSpec(memory_space=VM)
    hbm = pl.BlockSpec(memory_space=HB)
    V = pltpu.VMEM
    full = (4, rows, width)
    three = (4, rows, 3 * head_width)
    return pl.pallas_call(
        functools.partial(head_kernel, shards, chunks),
        name="head",
        out_shape=[
            jax.ShapeDtypeStruct(full, BF),
            jax.ShapeDtypeStruct(three, BF),
            jax.ShapeDtypeStruct((shards, 3, per, head_width), BF),
            jax.ShapeDtypeStruct((head_width, width), BF),
            jax.ShapeDtypeStruct((shards, per, 2 * hid), BF),
            jax.ShapeDtypeStruct((rows, width), BF),
            jax.ShapeDtypeStruct((4, rows, head_width), BF),
            jax.ShapeDtypeStruct((4, heads, rows), F32),
        ],
        in_specs=[vm] * 8 + [pl.BlockSpec(memory_space=SM), hbm],
        out_specs=[hbm] * 8,
        scratch_shapes=[
            V(full, BF), V((shards, 3, per, head_width), BF), V((shards, head_width, per), BF),
            V((head_width, width), BF), V((per, 2 * hid), BF), V(three, BF),
            V((4, rows, head_width), BF), V((4, head_width, rows), BF), V((4, head_width, rows), BF),
            V((4, rows, head_width), BF), V((4, heads, rows), F32),
        ]
        + [dma((chunks,))] * 6
        + [dma((lines,))] * 8
        + [dma((max(lines, 4),))] * 2
        + [dma((1,))] * 3
        + [dma((9,))],
        compiler_params=pltpu.CompilerParams(
            collective_id=0, has_side_effects=True, vmem_limit_bytes=56 << 20
        ),
        cost_estimate=pl.CostEstimate(flops=40 << 30, bytes_accessed=90 << 20, transcendentals=0),
    )(tokens, wq, wo, w1, w2, gain, bias, qv_bias, starts, cot)


def middle_kernel(
    shards, chunks,
    att, ot, tok, cot, up_far, fc_in, gain, bias, out_bias, fc_bias,
    hid_out, ghid_out, back_out, do_out, g1_out, w2_out, part_far, part_near, vec,
    wfc, wt, ott, upv, twov, actv, pgv, backv,
    s1, r1, a1, q1, near, hv, rx, sz, rz, wsum, wsum_t, dov,
    s1s, s1r, y1s, y1r, c2s, c2r, y2s, y2r, f2s, f2r,
    s3s, s3r, y3s, y3r, c4s, c4r, y4s, y4r, f4s, f4r,
    s5s, s5r, ups, upr, lsem, zs, zr, xs, xr, osem, gxs, gxr, gzs, gzr,
):
    f = lax.axis_index("fsdp")
    t = lax.axis_index("tensor")
    rows, width = tok.shape
    per = fc_in.shape[1]
    hid = fc_in.shape[2] // 2
    pre = [d for d in PRE if d < shards // 2]
    step = rows // chunks
    lines = shards // 2
    far = {"fsdp": f, "tensor": t ^ 2}
    sib = {"fsdp": f, "tensor": t ^ 1}
    side = {"fsdp": f ^ 1, "tensor": t}
    direct = [d for d in range(1, lines) if d not in pre]
    alongs = {d: {"fsdp": f ^ (2 * d), "tensor": t} for d in range(1, lines)}
    greet([far, sib, side] + [alongs[d] for d in range(1, lines)])
    sends = []

    def go(copy):
        copy.start()
        sends.append(copy)
        return copy

    def part(c):
        return pl.ds(c * step, step)

    halves = (pl.ds(0, hid), pl.ds(hid, hid))
    local = [
        pltpu.make_async_copy(fc_in.at[slot], wfc.at[slot], lsem.at[n])
        for n, slot in enumerate([f, f ^ 1] + [f ^ (2 * d) for d in pre])
    ]
    local.append(pltpu.make_async_copy(cot, upv.at[0], lsem.at[len(pre) + 2]))
    local.append(pltpu.make_async_copy(up_far, upv.at[2], lsem.at[len(pre) + 3]))
    for c in local:
        c.start()
    xf = {}
    zf = {}
    for h in range(2):
        for d in direct:
            zf[d, h] = go(
                remote(fc_in.at[f, :, halves[h]], wfc.at[f, :, halves[h]], zs.at[h, d], zr.at[h, d], alongs[d])
            )

    def forward_pre(h):
        for d in pre:
            slot = f ^ (2 * d)
            xf[d, h] = go(
                remote(
                    fc_in.at[slot, :, halves[h]], wfc.at[slot, :, halves[h]],
                    xs.at[h, d], xr.at[h, d], side,
                )
            )

    def forward_direct(h):
        for d in direct:
            zf[d, h].wait_recv()
            slot = f ^ (2 * d)
            xf[d, h] = go(
                remote(
                    wfc.at[slot, :, halves[h]], wfc.at[slot, :, halves[h]],
                    xs.at[h, d], xr.at[h, d], side,
                )
            )

    forward_pre(0)
    first, second, third = [], [], []
    for c in range(chunks):
        s1[0, part(c), :] = nn(att[3, part(c), :], ot[...]).astype(BF)
        first.append(go(remote(s1.at[0, part(c)], r1.at[0, part(c)], s1s.at[0, c], s1r.at[0, c], sib)))
    for c in range(chunks):
        mine = nn(att[2, part(c), :], ot[...])
        first[c].wait_recv()
        a1[0, part(c), :] = (mine + r1[0, part(c), :].astype(F32)).astype(BF)
        second.append(go(remote(a1.at[0, part(c)], q1.at[0, part(c)], y1s.at[c], y1r.at[c], far)))
    for c in range(chunks):
        s1[1, part(c), :] = nn(att[1, part(c), :], ot[...]).astype(BF)
        third.append(go(remote(s1.at[1, part(c)], r1.at[1, part(c)], s1s.at[1, c], s1r.at[1, c], sib)))
    ott[...] = ot[...].T
    up_copies = [
        go(remote(cot, upv.at[1], ups.at[0], upr.at[0], sib)),
        go(remote(up_far, upv.at[3], ups.at[1], upr.at[1], sib)),
    ]
    for c in range(chunks):
        mine = nn(att[0, part(c), :], ot[...])
        third[c].wait_recv()
        near[part(c), :] = mine + r1[1, part(c), :].astype(F32)
    vec[...] = jnp.zeros_like(vec)
    forward_direct(0)
    forward_pre(1)
    ag_far, ag_sib = [], []
    for c in range(chunks):
        second[c].wait_recv()
        hidden = (
            tok[part(c), :].astype(F32)
            + near[part(c), :]
            + q1[0, part(c), :].astype(F32)
            + out_bias[...]
        )
        hv[part(c), :] = hidden
        unit, _ = normalize(hidden)
        twov[0, part(c), :] = (unit * gain[...] + bias[...]).astype(BF)
        ag_far.append(go(remote(twov.at[0, part(c)], twov.at[2, part(c)], y2s.at[c], y2r.at[c], far)))
        ag_sib.append(go(remote(twov.at[0, part(c)], twov.at[1, part(c)], c2s.at[c], c2r.at[c], sib)))
        if c == 0:
            forward_direct(1)
    outs = [pltpu.make_async_copy(hv, hid_out, osem.at[0])]
    outs[0].start()
    for c in local:
        c.wait()
    for h in range(2):
        xo = [xf[d, h] for d in pre] + [xf[d, h] for d in direct]
        for c in xo:
            c.wait_recv()

        def flip(s, _, h=h):
            wt[pl.ds(h * hid, hid), pl.ds(pl.multiple_of(s * per, per), per)] = wfc[s, :, halves[h]].T
            return 0

        if per % 128 == 0:
            lax.fori_loop(0, shards, flip, 0)
        else:
            wt[pl.ds(h * hid, hid), :] = wfc[:, :, halves[h]].reshape(width, hid).T
    for c in up_copies:
        c.wait_recv()
    for c in ag_sib:
        c.wait_recv()
    start = pl.multiple_of(t * hid, hid)
    tile = hid // 2

    def feed(j, at):
        block = pl.ds(pl.multiple_of(at * step, step), step)
        two = twov[j, block, :]
        up = upv[j, block, :]
        total = None
        for n in range(2):
            cols = pl.ds(n * tile, tile)
            x = nn(two, wfc[:, :, cols].reshape(width, tile))
            x = x + fc_bias[:, pl.ds(pl.multiple_of(start + n * tile, tile), tile)]
            hg = nn(up, wfc[:, :, pl.ds(hid + n * tile, tile)].reshape(width, tile))
            sq = x * x
            th = jnp.tanh(GELU_SCALE * (x + GELU_CUBIC * (sq * x)))
            half = 0.5 * (1.0 + th)
            actv[j, block, cols] = (x * half).astype(BF)
            slope = half + (0.5 * GELU_SCALE) * x * (1.0 - th * th) * (1.0 + (3.0 * GELU_CUBIC) * sq)
            pg = (hg * slope).astype(BF)
            pgv[j, block, cols] = pg
            vec[0:1, cols] += jnp.sum(pg.astype(F32), axis=0, keepdims=True)
            term = nn(pg, wt[cols, :])
            total = term if total is None else total + term
        return total

    def copies(c):
        block = pl.ds(pl.multiple_of(c * step, step), step)
        return (
            remote(twov.at[0, block], twov.at[2, block], y2s.at[c], y2r.at[c], far),
            remote(twov.at[2, block], twov.at[3, block], f2s.at[c], f2r.at[c], sib),
            remote(a1.at[1, block], q1.at[1, block], y3s.at[c], y3r.at[c], far),
        )

    def core_copy(k, c):
        block = pl.ds(pl.multiple_of(c * step, step), step)
        return remote(s1.at[2 + k, block], r1.at[2 + k, block], s3s.at[k, c], s3r.at[k, c], sib)

    def chunk(c, _):
        block = pl.ds(pl.multiple_of(c * step, step), step)
        got, fwd, send2 = copies(c)
        got.wait_recv()
        fwd.start()
        fwd.wait_recv()

        def pair(k, _):
            give = core_copy(k, c)

            def one(i, _):
                total = feed(3 - 2 * k - i, c)

                @pl.when(i == 0)
                def _():
                    s1[2 + k, block, :] = total.astype(BF)
                    give.start()

                @pl.when(i == 1)
                def _():
                    near[block, :] = total

                return 0

            lax.fori_loop(0, 2, one, 0)

            @pl.when(k == 0)
            def _():
                give.wait_recv()
                a1[1, block, :] = (near[block, :] + r1[2, block, :].astype(F32)).astype(BF)
                send2.start()

            return 0

        lax.fori_loop(0, 2, pair, 0)
        return 0

    lax.fori_loop(0, chunks, chunk, 0)

    span = 256
    ratio = span // (2 * per)
    groups = width // span
    z = f // 2
    x = lax.rem(f, 2)

    def x_copy(d):
        return remote(wfc.at[(z ^ d) * 2 + (1 - x), :, halves[0]], rx.at[d], gxs.at[d], gxr.at[d], side)

    def z_copy(d):
        return remote(
            sz.at[d], rz.at[d], gzs.at[d], gzr.at[d], {"fsdp": f ^ (2 * d), "tensor": t}
        )

    def weight_grad(left, right, h, send):
        def group_of(i, _):
            near_group = groups - 1 - i
            group = near_group ^ (z // ratio)
            cols = pl.ds(pl.multiple_of(group * span, span), span)
            acc = None
            for j in range(4):
                term = nn(left[j, :, cols].T, right[j])
                acc = term if acc is None else acc + term
            count = span // per
            slots = pl.ds(group * count, count)
            wfc[slots, :, halves[h]] = acc.astype(BF).reshape(count, per, hid)
            if send:

                def launch(e, _):
                    x_copy(near_group * ratio + e).start()
                    return 0

                lax.fori_loop(0, ratio, launch, 0)
            return 0

        lax.fori_loop(0, groups, group_of, 0)

    def pass_on(d):
        x_copy(d).wait_recv()
        sz[d] = (wfc[(z ^ d) * 2 + x, :, halves[0]].astype(F32) + rx[d].astype(F32)).astype(BF)
        z_copy(d).start()

    for d in direct:
        for h in range(2):
            xf[d, h].wait_send()
    b_far, b_sib = [], []
    for c in range(chunks):
        _, _, send2 = copies(c)
        core_copy(1, c).wait_recv()
        send2.wait_recv()
        gn = near[part(c), :] + r1[3, part(c), :].astype(F32) + q1[1, part(c), :].astype(F32)
        unit, inv = normalize(hv[part(c), :])
        back, g_sum, b_sum = normalize_back(gn, unit, inv, gain[...])
        cots = upv[0, part(c), :].astype(F32)
        ghid = cots + back
        near[part(c), :] = ghid
        backv[0, part(c), :] = ghid.astype(BF)
        b_far.append(go(remote(backv.at[0, part(c)], backv.at[2, part(c)], y4s.at[c], y4r.at[c], far)))
        b_sib.append(go(remote(backv.at[0, part(c)], backv.at[1, part(c)], c4s.at[c], c4r.at[c], sib)))
        vec[1:2, :] += g_sum[None]
        vec[2:3, :] += b_sum[None]
        vec[3:4, :] += jnp.sum(ghid, axis=0, keepdims=True)
        vec[4:5, :] += jnp.sum(cots, axis=0, keepdims=True)
        if c == 0:
            weight_grad(upv, actv, 0, True)
    pass_on(lines - 1)
    outs.append(pltpu.make_async_copy(near, ghid_out, osem.at[1]))
    outs[1].start()

    for c in range(chunks):
        first[c].wait_send()
        third[c].wait_send()
        core_copy(0, c).wait_send()
        core_copy(1, c).wait_send()
    for k, slot in ((0, 0), (1, 1)):
        def give(c, _, j=3 - 2 * k, slot=slot):
            block = pl.ds(pl.multiple_of(c * step, step), step)
            s1[slot, block, :] = nn(actv[j, block, :], wt[hid:, :]).astype(BF)
            return 0

        lax.fori_loop(0, chunks, give, 0)
        given = go(remote(s1.at[slot], r1.at[slot], s5s.at[slot], s5r.at[slot], sib))

        def keep(c, _, j=2 - 2 * k, slot=slot):
            block = pl.ds(pl.multiple_of(c * step, step), step)
            s1[2 + slot, block, :] = nn(actv[j, block, :], wt[hid:, :]).astype(BF)
            return 0

        lax.fori_loop(0, chunks, keep, 0)
        given.wait_recv()
        summed = s1.at[2 + slot]
        summed[...] = (summed[...].astype(F32) + r1[slot].astype(F32)).astype(BF)
        outs.append(pltpu.make_async_copy(summed, part_near if k else part_far, osem.at[2 + k]))
        outs[-1].start()

    if lines > 2:
        pass_on(lines - 2)
    weight_grad(twov, pgv, 1, False)
    outs.append(pltpu.make_async_copy(wfc.at[:, :, halves[1]], g1_out, osem.at[5]))
    outs[-1].start()
    if lines > 3:

        def pass_more(i, _):
            pass_on(lines - 3 - i)
            return 0

        lax.fori_loop(0, lines - 3, pass_more, 0)
    for c in b_sib:
        c.wait_recv()

    def attended_grad(j, _):
        dov[j] = nn(backv[j], ott[...]).astype(BF)
        return 0

    lax.fori_loop(0, 2, attended_grad, 0)
    fwds = []
    for c in range(chunks):
        b_far[c].wait_recv()
        fwds.append(go(remote(backv.at[2, part(c)], backv.at[3, part(c)], f4s.at[c], f4r.at[c], sib)))
    x_copy(0).wait_recv()
    wsum[...] = wfc[z * 2 + x, :, halves[0]].astype(F32) + rx[0].astype(F32)

    def collect(i, _):
        d = lines - 1 - i
        z_copy(d).wait_recv()
        wsum[...] += rz[d].astype(F32)
        return 0

    lax.fori_loop(0, lines - 1, collect, 0)
    wsum_t[...] = wsum[...].T
    outs.append(pltpu.make_async_copy(wsum_t, w2_out, osem.at[6]))
    outs[-1].start()
    for c in fwds:
        c.wait_recv()
    outs.append(pltpu.make_async_copy(backv, back_out, osem.at[4]))
    outs[-1].start()
    lax.fori_loop(2, 4, attended_grad, 0)
    outs.append(pltpu.make_async_copy(dov, do_out, osem.at[7]))
    outs[-1].start()
    waited = first + third + [xf[d, h] for d in direct for h in range(2)]
    for c in sends:
        if not any(c is other for other in waited):
            c.wait_send()
    for c in range(chunks):
        _, fwd, send2 = copies(c)
        fwd.wait_send()
        send2.wait_send()

    def drain(d, _):
        x_copy(d).wait_send()

        @pl.when(d > 0)
        def _():
            z_copy(d).wait_send()

        return 0

    lax.fori_loop(0, lines, drain, 0)
    for c in outs:
        c.wait()


def middle(shards, att, ot, tok, cot, up_far, fc_in, gain, bias, out_bias, fc_bias):
    rows, width = tok.shape
    per, hid2 = fc_in.shape[1:]
    hid = hid2 // 2
    head_width = ot.shape[0]
    lines = shards // 2
    chunks = 2
    dma = pltpu.SemaphoreType.DMA
    vm = pl.BlockSpec(memory_space=VM)
    hbm = pl.BlockSpec(memory_space=HB)
    full = (4, rows, width)
    one = (rows, width)
    block = (lines, per, hid)
    V = pltpu.VMEM
    sems = [
        (2, chunks), (2, chunks), (chunks,), (chunks,), (chunks,), (chunks,),
        (chunks,), (chunks,), (chunks,), (chunks,),
        (2, chunks), (2, chunks), (chunks,), (chunks,), (chunks,), (chunks,),
        (chunks,), (chunks,), (chunks,), (chunks,),
        (2,), (2,), (2,), (2,), (8,),
        (2, lines), (2, lines), (2, lines), (2, lines), (8,),
        (lines,), (lines,), (lines,), (lines,),
    ]
    return pl.pallas_call(
        functools.partial(middle_kernel, shards, chunks),
        name="middle",
        out_shape=[
            jax.ShapeDtypeStruct(one, F32),
            jax.ShapeDtypeStruct(one, F32),
            jax.ShapeDtypeStruct(full, BF),
            jax.ShapeDtypeStruct((4, rows, head_width), BF),
            jax.ShapeDtypeStruct((shards, per, hid), BF),
            jax.ShapeDtypeStruct((hid, per), F32),
            jax.ShapeDtypeStruct(one, BF),
            jax.ShapeDtypeStruct(one, BF),
            jax.ShapeDtypeStruct((8, width), F32),
        ],
        in_specs=[vm, vm, vm, hbm, hbm, hbm] + [vm] * 4,
        out_specs=[hbm] * 8 + [vm],
        scratch_shapes=[
            V((shards, per, 2 * hid), BF), V((2 * hid, width), BF), V((width, head_width), BF),
            V(full, BF), V(full, BF), V((4, rows, hid), BF), V((4, rows, hid), BF), V(full, BF),
            V(full, BF), V(full, BF), V((2, rows, width), BF), V((2, rows, width), BF),
            V(one, F32), V(one, F32), V(block, BF), V(block, BF), V(block, BF),
            V((per, hid), F32), V((hid, per), F32), V((4, rows, head_width), BF),
        ]
        + [dma(s) for s in sems],
        compiler_params=pltpu.CompilerParams(
            collective_id=1, has_side_effects=True, vmem_limit_bytes=60 << 20
        ),
        cost_estimate=pl.CostEstimate(flops=60 << 30, bytes_accessed=200 << 20, transcendentals=0),
    )(att, ot, tok, cot, up_far, fc_in, gain, bias, out_bias, fc_bias)


def last_kernel(
    shards, chunks,
    dqkv, weights, one_in, back_in, att_in, tok_in, ghid_in, hid_in, pnear_in, pfar_in,
    vec, gain, bias, fc2_bias,
    out_out, tok_out, wq_out, wo_out, qv_out, fcb_out, g_a, g_b, g_c, g_d, g_e, g_f,
    hidv, pnearv, pfarv, wqs, wos, onev, backv, attv, tokv, ghidv, wt, s1, r1, a1, q1, near, grads, keep, rx, sz, rz, wsum,
    stats, lv, rv1, sv, rv2, gv,
    lsem, s1s, s1r, y1s, y1r, xs, xr, zs, zr, v1s, v1r, v2s, v2r, v3s, v3r, osem,
):
    f = lax.axis_index("fsdp")
    t = lax.axis_index("tensor")
    _, rows, width = onev.shape
    head_width = attv.shape[2]
    per = width // shards
    lines = shards // 2
    step = rows // chunks
    z = f // 2
    x = lax.rem(f, 2)
    far = {"fsdp": f, "tensor": t ^ 2}
    sib = {"fsdp": f, "tensor": t ^ 1}
    side = {"fsdp": f ^ 1, "tensor": t}
    mates = [{"fsdp": f, "tensor": t ^ j} for j in range(1, 4)]
    others = [{"fsdp": f ^ e, "tensor": t} for e in range(1, shards)]
    greet(mates + others)
    sends = []

    def go(copy):
        copy.start()
        sends.append(copy)
        return copy

    def part(c):
        return pl.ds(c * step, step)

    local = [
        pltpu.make_async_copy(src, dst, lsem.at[n])
        for n, (src, dst) in enumerate(
            [
                (one_in, onev), (back_in, backv), (att_in, attv), (tok_in, tokv), (ghid_in, ghidv),
                (hid_in, hidv), (pnear_in, pnearv), (pfar_in, pfarv),
            ]
        )
    ]
    for c in local:
        c.start()
    for k in range(3):
        wt[k * head_width : (k + 1) * head_width, :] = weights[:, k].reshape(width, head_width).T
    stats[...] = jnp.zeros_like(stats)
    local[0].wait()

    def norm_grad(j, c):
        mine = dqkv[j, part(c), :]
        total = nn(mine, wt[...])
        stats[0:1, :width] += jnp.sum(total * onev[j, part(c), :].astype(F32), axis=0, keepdims=True)
        stats[1:2, :width] += jnp.sum(total, axis=0, keepdims=True)
        stats[2:3, : 3 * head_width] += jnp.sum(mine.astype(F32), axis=0, keepdims=True)
        return total

    first, second, third = [], [], []
    for c in range(chunks):
        s1[0, part(c), :] = norm_grad(3, c).astype(BF)
        first.append(go(remote(s1.at[0, part(c)], r1.at[0, part(c)], s1s.at[0, c], s1r.at[0, c], sib)))
    for c in range(chunks):
        mine = norm_grad(2, c)
        first[c].wait_recv()
        a1[part(c), :] = (mine + r1[0, part(c), :].astype(F32)).astype(BF)
        second.append(go(remote(a1.at[part(c)], q1.at[part(c)], y1s.at[c], y1r.at[c], far)))
    for c in local[1:]:
        c.wait()
    span = 256
    ratio = span // (2 * per)
    groups = width // span

    def row(block):
        return pl.ds(pl.multiple_of(block * per, per), per)

    def x_copy(d):
        mine = (z ^ d) * 2 + (1 - x)
        return remote(grads.at[row(mine)], rx.at[d], xs.at[d], xr.at[d], side)

    def z_copy(d):
        return remote(sz.at[d], rz.at[d], zs.at[d], zr.at[d], {"fsdp": f ^ (2 * d), "tensor": t})

    def block(i, _):
        near_group = groups - 1 - i
        group = near_group ^ (z // ratio)
        cols = pl.ds(pl.multiple_of(group * span, span), span)
        acc, acc_out = None, None
        for j in range(4):
            term = nn(onev[j, :, cols].T, dqkv[j])
            acc = term if acc is None else acc + term
            term = nn(backv[j, :, cols].T, attv[j])
            acc_out = term if acc_out is None else acc_out + term
        keep[cols, : 3 * head_width] = acc
        keep[cols, 3 * head_width :] = acc_out
        grads[cols, : 3 * head_width] = acc.astype(BF)
        grads[cols, 3 * head_width :] = acc_out.astype(BF)

        def send(e, _):
            x_copy(near_group * ratio + e).start()
            return 0

        lax.fori_loop(0, ratio, send, 0)
        return 0

    lax.fori_loop(0, groups, block, 0)
    for c in range(chunks):
        s1[1, part(c), :] = norm_grad(1, c).astype(BF)
        third.append(go(remote(s1.at[1, part(c)], r1.at[1, part(c)], s1s.at[1, c], s1r.at[1, c], sib)))
    for c in range(chunks):
        near[part(c), :] = norm_grad(0, c)
    bias_sum = stats[1:2, :width]
    gain_sum = (stats[0:1, :width] - bias[...] * bias_sum) / gain[...]
    slot = lax.broadcasted_iota(jnp.int32, (4, head_width), 0)
    lv[...] = jnp.zeros_like(lv)
    qsum = stats[2:3, :head_width]
    vsum = stats[2:3, 2 * head_width : 3 * head_width]
    for u in range(4):
        cols = pl.ds(u * head_width, head_width)
        lv[u, 0:4, :] = jnp.where(slot == t, vec[0:1, cols], 0.0)
        here = (t == u).astype(F32)
        lv[u, 4:5, :] = qsum * here
        lv[u, 5:6, :] = vsum * here
        lv[u, 6:7, :] = vec[3:4, cols]
        lv[u, 7:8, :] = vec[4:5, cols]
        lv[u, 8:9, :] = vec[1:2, cols]
        lv[u, 9:10, :] = vec[2:3, cols]
        lv[u, 10:11, :] = gain_sum[:, u * head_width : (u + 1) * head_width]
        lv[u, 11:12, :] = bias_sum[:, u * head_width : (u + 1) * head_width]
    level1 = [
        go(remote(lv.at[t ^ j], rv1.at[j], v1s.at[j], v1r.at[j], mates[j - 1])) for j in range(1, 4)
    ]

    def pass_on(i, _):
        d = lines - 1 - i
        x_copy(d).wait_recv()
        sz[d] = (keep[row((z ^ d) * 2 + x), :] + rx[d].astype(F32)).astype(BF)
        z_copy(d).start()
        return 0

    lax.fori_loop(0, (lines - 1) // 2, pass_on, 0)
    hidv[...] = hidv[...] + pnearv[...].astype(F32) + pfarv[...].astype(F32) + fc2_bias[...]
    outs = [pltpu.make_async_copy(hidv, out_out, osem.at[0])]
    outs[0].start()
    for c in level1:
        c.wait_recv()
    sv[...] = lv[t] + rv1[1] + rv1[2] + rv1[3]
    level2 = [
        go(remote(sv, rv2.at[e], v2s.at[e], v2r.at[e], others[e - 1])) for e in range(1, shards)
    ]
    for c in third:
        c.wait_recv()

    def finish(c):
        second[c].wait_recv()
        gn = near[part(c), :] + r1[1, part(c), :].astype(F32) + q1[part(c), :].astype(F32)
        unit, inv = normalize(tokv[part(c), :].astype(F32))
        scaled = gn * gain[...]
        inner = (
            scaled
            - jnp.mean(scaled, axis=1, keepdims=True)
            - unit * jnp.mean(scaled * unit, axis=1, keepdims=True)
        )
        ghidv[part(c), :] = ghidv[part(c), :] + inv * inner

    for c in range(chunks - 1):
        finish(c)
    lax.fori_loop((lines - 1) // 2, lines - 1, pass_on, 0)
    for c in level2:
        c.wait_recv()
    total = sv[...]
    for e in range(1, shards):
        total = total + rv2[e]
    gv[t] = total
    level3 = [
        go(remote(gv.at[t], gv.at[t], v3s.at[j], v3r.at[j], mates[j - 1])) for j in range(1, 4)
    ]
    finish(chunks - 1)
    outs.append(pltpu.make_async_copy(ghidv, tok_out, osem.at[1]))
    outs[1].start()
    x_copy(0).wait_recv()
    wsum[...] = keep[row(f), :] + rx[0].astype(F32)

    def collect(i, _):
        d = lines - 1 - i
        z_copy(d).wait_recv()
        wsum[...] += rz[d].astype(F32)
        return 0

    lax.fori_loop(0, lines - 1, collect, 0)
    for k in range(3):
        wqs[k] = wsum[:, k * head_width : (k + 1) * head_width]
    wos[...] = wsum[:, 3 * head_width :].T
    outs.append(pltpu.make_async_copy(wqs, wq_out, osem.at[2]))
    outs.append(pltpu.make_async_copy(wos, wo_out, osem.at[3]))
    outs[2].start()
    outs[3].start()
    for c in level3:
        c.wait_recv()
    for u in range(4):
        cols = slice(u * head_width, (u + 1) * head_width)
        for r in range(4):
            fcb_out[:, r * width + u * head_width : r * width + (u + 1) * head_width] = gv[u, r : r + 1, :]
        qv_out[:, cols] = gv[u, 4:6, :]
        for r, ref in enumerate((g_a, g_b, g_c, g_d, g_e, g_f)):
            ref[:, cols] = gv[u, 6 + r : 7 + r, :]
    for c in sends:
        c.wait_send()

    def drain(d, _):
        x_copy(d).wait_send()

        @pl.when(d > 0)
        def _():
            z_copy(d).wait_send()

        return 0

    lax.fori_loop(0, lines, drain, 0)
    for c in outs:
        c.wait()


def last(shards, dqkv, weights, one, back, att, tok, ghid, hid, pnear, pfar, vec, gain, bias, fc2_bias):
    _, rows, width = one.shape
    head_width = att.shape[2]
    per = width // shards
    lines = shards // 2
    chunks = 2
    dma = pltpu.SemaphoreType.DMA
    vm = pl.BlockSpec(memory_space=VM)
    hbm = pl.BlockSpec(memory_space=HB)
    V = pltpu.VMEM
    sems = [
        (8,), (2, chunks), (2, chunks), (chunks,), (chunks,), (lines,), (lines,), (lines,), (lines,),
        (4,), (4,), (shards,), (shards,), (4,), (4,), (4,),
    ]
    return pl.pallas_call(
        functools.partial(last_kernel, shards, chunks),
        name="last",
        out_shape=[
            jax.ShapeDtypeStruct((rows, width), F32),
            jax.ShapeDtypeStruct((rows, width), F32),
            jax.ShapeDtypeStruct((3, per, head_width), F32),
            jax.ShapeDtypeStruct((head_width, per), F32),
            jax.ShapeDtypeStruct((2, width), F32),
            jax.ShapeDtypeStruct((1, 4 * width), F32),
        ]
        + [jax.ShapeDtypeStruct((1, width), F32)] * 6,
        in_specs=[vm, vm] + [hbm] * 8 + [vm] * 4,
        out_specs=[hbm] * 4 + [vm] * 8,
        scratch_shapes=[
            V((rows, width), F32), V((rows, width), BF), V((rows, width), BF),
            V((3, per, head_width), F32), V((head_width, per), F32),
            V((4, rows, width), BF), V((4, rows, width), BF), V((4, rows, head_width), BF),
            V((rows, width), BF), V((rows, width), F32), V((3 * head_width, width), BF),
            V((2, rows, width), BF), V((2, rows, width), BF), V((rows, width), BF), V((rows, width), BF),
            V((rows, width), F32), V((width, 4 * head_width), BF), V((width, 4 * head_width), F32),
            V((lines, per, 4 * head_width), BF), V((lines, per, 4 * head_width), BF),
            V((lines, per, 4 * head_width), BF), V((per, 4 * head_width), F32),
            V((8, width), F32), V((4, 16, head_width), F32), V((4, 16, head_width), F32),
            V((16, head_width), F32), V((shards, 16, head_width), F32), V((4, 16, head_width), F32),
        ]
        + [dma(s) for s in sems],
        compiler_params=pltpu.CompilerParams(
            collective_id=2, has_side_effects=True, vmem_limit_bytes=60 << 20
        ),
        cost_estimate=pl.CostEstimate(flops=30 << 30, bytes_accessed=100 << 20, transcendentals=0),
    )(dqkv, weights, one, back, att, tok, ghid, hid, pnear, pfar, vec, gain, bias, fc2_bias)


FAR = [(0, 2), (2, 0), (1, 3), (3, 1)]


def swap_far(v):
    return lax.ppermute(v, "tensor", FAR)


def body(
    tokens,
    cotangent,
    pic_starts,
    w_qkv,
    qv_bias,
    w_out,
    out_bias,
    ln1_gain,
    ln1_bias,
    w_fc1,
    fc1_bias,
    w_fc2,
    fc2_bias,
    ln2_gain,
    ln2_bias,
):
    rows, width = tokens.shape
    shards = lax.axis_size("fsdp")
    rank = lax.axis_index("tensor")
    meta = jnp.concatenate([rank.astype(jnp.int32)[None], pic_starts[0]])
    one, qkv, wq_full, out_full, fc_in, up_far, att, lse = head(
        shards, tokens, w_qkv.transpose(1, 0, 2), w_out, w_fc1, w_fc2,
        ln1_gain[None], ln1_bias[None], qv_bias, pic_starts, cotangent,
    )
    hidden_one, ghid, back, grad_att, fc1_part, fc2_grad, part_far, part_near, vec = middle(
        shards, att, out_full, tokens, cotangent, up_far, fc_in,
        ln2_gain[None], ln2_bias[None], out_bias[None], fc1_bias[None],
    )
    fc1_grad = lax.psum_scatter(
        fc1_part.reshape(width, -1), "fsdp", scatter_dimension=0, tiled=True
    ).astype(F32)
    ffn_far = swap_far(part_far)
    qkv_grad = attn_bwd(meta, qkv, grad_att, att, lse)
    output, input_grad, wq_grad, wo_grad, qv_grad, fc1_b, *vecs = last(
        shards, qkv_grad, wq_full, one, back, att, tokens, ghid, hidden_one, part_near, ffn_far,
        vec, ln1_gain[None], ln1_bias[None], fc2_bias[None],
    )
    out_b, fc2_b, gain_two, shift_two, gain_one, shift_one = [v[0] for v in vecs]
    return (
        output,
        input_grad,
        wq_grad.transpose(1, 0, 2),
        qv_grad,
        wo_grad,
        out_b,
        gain_one,
        shift_one,
        fc1_grad,
        fc1_b[0],
        fc2_grad,
        fc2_b,
        gain_two,
        shift_two,
    )


def solution(mesh):
    return jax.shard_map(
        body,
        mesh=mesh,
        in_specs=(
            P(("fsdp", "tensor"), None),
            P(("fsdp", "tensor"), None),
            P("fsdp", None),
            P("fsdp", None, "tensor"),
            P(),
            P("tensor", "fsdp"),
            P(),
            P(),
            P(),
            P("fsdp", "tensor"),
            P(),
            P("tensor", "fsdp"),
            P(),
            P(),
            P(),
        ),
        out_specs=(
            P(("fsdp", "tensor"), None),
            P(("fsdp", "tensor"), None),
            P("fsdp", None, "tensor"),
            P(),
            P("tensor", "fsdp"),
            P(),
            P(),
            P(),
            P("fsdp", "tensor"),
            P(),
            P("tensor", "fsdp"),
            P(),
            P(),
            P(),
        ),
        check_vma=False,
    )
```

```python
import functools
import math

import jax
import jax.numpy as jnp
from jax import lax
from jax.experimental import pallas as pl
from jax.experimental.pallas import tpu as pltpu
from jax.sharding import PartitionSpec as P

HD = 64
PIC = 256
F32 = jnp.float32
BF = jnp.bfloat16
NEG = -1e30
NORM_EPSILON = 1e-05
GELU_SCALE = math.sqrt(2.0 / math.pi)
GELU_CUBIC = 0.044715
VM = pltpu.MemorySpace.VMEM
SM = pltpu.MemorySpace.SMEM
HB = pltpu.MemorySpace.HBM
PRE = (1, 2)


def nn(a, b):
    return lax.dot_general(a, b, (((1,), (0,)), ((), ())), preferred_element_type=F32)


def nt(a, b):
    return lax.dot_general(a, b, (((1,), (1,)), ((), ())), preferred_element_type=F32)


def normalize(values):
    average = jnp.mean(values, axis=1, keepdims=True)
    centered = values - average
    inv_std = lax.rsqrt(jnp.mean(centered * centered, axis=1, keepdims=True) + NORM_EPSILON)
    return centered * inv_std, inv_std


def normalize_back(gradient, unit_rows, inv_std, gain_row):
    scaled = gradient * gain_row
    inner = (
        scaled
        - jnp.mean(scaled, axis=1, keepdims=True)
        - unit_rows * jnp.mean(scaled * unit_rows, axis=1, keepdims=True)
    )
    return inv_std * inner, jnp.sum(gradient * unit_rows, axis=0), jnp.sum(gradient, axis=0)


MESH = pl.DeviceIdType.MESH


def remote(src, dst, send, recv, where):
    return pltpu.make_async_remote_copy(
        src_ref=src, dst_ref=dst, send_sem=send, recv_sem=recv, device_id=where, device_id_type=MESH
    )


def greet(peers):
    barrier = pltpu.get_barrier_semaphore()
    for peer in peers:
        pl.semaphore_signal(barrier, inc=1, device_id=peer, device_id_type=MESH)
    pl.semaphore_wait(barrier, len(peers))


def head_kernel(
    shards, chunks,
    tok, wq, wo, w1, w2, gain, bias, qvb, starts, cot,
    n_out, qkv_out, wq_out, ot_out, fc_out, up_out, att_out, lse_out,
    nv, wqv, wov, otv, fcv, qv, kn, qT, vT, att, lsev,
    ysend, yrecv, csend, crecv, fsend, frecv, zqs, zqr, xqs, xqr, zos, zor, xos, xor,
    zfs, zfr, ups, upr, lsem, osem,
):
    f = lax.axis_index("fsdp")
    t = lax.axis_index("tensor")
    rows, width = tok.shape
    head_width, per = wo.shape
    hid = w1.shape[1]
    step = rows // chunks
    lines = shards // 2
    far = {"fsdp": f, "tensor": t ^ 2}
    sib = {"fsdp": f, "tensor": t ^ 1}
    side = {"fsdp": f ^ 1, "tensor": t}
    alongs = [{"fsdp": f ^ (2 * d), "tensor": t} for d in range(1, lines)]
    greet([far, sib, side] + alongs)
    sends = []

    def go(copy):
        copy.start()
        sends.append(copy)
        return copy

    zq, zo, xq, xo = [], [], [], []
    for d in range(1, lines):
        zq.append(go(remote(wq, wqv.at[f], zqs.at[d], zqr.at[d], alongs[d - 1])))
    xq.append(go(remote(wq, wqv.at[f], xqs.at[0], xqr.at[0], side)))
    ys, cs, fs = [], [], []
    for c in range(chunks):
        part = pl.ds(c * step, step)
        unit, _ = normalize(tok[part, :].astype(F32))
        nv[0, part, :] = (unit * gain[...] + bias[...]).astype(BF)
        ys.append(go(remote(nv.at[0, part], nv.at[2, part], ysend.at[c], yrecv.at[c], far)))
        cs.append(go(remote(nv.at[0, part], nv.at[1, part], csend.at[c], crecv.at[c], sib)))
    for d in range(1, lines):
        zo.append(go(remote(wo, wov.at[f], zos.at[d], zor.at[d], alongs[d - 1])))
    xo.append(go(remote(wo, wov.at[f], xos.at[0], xor.at[0], side)))
    wqv[f] = wq[...]
    wov[f] = wo[...]
    fcv[:, :hid] = w1[...]
    fcv[:, hid:] = w2[...].T
    local = [pltpu.make_async_copy(fcv, fc_out.at[f], lsem.at[0])]
    local[0].start()

    def forward_far(c):
        part = pl.ds(c * step, step)
        ys[c].wait_recv()
        fs.append(go(remote(nv.at[2, part], nv.at[3, part], fsend.at[c], frecv.at[c], sib)))

    todo = list(range(chunks))
    for d in range(1, lines):
        zq[d - 1].wait_recv()
        slot = f ^ (2 * d)
        xq.append(go(remote(wqv.at[slot], wqv.at[slot], xqs.at[d], xqr.at[d], side)))
        if len(todo) > 1:
            forward_far(todo.pop(0))
    for d in range(1, lines):
        zo[d - 1].wait_recv()
        slot = f ^ (2 * d)
        xo.append(go(remote(wov.at[slot], wov.at[slot], xos.at[d], xor.at[d], side)))
    fc = []
    for d in PRE:
        if d < lines:
            fc.append(go(remote(fcv, fc_out.at[f], zfs.at[d], zfr.at[d], alongs[d - 1])))
    for c in cs:
        c.wait_recv()
    for d in range(lines):
        xq[d].wait_recv()
    start = pl.multiple_of(t * head_width, head_width)
    adds = (qvb[0:1, pl.ds(start, head_width)], None, qvb[1:2, pl.ds(start, head_width)])

    def project(j, _):
        b = t ^ j
        for k in range(3):
            value = nn(nv[j], wqv[:, k].reshape(width, head_width))
            if adds[k] is not None:
                value = value + adds[k]
            value = value.astype(BF)
            qv[j, :, k * head_width : (k + 1) * head_width] = value
            if k == 0:
                qT[b] = (value * jnp.asarray(HD**-0.5, BF)).T
            elif k == 1:
                kn[b] = value
            else:
                vT[b] = value.T
        return 0

    lax.fori_loop(0, 2, project, 0)
    while todo:
        forward_far(todo.pop(0))
    up = go(remote(cot, up_out, ups.at[0], upr.at[0], far))
    for c in fs:
        c.wait_recv()
    lax.fori_loop(2, 4, project, 0)
    for d in range(lines):
        xo[d].wait_recv()
    fc.append(go(remote(fcv, fc_out.at[f], zfs.at[0], zfr.at[0], side)))
    if per % 128 == 0:
        def place(s, _):
            otv[:, pl.ds(pl.multiple_of(s * per, per), per)] = wov[s]
            return 0

        lax.fori_loop(0, shards, place, 0)
    else:
        for s in range(shards):
            otv[:, s * per : (s + 1) * per] = wov[s]
    outs = [
        pltpu.make_async_copy(src, dst, osem.at[n])
        for n, (src, dst) in enumerate([(nv, n_out), (qv, qkv_out), (wqv, wq_out), (otv, ot_out)])
    ]
    for c in outs:
        c.start()
    rowk = lax.broadcasted_iota(jnp.int32, (rows, rows), 0)
    colq = lax.broadcasted_iota(jnp.int32, (rows, rows), 1)
    half = lax.broadcasted_iota(jnp.int32, (2 * HD, rows), 0) < HD
    for i in range(4):
        at = starts[0, i] - i * rows

        def pair(p, _, i=i, at=at):
            col = pl.multiple_of(p * 2 * HD, 2 * HD)
            qp = qT[i, pl.ds(col, 2 * HD), :]
            zero = jnp.zeros_like(qp)
            masked = (jnp.where(half, qp, zero), jnp.where(half, zero, qp))
            found = []
            for hh in range(2):
                ss, top = [], None
                for m in range(i + 1):
                    s = nn(kn[m, :, pl.ds(col, 2 * HD)], masked[hh])
                    if m == i:
                        inside = (rowk >= at) & (rowk < at + PIC) & (colq >= at) & (colq < at + PIC)
                        s = jnp.where((rowk <= colq) | inside, s, NEG)
                    peak = jnp.max(s, axis=0, keepdims=True)
                    top = peak if top is None else jnp.maximum(top, peak)
                    ss.append(s)
                total, acc = 0.0, 0.0
                for m in range(i + 1):
                    e = jnp.exp(ss[m] - top)
                    total = total + jnp.sum(e, axis=0, keepdims=True)
                    acc = acc + nn(vT[m, pl.ds(col + hh * HD, HD), :], e.astype(BF))
                found.append(acc * (1.0 / total))
                lsev[t ^ i, pl.ds(p * 2 + hh, 1), :] = top + jnp.log(total)
            att[i, :, pl.ds(col, 2 * HD)] = jnp.concatenate(found, axis=0).astype(BF).T
            return 0

        lax.fori_loop(0, head_width // (2 * HD), pair, 0)
    outs += [pltpu.make_async_copy(att.at[t ^ j], att_out.at[j], osem.at[4 + j]) for j in range(4)]
    outs.append(pltpu.make_async_copy(lsev, lse_out, osem.at[8]))
    for c in outs[4:]:
        c.start()
    for c in fc + [up]:
        c.wait_recv()
    for c in sends:
        c.wait_send()
    for c in local + outs:
        c.wait()


def head(shards, tokens, wq, wo, w1, w2, gain, bias, qv_bias, starts, cot):
    rows, width = tokens.shape
    head_width, per = wo.shape
    hid = w1.shape[1]
    lines = shards // 2
    chunks = 4
    heads = head_width // HD
    dma = pltpu.SemaphoreType.DMA
    vm = pl.BlockSpec(memory_space=VM)
    hbm = pl.BlockSpec(memory_space=HB)
    V = pltpu.VMEM
    full = (4, rows, width)
    three = (4, rows, 3 * head_width)
    return pl.pallas_call(
        functools.partial(head_kernel, shards, chunks),
        name="head",
        out_shape=[
            jax.ShapeDtypeStruct(full, BF),
            jax.ShapeDtypeStruct(three, BF),
            jax.ShapeDtypeStruct((shards, 3, per, head_width), BF),
            jax.ShapeDtypeStruct((head_width, width), BF),
            jax.ShapeDtypeStruct((shards, per, 2 * hid), BF),
            jax.ShapeDtypeStruct((rows, width), BF),
            jax.ShapeDtypeStruct((4, rows, head_width), BF),
            jax.ShapeDtypeStruct((4, heads, rows), F32),
        ],
        in_specs=[vm] * 8 + [pl.BlockSpec(memory_space=SM), hbm],
        out_specs=[hbm] * 8,
        scratch_shapes=[
            V(full, BF), V((shards, 3, per, head_width), BF), V((shards, head_width, per), BF),
            V((head_width, width), BF), V((per, 2 * hid), BF), V(three, BF),
            V((4, rows, head_width), BF), V((4, head_width, rows), BF), V((4, head_width, rows), BF),
            V((4, rows, head_width), BF), V((4, heads, rows), F32),
        ]
        + [dma((chunks,))] * 6
        + [dma((lines,))] * 8
        + [dma((max(lines, 4),))] * 2
        + [dma((1,))] * 3
        + [dma((9,))],
        compiler_params=pltpu.CompilerParams(
            collective_id=0, has_side_effects=True, vmem_limit_bytes=56 << 20
        ),
        cost_estimate=pl.CostEstimate(flops=40 << 30, bytes_accessed=90 << 20, transcendentals=0),
    )(tokens, wq, wo, w1, w2, gain, bias, qv_bias, starts, cot)


def middle_kernel(
    shards, chunks,
    att, ot, tok, cot, up_far, fc_in, gain, bias, out_bias, fc_bias,
    hid_out, ghid_out, back_out, do_out, g1_out, w2_out, part_far, part_near, vec,
    wfc, wt, ott, upv, twov, actv, pgv, backv,
    s1, r1, a1, q1, near, hv, rx, sz, rz, wsum, wsum_t, dov,
    s1s, s1r, y1s, y1r, c2s, c2r, y2s, y2r, f2s, f2r,
    s3s, s3r, y3s, y3r, c4s, c4r, y4s, y4r, f4s, f4r,
    s5s, s5r, ups, upr, lsem, zs, zr, xs, xr, osem, gxs, gxr, gzs, gzr,
):
    f = lax.axis_index("fsdp")
    t = lax.axis_index("tensor")
    rows, width = tok.shape
    per = fc_in.shape[1]
    hid = fc_in.shape[2] // 2
    pre = [d for d in PRE if d < shards // 2]
    step = rows // chunks
    lines = shards // 2
    far = {"fsdp": f, "tensor": t ^ 2}
    sib = {"fsdp": f, "tensor": t ^ 1}
    side = {"fsdp": f ^ 1, "tensor": t}
    direct = [d for d in range(1, lines) if d not in pre]
    alongs = {d: {"fsdp": f ^ (2 * d), "tensor": t} for d in range(1, lines)}
    greet([far, sib, side] + [alongs[d] for d in range(1, lines)])
    sends = []

    def go(copy):
        copy.start()
        sends.append(copy)
        return copy

    def part(c):
        return pl.ds(c * step, step)

    halves = (pl.ds(0, hid), pl.ds(hid, hid))
    local = [
        pltpu.make_async_copy(fc_in.at[slot], wfc.at[slot], lsem.at[n])
        for n, slot in enumerate([f, f ^ 1] + [f ^ (2 * d) for d in pre])
    ]
    local.append(pltpu.make_async_copy(cot, upv.at[0], lsem.at[len(pre) + 2]))
    local.append(pltpu.make_async_copy(up_far, upv.at[2], lsem.at[len(pre) + 3]))
    for c in local:
        c.start()
    xf = {}
    zf = {}
    for h in range(2):
        for d in direct:
            zf[d, h] = go(
                remote(fc_in.at[f, :, halves[h]], wfc.at[f, :, halves[h]], zs.at[h, d], zr.at[h, d], alongs[d])
            )

    def forward_pre(h):
        for d in pre:
            slot = f ^ (2 * d)
            xf[d, h] = go(
                remote(
                    fc_in.at[slot, :, halves[h]], wfc.at[slot, :, halves[h]],
                    xs.at[h, d], xr.at[h, d], side,
                )
            )

    def forward_direct(h):
        for d in direct:
            zf[d, h].wait_recv()
            slot = f ^ (2 * d)
            xf[d, h] = go(
                remote(
                    wfc.at[slot, :, halves[h]], wfc.at[slot, :, halves[h]],
                    xs.at[h, d], xr.at[h, d], side,
                )
            )

    forward_pre(0)
    first, second, third = [], [], []
    for c in range(chunks):
        s1[0, part(c), :] = nn(att[3, part(c), :], ot[...]).astype(BF)
        first.append(go(remote(s1.at[0, part(c)], r1.at[0, part(c)], s1s.at[0, c], s1r.at[0, c], sib)))
    for c in range(chunks):
        mine = nn(att[2, part(c), :], ot[...])
        first[c].wait_recv()
        a1[0, part(c), :] = (mine + r1[0, part(c), :].astype(F32)).astype(BF)
        second.append(go(remote(a1.at[0, part(c)], q1.at[0, part(c)], y1s.at[c], y1r.at[c], far)))
    for c in range(chunks):
        s1[1, part(c), :] = nn(att[1, part(c), :], ot[...]).astype(BF)
        third.append(go(remote(s1.at[1, part(c)], r1.at[1, part(c)], s1s.at[1, c], s1r.at[1, c], sib)))
    ott[...] = ot[...].T
    up_copies = [
        go(remote(cot, upv.at[1], ups.at[0], upr.at[0], sib)),
        go(remote(up_far, upv.at[3], ups.at[1], upr.at[1], sib)),
    ]
    for c in range(chunks):
        mine = nn(att[0, part(c), :], ot[...])
        third[c].wait_recv()
        near[part(c), :] = mine + r1[1, part(c), :].astype(F32)
    vec[...] = jnp.zeros_like(vec)
    forward_direct(0)
    forward_pre(1)
    ag_far, ag_sib = [], []
    for c in range(chunks):
        second[c].wait_recv()
        hidden = (
            tok[part(c), :].astype(F32)
            + near[part(c), :]
            + q1[0, part(c), :].astype(F32)
            + out_bias[...]
        )
        hv[part(c), :] = hidden
        unit, _ = normalize(hidden)
        twov[0, part(c), :] = (unit * gain[...] + bias[...]).astype(BF)
        ag_far.append(go(remote(twov.at[0, part(c)], twov.at[2, part(c)], y2s.at[c], y2r.at[c], far)))
        ag_sib.append(go(remote(twov.at[0, part(c)], twov.at[1, part(c)], c2s.at[c], c2r.at[c], sib)))
        if c == 0:
            forward_direct(1)
    outs = [pltpu.make_async_copy(hv, hid_out, osem.at[0])]
    outs[0].start()
    for c in local:
        c.wait()
    for h in range(2):
        xo = [xf[d, h] for d in pre] + [xf[d, h] for d in direct]
        for c in xo:
            c.wait_recv()

        def flip(s, _, h=h):
            wt[pl.ds(h * hid, hid), pl.ds(pl.multiple_of(s * per, per), per)] = wfc[s, :, halves[h]].T
            return 0

        if per % 128 == 0:
            lax.fori_loop(0, shards, flip, 0)
        else:
            wt[pl.ds(h * hid, hid), :] = wfc[:, :, halves[h]].reshape(width, hid).T
    for c in up_copies:
        c.wait_recv()
    for c in ag_sib:
        c.wait_recv()
    start = pl.multiple_of(t * hid, hid)
    tile = hid // 2

    def feed(j, at):
        block = pl.ds(pl.multiple_of(at * step, step), step)
        two = twov[j, block, :]
        up = upv[j, block, :]
        total = None
        for n in range(2):
            cols = pl.ds(n * tile, tile)
            x = nn(two, wfc[:, :, cols].reshape(width, tile))
            x = x + fc_bias[:, pl.ds(pl.multiple_of(start + n * tile, tile), tile)]
            hg = nn(up, wfc[:, :, pl.ds(hid + n * tile, tile)].reshape(width, tile))
            sq = x * x
            th = jnp.tanh(GELU_SCALE * (x + GELU_CUBIC * (sq * x)))
            half = 0.5 * (1.0 + th)
            actv[j, block, cols] = (x * half).astype(BF)
            slope = half + (0.5 * GELU_SCALE) * x * (1.0 - th * th) * (1.0 + (3.0 * GELU_CUBIC) * sq)
            pg = (hg * slope).astype(BF)
            pgv[j, block, cols] = pg
            vec[0:1, cols] += jnp.sum(pg.astype(F32), axis=0, keepdims=True)
            term = nn(pg, wt[cols, :])
            total = term if total is None else total + term
        return total

    def copies(c):
        block = pl.ds(pl.multiple_of(c * step, step), step)
        return (
            remote(twov.at[0, block], twov.at[2, block], y2s.at[c], y2r.at[c], far),
            remote(twov.at[2, block], twov.at[3, block], f2s.at[c], f2r.at[c], sib),
            remote(a1.at[1, block], q1.at[1, block], y3s.at[c], y3r.at[c], far),
        )

    def core_copy(k, c):
        block = pl.ds(pl.multiple_of(c * step, step), step)
        return remote(s1.at[2 + k, block], r1.at[2 + k, block], s3s.at[k, c], s3r.at[k, c], sib)

    def chunk(c, _):
        block = pl.ds(pl.multiple_of(c * step, step), step)
        got, fwd, send2 = copies(c)
        got.wait_recv()
        fwd.start()
        fwd.wait_recv()

        def pair(k, _):
            give = core_copy(k, c)

            def one(i, _):
                total = feed(3 - 2 * k - i, c)

                @pl.when(i == 0)
                def _():
                    s1[2 + k, block, :] = total.astype(BF)
                    give.start()

                @pl.when(i == 1)
                def _():
                    near[block, :] = total

                return 0

            lax.fori_loop(0, 2, one, 0)

            @pl.when(k == 0)
            def _():
                give.wait_recv()
                a1[1, block, :] = (near[block, :] + r1[2, block, :].astype(F32)).astype(BF)
                send2.start()

            return 0

        lax.fori_loop(0, 2, pair, 0)
        return 0

    lax.fori_loop(0, chunks, chunk, 0)

    span = 256
    ratio = span // (2 * per)
    groups = width // span
    z = f // 2
    x = lax.rem(f, 2)

    def x_copy(d):
        return remote(wfc.at[(z ^ d) * 2 + (1 - x), :, halves[0]], rx.at[d], gxs.at[d], gxr.at[d], side)

    def z_copy(d):
        return remote(
            sz.at[d], rz.at[d], gzs.at[d], gzr.at[d], {"fsdp": f ^ (2 * d), "tensor": t}
        )

    def weight_grad(left, right, h, send):
        def group_of(i, _):
            near_group = groups - 1 - i
            group = near_group ^ (z // ratio)
            cols = pl.ds(pl.multiple_of(group * span, span), span)
            acc = None
            for j in range(4):
                term = nn(left[j, :, cols].T, right[j])
                acc = term if acc is None else acc + term
            count = span // per
            slots = pl.ds(group * count, count)
            wfc[slots, :, halves[h]] = acc.astype(BF).reshape(count, per, hid)
            if send:

                def launch(e, _):
                    x_copy(near_group * ratio + e).start()
                    return 0

                lax.fori_loop(0, ratio, launch, 0)
            return 0

        lax.fori_loop(0, groups, group_of, 0)

    def pass_on(d):
        x_copy(d).wait_recv()
        sz[d] = (wfc[(z ^ d) * 2 + x, :, halves[0]].astype(F32) + rx[d].astype(F32)).astype(BF)
        z_copy(d).start()

    for d in direct:
        for h in range(2):
            xf[d, h].wait_send()
    b_far, b_sib = [], []
    for c in range(chunks):
        _, _, send2 = copies(c)
        core_copy(1, c).wait_recv()
        send2.wait_recv()
        gn = near[part(c), :] + r1[3, part(c), :].astype(F32) + q1[1, part(c), :].astype(F32)
        unit, inv = normalize(hv[part(c), :])
        back, g_sum, b_sum = normalize_back(gn, unit, inv, gain[...])
        cots = upv[0, part(c), :].astype(F32)
        ghid = cots + back
        near[part(c), :] = ghid
        backv[0, part(c), :] = ghid.astype(BF)
        b_far.append(go(remote(backv.at[0, part(c)], backv.at[2, part(c)], y4s.at[c], y4r.at[c], far)))
        b_sib.append(go(remote(backv.at[0, part(c)], backv.at[1, part(c)], c4s.at[c], c4r.at[c], sib)))
        vec[1:2, :] += g_sum[None]
        vec[2:3, :] += b_sum[None]
        vec[3:4, :] += jnp.sum(ghid, axis=0, keepdims=True)
        vec[4:5, :] += jnp.sum(cots, axis=0, keepdims=True)
        if c == 0:
            weight_grad(upv, actv, 0, True)
    pass_on(lines - 1)
    outs.append(pltpu.make_async_copy(near, ghid_out, osem.at[1]))
    outs[1].start()

    for c in range(chunks):
        first[c].wait_send()
        third[c].wait_send()
        core_copy(0, c).wait_send()
        core_copy(1, c).wait_send()
    for k, slot in ((0, 0), (1, 1)):
        def give(c, _, j=3 - 2 * k, slot=slot):
            block = pl.ds(pl.multiple_of(c * step, step), step)
            s1[slot, block, :] = nn(actv[j, block, :], wt[hid:, :]).astype(BF)
            return 0

        lax.fori_loop(0, chunks, give, 0)
        given = go(remote(s1.at[slot], r1.at[slot], s5s.at[slot], s5r.at[slot], sib))

        def keep(c, _, j=2 - 2 * k, slot=slot):
            block = pl.ds(pl.multiple_of(c * step, step), step)
            s1[2 + slot, block, :] = nn(actv[j, block, :], wt[hid:, :]).astype(BF)
            return 0

        lax.fori_loop(0, chunks, keep, 0)
        given.wait_recv()
        summed = s1.at[2 + slot]
        summed[...] = (summed[...].astype(F32) + r1[slot].astype(F32)).astype(BF)
        outs.append(pltpu.make_async_copy(summed, part_near if k else part_far, osem.at[2 + k]))
        outs[-1].start()

    if lines > 2:
        pass_on(lines - 2)
    weight_grad(twov, pgv, 1, False)
    outs.append(pltpu.make_async_copy(wfc.at[:, :, halves[1]], g1_out, osem.at[5]))
    outs[-1].start()
    if lines > 3:

        def pass_more(i, _):
            pass_on(lines - 3 - i)
            return 0

        lax.fori_loop(0, lines - 3, pass_more, 0)
    for c in b_sib:
        c.wait_recv()

    def attended_grad(j, _):
        dov[j] = nn(backv[j], ott[...]).astype(BF)
        return 0

    lax.fori_loop(0, 2, attended_grad, 0)
    fwds = []
    for c in range(chunks):
        b_far[c].wait_recv()
        fwds.append(go(remote(backv.at[2, part(c)], backv.at[3, part(c)], f4s.at[c], f4r.at[c], sib)))
    x_copy(0).wait_recv()
    wsum[...] = wfc[z * 2 + x, :, halves[0]].astype(F32) + rx[0].astype(F32)

    def collect(i, _):
        d = lines - 1 - i
        z_copy(d).wait_recv()
        wsum[...] += rz[d].astype(F32)
        return 0

    lax.fori_loop(0, lines - 1, collect, 0)
    wsum_t[...] = wsum[...].T
    outs.append(pltpu.make_async_copy(wsum_t, w2_out, osem.at[6]))
    outs[-1].start()
    for c in fwds:
        c.wait_recv()
    outs.append(pltpu.make_async_copy(backv, back_out, osem.at[4]))
    outs[-1].start()
    lax.fori_loop(2, 4, attended_grad, 0)
    outs.append(pltpu.make_async_copy(dov, do_out, osem.at[7]))
    outs[-1].start()
    waited = first + third + [xf[d, h] for d in direct for h in range(2)]
    for c in sends:
        if not any(c is other for other in waited):
            c.wait_send()
    for c in range(chunks):
        _, fwd, send2 = copies(c)
        fwd.wait_send()
        send2.wait_send()

    def drain(d, _):
        x_copy(d).wait_send()

        @pl.when(d > 0)
        def _():
            z_copy(d).wait_send()

        return 0

    lax.fori_loop(0, lines, drain, 0)
    for c in outs:
        c.wait()


def middle(shards, att, ot, tok, cot, up_far, fc_in, gain, bias, out_bias, fc_bias):
    rows, width = tok.shape
    per, hid2 = fc_in.shape[1:]
    hid = hid2 // 2
    head_width = ot.shape[0]
    lines = shards // 2
    chunks = 2
    dma = pltpu.SemaphoreType.DMA
    vm = pl.BlockSpec(memory_space=VM)
    hbm = pl.BlockSpec(memory_space=HB)
    full = (4, rows, width)
    one = (rows, width)
    block = (lines, per, hid)
    V = pltpu.VMEM
    sems = [
        (2, chunks), (2, chunks), (chunks,), (chunks,), (chunks,), (chunks,),
        (chunks,), (chunks,), (chunks,), (chunks,),
        (2, chunks), (2, chunks), (chunks,), (chunks,), (chunks,), (chunks,),
        (chunks,), (chunks,), (chunks,), (chunks,),
        (2,), (2,), (2,), (2,), (8,),
        (2, lines), (2, lines), (2, lines), (2, lines), (8,),
        (lines,), (lines,), (lines,), (lines,),
    ]
    return pl.pallas_call(
        functools.partial(middle_kernel, shards, chunks),
        name="middle",
        out_shape=[
            jax.ShapeDtypeStruct(one, F32),
            jax.ShapeDtypeStruct(one, F32),
            jax.ShapeDtypeStruct(full, BF),
            jax.ShapeDtypeStruct((4, rows, head_width), BF),
            jax.ShapeDtypeStruct((shards, per, hid), BF),
            jax.ShapeDtypeStruct((hid, per), F32),
            jax.ShapeDtypeStruct(one, BF),
            jax.ShapeDtypeStruct(one, BF),
            jax.ShapeDtypeStruct((8, width), F32),
        ],
        in_specs=[vm, vm, vm, hbm, hbm, hbm] + [vm] * 4,
        out_specs=[hbm] * 8 + [vm],
        scratch_shapes=[
            V((shards, per, 2 * hid), BF), V((2 * hid, width), BF), V((width, head_width), BF),
            V(full, BF), V(full, BF), V((4, rows, hid), BF), V((4, rows, hid), BF), V(full, BF),
            V(full, BF), V(full, BF), V((2, rows, width), BF), V((2, rows, width), BF),
            V(one, F32), V(one, F32), V(block, BF), V(block, BF), V(block, BF),
            V((per, hid), F32), V((hid, per), F32), V((4, rows, head_width), BF),
        ]
        + [dma(s) for s in sems],
        compiler_params=pltpu.CompilerParams(
            collective_id=1, has_side_effects=True, vmem_limit_bytes=60 << 20
        ),
        cost_estimate=pl.CostEstimate(flops=60 << 30, bytes_accessed=200 << 20, transcendentals=0),
    )(att, ot, tok, cot, up_far, fc_in, gain, bias, out_bias, fc_bias)


def tail_kernel(
    shards, chunks,
    qs, dos, ats, lse, starts, weights, vec, gain, bias, fc2_bias,
    one_in, back_in, tok_in, ghid_in, hid_in, pnear_in, pfar_in, g1_in,
    out_out, tok_out, wq_out, wo_out, w1_out, qv_out, fcb_out, g_a, g_b, g_c, g_d, g_e, g_f,
    qT, kT, doT, dk, dv, dl, dqkv,
    onev, backv, tokv, ghidv, hidv, pnearv, pfarv, wt,
    s1, r1, a1, q1, near, gq, go_, rx, sz, rz, rxo, szo, rzo, rx1, sz1, rz1, sum1, wqs, wos,
    stats, lv, rv1, sv, rv2, gv,
    lsem, s1s, s1r, y1s, y1r, xs, xr, zs, zr, v1s, v1r, v2s, v2r, v3s, v3r, pfs, pfr, osem,
):
    f = lax.axis_index("fsdp")
    t = lax.axis_index("tensor")
    _, rows, width = onev.shape
    head_width = ats.shape[2]
    per = width // shards
    lines = shards // 2
    step = rows // chunks
    z = f // 2
    x = lax.rem(f, 2)
    far = {"fsdp": f, "tensor": t ^ 2}
    sib = {"fsdp": f, "tensor": t ^ 1}
    side = {"fsdp": f ^ 1, "tensor": t}
    mates = [{"fsdp": f, "tensor": t ^ j} for j in range(1, 4)]
    others = [{"fsdp": f ^ e, "tensor": t} for e in range(1, shards)]
    greet(mates + others)
    sends = []

    def go(copy):
        copy.start()
        sends.append(copy)
        return copy

    def part(c):
        return pl.ds(c * step, step)

    def row(block):
        return pl.ds(pl.multiple_of(block * per, per), per)

    sources = (lambda b: g1_in.at[b], lambda b: go_.at[row(b)], lambda b: gq.at[row(b)])
    lands = ((rx1, sz1, rz1), (rxo, szo, rzo), (rx, sz, rz))

    def x_copy(k, d):
        return remote(
            sources[k]((z ^ d) * 2 + (1 - x)), lands[k][0].at[d], xs.at[k, d], xr.at[k, d], side
        )

    def z_copy(k, d):
        return remote(
            lands[k][1].at[d], lands[k][2].at[d], zs.at[k, d], zr.at[k, d],
            {"fsdp": f ^ (2 * d), "tensor": t},
        )

    def pass_on(k, d, own):
        x_copy(k, d).wait_recv()
        lands[k][1][d] = (own(d).astype(F32) + lands[k][0][d].astype(F32)).astype(BF)
        z_copy(k, d).start()

    def keep_of(d):
        return (z ^ d) * 2 + x

    def launch(i, _):
        x_copy(0, lines - 1 - i).start()
        return 0

    lax.fori_loop(0, lines, launch, 0)
    pf = go(remote(pfar_in, pfarv, pfs.at[0], pfr.at[0], far))
    local = [
        pltpu.make_async_copy(src, dst, lsem.at[n])
        for n, (src, dst) in enumerate(
            [
                (back_in, backv), (one_in, onev), (tok_in, tokv), (ghid_in, ghidv),
                (hid_in, hidv), (pnear_in, pnearv),
            ]
        )
    ]
    for c in local:
        c.start()
    keeps = []

    def own_block(d, _):
        pltpu.make_async_copy(g1_in.at[keep_of(d)], sz1.at[d], lsem.at[8 + d]).start()
        return 0

    lax.fori_loop(0, lines, own_block, 0)

    def pass_fc1(d):
        pltpu.make_async_copy(g1_in.at[keep_of(d)], sz1.at[d], lsem.at[8 + d]).wait()
        pass_on(0, d, lambda d: sz1[d])

    for j in range(4):
        b = t ^ j
        qT[b] = (qs[j, :, :head_width] * jnp.asarray(HD**-0.5, BF)).T
        kT[b] = qs[j, :, head_width : 2 * head_width].T
        do = dos[j]
        doT[b] = do.T
        prod = (do.astype(F32) * ats[j].astype(F32)).T
        for h in range(head_width // HD):
            dl[b, h : h + 1, :] = jnp.sum(prod[h * HD : (h + 1) * HD], axis=0, keepdims=True)
    dk[...] = jnp.zeros_like(dk)
    dv[...] = jnp.zeros_like(dv)
    for k in range(3):
        wt[k * head_width : (k + 1) * head_width, :] = weights[:, k].reshape(width, head_width).T

    span = 256
    ratio = span // (2 * per)
    groups = width // span

    def weight_grad(k, left, right, target):
        def group_of(i, _):
            near_group = groups - 1 - i
            group = near_group ^ (z // ratio)
            cols = pl.ds(pl.multiple_of(group * span, span), span)
            acc = None
            for j in range(4):
                term = nn(left[j, :, cols].T, right[j])
                acc = term if acc is None else acc + term
            target[cols, :] = acc.astype(BF)

            def send(e, _):
                x_copy(k, near_group * ratio + e).start()
                return 0

            lax.fori_loop(0, ratio, send, 0)
            return 0

        lax.fori_loop(0, groups, group_of, 0)

    rowk = lax.broadcasted_iota(jnp.int32, (rows, rows), 0)
    colq = lax.broadcasted_iota(jnp.int32, (rows, rows), 1)
    hrow = lax.broadcasted_iota(jnp.int32, (2 * HD, rows), 0) < HD
    hcol = lax.broadcasted_iota(jnp.int32, (rows, 2 * HD), 1) < HD

    def two(v, m):
        zero = jnp.zeros_like(v)
        return (jnp.where(m, v, zero), jnp.where(m, zero, v))

    def attend(i):
        at = starts[0, i] - i * rows
        jj = t ^ i

        def pair(p, _):
            col = pl.multiple_of(p * 2 * HD, 2 * HD)
            kcol = pl.multiple_of(head_width + p * 2 * HD, 2 * HD)
            vcol = pl.multiple_of(2 * head_width + p * 2 * HD, 2 * HD)
            qTz = two(qT[i, pl.ds(col, 2 * HD), :], hrow)
            doTz = two(doT[i, pl.ds(col, 2 * HD), :], hrow)
            qz = two(qs[jj, :, pl.ds(col, 2 * HD)], hcol)
            doz = two(dos[jj, :, pl.ds(col, 2 * HD)], hcol)
            ls = [lse[jj, pl.ds(p * 2 + hh, 1), :] for hh in range(2)]
            dlt = [dl[i, pl.ds(p * 2 + hh, 1), :] for hh in range(2)]

            def block(m, carry, diag):
                kb = qs[t ^ m, :, pl.ds(kcol, 2 * HD)]
                vb = qs[t ^ m, :, pl.ds(vcol, 2 * HD)]
                ktb = kT[m, pl.ds(col, 2 * HD), :]
                dvs, dks, new = 0.0, 0.0, []
                for hh in range(2):
                    s = nn(kb, qTz[hh])
                    if diag:
                        inside = (rowk >= at) & (rowk < at + PIC) & (colq >= at) & (colq < at + PIC)
                        s = jnp.where((rowk <= colq) | inside, s, NEG)
                    pr = jnp.exp(s - ls[hh])
                    dp = nn(vb, doTz[hh])
                    ds = (pr * (dp - dlt[hh])).astype(BF)
                    dvs = dvs + nn(pr.astype(BF), doz[hh])
                    dks = dks + nn(ds, qz[hh])
                    new.append(carry[hh] + nn(ktb[hh * HD : (hh + 1) * HD], ds))
                dv[m, :, pl.ds(col, 2 * HD)] += dvs
                dk[m, :, pl.ds(col, 2 * HD)] += dks
                return tuple(new)

            c = tuple(jnp.zeros((HD, rows), F32) for _ in range(2))
            c = block(i, c, True)
            if i > 0:
                c = lax.fori_loop(0, i, lambda m, c: block(m, c, False), c)
            dq = (jnp.concatenate(c, axis=0) * (HD**-0.5)).astype(BF)
            dqkv[jj, :, pl.ds(col, 2 * HD)] = dq.T
            return 0

        lax.fori_loop(0, head_width // (2 * HD), pair, 0)

    attend(0)
    local[0].wait()
    weight_grad(1, backv, ats, go_)
    pass_fc1(lines - 1)
    attend(1)
    if lines > 2:
        pass_fc1(lines - 2)
    attend(2)
    if lines > 3:

        def pass_more(i, _):
            pass_fc1(lines - 3 - i)
            return 0

        lax.fori_loop(0, lines - 3, pass_more, 0)
    attend(3)
    for j in range(4):
        b = t ^ j
        dqkv[j, :, head_width : 2 * head_width] = (dk[b] * (HD**-0.5)).astype(BF)
        dqkv[j, :, 2 * head_width :] = dv[b].astype(BF)
    for c in local[1:]:
        c.wait()
    stats[...] = jnp.zeros_like(stats)

    def norm_grad(j, c):
        mine = dqkv[j, part(c), :]
        total = nn(mine, wt[...])
        stats[0:1, :width] += jnp.sum(total * onev[j, part(c), :].astype(F32), axis=0, keepdims=True)
        stats[1:2, :width] += jnp.sum(total, axis=0, keepdims=True)
        stats[2:3, : 3 * head_width] += jnp.sum(mine.astype(F32), axis=0, keepdims=True)
        return total

    first, second, third = [], [], []
    for c in range(chunks):
        s1[0, part(c), :] = norm_grad(3, c).astype(BF)
        first.append(go(remote(s1.at[0, part(c)], r1.at[0, part(c)], s1s.at[0, c], s1r.at[0, c], sib)))
    for c in range(chunks):
        mine = norm_grad(2, c)
        first[c].wait_recv()
        a1[part(c), :] = (mine + r1[0, part(c), :].astype(F32)).astype(BF)
        second.append(go(remote(a1.at[part(c)], q1.at[part(c)], y1s.at[c], y1r.at[c], far)))
    weight_grad(2, onev, dqkv, gq)

    def pass_out(i, _):
        pass_on(1, lines - 1 - i, lambda d: go_[row(keep_of(d)), :])
        return 0

    lax.fori_loop(0, lines - 1, pass_out, 0)
    for c in range(chunks):
        s1[1, part(c), :] = norm_grad(1, c).astype(BF)
        third.append(go(remote(s1.at[1, part(c)], r1.at[1, part(c)], s1s.at[1, c], s1r.at[1, c], sib)))
    for c in range(chunks):
        near[part(c), :] = norm_grad(0, c)
    bias_sum = stats[1:2, :width]
    gain_sum = (stats[0:1, :width] - bias[...] * bias_sum) / gain[...]
    slot = lax.broadcasted_iota(jnp.int32, (4, head_width), 0)
    lv[...] = jnp.zeros_like(lv)
    qsum = stats[2:3, :head_width]
    vsum = stats[2:3, 2 * head_width : 3 * head_width]
    for u in range(4):
        cols = pl.ds(u * head_width, head_width)
        lv[u, 0:4, :] = jnp.where(slot == t, vec[0:1, cols], 0.0)
        here = (t == u).astype(F32)
        lv[u, 4:5, :] = qsum * here
        lv[u, 5:6, :] = vsum * here
        lv[u, 6:7, :] = vec[3:4, cols]
        lv[u, 7:8, :] = vec[4:5, cols]
        lv[u, 8:9, :] = vec[1:2, cols]
        lv[u, 9:10, :] = vec[2:3, cols]
        lv[u, 10:11, :] = gain_sum[:, u * head_width : (u + 1) * head_width]
        lv[u, 11:12, :] = bias_sum[:, u * head_width : (u + 1) * head_width]
    level1 = [
        go(remote(lv.at[t ^ j], rv1.at[j], v1s.at[j], v1r.at[j], mates[j - 1])) for j in range(1, 4)
    ]

    def pass_qkv(i, _):
        pass_on(2, lines - 1 - i, lambda d: gq[row(keep_of(d)), :])
        return 0

    lax.fori_loop(0, (lines - 1) // 2, pass_qkv, 0)
    pf.wait_recv()
    hidv[...] = hidv[...] + pnearv[...].astype(F32) + pfarv[...].astype(F32) + fc2_bias[...]
    outs = [pltpu.make_async_copy(hidv, out_out, osem.at[0])]
    outs[0].start()
    for c in level1:
        c.wait_recv()
    sv[...] = lv[t] + rv1[1] + rv1[2] + rv1[3]
    level2 = [
        go(remote(sv, rv2.at[e], v2s.at[e], v2r.at[e], others[e - 1])) for e in range(1, shards)
    ]
    lax.fori_loop((lines - 1) // 2, max((lines - 1) // 2, lines - 2), pass_qkv, 0)
    for c in third:
        c.wait_recv()

    def finish(c):
        second[c].wait_recv()
        gn = near[part(c), :] + r1[1, part(c), :].astype(F32) + q1[part(c), :].astype(F32)
        unit, inv = normalize(tokv[part(c), :].astype(F32))
        scaled = gn * gain[...]
        inner = (
            scaled
            - jnp.mean(scaled, axis=1, keepdims=True)
            - unit * jnp.mean(scaled * unit, axis=1, keepdims=True)
        )
        ghidv[part(c), :] = ghidv[part(c), :] + inv * inner

    for c in range(chunks - 1):
        finish(c)
    lax.fori_loop(max((lines - 1) // 2, lines - 2), lines - 1, pass_qkv, 0)
    for c in level2:
        c.wait_recv()
    total = sv[...]
    for e in range(1, shards):
        total = total + rv2[e]
    gv[t] = total
    level3 = [
        go(remote(gv.at[t], gv.at[t], v3s.at[j], v3r.at[j], mates[j - 1])) for j in range(1, 4)
    ]

    def reduced(k, own):
        x_copy(k, 0).wait_recv()
        land = lands[k]
        result = own.astype(F32) + land[0][0].astype(F32)
        if lines <= 8:
            for d in range(lines - 1, 0, -1):
                z_copy(k, d).wait_recv()
                result = result + land[2][d].astype(F32)
            return result

        def collect(i, acc):
            d = lines - 1 - i
            z_copy(k, d).wait_recv()
            return acc + land[2][d].astype(F32)

        return lax.fori_loop(0, lines - 1, collect, result)

    pltpu.make_async_copy(g1_in.at[keep_of(0)], sz1.at[0], lsem.at[8]).wait()
    sum1[...] = reduced(0, sz1[0])
    outs.append(pltpu.make_async_copy(sum1, w1_out, osem.at[1]))
    outs[-1].start()
    wos[...] = reduced(1, go_[row(f), :]).T
    outs.append(pltpu.make_async_copy(wos, wo_out, osem.at[2]))
    outs[-1].start()
    finish(chunks - 1)
    outs.append(pltpu.make_async_copy(ghidv, tok_out, osem.at[3]))
    outs[-1].start()
    mine = reduced(2, gq[row(f), :])
    for k in range(3):
        wqs[k] = mine[:, k * head_width : (k + 1) * head_width]
    outs.append(pltpu.make_async_copy(wqs, wq_out, osem.at[4]))
    outs[-1].start()
    for c in level3:
        c.wait_recv()
    for u in range(4):
        cols = slice(u * head_width, (u + 1) * head_width)
        for r in range(4):
            fcb_out[:, r * width + u * head_width : r * width + (u + 1) * head_width] = gv[u, r : r + 1, :]
        qv_out[:, cols] = gv[u, 4:6, :]
        for r, ref in enumerate((g_a, g_b, g_c, g_d, g_e, g_f)):
            ref[:, cols] = gv[u, 6 + r : 7 + r, :]
    for c in sends:
        c.wait_send()

    def drain(d, _):
        for k in range(3):
            x_copy(k, d).wait_send()

        @pl.when(d > 0)
        def _():
            for k in range(3):
                z_copy(k, d).wait_send()

        return 0

    lax.fori_loop(0, lines, drain, 0)
    for c in outs:
        c.wait()


def tail(shards, qkv, grad_att, att, lse, starts, weights, vec, gain, bias, fc2_bias, one, back, tok, ghid, hid, pnear, pfar, g1):
    _, rows, width = one.shape
    head_width = att.shape[2]
    hidden = g1.shape[2]
    heads = head_width // HD
    per = width // shards
    lines = shards // 2
    chunks = 2
    dma = pltpu.SemaphoreType.DMA
    vm = pl.BlockSpec(memory_space=VM)
    hbm = pl.BlockSpec(memory_space=HB)
    V = pltpu.VMEM
    small = (4, 16, head_width)
    sems = [
        (8 + lines,), (2, chunks), (2, chunks), (chunks,), (chunks,),
        (3, lines), (3, lines), (3, lines), (3, lines),
        (4,), (4,), (shards,), (shards,), (4,), (4,), (1,), (1,), (5,),
    ]
    turned = V((4, head_width, rows), BF)
    one_row = (rows, width)
    return pl.pallas_call(
        functools.partial(tail_kernel, shards, chunks),
        name="tail",
        out_shape=[
            jax.ShapeDtypeStruct(one_row, F32),
            jax.ShapeDtypeStruct(one_row, F32),
            jax.ShapeDtypeStruct((3, per, head_width), F32),
            jax.ShapeDtypeStruct((head_width, per), F32),
            jax.ShapeDtypeStruct((per, hidden), F32),
            jax.ShapeDtypeStruct((2, width), F32),
            jax.ShapeDtypeStruct((1, 4 * width), F32),
        ]
        + [jax.ShapeDtypeStruct((1, width), F32)] * 6,
        in_specs=[vm] * 4 + [pl.BlockSpec(memory_space=SM)] + [vm] * 5 + [hbm] * 8,
        out_specs=[hbm] * 5 + [vm] * 8,
        scratch_shapes=[
            turned, turned, turned,
            V((4, rows, head_width), F32), V((4, rows, head_width), F32), V((4, heads, rows), F32),
            V((4, rows, 3 * head_width), BF),
            V((4, rows, width), BF), V((4, rows, width), BF), V(one_row, BF), V(one_row, F32),
            V(one_row, F32), V(one_row, BF), V(one_row, BF), V((3 * head_width, width), BF),
            V((2, rows, width), BF), V((2, rows, width), BF), V(one_row, BF), V(one_row, BF),
            V(one_row, F32), V((width, 3 * head_width), BF), V((width, head_width), BF),
        ]
        + [V((lines, per, 3 * head_width), BF)] * 3
        + [V((lines, per, head_width), BF)] * 3
        + [V((lines, per, hidden), BF)] * 3
        + [
            V((per, hidden), F32), V((3, per, head_width), F32), V((head_width, per), F32),
            V((8, width), F32), V(small, F32), V(small, F32),
            V((16, head_width), F32), V((shards, 16, head_width), F32), V(small, F32),
        ]
        + [dma(s) for s in sems],
        compiler_params=pltpu.CompilerParams(
            collective_id=2, has_side_effects=True, vmem_limit_bytes=60 << 20
        ),
        cost_estimate=pl.CostEstimate(flops=60 << 30, bytes_accessed=100 << 20, transcendentals=0),
    )(qkv, grad_att, att, lse, starts, weights, vec, gain, bias, fc2_bias, one, back, tok, ghid, hid, pnear, pfar, g1)


def finish_kernel(parts, *refs):
    count = len(parts)
    held, sems = refs[2 * count : 3 * count], refs[-1]
    loads, stores = [], []
    for n, pieces in enumerate(parts):
        rows = held[n].shape[0] // pieces
        for i in range(pieces):
            block, k = pl.ds(i * rows, rows), len(loads)
            loads.append(
                pltpu.make_async_copy(refs[n].at[block], held[n].at[block], sems.at[0, k])
            )
            stores.append(
                pltpu.make_async_copy(held[n].at[block], refs[count + n].at[block], sems.at[1, k])
            )
    for c in loads:
        c.start()
    for load, store in zip(loads, stores):
        load.wait()
        store.start()
    for c in stores:
        c.wait()


def finish(arrays):
    parts = [4 if a.size >= 1 << 18 else 1 for a in arrays]
    hbm = pl.BlockSpec(memory_space=HB)
    return pl.pallas_call(
        functools.partial(finish_kernel, parts),
        name="finish",
        out_shape=[jax.ShapeDtypeStruct(a.shape, a.dtype) for a in arrays],
        in_specs=[hbm] * len(arrays),
        out_specs=[hbm] * len(arrays),
        scratch_shapes=[pltpu.VMEM(a.shape, a.dtype) for a in arrays]
        + [pltpu.SemaphoreType.DMA((2, sum(parts)))],
    )(*arrays)


def body(
    tokens,
    cotangent,
    pic_starts,
    w_qkv,
    qv_bias,
    w_out,
    out_bias,
    ln1_gain,
    ln1_bias,
    w_fc1,
    fc1_bias,
    w_fc2,
    fc2_bias,
    ln2_gain,
    ln2_bias,
):
    rows, width = tokens.shape
    shards = lax.axis_size("fsdp")
    one, qkv, wq_full, out_full, fc_in, up_far, att, lse = head(
        shards, tokens, w_qkv.transpose(1, 0, 2), w_out, w_fc1, w_fc2,
        ln1_gain[None], ln1_bias[None], qv_bias, pic_starts, cotangent,
    )
    hidden_one, ghid, back, grad_att, fc1_part, fc2_grad, part_far, part_near, vec = middle(
        shards, att, out_full, tokens, cotangent, up_far, fc_in,
        ln2_gain[None], ln2_bias[None], out_bias[None], fc1_bias[None],
    )
    results = tail(
        shards, qkv, grad_att, att, lse, pic_starts, wq_full, vec, ln1_gain[None], ln1_bias[None],
        fc2_bias[None], one, back, tokens, ghid, hidden_one, part_near, part_far, fc1_part,
    )
    fc2_grad, output, input_grad, wq_grad, wo_grad, fc1_grad, qv_grad, fc1_b, *vecs = finish(
        [fc2_grad, *results]
    )
    out_b, fc2_b, gain_two, shift_two, gain_one, shift_one = [v[0] for v in vecs]
    return (
        output,
        input_grad,
        wq_grad.transpose(1, 0, 2),
        qv_grad,
        wo_grad,
        out_b,
        gain_one,
        shift_one,
        fc1_grad,
        fc1_b[0],
        fc2_grad,
        fc2_b,
        gain_two,
        shift_two,
    )


def solution(mesh):
    return jax.shard_map(
        body,
        mesh=mesh,
        in_specs=(
            P(("fsdp", "tensor"), None),
            P(("fsdp", "tensor"), None),
            P("fsdp", None),
            P("fsdp", None, "tensor"),
            P(),
            P("tensor", "fsdp"),
            P(),
            P(),
            P(),
            P("fsdp", "tensor"),
            P(),
            P("tensor", "fsdp"),
            P(),
            P(),
            P(),
        ),
        out_specs=(
            P(("fsdp", "tensor"), None),
            P(("fsdp", "tensor"), None),
            P("fsdp", None, "tensor"),
            P(),
            P("tensor", "fsdp"),
            P(),
            P(),
            P(),
            P("fsdp", "tensor"),
            P(),
            P("tensor", "fsdp"),
            P(),
            P(),
            P(),
        ),
        check_vma=False,
    )
```

```python
import functools
import math

import jax
import jax.numpy as jnp
from jax import lax
from jax.experimental import pallas as pl
from jax.experimental.pallas import tpu as pltpu
from jax.sharding import PartitionSpec as P

HD = 64
PIC = 256
F32 = jnp.float32
BF = jnp.bfloat16
NEG = -1e30
NORM_EPSILON = 1e-05
GELU_SCALE = math.sqrt(2.0 / math.pi)
GELU_CUBIC = 0.044715
VM = pltpu.MemorySpace.VMEM
SM = pltpu.MemorySpace.SMEM
HB = pltpu.MemorySpace.HBM
PRE = (1, 2)


def nn(a, b):
    return lax.dot_general(a, b, (((1,), (0,)), ((), ())), preferred_element_type=F32)


def nt(a, b):
    return lax.dot_general(a, b, (((1,), (1,)), ((), ())), preferred_element_type=F32)


def normalize(values):
    average = jnp.mean(values, axis=1, keepdims=True)
    centered = values - average
    inv_std = lax.rsqrt(jnp.mean(centered * centered, axis=1, keepdims=True) + NORM_EPSILON)
    return centered * inv_std, inv_std


def normalize_back(gradient, unit_rows, inv_std, gain_row):
    scaled = gradient * gain_row
    inner = (
        scaled
        - jnp.mean(scaled, axis=1, keepdims=True)
        - unit_rows * jnp.mean(scaled * unit_rows, axis=1, keepdims=True)
    )
    return inv_std * inner, jnp.sum(gradient * unit_rows, axis=0), jnp.sum(gradient, axis=0)


MESH = pl.DeviceIdType.MESH


def remote(src, dst, send, recv, where):
    return pltpu.make_async_remote_copy(
        src_ref=src, dst_ref=dst, send_sem=send, recv_sem=recv, device_id=where, device_id_type=MESH
    )


def greet(peers):
    barrier = pltpu.get_barrier_semaphore()
    for peer in peers:
        pl.semaphore_signal(barrier, inc=1, device_id=peer, device_id_type=MESH)
    pl.semaphore_wait(barrier, len(peers))


def head_kernel(
    shards, chunks,
    tok, wq, wo, w1, w2, gain, bias, qvb, starts, cot,
    n_out, qkv_out, wq_out, wo_out, fc_out, up_out, att_out, lse_out, mix_out,
    nv, wqv, wov, otv, fcv, qv, kn, qT, vT, att, lsev,
    ysend, yrecv, csend, crecv, fsend, frecv, zqs, zqr, xqs, xqr, zos, zor, xos, xor,
    zfs, zfr, zds, zdr, xfs, xfr, ups, upr, wos, wor, ats, atr, lsem, osem,
):
    f = lax.axis_index("fsdp")
    t = lax.axis_index("tensor")
    rows, width = tok.shape
    head_width, per = wo.shape
    hid = w1.shape[1]
    step = rows // chunks
    lines = shards // 2
    far = {"fsdp": f, "tensor": t ^ 2}
    sib = {"fsdp": f, "tensor": t ^ 1}
    side = {"fsdp": f ^ 1, "tensor": t}
    alongs = [{"fsdp": f ^ (2 * d), "tensor": t} for d in range(1, lines)]
    mates = [{"fsdp": f, "tensor": t ^ j} for j in range(4)]
    greet(mates[1:] + [side] + alongs)
    sends = []

    def go(copy):
        copy.start()
        sends.append(copy)
        return copy

    zq, zo, xq, xo = [], [], [], []
    for d in range(1, lines):
        zq.append(go(remote(wq, wqv.at[f], zqs.at[d], zqr.at[d], alongs[d - 1])))
    xq.append(go(remote(wq, wqv.at[f], xqs.at[0], xqr.at[0], side)))
    ys, cs, fs = [], [], []
    for c in range(chunks):
        part = pl.ds(c * step, step)
        unit, _ = normalize(tok[part, :].astype(F32))
        nv[0, part, :] = (unit * gain[...] + bias[...]).astype(BF)
        ys.append(go(remote(nv.at[0, part], nv.at[2, part], ysend.at[c], yrecv.at[c], far)))
        cs.append(go(remote(nv.at[0, part], nv.at[1, part], csend.at[c], crecv.at[c], sib)))
    for d in range(1, lines):
        zo.append(go(remote(wo, wov.at[f], zos.at[d], zor.at[d], alongs[d - 1])))
    xo.append(go(remote(wo, wov.at[f], xos.at[0], xor.at[0], side)))
    wqv[f] = wq[...]
    wov[f] = wo[...]
    fcv[:, :hid] = w1[...]
    fcv[:, hid:] = w2[...].T
    local = [pltpu.make_async_copy(fcv, fc_out.at[f], lsem.at[0])]
    local[0].start()

    def forward_far(c):
        part = pl.ds(c * step, step)
        ys[c].wait_recv()
        fs.append(go(remote(nv.at[2, part], nv.at[3, part], fsend.at[c], frecv.at[c], sib)))

    todo = list(range(chunks))
    for d in range(1, lines):
        zq[d - 1].wait_recv()
        slot = f ^ (2 * d)
        xq.append(go(remote(wqv.at[slot], wqv.at[slot], xqs.at[d], xqr.at[d], side)))
        if len(todo) > 1:
            forward_far(todo.pop(0))
    for d in range(1, lines):
        zo[d - 1].wait_recv()
        slot = f ^ (2 * d)
        xo.append(go(remote(wov.at[slot], wov.at[slot], xos.at[d], xor.at[d], side)))
    fc = []
    for d in PRE:
        if d < lines:
            fc.append(go(remote(fcv, fc_out.at[f], zfs.at[d], zfr.at[d], alongs[d - 1])))
    for c in cs:
        c.wait_recv()
    for d in range(lines):
        xq[d].wait_recv()
    start = pl.multiple_of(t * head_width, head_width)
    adds = (qvb[0:1, pl.ds(start, head_width)], None, qvb[1:2, pl.ds(start, head_width)])

    def project(j, _):
        b = t ^ j
        for k in range(3):
            value = nn(nv[j], wqv[:, k].reshape(width, head_width))
            if adds[k] is not None:
                value = value + adds[k]
            value = value.astype(BF)
            qv[j, :, k * head_width : (k + 1) * head_width] = value
            if k == 0:
                qT[b] = (value * jnp.asarray(HD**-0.5, BF)).T
            elif k == 1:
                kn[b] = value
            else:
                vT[b] = value.T
        return 0

    lax.fori_loop(0, 2, project, 0)
    while todo:
        forward_far(todo.pop(0))
    up = go(remote(cot, up_out, ups.at[0], upr.at[0], far))
    for c in fs:
        c.wait_recv()
    lax.fori_loop(2, 4, project, 0)
    for d in range(lines):
        xo[d].wait_recv()
    fc.append(go(remote(fcv, fc_out.at[f], zfs.at[0], zfr.at[0], side)))
    if per % 128 == 0:
        def place(s, _):
            otv[:, pl.ds(pl.multiple_of(s * per, per), per)] = wov[s]
            return 0

        lax.fori_loop(0, shards, place, 0)
    else:
        for s in range(shards):
            otv[:, s * per : (s + 1) * per] = wov[s]
    outs = [
        pltpu.make_async_copy(src, dst, osem.at[n])
        for n, (src, dst) in enumerate([(nv, n_out), (qv, qkv_out), (wqv, wq_out), (otv, wo_out.at[t])])
    ]
    for c in outs:
        c.start()
    shared = [
        go(remote(otv, wo_out.at[t], wos.at[1], wor.at[1], sib)),
        go(remote(otv, wo_out.at[t], wos.at[2], wor.at[2], far)),
    ]
    rowk = lax.broadcasted_iota(jnp.int32, (rows, rows), 0)
    colq = lax.broadcasted_iota(jnp.int32, (rows, rows), 1)
    half = lax.broadcasted_iota(jnp.int32, (2 * HD, rows), 0) < HD
    more = []

    def mixed(i):
        return remote(att.at[i], mix_out.at[t], ats.at[i], atr.at[t ^ i], mates_of(i))

    def mates_of(i):
        return {"fsdp": f, "tensor": t * 0 + i}

    for i in range(4):
        at = starts[0, i] - i * rows
        if i == 3:
            pre = [d for d in PRE if d < lines]
            for n, d in enumerate(pre):
                fc[n].wait_recv()
                block = fc_out.at[f ^ (2 * d)]
                more.append(go(remote(block, block, xfs.at[d], xfr.at[d], side)))
            for d in range(1, lines):
                if d not in pre:
                    more.append(
                        go(remote(fcv, fc_out.at[f], zds.at[d], zdr.at[d], alongs[d - 1]))
                    )

        def pair(p, _, i=i, at=at):
            col = pl.multiple_of(p * 2 * HD, 2 * HD)
            qp = qT[i, pl.ds(col, 2 * HD), :]
            zero = jnp.zeros_like(qp)
            masked = (jnp.where(half, qp, zero), jnp.where(half, zero, qp))
            found = []
            for hh in range(2):
                ss, top = [], None
                for m in range(i + 1):
                    s = nn(kn[m, :, pl.ds(col, 2 * HD)], masked[hh])
                    if m == i:
                        inside = (rowk >= at) & (rowk < at + PIC) & (colq >= at) & (colq < at + PIC)
                        s = jnp.where((rowk <= colq) | inside, s, NEG)
                    peak = jnp.max(s, axis=0, keepdims=True)
                    top = peak if top is None else jnp.maximum(top, peak)
                    ss.append(s)
                total, acc = 0.0, 0.0
                for m in range(i + 1):
                    e = jnp.exp(ss[m] - top)
                    total = total + jnp.sum(e, axis=0, keepdims=True)
                    acc = acc + nn(vT[m, pl.ds(col + hh * HD, HD), :], e.astype(BF))
                found.append(acc * (1.0 / total))
                lsev[t ^ i, pl.ds(p * 2 + hh, 1), :] = top + jnp.log(total)
            att[i, :, pl.ds(col, 2 * HD)] = jnp.concatenate(found, axis=0).astype(BF).T
            return 0

        lax.fori_loop(0, head_width // (2 * HD), pair, 0)

        @pl.when(t != i)
        def _(i=i):
            mixed(i).start()

    outs += [pltpu.make_async_copy(att.at[t ^ j], att_out.at[j], osem.at[4 + j]) for j in range(4)]
    outs.append(pltpu.make_async_copy(lsev, lse_out, osem.at[8]))
    outs.append(pltpu.make_async_copy(att.at[t], mix_out.at[t], osem.at[9]))
    for c in outs[4:]:
        c.start()
    shared[1].wait_recv()
    shared.append(go(remote(wo_out.at[t ^ 2], wo_out.at[t ^ 2], wos.at[3], wor.at[3], sib)))
    shared[0].wait_recv()
    shared[2].wait_recv()
    for j in range(1, 4):
        remote(att.at[0], mix_out.at[t ^ j], ats.at[0], atr.at[j], mates[j]).wait_recv()
    for i in range(4):

        @pl.when(t != i)
        def _(i=i):
            mixed(i).wait_send()

    for c in fc[len(pre) :] + [up] + more:
        c.wait_recv()
    for c in sends:
        c.wait_send()
    for c in local + outs:
        c.wait()


def head(shards, tokens, wq, wo, w1, w2, gain, bias, qv_bias, starts, cot):
    rows, width = tokens.shape
    head_width, per = wo.shape
    hid = w1.shape[1]
    lines = shards // 2
    chunks = 4
    heads = head_width // HD
    dma = pltpu.SemaphoreType.DMA
    vm = pl.BlockSpec(memory_space=VM)
    hbm = pl.BlockSpec(memory_space=HB)
    V = pltpu.VMEM
    full = (4, rows, width)
    three = (4, rows, 3 * head_width)
    return pl.pallas_call(
        functools.partial(head_kernel, shards, chunks),
        name="head",
        out_shape=[
            jax.ShapeDtypeStruct(full, BF),
            jax.ShapeDtypeStruct(three, BF),
            jax.ShapeDtypeStruct((shards, 3, per, head_width), BF),
            jax.ShapeDtypeStruct((4, head_width, width), BF),
            jax.ShapeDtypeStruct((shards, per, 2 * hid), BF),
            jax.ShapeDtypeStruct((rows, width), BF),
            jax.ShapeDtypeStruct((4, rows, head_width), BF),
            jax.ShapeDtypeStruct((4, heads, rows), F32),
            jax.ShapeDtypeStruct((4, rows, head_width), BF),
        ],
        in_specs=[vm] * 8 + [pl.BlockSpec(memory_space=SM), hbm],
        out_specs=[hbm] * 9,
        scratch_shapes=[
            V(full, BF), V((shards, 3, per, head_width), BF), V((shards, head_width, per), BF),
            V((head_width, width), BF), V((per, 2 * hid), BF), V(three, BF),
            V((4, rows, head_width), BF), V((4, head_width, rows), BF), V((4, head_width, rows), BF),
            V((4, rows, head_width), BF), V((4, heads, rows), F32),
        ]
        + [dma((chunks,))] * 6
        + [dma((lines,))] * 8
        + [dma((max(lines, 4),))] * 6
        + [dma((1,))] * 2
        + [dma((4,))] * 4
        + [dma((1,)), dma((10,))],
        compiler_params=pltpu.CompilerParams(
            collective_id=0, has_side_effects=True, vmem_limit_bytes=56 << 20
        ),
        cost_estimate=pl.CostEstimate(flops=40 << 30, bytes_accessed=90 << 20, transcendentals=0),
    )(tokens, wq, wo, w1, w2, gain, bias, qv_bias, starts, cot)


def middle_kernel(
    shards, chunks,
    mix, wo, tok, cot, up_far, fc_in, gain, bias, out_bias, fc_bias,
    hid_out, ghid_out, back_out, do_out, g1_out, g2_out, part_far, vec,
    wfc, wt, wot, upv, twov, actv, pgv, backv,
    s1, r1, a1, q1, near, hv, rx, sz, dov,
    dos, dor, c2s, c2r, y2s, y2r, f2s, f2r,
    s3s, s3r, y3s, y3r,
    s5s, s5r, ups, upr, lsem, xs, xr, osem, gxs, gxr,
):
    f = lax.axis_index("fsdp")
    t = lax.axis_index("tensor")
    rows, width = tok.shape
    per = fc_in.shape[1]
    hid = fc_in.shape[2] // 2
    pre = [d for d in PRE if d < shards // 2]
    step = rows // chunks
    lines = shards // 2
    far = {"fsdp": f, "tensor": t ^ 2}
    sib = {"fsdp": f, "tensor": t ^ 1}
    side = {"fsdp": f ^ 1, "tensor": t}
    direct = [d for d in range(1, lines) if d not in pre]
    mates = [{"fsdp": f, "tensor": t ^ j} for j in range(4)]
    greet(mates[1:] + [side])
    sends = []

    def go(copy):
        copy.start()
        sends.append(copy)
        return copy

    def part(c):
        return pl.ds(c * step, step)

    halves = (pl.ds(0, hid), pl.ds(hid, hid))
    late = [2 * d + 1 for d in direct]
    early = [e for e in range(shards) if e not in late]
    local = [
        pltpu.make_async_copy(fc_in.at[f ^ e], wfc.at[f ^ e], lsem.at[n])
        for n, e in enumerate(early)
    ]
    local.append(pltpu.make_async_copy(cot, upv.at[0], lsem.at[shards]))
    local.append(pltpu.make_async_copy(up_far, upv.at[2], lsem.at[shards + 1]))
    for c in local:
        c.start()
    xf = []
    for d in direct:
        block = f ^ (2 * d)
        xf.append(go(remote(fc_in.at[block], wfc.at[block], xs.at[d], xr.at[d], side)))
    up_copies = [
        go(remote(cot, upv.at[1], ups.at[0], upr.at[0], sib)),
        go(remote(up_far, upv.at[3], ups.at[1], upr.at[1], sib)),
    ]
    vec[...] = jnp.zeros_like(vec)
    ag_far, ag_sib = [], []
    for c in range(chunks):
        hidden = tok[part(c), :].astype(F32) + out_bias[...]
        for s in range(4):
            hidden = hidden + nn(mix[s, part(c), :], wo[s])
        hv[part(c), :] = hidden
        unit, _ = normalize(hidden)
        twov[0, part(c), :] = (unit * gain[...] + bias[...]).astype(BF)
        ag_far.append(go(remote(twov.at[0, part(c)], twov.at[2, part(c)], y2s.at[c], y2r.at[c], far)))
        ag_sib.append(go(remote(twov.at[0, part(c)], twov.at[1, part(c)], c2s.at[c], c2r.at[c], sib)))
    for s in range(4):
        wot[s] = wo[s].T
    outs = []
    for c in local:
        c.wait()

    def flip(slot):
        if per % 128 == 0:
            wt[:, pl.ds(pl.multiple_of(slot * per, per), per)] = wfc[slot].T

    def flip_early(e, _):
        flip(f ^ e)
        return 0

    if early == list(range(len(early))):
        lax.fori_loop(0, len(early), flip_early, 0)
    else:
        for e in early:
            flip(f ^ e)
    for c in xf:
        c.wait_recv()
    for e in late:
        flip(f ^ e)
    if per % 128:
        wt[...] = wfc[...].reshape(width, 2 * hid).T
    for c in up_copies:
        c.wait_recv()
    for c in ag_sib:
        c.wait_recv()
    start = pl.multiple_of(t * hid, hid)
    tile = hid // 2

    def feed(j, at):
        block = pl.ds(pl.multiple_of(at * step, step), step)
        two = twov[j, block, :]
        up = upv[j, block, :]
        total = None
        for n in range(2):
            cols = pl.ds(n * tile, tile)
            x = nn(two, wfc[:, :, cols].reshape(width, tile))
            x = x + fc_bias[:, pl.ds(pl.multiple_of(start + n * tile, tile), tile)]
            hg = nn(up, wfc[:, :, pl.ds(hid + n * tile, tile)].reshape(width, tile))
            sq = x * x
            th = jnp.tanh(GELU_SCALE * (x + GELU_CUBIC * (sq * x)))
            half = 0.5 * (1.0 + th)
            actv[j, block, cols] = (x * half).astype(BF)
            slope = half + (0.5 * GELU_SCALE) * x * (1.0 - th * th) * (1.0 + (3.0 * GELU_CUBIC) * sq)
            pg = (hg * slope).astype(BF)
            pgv[j, block, cols] = pg
            vec[0:1, cols] += jnp.sum(pg.astype(F32), axis=0, keepdims=True)
            term = nn(pg, wt[cols, :])
            total = term if total is None else total + term
        return total

    def copies(c):
        block = pl.ds(pl.multiple_of(c * step, step), step)
        return (
            remote(twov.at[0, block], twov.at[2, block], y2s.at[c], y2r.at[c], far),
            remote(twov.at[2, block], twov.at[3, block], f2s.at[c], f2r.at[c], sib),
            remote(a1.at[block], q1.at[block], y3s.at[c], y3r.at[c], far),
        )

    def core_copy(k, c):
        block = pl.ds(pl.multiple_of(c * step, step), step)
        return remote(s1.at[2 + k, block], r1.at[2 + k, block], s3s.at[k, c], s3r.at[k, c], sib)

    def rows_of(c, _):
        block = pl.ds(pl.multiple_of(c * step, step), step)
        got, fwd, send2 = copies(c)

        def one(i, _):
            total = feed(i ^ 1, c)

            @pl.when(i == 0)
            def _():
                s1[3, block, :] = total.astype(BF)
                core_copy(1, c).start()
                got.wait_recv()
                fwd.start()

            @pl.when(i == 1)
            def _():
                near[block, :] = total
                fwd.wait_recv()

            @pl.when(i == 2)
            def _():
                s1[2, block, :] = total.astype(BF)
                core_copy(0, c).start()

            @pl.when(i == 3)
            def _():
                core_copy(0, c).wait_recv()
                a1[block, :] = (total + r1[2, block, :].astype(F32)).astype(BF)
                send2.start()

            return 0

        lax.fori_loop(0, 4, one, 0)
        return 0

    lax.fori_loop(0, chunks, rows_of, 0)

    span = 256
    ratio = span // (2 * per)
    groups = width // span
    z = f // 2
    x = lax.rem(f, 2)

    def x_copy(d):
        return remote(wfc.at[(z ^ d) * 2 + (1 - x), :, halves[0]], rx.at[d], gxs.at[d], gxr.at[d], side)

    def weight_grad(left, right, h, send):
        def group_of(i, _):
            near_group = groups - 1 - i
            group = near_group ^ (z // ratio)
            cols = pl.ds(pl.multiple_of(group * span, span), span)
            acc = None
            for j in range(4):
                term = nn(left[j, :, cols].T, right[j])
                acc = term if acc is None else acc + term
            count = span // per
            slots = pl.ds(group * count, count)
            wfc[slots, :, halves[h]] = acc.astype(BF).reshape(count, per, hid)
            if send:

                def launch(e, _):
                    x_copy(near_group * ratio + e).start()
                    return 0

                lax.fori_loop(0, ratio, launch, 0)
            return 0

        lax.fori_loop(0, groups, group_of, 0)

    def feed_part(k):
        for c in range(chunks):
            core_copy(k, c).wait_send()

        def give(c, _):
            block = pl.ds(pl.multiple_of(c * step, step), step)
            s1[k, block, :] = nn(actv[3 - 2 * k, block, :], wt[hid:, :]).astype(BF)
            return 0

        lax.fori_loop(0, chunks, give, 0)
        given = go(remote(s1.at[k], r1.at[k], s5s.at[k], s5r.at[k], sib))

        def keep(c, _):
            block = pl.ds(pl.multiple_of(c * step, step), step)
            mine = nn(actv[2 - 2 * k, block, :], wt[hid:, :])
            if k:
                hv[block, :] += mine
            else:
                s1[2, block, :] = mine.astype(BF)
            return 0

        lax.fori_loop(0, chunks, keep, 0)
        given.wait_recv()
        if k:
            hv[...] += r1[k].astype(F32)
            outs.append(pltpu.make_async_copy(hv, hid_out, osem.at[0]))
        else:
            s1[2] = (s1[2].astype(F32) + r1[k].astype(F32)).astype(BF)
            outs.append(pltpu.make_async_copy(s1.at[2], part_far, osem.at[2]))
        outs[-1].start()

    weight_grad(upv, actv, 0, True)
    given_do = []
    for c in range(chunks):
        _, _, send2 = copies(c)
        core_copy(1, c).wait_recv()
        send2.wait_recv()
        gn = near[part(c), :] + r1[3, part(c), :].astype(F32) + q1[part(c), :].astype(F32)
        unit, inv = normalize(hv[part(c), :])
        back, g_sum, b_sum = normalize_back(gn, unit, inv, gain[...])
        cots = upv[0, part(c), :].astype(F32)
        ghid = cots + back
        near[part(c), :] = ghid
        low = ghid.astype(BF)
        backv[part(c), :] = low
        for j in (2, 3, 1, 0):
            dov[j, part(c), :] = nn(low, wot[t ^ j]).astype(BF)
            if j > 0:
                given_do.append(
                    go(remote(dov.at[j, part(c)], do_out.at[j, part(c)], dos.at[j, c], dor.at[j, c], mates[j]))
                )
        vec[1:2, :] += g_sum[None]
        vec[2:3, :] += b_sum[None]
        vec[3:4, :] += jnp.sum(ghid, axis=0, keepdims=True)
        vec[4:5, :] += jnp.sum(cots, axis=0, keepdims=True)
        feed_part(c) if c < 2 else None
    outs.append(pltpu.make_async_copy(near, ghid_out, osem.at[1]))
    outs[-1].start()

    weight_grad(twov, pgv, 1, False)
    outs.append(pltpu.make_async_copy(wfc.at[:, :, halves[1]], g1_out, osem.at[5]))
    outs[-1].start()
    outs.append(pltpu.make_async_copy(dov.at[0], do_out.at[0], osem.at[7]))
    outs[-1].start()
    outs.append(pltpu.make_async_copy(backv, back_out, osem.at[4]))
    outs[-1].start()

    def side_sum(i, _):
        d = lines - 1 - i
        x_copy(d).wait_recv()
        sz[d] = (wfc[(z ^ d) * 2 + x, :, halves[0]].astype(F32) + rx[d].astype(F32)).astype(BF)
        return 0

    lax.fori_loop(0, lines, side_sum, 0)
    outs.append(pltpu.make_async_copy(sz, g2_out, osem.at[6]))
    outs[-1].start()
    for c in given_do:
        c.wait_recv()
    for c in sends:
        c.wait_send()
    for c in range(chunks):
        _, fwd, send2 = copies(c)
        fwd.wait_send()
        send2.wait_send()

    def drain(d, _):
        x_copy(d).wait_send()
        return 0

    lax.fori_loop(0, lines, drain, 0)
    for c in outs:
        c.wait()


def middle(shards, mix, wo, tok, cot, up_far, fc_in, gain, bias, out_bias, fc_bias):
    rows, width = tok.shape
    per, hid2 = fc_in.shape[1:]
    hid = hid2 // 2
    head_width = wo.shape[1]
    lines = shards // 2
    chunks = 2
    step = rows // chunks
    dma = pltpu.SemaphoreType.DMA
    vm = pl.BlockSpec(memory_space=VM)
    hbm = pl.BlockSpec(memory_space=HB)
    full = (4, rows, width)
    one = (rows, width)
    block = (lines, per, hid)
    V = pltpu.VMEM
    sems = [
        (4, chunks), (4, chunks), (chunks,), (chunks,),
        (chunks,), (chunks,), (chunks,), (chunks,),
        (2, chunks), (2, chunks), (chunks,), (chunks,),
        (2,), (2,), (2,), (2,), (shards + 2,), (lines,), (lines,), (8,), (lines,), (lines,),
    ]
    return pl.pallas_call(
        functools.partial(middle_kernel, shards, chunks),
        name="middle",
        out_shape=[
            jax.ShapeDtypeStruct(one, F32),
            jax.ShapeDtypeStruct(one, F32),
            jax.ShapeDtypeStruct(one, BF),
            jax.ShapeDtypeStruct((4, rows, head_width), BF),
            jax.ShapeDtypeStruct((shards, per, hid), BF),
            jax.ShapeDtypeStruct(block, BF),
            jax.ShapeDtypeStruct(one, BF),
            jax.ShapeDtypeStruct((8, width), F32),
        ],
        in_specs=[vm, vm, vm, hbm, hbm, hbm] + [vm] * 4,
        out_specs=[hbm] * 7 + [vm],
        scratch_shapes=[
            V((shards, per, 2 * hid), BF), V((2 * hid, width), BF), V((4, width, head_width), BF),
            V(full, BF), V(full, BF), V((4, rows, hid), BF), V((4, rows, hid), BF), V(one, BF),
            V(full, BF), V(full, BF), V(one, BF), V(one, BF),
            V(one, F32), V(one, F32), V(block, BF), V(block, BF), V((4, rows, head_width), BF),
        ]
        + [dma(s) for s in sems],
        compiler_params=pltpu.CompilerParams(
            collective_id=1, has_side_effects=True, vmem_limit_bytes=60 << 20
        ),
        cost_estimate=pl.CostEstimate(flops=60 << 30, bytes_accessed=200 << 20, transcendentals=0),
    )(mix, wo, tok, cot, up_far, fc_in, gain, bias, out_bias, fc_bias)


def tail_kernel(
    shards, chunks,
    qs, dos, ats, lse, starts, weights, vec, gain, bias, fc2_bias,
    one_in, back_in, tok_in, ghid_in, hid_in, pfar_in, g1_in, g2_in,
    out_out, tok_out, wq_out, wo_out, w1_out, w2_out, qv_out, fcb_out, g_a, g_b, g_c, g_d, g_e, g_f,
    qT, kT, doT, dk, dv, dl, dqkv,
    onev, backv, tokv, ghidv, hidv, pfarv, wt,
    s1, r1, a1, q1, near, gq, go_, rx, sz, rz, rxo, szo, rzo, rx1, sz1, rz1, rz2, sum1, sum2, wqs, wos,
    stats, lv, rv1, sv, rv2, gv,
    lsem, s1s, s1r, y1s, y1r, xs, xr, zs, zr, v1s, v1r, v2s, v2r, v3s, v3r, pfs, pfr, z2s, z2r, osem,
):
    f = lax.axis_index("fsdp")
    t = lax.axis_index("tensor")
    _, rows, width = onev.shape
    head_width = ats.shape[2]
    per = width // shards
    lines = shards // 2
    step = rows // chunks
    z = f // 2
    x = lax.rem(f, 2)
    far = {"fsdp": f, "tensor": t ^ 2}
    sib = {"fsdp": f, "tensor": t ^ 1}
    side = {"fsdp": f ^ 1, "tensor": t}
    mates = [{"fsdp": f, "tensor": t ^ j} for j in range(1, 4)]
    others = [{"fsdp": f ^ e, "tensor": t} for e in range(1, shards)]
    greet(mates + others)
    sends = []

    def go(copy):
        copy.start()
        sends.append(copy)
        return copy

    def part(c):
        return pl.ds(c * step, step)

    def row(block):
        return pl.ds(pl.multiple_of(block * per, per), per)

    sources = (lambda b: g1_in.at[b], lambda b: go_.at[row(b)], lambda b: gq.at[row(b)])
    lands = ((rx1, sz1, rz1), (rxo, szo, rzo), (rx, sz, rz))

    def x_copy(k, d):
        return remote(
            sources[k]((z ^ d) * 2 + (1 - x)), lands[k][0].at[d], xs.at[k, d], xr.at[k, d], side
        )

    def z_copy(k, d):
        return remote(
            lands[k][1].at[d], lands[k][2].at[d], zs.at[k, d], zr.at[k, d],
            {"fsdp": f ^ (2 * d), "tensor": t},
        )

    def pass_on(k, d, own):
        x_copy(k, d).wait_recv()
        lands[k][1][d] = (own(d).astype(F32) + lands[k][0][d].astype(F32)).astype(BF)
        z_copy(k, d).start()

    def keep_of(d):
        return (z ^ d) * 2 + x

    def launch(i, _):
        x_copy(0, lines - 1 - i).start()
        return 0

    lax.fori_loop(0, lines, launch, 0)
    def z2_copy(d):
        return remote(
            g2_in.at[d], rz2.at[d], z2s.at[d], z2r.at[d], {"fsdp": f ^ (2 * d), "tensor": t}
        )

    def launch2(i, _):
        z2_copy(lines - 1 - i).start()
        return 0

    lax.fori_loop(0, lines - 1, launch2, 0)
    back_far = go(remote(back_in, backv.at[2], pfs.at[1], pfr.at[1], far))
    back_sib = go(remote(back_in, backv.at[1], pfs.at[2], pfr.at[2], sib))
    local = [
        pltpu.make_async_copy(src, dst, lsem.at[n])
        for n, (src, dst) in enumerate(
            [
                (back_in, backv.at[0]), (one_in, onev), (tok_in, tokv), (ghid_in, ghidv),
                (hid_in, hidv), (g2_in.at[0], rz2.at[0]),
            ]
        )
    ]
    for c in local:
        c.start()
    keeps = []

    def own_block(d, _):
        pltpu.make_async_copy(g1_in.at[keep_of(d)], sz1.at[d], lsem.at[8 + d]).start()
        return 0

    lax.fori_loop(0, lines, own_block, 0)

    def pass_fc1(d):
        pltpu.make_async_copy(g1_in.at[keep_of(d)], sz1.at[d], lsem.at[8 + d]).wait()
        pass_on(0, d, lambda d: sz1[d])

    for j in range(4):
        b = t ^ j
        qT[b] = (qs[j, :, :head_width] * jnp.asarray(HD**-0.5, BF)).T
        kT[b] = qs[j, :, head_width : 2 * head_width].T
        do = dos[j]
        doT[b] = do.T
        prod = (do.astype(F32) * ats[j].astype(F32)).T
        for h in range(head_width // HD):
            dl[b, h : h + 1, :] = jnp.sum(prod[h * HD : (h + 1) * HD], axis=0, keepdims=True)
    dk[...] = jnp.zeros_like(dk)
    dv[...] = jnp.zeros_like(dv)
    for k in range(3):
        wt[k * head_width : (k + 1) * head_width, :] = weights[:, k].reshape(width, head_width).T

    span = 256
    ratio = span // (2 * per)
    groups = width // span

    def weight_grad(k, left, right, target):
        def group_of(i, _):
            near_group = groups - 1 - i
            group = near_group ^ (z // ratio)
            cols = pl.ds(pl.multiple_of(group * span, span), span)
            acc = None
            for j in range(4):
                term = nn(left[j, :, cols].T, right[j])
                acc = term if acc is None else acc + term
            target[cols, :] = acc.astype(BF)

            def send(e, _):
                x_copy(k, near_group * ratio + e).start()
                return 0

            lax.fori_loop(0, ratio, send, 0)
            return 0

        lax.fori_loop(0, groups, group_of, 0)

    rowk = lax.broadcasted_iota(jnp.int32, (rows, rows), 0)
    colq = lax.broadcasted_iota(jnp.int32, (rows, rows), 1)
    hrow = lax.broadcasted_iota(jnp.int32, (2 * HD, rows), 0) < HD
    hcol = lax.broadcasted_iota(jnp.int32, (rows, 2 * HD), 1) < HD

    def two(v, m):
        zero = jnp.zeros_like(v)
        return (jnp.where(m, v, zero), jnp.where(m, zero, v))

    def attend(i):
        at = starts[0, i] - i * rows
        jj = t ^ i

        def pair(p, _):
            col = pl.multiple_of(p * 2 * HD, 2 * HD)
            kcol = pl.multiple_of(head_width + p * 2 * HD, 2 * HD)
            vcol = pl.multiple_of(2 * head_width + p * 2 * HD, 2 * HD)
            qTz = two(qT[i, pl.ds(col, 2 * HD), :], hrow)
            doTz = two(doT[i, pl.ds(col, 2 * HD), :], hrow)
            qz = two(qs[jj, :, pl.ds(col, 2 * HD)], hcol)
            doz = two(dos[jj, :, pl.ds(col, 2 * HD)], hcol)
            ls = [lse[jj, pl.ds(p * 2 + hh, 1), :] for hh in range(2)]
            dlt = [dl[i, pl.ds(p * 2 + hh, 1), :] for hh in range(2)]

            def block(m, carry, diag):
                kb = qs[t ^ m, :, pl.ds(kcol, 2 * HD)]
                vb = qs[t ^ m, :, pl.ds(vcol, 2 * HD)]
                ktb = kT[m, pl.ds(col, 2 * HD), :]
                dvs, dks, new = 0.0, 0.0, []
                for hh in range(2):
                    s = nn(kb, qTz[hh])
                    if diag:
                        inside = (rowk >= at) & (rowk < at + PIC) & (colq >= at) & (colq < at + PIC)
                        s = jnp.where((rowk <= colq) | inside, s, NEG)
                    pr = jnp.exp(s - ls[hh])
                    dp = nn(vb, doTz[hh])
                    ds = (pr * (dp - dlt[hh])).astype(BF)
                    dvs = dvs + nn(pr.astype(BF), doz[hh])
                    dks = dks + nn(ds, qz[hh])
                    new.append(carry[hh] + nn(ktb[hh * HD : (hh + 1) * HD], ds))
                dv[m, :, pl.ds(col, 2 * HD)] += dvs
                dk[m, :, pl.ds(col, 2 * HD)] += dks
                return tuple(new)

            c = tuple(jnp.zeros((HD, rows), F32) for _ in range(2))
            c = block(i, c, True)
            if i > 0:
                c = lax.fori_loop(0, i, lambda m, c: block(m, c, False), c)
            dq = (jnp.concatenate(c, axis=0) * (HD**-0.5)).astype(BF)
            dqkv[jj, :, pl.ds(col, 2 * HD)] = dq.T
            return 0

        lax.fori_loop(0, head_width // (2 * HD), pair, 0)

    attend(0)
    pass_fc1(lines - 1)
    attend(1)
    if lines > 2:
        pass_fc1(lines - 2)
    attend(2)
    back_far.wait_recv()
    back_fwd = go(remote(backv.at[2], backv.at[3], pfs.at[3], pfr.at[3], sib))
    pf = go(remote(pfar_in, pfarv, pfs.at[0], pfr.at[0], far))
    local[0].wait()
    back_sib.wait_recv()
    if lines > 3:

        def pass_more(i, _):
            pass_fc1(lines - 3 - i)
            return 0

        lax.fori_loop(0, lines - 3, pass_more, 0)
    back_fwd.wait_recv()
    weight_grad(1, backv, ats, go_)
    attend(3)
    for j in range(4):
        b = t ^ j
        dqkv[j, :, head_width : 2 * head_width] = (dk[b] * (HD**-0.5)).astype(BF)
        dqkv[j, :, 2 * head_width :] = dv[b].astype(BF)
    for c in local[1:]:
        c.wait()
    stats[...] = jnp.zeros_like(stats)

    def norm_grad(j, c):
        mine = dqkv[j, part(c), :]
        total = nn(mine, wt[...])
        stats[0:1, :width] += jnp.sum(total * onev[j, part(c), :].astype(F32), axis=0, keepdims=True)
        stats[1:2, :width] += jnp.sum(total, axis=0, keepdims=True)
        stats[2:3, : 3 * head_width] += jnp.sum(mine.astype(F32), axis=0, keepdims=True)
        return total

    first, second, third = [], [], []
    for c in range(chunks):
        s1[0, part(c), :] = norm_grad(3, c).astype(BF)
        first.append(go(remote(s1.at[0, part(c)], r1.at[0, part(c)], s1s.at[0, c], s1r.at[0, c], sib)))
    for c in range(chunks):
        mine = norm_grad(2, c)
        first[c].wait_recv()
        a1[part(c), :] = (mine + r1[0, part(c), :].astype(F32)).astype(BF)
        second.append(go(remote(a1.at[part(c)], q1.at[part(c)], y1s.at[c], y1r.at[c], far)))
    weight_grad(2, onev, dqkv, gq)

    def pass_out(i, _):
        pass_on(1, lines - 1 - i, lambda d: go_[row(keep_of(d)), :])
        return 0

    lax.fori_loop(0, lines - 1, pass_out, 0)
    for c in range(chunks):
        s1[1, part(c), :] = norm_grad(1, c).astype(BF)
        third.append(go(remote(s1.at[1, part(c)], r1.at[1, part(c)], s1s.at[1, c], s1r.at[1, c], sib)))
    for c in range(chunks):
        near[part(c), :] = norm_grad(0, c)
    bias_sum = stats[1:2, :width]
    gain_sum = (stats[0:1, :width] - bias[...] * bias_sum) / gain[...]
    slot = lax.broadcasted_iota(jnp.int32, (4, head_width), 0)
    lv[...] = jnp.zeros_like(lv)
    qsum = stats[2:3, :head_width]
    vsum = stats[2:3, 2 * head_width : 3 * head_width]
    for u in range(4):
        cols = pl.ds(u * head_width, head_width)
        lv[u, 0:4, :] = jnp.where(slot == t, vec[0:1, cols], 0.0)
        here = (t == u).astype(F32)
        lv[u, 4:5, :] = qsum * here
        lv[u, 5:6, :] = vsum * here
        lv[u, 6:7, :] = vec[3:4, cols]
        lv[u, 7:8, :] = vec[4:5, cols]
        lv[u, 8:9, :] = vec[1:2, cols]
        lv[u, 9:10, :] = vec[2:3, cols]
        lv[u, 10:11, :] = gain_sum[:, u * head_width : (u + 1) * head_width]
        lv[u, 11:12, :] = bias_sum[:, u * head_width : (u + 1) * head_width]
    level1 = [
        go(remote(lv.at[t ^ j], rv1.at[j], v1s.at[j], v1r.at[j], mates[j - 1])) for j in range(1, 4)
    ]

    def pass_qkv(i, _):
        pass_on(2, lines - 1 - i, lambda d: gq[row(keep_of(d)), :])
        return 0

    lax.fori_loop(0, (lines - 1) // 2, pass_qkv, 0)
    pf.wait_recv()
    hidv[...] = hidv[...] + pfarv[...].astype(F32) + fc2_bias[...]
    outs = [pltpu.make_async_copy(hidv, out_out, osem.at[0])]
    outs[0].start()
    for c in level1:
        c.wait_recv()
    sv[...] = lv[t] + rv1[1] + rv1[2] + rv1[3]
    level2 = [
        go(remote(sv, rv2.at[e], v2s.at[e], v2r.at[e], others[e - 1])) for e in range(1, shards)
    ]
    lax.fori_loop((lines - 1) // 2, max((lines - 1) // 2, lines - 2), pass_qkv, 0)
    for c in third:
        c.wait_recv()

    def finish(c):
        second[c].wait_recv()
        gn = near[part(c), :] + r1[1, part(c), :].astype(F32) + q1[part(c), :].astype(F32)
        unit, inv = normalize(tokv[part(c), :].astype(F32))
        scaled = gn * gain[...]
        inner = (
            scaled
            - jnp.mean(scaled, axis=1, keepdims=True)
            - unit * jnp.mean(scaled * unit, axis=1, keepdims=True)
        )
        ghidv[part(c), :] = ghidv[part(c), :] + inv * inner

    for c in range(chunks - 1):
        finish(c)
    lax.fori_loop(max((lines - 1) // 2, lines - 2), lines - 1, pass_qkv, 0)
    for c in level2:
        c.wait_recv()
    total = sv[...]
    for e in range(1, shards):
        total = total + rv2[e]
    gv[t] = total
    level3 = [
        go(remote(gv.at[t], gv.at[t], v3s.at[j], v3r.at[j], mates[j - 1])) for j in range(1, 4)
    ]

    def reduced(k, own):
        x_copy(k, 0).wait_recv()
        land = lands[k]
        result = own.astype(F32) + land[0][0].astype(F32)
        if lines <= 8:
            for d in range(lines - 1, 0, -1):
                z_copy(k, d).wait_recv()
                result = result + land[2][d].astype(F32)
            return result

        def collect(i, acc):
            d = lines - 1 - i
            z_copy(k, d).wait_recv()
            return acc + land[2][d].astype(F32)

        return lax.fori_loop(0, lines - 1, collect, result)

    pltpu.make_async_copy(g1_in.at[keep_of(0)], sz1.at[0], lsem.at[8]).wait()
    sum1[...] = reduced(0, sz1[0])
    outs.append(pltpu.make_async_copy(sum1, w1_out, osem.at[1]))
    outs[-1].start()
    total2 = rz2[0].astype(F32)
    for d in range(lines - 1, 0, -1):
        z2_copy(d).wait_recv()
        total2 = total2 + rz2[d].astype(F32)
    sum2[...] = total2.T
    outs.append(pltpu.make_async_copy(sum2, w2_out, osem.at[5]))
    outs[-1].start()
    wos[...] = reduced(1, go_[row(f), :]).T
    outs.append(pltpu.make_async_copy(wos, wo_out, osem.at[2]))
    outs[-1].start()
    finish(chunks - 1)
    outs.append(pltpu.make_async_copy(ghidv, tok_out, osem.at[3]))
    outs[-1].start()
    mine = reduced(2, gq[row(f), :])
    for k in range(3):
        wqs[k] = mine[:, k * head_width : (k + 1) * head_width]
    outs.append(pltpu.make_async_copy(wqs, wq_out, osem.at[4]))
    outs[-1].start()
    for c in level3:
        c.wait_recv()
    for u in range(4):
        cols = slice(u * head_width, (u + 1) * head_width)
        for r in range(4):
            fcb_out[:, r * width + u * head_width : r * width + (u + 1) * head_width] = gv[u, r : r + 1, :]
        qv_out[:, cols] = gv[u, 4:6, :]
        for r, ref in enumerate((g_a, g_b, g_c, g_d, g_e, g_f)):
            ref[:, cols] = gv[u, 6 + r : 7 + r, :]
    for c in sends:
        c.wait_send()

    def drain(d, _):
        for k in range(3):
            x_copy(k, d).wait_send()

        @pl.when(d > 0)
        def _():
            z2_copy(d).wait_send()
            for k in range(3):
                z_copy(k, d).wait_send()

        return 0

    lax.fori_loop(0, lines, drain, 0)
    for c in outs:
        c.wait()


def tail(shards, qkv, grad_att, att, lse, starts, weights, vec, gain, bias, fc2_bias, one, back, tok, ghid, hid, pfar, g1, g2):
    _, rows, width = one.shape
    head_width = att.shape[2]
    hidden = g1.shape[2]
    heads = head_width // HD
    per = width // shards
    lines = shards // 2
    chunks = 2
    dma = pltpu.SemaphoreType.DMA
    vm = pl.BlockSpec(memory_space=VM)
    hbm = pl.BlockSpec(memory_space=HB)
    V = pltpu.VMEM
    small = (4, 16, head_width)
    sems = [
        (8 + lines,), (2, chunks), (2, chunks), (chunks,), (chunks,),
        (3, lines), (3, lines), (3, lines), (3, lines),
        (4,), (4,), (shards,), (shards,), (4,), (4,), (4,), (4,), (lines,), (lines,), (6,),
    ]
    turned = V((4, head_width, rows), BF)
    one_row = (rows, width)
    return pl.pallas_call(
        functools.partial(tail_kernel, shards, chunks),
        name="tail",
        out_shape=[
            jax.ShapeDtypeStruct(one_row, F32),
            jax.ShapeDtypeStruct(one_row, F32),
            jax.ShapeDtypeStruct((3, per, head_width), F32),
            jax.ShapeDtypeStruct((head_width, per), F32),
            jax.ShapeDtypeStruct((per, hidden), F32),
            jax.ShapeDtypeStruct((hidden, per), F32),
            jax.ShapeDtypeStruct((2, width), F32),
            jax.ShapeDtypeStruct((1, 4 * width), F32),
        ]
        + [jax.ShapeDtypeStruct((1, width), F32)] * 6,
        in_specs=[vm] * 4 + [pl.BlockSpec(memory_space=SM)] + [vm] * 5 + [hbm] * 8,
        out_specs=[hbm] * 6 + [vm] * 8,
        scratch_shapes=[
            turned, turned, turned,
            V((4, rows, head_width), F32), V((4, rows, head_width), F32), V((4, heads, rows), F32),
            V((4, rows, 3 * head_width), BF),
            V((4, rows, width), BF), V((4, rows, width), BF), V(one_row, BF), V(one_row, F32),
            V(one_row, F32), V(one_row, BF), V((3 * head_width, width), BF),
            V((2, rows, width), BF), V((2, rows, width), BF), V(one_row, BF), V(one_row, BF),
            V(one_row, F32), V((width, 3 * head_width), BF), V((width, head_width), BF),
        ]
        + [V((lines, per, 3 * head_width), BF)] * 3
        + [V((lines, per, head_width), BF)] * 3
        + [V((lines, per, hidden), BF)] * 4
        + [
            V((per, hidden), F32), V((hidden, per), F32), V((3, per, head_width), F32), V((head_width, per), F32),
            V((8, width), F32), V(small, F32), V(small, F32),
            V((16, head_width), F32), V((shards, 16, head_width), F32), V(small, F32),
        ]
        + [dma(s) for s in sems],
        compiler_params=pltpu.CompilerParams(
            collective_id=2, has_side_effects=True, vmem_limit_bytes=60 << 20
        ),
        cost_estimate=pl.CostEstimate(flops=60 << 30, bytes_accessed=100 << 20, transcendentals=0),
    )(qkv, grad_att, att, lse, starts, weights, vec, gain, bias, fc2_bias, one, back, tok, ghid, hid, pfar, g1, g2)


def finish_kernel(parts, *refs):
    count = len(parts)
    held, sems = refs[2 * count : 3 * count], refs[-1]
    loads, stores = [], []
    for n, pieces in enumerate(parts):
        rows = held[n].shape[0] // pieces
        for i in range(pieces):
            block, k = pl.ds(i * rows, rows), len(loads)
            loads.append(
                pltpu.make_async_copy(refs[n].at[block], held[n].at[block], sems.at[0, k])
            )
            stores.append(
                pltpu.make_async_copy(held[n].at[block], refs[count + n].at[block], sems.at[1, k])
            )
    for c in loads:
        c.start()
    for load, store in zip(loads, stores):
        load.wait()
        store.start()
    for c in stores:
        c.wait()


def finish(arrays):
    parts = [4 if a.size >= 1 << 18 else 1 for a in arrays]
    hbm = pl.BlockSpec(memory_space=HB)
    return pl.pallas_call(
        functools.partial(finish_kernel, parts),
        name="finish",
        out_shape=[jax.ShapeDtypeStruct(a.shape, a.dtype) for a in arrays],
        in_specs=[hbm] * len(arrays),
        out_specs=[hbm] * len(arrays),
        scratch_shapes=[pltpu.VMEM(a.shape, a.dtype) for a in arrays]
        + [pltpu.SemaphoreType.DMA((2, sum(parts)))],
    )(*arrays)


def body(
    tokens,
    cotangent,
    pic_starts,
    w_qkv,
    qv_bias,
    w_out,
    out_bias,
    ln1_gain,
    ln1_bias,
    w_fc1,
    fc1_bias,
    w_fc2,
    fc2_bias,
    ln2_gain,
    ln2_bias,
):
    rows, width = tokens.shape
    shards = lax.axis_size("fsdp")
    one, qkv, wq_full, out_full, fc_in, up_far, att, lse, mix = head(
        shards, tokens, w_qkv.transpose(1, 0, 2), w_out, w_fc1, w_fc2,
        ln1_gain[None], ln1_bias[None], qv_bias, pic_starts, cotangent,
    )
    hidden_one, ghid, back, grad_att, fc1_part, fc2_part, part_far, vec = middle(
        shards, mix, out_full, tokens, cotangent, up_far, fc_in,
        ln2_gain[None], ln2_bias[None], out_bias[None], fc1_bias[None],
    )
    results = tail(
        shards, qkv, grad_att, att, lse, pic_starts, wq_full, vec, ln1_gain[None], ln1_bias[None],
        fc2_bias[None], one, back, tokens, ghid, hidden_one, part_far, fc1_part, fc2_part,
    )
    output, input_grad, wq_grad, wo_grad, fc1_grad, fc2_grad, qv_grad, fc1_b, *vecs = finish(results)
    out_b, fc2_b, gain_two, shift_two, gain_one, shift_one = [v[0] for v in vecs]
    return (
        output,
        input_grad,
        wq_grad.transpose(1, 0, 2),
        qv_grad,
        wo_grad,
        out_b,
        gain_one,
        shift_one,
        fc1_grad,
        fc1_b[0],
        fc2_grad,
        fc2_b,
        gain_two,
        shift_two,
    )


def solution(mesh):
    return jax.shard_map(
        body,
        mesh=mesh,
        in_specs=(
            P(("fsdp", "tensor"), None),
            P(("fsdp", "tensor"), None),
            P("fsdp", None),
            P("fsdp", None, "tensor"),
            P(),
            P("tensor", "fsdp"),
            P(),
            P(),
            P(),
            P("fsdp", "tensor"),
            P(),
            P("tensor", "fsdp"),
            P(),
            P(),
            P(),
        ),
        out_specs=(
            P(("fsdp", "tensor"), None),
            P(("fsdp", "tensor"), None),
            P("fsdp", None, "tensor"),
            P(),
            P("tensor", "fsdp"),
            P(),
            P(),
            P(),
            P("fsdp", "tensor"),
            P(),
            P("tensor", "fsdp"),
            P(),
            P(),
            P(),
        ),
        check_vma=False,
    )
```

```python
import functools
import math

import jax
import jax.numpy as jnp
from jax import lax
from jax.experimental import pallas as pl
from jax.experimental.pallas import tpu as pltpu
from jax.sharding import PartitionSpec as P

HD = 64
PIC = 256
F32 = jnp.float32
BF = jnp.bfloat16
NEG = -1e30
NORM_EPSILON = 1e-05
GELU_SCALE = math.sqrt(2.0 / math.pi)
GELU_CUBIC = 0.044715
VM = pltpu.MemorySpace.VMEM
SM = pltpu.MemorySpace.SMEM
HB = pltpu.MemorySpace.HBM
PRE = (1, 2)


def nn(a, b):
    return lax.dot_general(a, b, (((1,), (0,)), ((), ())), preferred_element_type=F32)


def nt(a, b):
    return lax.dot_general(a, b, (((1,), (1,)), ((), ())), preferred_element_type=F32)


def normalize(values):
    average = jnp.mean(values, axis=1, keepdims=True)
    centered = values - average
    inv_std = lax.rsqrt(jnp.mean(centered * centered, axis=1, keepdims=True) + NORM_EPSILON)
    return centered * inv_std, inv_std


def normalize_back(gradient, unit_rows, inv_std, gain_row):
    scaled = gradient * gain_row
    inner = (
        scaled
        - jnp.mean(scaled, axis=1, keepdims=True)
        - unit_rows * jnp.mean(scaled * unit_rows, axis=1, keepdims=True)
    )
    return inv_std * inner, jnp.sum(gradient * unit_rows, axis=0), jnp.sum(gradient, axis=0)


MESH = pl.DeviceIdType.MESH


def remote(src, dst, send, recv, where):
    return pltpu.make_async_remote_copy(
        src_ref=src, dst_ref=dst, send_sem=send, recv_sem=recv, device_id=where, device_id_type=MESH
    )


def greet(peers):
    barrier = pltpu.get_barrier_semaphore()
    for peer in peers:
        pl.semaphore_signal(barrier, inc=1, device_id=peer, device_id_type=MESH)
    pl.semaphore_wait(barrier, len(peers))


def head_kernel(
    shards, chunks,
    tok, wq, wo, w1, w2, gain, bias, qvb, starts, cot,
    n_out, qkv_out, wq_out, wo_out, fc_out, up_out, att_out, lse_out, mix_out,
    nv, wqv, wov, otv, fcv, qv, kn, qT, vT, att, lsev,
    ysend, yrecv, csend, crecv, fsend, frecv, zqs, zqr, xqs, xqr, zos, zor, xos, xor,
    zfs, zfr, zds, zdr, xfs, xfr, ups, upr, wos, wor, ats, atr, lsem, osem,
):
    f = lax.axis_index("fsdp")
    t = lax.axis_index("tensor")
    rows, width = tok.shape
    head_width, per = wo.shape
    hid = w1.shape[1]
    step = rows // chunks
    lines = shards // 2
    far = {"fsdp": f, "tensor": t ^ 2}
    sib = {"fsdp": f, "tensor": t ^ 1}
    side = {"fsdp": f ^ 1, "tensor": t}
    alongs = [{"fsdp": f ^ (2 * d), "tensor": t} for d in range(1, lines)]
    mates = [{"fsdp": f, "tensor": t ^ j} for j in range(4)]
    greet(mates[1:] + [side] + alongs)
    sends = []

    def go(copy):
        copy.start()
        sends.append(copy)
        return copy

    zq, zo, xq, xo = [], [], [], []
    for d in range(1, lines):
        zq.append(go(remote(wq, wqv.at[f], zqs.at[d], zqr.at[d], alongs[d - 1])))
    xq.append(go(remote(wq, wqv.at[f], xqs.at[0], xqr.at[0], side)))
    ys, cs, fs = [], [], []
    for c in range(chunks):
        part = pl.ds(c * step, step)
        unit, _ = normalize(tok[part, :].astype(F32))
        nv[0, part, :] = (unit * gain[...] + bias[...]).astype(BF)
        ys.append(go(remote(nv.at[0, part], nv.at[2, part], ysend.at[c], yrecv.at[c], far)))
        cs.append(go(remote(nv.at[0, part], nv.at[1, part], csend.at[c], crecv.at[c], sib)))
    for d in range(1, lines):
        zo.append(go(remote(wo, wov.at[f], zos.at[d], zor.at[d], alongs[d - 1])))
    xo.append(go(remote(wo, wov.at[f], xos.at[0], xor.at[0], side)))
    wqv[f] = wq[...]
    wov[f] = wo[...]
    fcv[:, :hid] = w1[...]
    fcv[:, hid:] = w2[...].T
    local = [pltpu.make_async_copy(fcv, fc_out.at[f], lsem.at[0])]
    local[0].start()

    def forward_far(c):
        part = pl.ds(c * step, step)
        ys[c].wait_recv()
        fs.append(go(remote(nv.at[2, part], nv.at[3, part], fsend.at[c], frecv.at[c], sib)))

    todo = list(range(chunks))
    for d in range(1, lines):
        zq[d - 1].wait_recv()
        slot = f ^ (2 * d)
        xq.append(go(remote(wqv.at[slot], wqv.at[slot], xqs.at[d], xqr.at[d], side)))
        if len(todo) > 1:
            forward_far(todo.pop(0))
    for d in range(1, lines):
        zo[d - 1].wait_recv()
        slot = f ^ (2 * d)
        xo.append(go(remote(wov.at[slot], wov.at[slot], xos.at[d], xor.at[d], side)))
    fc = []
    for d in PRE:
        if d < lines:
            fc.append(go(remote(fcv, fc_out.at[f], zfs.at[d], zfr.at[d], alongs[d - 1])))
    while todo:
        forward_far(todo.pop(0))
    up = go(remote(cot, up_out, ups.at[0], upr.at[0], far))
    for c in cs:
        c.wait_recv()
    for d in range(lines):
        xq[d].wait_recv()
    start = pl.multiple_of(t * head_width, head_width)
    adds = (qvb[0:1, pl.ds(start, head_width)], None, qvb[1:2, pl.ds(start, head_width)])

    def project(j, _):
        b = t ^ j
        for k in range(3):
            value = nn(nv[j], wqv[:, k].reshape(width, head_width))
            if adds[k] is not None:
                value = value + adds[k]
            value = value.astype(BF)
            qv[j, :, k * head_width : (k + 1) * head_width] = value
            if k == 0:
                qT[b] = (value * jnp.asarray(HD**-0.5, BF)).T
            elif k == 1:
                kn[b] = value
            else:
                vT[b] = value.T
        return 0

    lax.fori_loop(0, 2, project, 0)
    for c in fs:
        c.wait_recv()
    lax.fori_loop(2, 4, project, 0)
    for d in range(lines):
        xo[d].wait_recv()
    fc.append(go(remote(fcv, fc_out.at[f], zfs.at[0], zfr.at[0], side)))
    if per % 128 == 0:
        def place(s, _):
            otv[:, pl.ds(pl.multiple_of(s * per, per), per)] = wov[s]
            return 0

        lax.fori_loop(0, shards, place, 0)
    else:
        for s in range(shards):
            otv[:, s * per : (s + 1) * per] = wov[s]
    outs = [
        pltpu.make_async_copy(src, dst, osem.at[n])
        for n, (src, dst) in enumerate([(nv, n_out), (qv, qkv_out), (wqv, wq_out), (otv, wo_out.at[t])])
    ]
    for c in outs:
        c.start()
    shared = [
        go(remote(otv, wo_out.at[t], wos.at[1], wor.at[1], sib)),
        go(remote(otv, wo_out.at[t], wos.at[2], wor.at[2], far)),
    ]
    rowk = lax.broadcasted_iota(jnp.int32, (rows, rows), 0)
    colq = lax.broadcasted_iota(jnp.int32, (rows, rows), 1)
    half = lax.broadcasted_iota(jnp.int32, (2 * HD, rows), 0) < HD
    def mixed(i):
        return remote(
            att.at[i], mix_out.at[t], ats.at[i], atr.at[t ^ i], {"fsdp": f, "tensor": t * 0 + i}
        )

    pre = [d for d in PRE if d < lines]
    direct = [d for d in range(1, lines) if d not in pre]
    later = [remote(fcv, fc_out.at[f], zds.at[d], zdr.at[d], alongs[d - 1]) for d in direct]
    passed = []
    for d in pre:
        shard = fc_out.at[f ^ (2 * d)]
        passed.append(remote(shard, shard, xfs.at[d], xfr.at[d], side))
    more = later + passed
    sends += more

    def attend(i, _):
        at = starts[0, i] - i * rows

        @pl.when(i == 2)
        def _():
            for c in later:
                c.start()

        @pl.when(i == 3)
        def _():
            for n in range(len(pre)):
                fc[n].wait_recv()
                passed[n].start()

        def pair(p, _):
            col = pl.multiple_of(p * 2 * HD, 2 * HD)
            qp = qT[i, pl.ds(col, 2 * HD), :]
            zero = jnp.zeros_like(qp)
            masked = (jnp.where(half, qp, zero), jnp.where(half, zero, qp))

            def block(m, carry, diag):
                kb = kn[m, :, pl.ds(col, 2 * HD)]
                vb = vT[m, pl.ds(col, 2 * HD), :]
                new = []
                for hh in range(2):
                    top, total, acc = carry[hh]
                    s = nn(kb, masked[hh])
                    if diag:
                        inside = (rowk >= at) & (rowk < at + PIC) & (colq >= at) & (colq < at + PIC)
                        s = jnp.where((rowk <= colq) | inside, s, NEG)
                    peak = jnp.maximum(top, jnp.max(s, axis=0, keepdims=True))
                    shrink = jnp.exp(top - peak)
                    e = jnp.exp(s - peak)
                    total = total * shrink + jnp.sum(e, axis=0, keepdims=True)
                    acc = acc * shrink + nn(vb[hh * HD : (hh + 1) * HD], e.astype(BF))
                    new.append((peak, total, acc))
                return tuple(new)

            blank = (
                jnp.full((1, rows), NEG, F32), jnp.zeros((1, rows), F32), jnp.zeros((HD, rows), F32)
            )
            c = block(i, (blank, blank), True)
            c = lax.fori_loop(0, i, lambda m, c: block(m, c, False), c)
            found = []
            for hh in range(2):
                top, total, acc = c[hh]
                found.append(acc * (1.0 / total))
                lsev[t ^ i, pl.ds(p * 2 + hh, 1), :] = top + jnp.log(total)
            att[i, :, pl.ds(col, 2 * HD)] = jnp.concatenate(found, axis=0).astype(BF).T
            return 0

        lax.fori_loop(0, head_width // (2 * HD), pair, 0)

        @pl.when(t != i)
        def _():
            mixed(i).start()

        return 0

    lax.fori_loop(0, 4, attend, 0)
    outs += [pltpu.make_async_copy(att.at[t ^ j], att_out.at[j], osem.at[4 + j]) for j in range(4)]
    outs.append(pltpu.make_async_copy(lsev, lse_out, osem.at[8]))
    outs.append(pltpu.make_async_copy(att.at[t], mix_out.at[t], osem.at[9]))
    for c in outs[4:]:
        c.start()
    shared[1].wait_recv()
    shared.append(go(remote(wo_out.at[t ^ 2], wo_out.at[t ^ 2], wos.at[3], wor.at[3], sib)))
    shared[0].wait_recv()
    shared[2].wait_recv()
    for j in range(1, 4):
        remote(att.at[0], mix_out.at[t ^ j], ats.at[0], atr.at[j], mates[j]).wait_recv()
    for i in range(4):

        @pl.when(t != i)
        def _(i=i):
            mixed(i).wait_send()

    for c in fc[len(pre) :] + [up] + more:
        c.wait_recv()
    for c in sends:
        c.wait_send()
    for c in local + outs:
        c.wait()


def head(shards, tokens, wq, wo, w1, w2, gain, bias, qv_bias, starts, cot):
    rows, width = tokens.shape
    head_width, per = wo.shape
    hid = w1.shape[1]
    lines = shards // 2
    chunks = 4
    heads = head_width // HD
    dma = pltpu.SemaphoreType.DMA
    vm = pl.BlockSpec(memory_space=VM)
    hbm = pl.BlockSpec(memory_space=HB)
    V = pltpu.VMEM
    full = (4, rows, width)
    three = (4, rows, 3 * head_width)
    return pl.pallas_call(
        functools.partial(head_kernel, shards, chunks),
        name="head",
        out_shape=[
            jax.ShapeDtypeStruct(full, BF),
            jax.ShapeDtypeStruct(three, BF),
            jax.ShapeDtypeStruct((shards, 3, per, head_width), BF),
            jax.ShapeDtypeStruct((4, head_width, width), BF),
            jax.ShapeDtypeStruct((shards, per, 2 * hid), BF),
            jax.ShapeDtypeStruct((rows, width), BF),
            jax.ShapeDtypeStruct((4, rows, head_width), BF),
            jax.ShapeDtypeStruct((4, heads, rows), F32),
            jax.ShapeDtypeStruct((4, rows, head_width), BF),
        ],
        in_specs=[vm] * 8 + [pl.BlockSpec(memory_space=SM), hbm],
        out_specs=[hbm] * 9,
        scratch_shapes=[
            V(full, BF), V((shards, 3, per, head_width), BF), V((shards, head_width, per), BF),
            V((head_width, width), BF), V((per, 2 * hid), BF), V(three, BF),
            V((4, rows, head_width), BF), V((4, head_width, rows), BF), V((4, head_width, rows), BF),
            V((4, rows, head_width), BF), V((4, heads, rows), F32),
        ]
        + [dma((chunks,))] * 6
        + [dma((lines,))] * 8
        + [dma((max(lines, 4),))] * 6
        + [dma((1,))] * 2
        + [dma((4,))] * 4
        + [dma((1,)), dma((10,))],
        compiler_params=pltpu.CompilerParams(
            collective_id=0, has_side_effects=True, vmem_limit_bytes=56 << 20
        ),
        cost_estimate=pl.CostEstimate(flops=40 << 30, bytes_accessed=90 << 20, transcendentals=0),
    )(tokens, wq, wo, w1, w2, gain, bias, qv_bias, starts, cot)


def middle_kernel(
    shards, chunks,
    mix, wo, tok, cot, up_far, fc_in, gain, bias, out_bias, fc_bias,
    hid_out, ghid_out, back_out, do_out, g1_out, g2_out, part_far, vec,
    wfc, wt, wot, upv, twov, actv, pgv, backv,
    s1, r1, a1, q1, near, hv, rx, sz, dov,
    dos, dor, c2s, c2r, y2s, y2r, f2s, f2r,
    s3s, s3r, y3s, y3r,
    s5s, s5r, ups, upr, lsem, xs, xr, osem, gxs, gxr,
):
    f = lax.axis_index("fsdp")
    t = lax.axis_index("tensor")
    rows, width = tok.shape
    per = fc_in.shape[1]
    hid = fc_in.shape[2] // 2
    pre = [d for d in PRE if d < shards // 2]
    step = rows // chunks
    lines = shards // 2
    far = {"fsdp": f, "tensor": t ^ 2}
    sib = {"fsdp": f, "tensor": t ^ 1}
    side = {"fsdp": f ^ 1, "tensor": t}
    direct = [d for d in range(1, lines) if d not in pre]
    mates = [{"fsdp": f, "tensor": t ^ j} for j in range(4)]
    greet(mates[1:] + [side])
    sends = []

    def go(copy):
        copy.start()
        sends.append(copy)
        return copy

    def part(c):
        return pl.ds(c * step, step)

    halves = (pl.ds(0, hid), pl.ds(hid, hid))
    late = [2 * d + 1 for d in direct]
    early = [e for e in range(shards) if e not in late]
    local = [
        pltpu.make_async_copy(fc_in.at[f ^ e], wfc.at[f ^ e], lsem.at[n])
        for n, e in enumerate(early)
    ]
    local.append(pltpu.make_async_copy(cot, upv.at[0], lsem.at[shards]))
    local.append(pltpu.make_async_copy(up_far, upv.at[2], lsem.at[shards + 1]))
    for c in local:
        c.start()
    xf = []
    for d in direct:
        block = f ^ (2 * d)
        xf.append(go(remote(fc_in.at[block], wfc.at[block], xs.at[d], xr.at[d], side)))
    up_copies = [
        go(remote(cot, upv.at[1], ups.at[0], upr.at[0], sib)),
        go(remote(up_far, upv.at[3], ups.at[1], upr.at[1], sib)),
    ]
    vec[...] = jnp.zeros_like(vec)
    ag_far, ag_sib = [], []
    for c in range(chunks):
        hidden = tok[part(c), :].astype(F32) + out_bias[...]
        for s in range(4):
            hidden = hidden + nn(mix[s, part(c), :], wo[s])
        hv[part(c), :] = hidden
        unit, _ = normalize(hidden)
        twov[0, part(c), :] = (unit * gain[...] + bias[...]).astype(BF)
        ag_far.append(go(remote(twov.at[0, part(c)], twov.at[2, part(c)], y2s.at[c], y2r.at[c], far)))
        ag_sib.append(go(remote(twov.at[0, part(c)], twov.at[1, part(c)], c2s.at[c], c2r.at[c], sib)))
    for s in range(4):
        wot[s] = wo[s].T
    outs = []
    for c in local:
        c.wait()

    def flip(slot):
        if per % 128 == 0:
            wt[:, pl.ds(pl.multiple_of(slot * per, per), per)] = wfc[slot].T

    def flip_early(e, _):
        flip(f ^ e)
        return 0

    if early == list(range(len(early))):
        lax.fori_loop(0, len(early), flip_early, 0)
    else:
        for e in early:
            flip(f ^ e)
    for c in xf:
        c.wait_recv()
    for e in late:
        flip(f ^ e)
    if per % 128:
        wt[...] = wfc[...].reshape(width, 2 * hid).T
    for c in up_copies:
        c.wait_recv()
    for c in ag_sib:
        c.wait_recv()
    start = pl.multiple_of(t * hid, hid)
    tile = hid // 2

    def feed(j, at):
        block = pl.ds(pl.multiple_of(at * step, step), step)
        two = twov[j, block, :]
        up = upv[j, block, :]
        total = None
        for n in range(2):
            cols = pl.ds(n * tile, tile)
            x = nn(two, wfc[:, :, cols].reshape(width, tile))
            x = x + fc_bias[:, pl.ds(pl.multiple_of(start + n * tile, tile), tile)]
            hg = nn(up, wfc[:, :, pl.ds(hid + n * tile, tile)].reshape(width, tile))
            sq = x * x
            th = jnp.tanh(GELU_SCALE * (x + GELU_CUBIC * (sq * x)))
            half = 0.5 * (1.0 + th)
            actv[j, block, cols] = (x * half).astype(BF)
            slope = half + (0.5 * GELU_SCALE) * x * (1.0 - th * th) * (1.0 + (3.0 * GELU_CUBIC) * sq)
            pg = (hg * slope).astype(BF)
            pgv[j, block, cols] = pg
            vec[0:1, cols] += jnp.sum(pg.astype(F32), axis=0, keepdims=True)
            term = nn(pg, wt[cols, :])
            total = term if total is None else total + term
        return total

    def copies(c):
        block = pl.ds(pl.multiple_of(c * step, step), step)
        return (
            remote(twov.at[0, block], twov.at[2, block], y2s.at[c], y2r.at[c], far),
            remote(twov.at[2, block], twov.at[3, block], f2s.at[c], f2r.at[c], sib),
            remote(a1.at[block], q1.at[block], y3s.at[c], y3r.at[c], far),
        )

    def core_copy(k, c):
        block = pl.ds(pl.multiple_of(c * step, step), step)
        return remote(s1.at[2 + k, block], r1.at[2 + k, block], s3s.at[k, c], s3r.at[k, c], sib)

    def rows_of(c, _):
        block = pl.ds(pl.multiple_of(c * step, step), step)
        got, fwd, send2 = copies(c)

        def one(i, _):
            total = feed(i ^ 1, c)

            @pl.when(i == 0)
            def _():
                s1[3, block, :] = total.astype(BF)
                core_copy(1, c).start()
                got.wait_recv()
                fwd.start()

            @pl.when(i == 1)
            def _():
                near[block, :] = total
                fwd.wait_recv()

            @pl.when(i == 2)
            def _():
                s1[2, block, :] = total.astype(BF)
                core_copy(0, c).start()

            @pl.when(i == 3)
            def _():
                core_copy(0, c).wait_recv()
                a1[block, :] = (total + r1[2, block, :].astype(F32)).astype(BF)
                send2.start()

            return 0

        lax.fori_loop(0, 4, one, 0)
        return 0

    lax.fori_loop(0, chunks, rows_of, 0)

    span = 256
    ratio = span // (2 * per)
    groups = width // span
    z = f // 2
    x = lax.rem(f, 2)

    def x_copy(d):
        return remote(wfc.at[(z ^ d) * 2 + (1 - x), :, halves[0]], rx.at[d], gxs.at[d], gxr.at[d], side)

    def weight_grad(left, right, h, send):
        def group_of(i, _):
            near_group = groups - 1 - i
            group = near_group ^ (z // ratio)
            cols = pl.ds(pl.multiple_of(group * span, span), span)
            acc = None
            for j in range(4):
                term = nn(left[j, :, cols].T, right[j])
                acc = term if acc is None else acc + term
            count = span // per
            slots = pl.ds(group * count, count)
            wfc[slots, :, halves[h]] = acc.astype(BF).reshape(count, per, hid)
            if send:

                def launch(e, _):
                    x_copy(near_group * ratio + e).start()
                    return 0

                lax.fori_loop(0, ratio, launch, 0)
            return 0

        lax.fori_loop(0, groups, group_of, 0)

    def feed_part(k):
        for c in range(chunks):
            core_copy(k, c).wait_send()

        def give(c, _):
            block = pl.ds(pl.multiple_of(c * step, step), step)
            s1[k, block, :] = nn(actv[3 - 2 * k, block, :], wt[hid:, :]).astype(BF)
            return 0

        lax.fori_loop(0, chunks, give, 0)
        given = go(remote(s1.at[k], r1.at[k], s5s.at[k], s5r.at[k], sib))

        def keep(c, _):
            block = pl.ds(pl.multiple_of(c * step, step), step)
            mine = nn(actv[2 - 2 * k, block, :], wt[hid:, :])
            if k:
                hv[block, :] += mine
            else:
                s1[2, block, :] = mine.astype(BF)
            return 0

        lax.fori_loop(0, chunks, keep, 0)
        given.wait_recv()
        if k:
            hv[...] += r1[k].astype(F32)
            outs.append(pltpu.make_async_copy(hv, hid_out, osem.at[0]))
        else:
            s1[2] = (s1[2].astype(F32) + r1[k].astype(F32)).astype(BF)
            outs.append(pltpu.make_async_copy(s1.at[2], part_far, osem.at[2]))
        outs[-1].start()

    weight_grad(upv, actv, 0, True)
    given_do = []
    for c in range(chunks):
        _, _, send2 = copies(c)
        core_copy(1, c).wait_recv()
        send2.wait_recv()
        gn = near[part(c), :] + r1[3, part(c), :].astype(F32) + q1[part(c), :].astype(F32)
        unit, inv = normalize(hv[part(c), :])
        back, g_sum, b_sum = normalize_back(gn, unit, inv, gain[...])
        cots = upv[0, part(c), :].astype(F32)
        ghid = cots + back
        near[part(c), :] = ghid
        low = ghid.astype(BF)
        backv[part(c), :] = low
        for j in (2, 3, 1, 0):
            dov[j, part(c), :] = nn(low, wot[t ^ j]).astype(BF)
            if j > 0:
                given_do.append(
                    go(remote(dov.at[j, part(c)], do_out.at[j, part(c)], dos.at[j, c], dor.at[j, c], mates[j]))
                )
        vec[1:2, :] += g_sum[None]
        vec[2:3, :] += b_sum[None]
        vec[3:4, :] += jnp.sum(ghid, axis=0, keepdims=True)
        vec[4:5, :] += jnp.sum(cots, axis=0, keepdims=True)
        feed_part(c) if c < 2 else None
    outs.append(pltpu.make_async_copy(near, ghid_out, osem.at[1]))
    outs[-1].start()

    weight_grad(twov, pgv, 1, False)
    outs.append(pltpu.make_async_copy(wfc.at[:, :, halves[1]], g1_out, osem.at[5]))
    outs[-1].start()
    outs.append(pltpu.make_async_copy(dov.at[0], do_out.at[0], osem.at[7]))
    outs[-1].start()
    outs.append(pltpu.make_async_copy(backv, back_out, osem.at[4]))
    outs[-1].start()

    def side_sum(i, _):
        d = lines - 1 - i
        x_copy(d).wait_recv()
        sz[d] = (wfc[(z ^ d) * 2 + x, :, halves[0]].astype(F32) + rx[d].astype(F32)).astype(BF)
        return 0

    lax.fori_loop(0, lines, side_sum, 0)
    outs.append(pltpu.make_async_copy(sz, g2_out, osem.at[6]))
    outs[-1].start()
    for c in given_do:
        c.wait_recv()
    for c in sends:
        c.wait_send()
    for c in range(chunks):
        _, fwd, send2 = copies(c)
        fwd.wait_send()
        send2.wait_send()

    def drain(d, _):
        x_copy(d).wait_send()
        return 0

    lax.fori_loop(0, lines, drain, 0)
    for c in outs:
        c.wait()


def middle(shards, mix, wo, tok, cot, up_far, fc_in, gain, bias, out_bias, fc_bias):
    rows, width = tok.shape
    per, hid2 = fc_in.shape[1:]
    hid = hid2 // 2
    head_width = wo.shape[1]
    lines = shards // 2
    chunks = 2
    step = rows // chunks
    dma = pltpu.SemaphoreType.DMA
    vm = pl.BlockSpec(memory_space=VM)
    hbm = pl.BlockSpec(memory_space=HB)
    full = (4, rows, width)
    one = (rows, width)
    block = (lines, per, hid)
    V = pltpu.VMEM
    sems = [
        (4, chunks), (4, chunks), (chunks,), (chunks,),
        (chunks,), (chunks,), (chunks,), (chunks,),
        (2, chunks), (2, chunks), (chunks,), (chunks,),
        (2,), (2,), (2,), (2,), (shards + 2,), (lines,), (lines,), (8,), (lines,), (lines,),
    ]
    return pl.pallas_call(
        functools.partial(middle_kernel, shards, chunks),
        name="middle",
        out_shape=[
            jax.ShapeDtypeStruct(one, F32),
            jax.ShapeDtypeStruct(one, F32),
            jax.ShapeDtypeStruct(one, BF),
            jax.ShapeDtypeStruct((4, rows, head_width), BF),
            jax.ShapeDtypeStruct((shards, per, hid), BF),
            jax.ShapeDtypeStruct(block, BF),
            jax.ShapeDtypeStruct(one, BF),
            jax.ShapeDtypeStruct((8, width), F32),
        ],
        in_specs=[vm, vm, vm, hbm, hbm, hbm] + [vm] * 4,
        out_specs=[hbm] * 7 + [vm],
        scratch_shapes=[
            V((shards, per, 2 * hid), BF), V((2 * hid, width), BF), V((4, width, head_width), BF),
            V(full, BF), V(full, BF), V((4, rows, hid), BF), V((4, rows, hid), BF), V(one, BF),
            V(full, BF), V(full, BF), V(one, BF), V(one, BF),
            V(one, F32), V(one, F32), V(block, BF), V(block, BF), V((4, rows, head_width), BF),
        ]
        + [dma(s) for s in sems],
        compiler_params=pltpu.CompilerParams(
            collective_id=1, has_side_effects=True, vmem_limit_bytes=60 << 20
        ),
        cost_estimate=pl.CostEstimate(flops=60 << 30, bytes_accessed=200 << 20, transcendentals=0),
    )(mix, wo, tok, cot, up_far, fc_in, gain, bias, out_bias, fc_bias)


def tail_kernel(
    shards, chunks,
    qs, dos, ats, lse, starts, weights, vec, gain, bias, fc2_bias,
    one_in, back_in, tok_in, ghid_in, hid_in, pfar_in, g1_in, g2_in,
    out_out, tok_out, wq_out, wo_out, w1_out, w2_out, qv_out, fcb_out, g_a, g_b, g_c, g_d, g_e, g_f,
    qT, kT, doT, dk, dv, dl, dqkv,
    onev, backv, tokv, ghidv, hidv, pfarv, wt,
    s1, r1, a1, q1, near, gq, go_, rx, sz, rz, rxo, szo, rzo, rx1, sz1, rz1, rz2, sum1, sum2, wqs, wos,
    smat, lv, rv1, sv, rv2, gv,
    lsem, s1s, s1r, y1s, y1r, xs, xr, zs, zr, v1s, v1r, v2s, v2r, v3s, v3r, pfs, pfr, z2s, z2r, osem,
):
    f = lax.axis_index("fsdp")
    t = lax.axis_index("tensor")
    _, rows, width = onev.shape
    head_width = ats.shape[2]
    per = width // shards
    lines = shards // 2
    step = rows // chunks
    z = f // 2
    x = lax.rem(f, 2)
    far = {"fsdp": f, "tensor": t ^ 2}
    sib = {"fsdp": f, "tensor": t ^ 1}
    side = {"fsdp": f ^ 1, "tensor": t}
    mates = [{"fsdp": f, "tensor": t ^ j} for j in range(1, 4)]
    others = [{"fsdp": f ^ e, "tensor": t} for e in range(1, shards)]
    greet(mates + others)
    sends = []

    def go(copy):
        copy.start()
        sends.append(copy)
        return copy

    def part(c):
        return pl.ds(c * step, step)

    def row(block):
        return pl.ds(pl.multiple_of(block * per, per), per)

    pairs = head_width // (2 * HD)
    sums = 2 + pairs
    sources = [lambda b: g1_in.at[b], lambda b: go_.at[row(b)]]
    lands = [(rx1, sz1, rz1), (rxo, szo, rzo)]
    for p in range(pairs):
        sources.append(lambda b, p=p: gq.at[p, row(b)])
        lands.append((rx.at[p], sz.at[p], rz.at[p]))

    def x_copy(k, d):
        return remote(
            sources[k]((z ^ d) * 2 + (1 - x)), lands[k][0].at[d], xs.at[k, d], xr.at[k, d], side
        )

    def z_copy(k, d):
        return remote(
            lands[k][1].at[d], lands[k][2].at[d], zs.at[k, d], zr.at[k, d],
            {"fsdp": f ^ (2 * d), "tensor": t},
        )

    def pass_on(k, d, own):
        x_copy(k, d).wait_recv()
        lands[k][1][d] = (own(d).astype(F32) + lands[k][0][d].astype(F32)).astype(BF)
        z_copy(k, d).start()

    def keep_of(d):
        return (z ^ d) * 2 + x

    def launch(i, _):
        x_copy(0, lines - 1 - i).start()
        return 0

    lax.fori_loop(0, lines, launch, 0)
    def z2_copy(d):
        return remote(
            g2_in.at[d], rz2.at[d], z2s.at[d], z2r.at[d], {"fsdp": f ^ (2 * d), "tensor": t}
        )

    def launch2(i, _):
        z2_copy(lines - 1 - i).start()
        return 0

    lax.fori_loop(0, lines - 1, launch2, 0)
    back_far = go(remote(back_in, backv.at[2], pfs.at[1], pfr.at[1], far))
    back_sib = go(remote(back_in, backv.at[1], pfs.at[2], pfr.at[2], sib))
    local = [
        pltpu.make_async_copy(src, dst, lsem.at[n])
        for n, (src, dst) in enumerate(
            [
                (back_in, backv.at[0]), (one_in, onev), (tok_in, tokv), (ghid_in, ghidv),
                (hid_in, hidv), (g2_in.at[0], rz2.at[0]),
            ]
        )
    ]
    for c in local:
        c.start()
    keeps = []

    def own_block(d, _):
        pltpu.make_async_copy(g1_in.at[keep_of(d)], sz1.at[d], lsem.at[8 + d]).start()
        return 0

    lax.fori_loop(0, lines, own_block, 0)

    def pass_fc1(d):
        pltpu.make_async_copy(g1_in.at[keep_of(d)], sz1.at[d], lsem.at[8 + d]).wait()
        pass_on(0, d, lambda d: sz1[d])

    for j in range(4):
        b = t ^ j
        qT[b] = (qs[j, :, :head_width] * jnp.asarray(HD**-0.5, BF)).T
        kT[b] = qs[j, :, head_width : 2 * head_width].T
        do = dos[j]
        doT[b] = do.T
        prod = (do.astype(F32) * ats[j].astype(F32)).T
        for h in range(head_width // HD):
            dl[b, h : h + 1, :] = jnp.sum(prod[h * HD : (h + 1) * HD], axis=0, keepdims=True)
    dk[...] = jnp.zeros_like(dk)
    dv[...] = jnp.zeros_like(dv)
    for k in range(3):
        wt[k * head_width : (k + 1) * head_width, :] = weights[:, k].reshape(width, head_width).T

    span = 256
    ratio = span // (2 * per)
    groups = width // span

    smat[...] = jnp.zeros_like(smat)

    def weight_grad(k, left, rights, target, p=None):
        def group_of(i, _):
            near_group = groups - 1 - i
            group = near_group ^ (z // ratio)
            cols = pl.ds(pl.multiple_of(group * span, span), span)
            turned = [left[j, :, cols].T for j in range(4)]
            count = span // per
            for n, (at, right) in enumerate(rights):
                acc = None
                for j in range(4):
                    term = nn(turned[j], right(j))
                    acc = term if acc is None else acc + term
                target[cols, at : at + acc.shape[1]] = acc.astype(BF)
                if p is not None:
                    block = weights[pl.ds(group * count, count), n, :, p * 2 * HD : (p + 1) * 2 * HD]
                    smat[cols, :] += acc * block.reshape(span, 2 * HD).astype(F32)

            def send(e, _):
                x_copy(k, near_group * ratio + e).start()
                return 0

            lax.fori_loop(0, ratio, send, 0)
            return 0

        lax.fori_loop(0, groups, group_of, 0)

    rowk = lax.broadcasted_iota(jnp.int32, (rows, rows), 0)
    colq = lax.broadcasted_iota(jnp.int32, (rows, rows), 1)
    hrow = lax.broadcasted_iota(jnp.int32, (2 * HD, rows), 0) < HD
    hcol = lax.broadcasted_iota(jnp.int32, (rows, 2 * HD), 1) < HD

    def two(v, m):
        zero = jnp.zeros_like(v)
        return (jnp.where(m, v, zero), jnp.where(m, zero, v))

    def attend(p, i):
        at = starts[0, i] - i * rows
        jj = t ^ i

        if True:
            col = pl.multiple_of(p * 2 * HD, 2 * HD)
            kcol = pl.multiple_of(head_width + p * 2 * HD, 2 * HD)
            vcol = pl.multiple_of(2 * head_width + p * 2 * HD, 2 * HD)
            qTz = two(qT[i, pl.ds(col, 2 * HD), :], hrow)
            doTz = two(doT[i, pl.ds(col, 2 * HD), :], hrow)
            qz = two(qs[jj, :, pl.ds(col, 2 * HD)], hcol)
            doz = two(dos[jj, :, pl.ds(col, 2 * HD)], hcol)
            ls = [lse[jj, pl.ds(p * 2 + hh, 1), :] for hh in range(2)]
            dlt = [dl[i, pl.ds(p * 2 + hh, 1), :] for hh in range(2)]

            def block(m, carry, diag):
                kb = qs[t ^ m, :, pl.ds(kcol, 2 * HD)]
                vb = qs[t ^ m, :, pl.ds(vcol, 2 * HD)]
                ktb = kT[m, pl.ds(col, 2 * HD), :]
                dvs, dks, new = 0.0, 0.0, []
                for hh in range(2):
                    s = nn(kb, qTz[hh])
                    if diag:
                        inside = (rowk >= at) & (rowk < at + PIC) & (colq >= at) & (colq < at + PIC)
                        s = jnp.where((rowk <= colq) | inside, s, NEG)
                    pr = jnp.exp(s - ls[hh])
                    dp = nn(vb, doTz[hh])
                    ds = (pr * (dp - dlt[hh])).astype(BF)
                    dvs = dvs + nn(pr.astype(BF), doz[hh])
                    dks = dks + nn(ds, qz[hh])
                    new.append(carry[hh] + nn(ktb[hh * HD : (hh + 1) * HD], ds))
                dv[m, :, pl.ds(col, 2 * HD)] += dvs
                dk[m, :, pl.ds(col, 2 * HD)] += dks
                return tuple(new)

            c = tuple(jnp.zeros((HD, rows), F32) for _ in range(2))
            c = block(i, c, True)
            c = lax.fori_loop(0, i, lambda m, c: block(m, c, False), c)
            dq = (jnp.concatenate(c, axis=0) * (HD**-0.5)).astype(BF)
            dqkv[jj, :, pl.ds(col, 2 * HD)] = dq.T

    back_fwd = remote(backv.at[2], backv.at[3], pfs.at[3], pfr.at[3], sib)
    pf = remote(pfar_in, pfarv, pfs.at[0], pfr.at[0], far)
    sends += [back_fwd, pf]

    def columns(p):
        return [
            (k * 2 * HD, lambda j, k=k: dqkv[j, :, k * head_width + p * 2 * HD : k * head_width + (p + 1) * 2 * HD])
            for k in range(3)
        ]

    def settle(p):
        kcol = pl.ds(pl.multiple_of(head_width + p * 2 * HD, 2 * HD), 2 * HD)
        vcol = pl.ds(pl.multiple_of(2 * head_width + p * 2 * HD, 2 * HD), 2 * HD)
        col = pl.ds(pl.multiple_of(p * 2 * HD, 2 * HD), 2 * HD)
        for j in range(4):
            dqkv[j, :, kcol] = (dk[t ^ j, :, col] * (HD**-0.5)).astype(BF)
            dqkv[j, :, vcol] = dv[t ^ j, :, col].astype(BF)

    def pass_pair(p):
        def one(i, _):
            pass_on(2 + p, lines - 1 - i, lambda d: gq[p, row(keep_of(d)), :])
            return 0

        lax.fori_loop(0, lines - 1, one, 0)

    def heads_of(p, _):
        def step_of(i, _):
            attend(p, i)

            @pl.when((p == 0) & (i == 1))
            def _():
                pass_fc1(lines - 1)
                if lines > 2:
                    pass_fc1(lines - 2)

            @pl.when((p == 0) & (i == 2))
            def _():
                if lines > 3:

                    def pass_more(n, _):
                        pass_fc1(lines - 3 - n)
                        return 0

                    lax.fori_loop(0, lines - 3, pass_more, 0)

            @pl.when((p == 1) & (i == 1))
            def _():
                local[0].wait()
                back_sib.wait_recv()
                back_fwd.wait_recv()
                weight_grad(1, backv, [(0, lambda j: ats[j])], go_)

            @pl.when((p == 1) & (i == 2))
            def _():
                pass_pair(0)

            return 0

        lax.fori_loop(0, 4, step_of, 0)
        settle(p)

        @pl.when(p == 0)
        def _():
            back_far.wait_recv()
            back_fwd.start()
            pf.start()
            local[1].wait()
            weight_grad(2, onev, columns(0), gq.at[0], 0)

        return 0

    lax.fori_loop(0, pairs, heads_of, 0)
    for c in local[2:]:
        c.wait()

    def norm_grad(j, c):
        return nn(dqkv[j, part(c), :], wt[...])

    first, second, third = [], [], []
    def far_chunk(c):
        s1[0, part(c), :] = norm_grad(3, c).astype(BF)
        first.append(go(remote(s1.at[0, part(c)], r1.at[0, part(c)], s1s.at[0, c], s1r.at[0, c], sib)))
        mine = norm_grad(2, c)
        first[c].wait_recv()
        a1[part(c), :] = (mine + r1[0, part(c), :].astype(F32)).astype(BF)
        second.append(go(remote(a1.at[part(c)], q1.at[part(c)], y1s.at[c], y1r.at[c], far)))

    far_chunk(0)
    for p in range(1, pairs):
        weight_grad(2 + p, onev, columns(p), gq.at[p], p)
    column_sum = jnp.sum(dqkv[0].astype(F32), axis=0, keepdims=True)
    for j in range(1, 4):
        column_sum = column_sum + jnp.sum(dqkv[j].astype(F32), axis=0, keepdims=True)
    high = column_sum.astype(BF)
    low = (column_sum - high.astype(F32)).astype(BF)
    bias_sum = nn(high, wt[...]) + nn(low, wt[...])
    product = jnp.sum(smat[...].T, axis=0, keepdims=True)
    gain_sum = (product - bias[...] * bias_sum) / gain[...]

    slot = lax.broadcasted_iota(jnp.int32, (4, head_width), 0)
    lv[...] = jnp.zeros_like(lv)
    qsum = column_sum[:, :head_width]
    vsum = column_sum[:, 2 * head_width :]
    for u in range(4):
        cols = pl.ds(u * head_width, head_width)
        lv[u, 0:4, :] = jnp.where(slot == t, vec[0:1, cols], 0.0)
        here = (t == u).astype(F32)
        lv[u, 4:5, :] = qsum * here
        lv[u, 5:6, :] = vsum * here
        lv[u, 6:7, :] = vec[3:4, cols]
        lv[u, 7:8, :] = vec[4:5, cols]
        lv[u, 8:9, :] = vec[1:2, cols]
        lv[u, 9:10, :] = vec[2:3, cols]
        lv[u, 10:11, :] = gain_sum[:, u * head_width : (u + 1) * head_width]
        lv[u, 11:12, :] = bias_sum[:, u * head_width : (u + 1) * head_width]
    level1 = [
        go(remote(lv.at[t ^ j], rv1.at[j], v1s.at[j], v1r.at[j], mates[j - 1])) for j in range(1, 4)
    ]
    for c in range(1, chunks):
        far_chunk(c)

    def pass_out(i, _):
        pass_on(1, lines - 1 - i, lambda d: go_[row(keep_of(d)), :])
        return 0

    lax.fori_loop(0, lines - 1, pass_out, 0)
    for c in range(chunks):
        s1[1, part(c), :] = norm_grad(1, c).astype(BF)
        third.append(go(remote(s1.at[1, part(c)], r1.at[1, part(c)], s1s.at[1, c], s1r.at[1, c], sib)))
    for c in range(chunks):
        near[part(c), :] = norm_grad(0, c)

    def pass_qkv(i, _):
        for p in range(1, pairs):
            pass_on(2 + p, lines - 1 - i, lambda d, p=p: gq[p, row(keep_of(d)), :])
        return 0

    lax.fori_loop(0, (lines - 1) // 2, pass_qkv, 0)
    pf.wait_recv()
    hidv[...] = hidv[...] + pfarv[...].astype(F32) + fc2_bias[...]
    outs = [pltpu.make_async_copy(hidv, out_out, osem.at[0])]
    outs[0].start()
    for c in level1:
        c.wait_recv()
    sv[...] = lv[t] + rv1[1] + rv1[2] + rv1[3]
    level2 = [
        go(remote(sv, rv2.at[e], v2s.at[e], v2r.at[e], others[e - 1])) for e in range(1, shards)
    ]
    lax.fori_loop((lines - 1) // 2, max((lines - 1) // 2, lines - 2), pass_qkv, 0)
    for c in third:
        c.wait_recv()

    def finish(c):
        second[c].wait_recv()
        gn = near[part(c), :] + r1[1, part(c), :].astype(F32) + q1[part(c), :].astype(F32)
        unit, inv = normalize(tokv[part(c), :].astype(F32))
        scaled = gn * gain[...]
        inner = (
            scaled
            - jnp.mean(scaled, axis=1, keepdims=True)
            - unit * jnp.mean(scaled * unit, axis=1, keepdims=True)
        )
        ghidv[part(c), :] = ghidv[part(c), :] + inv * inner

    for c in range(chunks - 1):
        finish(c)
    lax.fori_loop(max((lines - 1) // 2, lines - 2), lines - 1, pass_qkv, 0)
    for c in level2:
        c.wait_recv()
    total = sv[...]
    for e in range(1, shards):
        total = total + rv2[e]
    gv[t] = total
    level3 = [
        go(remote(gv.at[t], gv.at[t], v3s.at[j], v3r.at[j], mates[j - 1])) for j in range(1, 4)
    ]

    def reduced(k, own):
        x_copy(k, 0).wait_recv()
        land = lands[k]
        result = own.astype(F32) + land[0][0].astype(F32)
        if lines <= 8:
            for d in range(lines - 1, 0, -1):
                z_copy(k, d).wait_recv()
                result = result + land[2][d].astype(F32)
            return result

        def collect(i, acc):
            d = lines - 1 - i
            z_copy(k, d).wait_recv()
            return acc + land[2][d].astype(F32)

        return lax.fori_loop(0, lines - 1, collect, result)

    pltpu.make_async_copy(g1_in.at[keep_of(0)], sz1.at[0], lsem.at[8]).wait()
    sum1[...] = reduced(0, sz1[0])
    outs.append(pltpu.make_async_copy(sum1, w1_out, osem.at[1]))
    outs[-1].start()
    total2 = rz2[0].astype(F32)
    for d in range(lines - 1, 0, -1):
        z2_copy(d).wait_recv()
        total2 = total2 + rz2[d].astype(F32)
    sum2[...] = total2.T
    outs.append(pltpu.make_async_copy(sum2, w2_out, osem.at[5]))
    outs[-1].start()
    wos[...] = reduced(1, go_[row(f), :]).T
    outs.append(pltpu.make_async_copy(wos, wo_out, osem.at[2]))
    outs[-1].start()
    finish(chunks - 1)
    outs.append(pltpu.make_async_copy(ghidv, tok_out, osem.at[3]))
    outs[-1].start()
    for p in range(pairs):
        mine = reduced(2 + p, gq[p, row(f), :])
        for k in range(3):
            wqs[k, :, p * 2 * HD : (p + 1) * 2 * HD] = mine[:, k * 2 * HD : (k + 1) * 2 * HD]
    outs.append(pltpu.make_async_copy(wqs, wq_out, osem.at[4]))
    outs[-1].start()
    for c in level3:
        c.wait_recv()
    for u in range(4):
        cols = slice(u * head_width, (u + 1) * head_width)
        for r in range(4):
            fcb_out[:, r * width + u * head_width : r * width + (u + 1) * head_width] = gv[u, r : r + 1, :]
        qv_out[:, cols] = gv[u, 4:6, :]
        for r, ref in enumerate((g_a, g_b, g_c, g_d, g_e, g_f)):
            ref[:, cols] = gv[u, 6 + r : 7 + r, :]
    for c in sends:
        c.wait_send()

    def drain(d, _):
        for k in range(sums):
            x_copy(k, d).wait_send()

        @pl.when(d > 0)
        def _():
            z2_copy(d).wait_send()
            for k in range(sums):
                z_copy(k, d).wait_send()

        return 0

    lax.fori_loop(0, lines, drain, 0)
    for c in outs:
        c.wait()


def tail(shards, qkv, grad_att, att, lse, starts, weights, vec, gain, bias, fc2_bias, one, back, tok, ghid, hid, pfar, g1, g2):
    _, rows, width = one.shape
    head_width = att.shape[2]
    hidden = g1.shape[2]
    heads = head_width // HD
    pairs = heads // 2
    per = width // shards
    lines = shards // 2
    chunks = 2
    dma = pltpu.SemaphoreType.DMA
    vm = pl.BlockSpec(memory_space=VM)
    hbm = pl.BlockSpec(memory_space=HB)
    V = pltpu.VMEM
    small = (4, 16, head_width)
    sems = [
        (8 + lines,), (2, chunks), (2, chunks), (chunks,), (chunks,),
        (2 + pairs, lines), (2 + pairs, lines), (2 + pairs, lines), (2 + pairs, lines),
        (4,), (4,), (shards,), (shards,), (4,), (4,), (4,), (4,), (lines,), (lines,), (6,),
    ]
    turned = V((4, head_width, rows), BF)
    one_row = (rows, width)
    return pl.pallas_call(
        functools.partial(tail_kernel, shards, chunks),
        name="tail",
        out_shape=[
            jax.ShapeDtypeStruct(one_row, F32),
            jax.ShapeDtypeStruct(one_row, F32),
            jax.ShapeDtypeStruct((3, per, head_width), F32),
            jax.ShapeDtypeStruct((head_width, per), F32),
            jax.ShapeDtypeStruct((per, hidden), F32),
            jax.ShapeDtypeStruct((hidden, per), F32),
            jax.ShapeDtypeStruct((2, width), F32),
            jax.ShapeDtypeStruct((1, 4 * width), F32),
        ]
        + [jax.ShapeDtypeStruct((1, width), F32)] * 6,
        in_specs=[vm] * 4 + [pl.BlockSpec(memory_space=SM)] + [vm] * 5 + [hbm] * 8,
        out_specs=[hbm] * 6 + [vm] * 8,
        scratch_shapes=[
            turned, turned, turned,
            V((4, rows, head_width), F32), V((4, rows, head_width), F32), V((4, heads, rows), F32),
            V((4, rows, 3 * head_width), BF),
            V((4, rows, width), BF), V((4, rows, width), BF), V(one_row, BF), V(one_row, F32),
            V(one_row, F32), V(one_row, BF), V((3 * head_width, width), BF),
            V((2, rows, width), BF), V((2, rows, width), BF), V(one_row, BF), V(one_row, BF),
            V(one_row, F32), V((pairs, width, 6 * HD), BF), V((width, head_width), BF),
        ]
        + [V((pairs, lines, per, 6 * HD), BF)] * 3
        + [V((lines, per, head_width), BF)] * 3
        + [V((lines, per, hidden), BF)] * 4
        + [
            V((per, hidden), F32), V((hidden, per), F32), V((3, per, head_width), F32), V((head_width, per), F32),
            V((width, 2 * HD), F32), V(small, F32), V(small, F32),
            V((16, head_width), F32), V((shards, 16, head_width), F32), V(small, F32),
        ]
        + [dma(s) for s in sems],
        compiler_params=pltpu.CompilerParams(
            collective_id=2, has_side_effects=True, vmem_limit_bytes=62 << 20
        ),
        cost_estimate=pl.CostEstimate(flops=60 << 30, bytes_accessed=100 << 20, transcendentals=0),
    )(qkv, grad_att, att, lse, starts, weights, vec, gain, bias, fc2_bias, one, back, tok, ghid, hid, pfar, g1, g2)


def finish_kernel(parts, *refs):
    count = len(parts)
    held, sems = refs[2 * count : 3 * count], refs[-1]
    loads, stores = [], []
    for n, pieces in enumerate(parts):
        rows = held[n].shape[0] // pieces
        for i in range(pieces):
            block, k = pl.ds(i * rows, rows), len(loads)
            loads.append(
                pltpu.make_async_copy(refs[n].at[block], held[n].at[block], sems.at[0, k])
            )
            stores.append(
                pltpu.make_async_copy(held[n].at[block], refs[count + n].at[block], sems.at[1, k])
            )
    for c in loads:
        c.start()
    for load, store in zip(loads, stores):
        load.wait()
        store.start()
    for c in stores:
        c.wait()


def finish(arrays):
    parts = [4 if a.size >= 1 << 18 else 1 for a in arrays]
    hbm = pl.BlockSpec(memory_space=HB)
    return pl.pallas_call(
        functools.partial(finish_kernel, parts),
        name="finish",
        out_shape=[jax.ShapeDtypeStruct(a.shape, a.dtype) for a in arrays],
        in_specs=[hbm] * len(arrays),
        out_specs=[hbm] * len(arrays),
        scratch_shapes=[pltpu.VMEM(a.shape, a.dtype) for a in arrays]
        + [pltpu.SemaphoreType.DMA((2, sum(parts)))],
    )(*arrays)


def body(
    tokens,
    cotangent,
    pic_starts,
    w_qkv,
    qv_bias,
    w_out,
    out_bias,
    ln1_gain,
    ln1_bias,
    w_fc1,
    fc1_bias,
    w_fc2,
    fc2_bias,
    ln2_gain,
    ln2_bias,
):
    rows, width = tokens.shape
    shards = lax.axis_size("fsdp")
    one, qkv, wq_full, out_full, fc_in, up_far, att, lse, mix = head(
        shards, tokens, w_qkv.transpose(1, 0, 2), w_out, w_fc1, w_fc2,
        ln1_gain[None], ln1_bias[None], qv_bias, pic_starts, cotangent,
    )
    hidden_one, ghid, back, grad_att, fc1_part, fc2_part, part_far, vec = middle(
        shards, mix, out_full, tokens, cotangent, up_far, fc_in,
        ln2_gain[None], ln2_bias[None], out_bias[None], fc1_bias[None],
    )
    results = tail(
        shards, qkv, grad_att, att, lse, pic_starts, wq_full, vec, ln1_gain[None], ln1_bias[None],
        fc2_bias[None], one, back, tokens, ghid, hidden_one, part_far, fc1_part, fc2_part,
    )
    output, input_grad, wq_grad, wo_grad, fc1_grad, fc2_grad, qv_grad, fc1_b, *vecs = finish(results)
    out_b, fc2_b, gain_two, shift_two, gain_one, shift_one = [v[0] for v in vecs]
    return (
        output,
        input_grad,
        wq_grad.transpose(1, 0, 2),
        qv_grad,
        wo_grad,
        out_b,
        gain_one,
        shift_one,
        fc1_grad,
        fc1_b[0],
        fc2_grad,
        fc2_b,
        gain_two,
        shift_two,
    )


def solution(mesh):
    return jax.shard_map(
        body,
        mesh=mesh,
        in_specs=(
            P(("fsdp", "tensor"), None),
            P(("fsdp", "tensor"), None),
            P("fsdp", None),
            P("fsdp", None, "tensor"),
            P(),
            P("tensor", "fsdp"),
            P(),
            P(),
            P(),
            P("fsdp", "tensor"),
            P(),
            P("tensor", "fsdp"),
            P(),
            P(),
            P(),
        ),
        out_specs=(
            P(("fsdp", "tensor"), None),
            P(("fsdp", "tensor"), None),
            P("fsdp", None, "tensor"),
            P(),
            P("tensor", "fsdp"),
            P(),
            P(),
            P(),
            P("fsdp", "tensor"),
            P(),
            P("tensor", "fsdp"),
            P(),
            P(),
            P(),
        ),
        check_vma=False,
    )
```

```python
import functools
import math

import jax
import jax.numpy as jnp
from jax import lax
from jax.experimental import pallas as pl
from jax.experimental.pallas import tpu as pltpu
from jax.sharding import PartitionSpec as P

HD = 64
PIC = 256
F32 = jnp.float32
BF = jnp.bfloat16
NEG = -1e30
NORM_EPSILON = 1e-05
GELU_SCALE = math.sqrt(2.0 / math.pi)
GELU_CUBIC = 0.044715
VM = pltpu.MemorySpace.VMEM
SM = pltpu.MemorySpace.SMEM
HB = pltpu.MemorySpace.HBM
PRE = (1, 2)


def nn(a, b):
    return lax.dot_general(a, b, (((1,), (0,)), ((), ())), preferred_element_type=F32)


def nt(a, b):
    return lax.dot_general(a, b, (((1,), (1,)), ((), ())), preferred_element_type=F32)


def normalize(values):
    average = jnp.mean(values, axis=1, keepdims=True)
    centered = values - average
    inv_std = lax.rsqrt(jnp.mean(centered * centered, axis=1, keepdims=True) + NORM_EPSILON)
    return centered * inv_std, inv_std


def normalize_back(gradient, unit_rows, inv_std, gain_row):
    scaled = gradient * gain_row
    inner = (
        scaled
        - jnp.mean(scaled, axis=1, keepdims=True)
        - unit_rows * jnp.mean(scaled * unit_rows, axis=1, keepdims=True)
    )
    return inv_std * inner, jnp.sum(gradient * unit_rows, axis=0), jnp.sum(gradient, axis=0)


MESH = pl.DeviceIdType.MESH


def remote(src, dst, send, recv, where):
    return pltpu.make_async_remote_copy(
        src_ref=src, dst_ref=dst, send_sem=send, recv_sem=recv, device_id=where, device_id_type=MESH
    )


def greet(peers):
    barrier = pltpu.get_barrier_semaphore()
    for peer in peers:
        pl.semaphore_signal(barrier, inc=1, device_id=peer, device_id_type=MESH)
    pl.semaphore_wait(barrier, len(peers))


def head_kernel(
    shards, chunks,
    tok, wq, wo, w1, w2, gain, bias, qvb, starts, cot,
    n_out, qkv_out, wq_out, wo_out, fc_out, up_out, att_out, lse_out, mix_out, wqt_out, qT_out, kT_out,
    nv, wqv, wov, otv, fcv, qv, kn, qT, vT, att, lsev, wqt, kT,
    ysend, yrecv, csend, crecv, fsend, frecv, zqs, zqr, xqs, xqr, zos, zor, xos, xor,
    zfs, zfr, zds, zdr, xfs, xfr, ups, upr, wos, wor, ats, atr, lsem, osem,
):
    f = lax.axis_index("fsdp")
    t = lax.axis_index("tensor")
    rows, width = tok.shape
    head_width, per = wo.shape
    hid = w1.shape[1]
    step = rows // chunks
    lines = shards // 2
    far = {"fsdp": f, "tensor": t ^ 2}
    sib = {"fsdp": f, "tensor": t ^ 1}
    side = {"fsdp": f ^ 1, "tensor": t}
    alongs = [{"fsdp": f ^ (2 * d), "tensor": t} for d in range(1, lines)]
    mates = [{"fsdp": f, "tensor": t ^ j} for j in range(4)]
    greet(mates[1:] + [side] + alongs)
    sends = []

    def go(copy):
        copy.start()
        sends.append(copy)
        return copy

    zq, zo, xq, xo = [], [], [], []
    for d in range(1, lines):
        zq.append(go(remote(wq, wqv.at[f], zqs.at[d], zqr.at[d], alongs[d - 1])))
    xq.append(go(remote(wq, wqv.at[f], xqs.at[0], xqr.at[0], side)))
    ys, cs, fs = [], [], []
    for c in range(chunks):
        part = pl.ds(c * step, step)
        unit, _ = normalize(tok[part, :].astype(F32))
        nv[0, part, :] = (unit * gain[...] + bias[...]).astype(BF)
        ys.append(go(remote(nv.at[0, part], nv.at[2, part], ysend.at[c], yrecv.at[c], far)))
        cs.append(go(remote(nv.at[0, part], nv.at[1, part], csend.at[c], crecv.at[c], sib)))
    for d in range(1, lines):
        zo.append(go(remote(wo, wov.at[f], zos.at[d], zor.at[d], alongs[d - 1])))
    xo.append(go(remote(wo, wov.at[f], xos.at[0], xor.at[0], side)))
    wqv[f] = wq[...]
    wov[f] = wo[...]
    fcv[:, :hid] = w1[...]
    fcv[:, hid:] = w2[...].T
    local = [pltpu.make_async_copy(fcv, fc_out.at[f], lsem.at[0])]
    local[0].start()

    def forward_far(c):
        part = pl.ds(c * step, step)
        ys[c].wait_recv()
        fs.append(go(remote(nv.at[2, part], nv.at[3, part], fsend.at[c], frecv.at[c], sib)))

    todo = list(range(chunks))
    for d in range(1, lines):
        zq[d - 1].wait_recv()
        slot = f ^ (2 * d)
        xq.append(go(remote(wqv.at[slot], wqv.at[slot], xqs.at[d], xqr.at[d], side)))
        if len(todo) > 1:
            forward_far(todo.pop(0))
    for d in range(1, lines):
        zo[d - 1].wait_recv()
        slot = f ^ (2 * d)
        xo.append(go(remote(wov.at[slot], wov.at[slot], xos.at[d], xor.at[d], side)))
    fc = []
    for d in PRE:
        if d < lines:
            fc.append(go(remote(fcv, fc_out.at[f], zfs.at[d], zfr.at[d], alongs[d - 1])))
    while todo:
        forward_far(todo.pop(0))
    up = go(remote(cot, up_out, ups.at[0], upr.at[0], far))
    for c in cs:
        c.wait_recv()
    for d in range(lines):
        xq[d].wait_recv()
    start = pl.multiple_of(t * head_width, head_width)
    adds = (qvb[0:1, pl.ds(start, head_width)], None, qvb[1:2, pl.ds(start, head_width)])

    def project(j, _):
        b = t ^ j
        for k in range(3):
            value = nn(nv[j], wqv[:, k].reshape(width, head_width))
            if adds[k] is not None:
                value = value + adds[k]
            value = value.astype(BF)
            qv[j, :, k * head_width : (k + 1) * head_width] = value
            if k == 0:
                qT[b] = (value * jnp.asarray(HD**-0.5, BF)).T
            elif k == 1:
                kn[b] = value
                kT[b] = value.T
            else:
                vT[b] = value.T
        return 0

    lax.fori_loop(0, 2, project, 0)
    for c in fs:
        c.wait_recv()
    lax.fori_loop(2, 4, project, 0)
    for d in range(lines):
        xo[d].wait_recv()
    fc.append(go(remote(fcv, fc_out.at[f], zfs.at[0], zfr.at[0], side)))
    if per % 128 == 0:
        def place(s, _):
            otv[:, pl.ds(pl.multiple_of(s * per, per), per)] = wov[s]
            return 0

        lax.fori_loop(0, shards, place, 0)
    else:
        for s in range(shards):
            otv[:, s * per : (s + 1) * per] = wov[s]
    outs = [
        pltpu.make_async_copy(src, dst, osem.at[n])
        for n, (src, dst) in enumerate([(nv, n_out), (qv, qkv_out), (wqv, wq_out), (otv, wo_out.at[t])])
    ]
    for k in range(3):
        wqt[k * head_width : (k + 1) * head_width, :] = wqv[:, k].reshape(width, head_width).T
    outs += [
        pltpu.make_async_copy(src, dst, osem.at[10 + n])
        for n, (src, dst) in enumerate([(wqt, wqt_out), (qT, qT_out), (kT, kT_out)])
    ]
    for c in outs:
        c.start()
    shared = [
        go(remote(otv, wo_out.at[t], wos.at[1], wor.at[1], sib)),
        go(remote(otv, wo_out.at[t], wos.at[2], wor.at[2], far)),
    ]
    rowk = lax.broadcasted_iota(jnp.int32, (rows, rows), 0)
    colq = lax.broadcasted_iota(jnp.int32, (rows, rows), 1)
    half = lax.broadcasted_iota(jnp.int32, (2 * HD, rows), 0) < HD
    def mixed(i):
        return remote(
            att.at[i], mix_out.at[t], ats.at[i], atr.at[t ^ i], {"fsdp": f, "tensor": t * 0 + i}
        )

    pre = [d for d in PRE if d < lines]
    direct = [d for d in range(1, lines) if d not in pre]
    later = [remote(fcv, fc_out.at[f], zds.at[d], zdr.at[d], alongs[d - 1]) for d in direct]
    passed = []
    for d in pre:
        shard = fc_out.at[f ^ (2 * d)]
        passed.append(remote(shard, shard, xfs.at[d], xfr.at[d], side))
    more = later + passed
    sends += more

    def attend(i, _):
        at = starts[0, i] - i * rows

        @pl.when(i == 2)
        def _():
            for c in later:
                c.start()

        @pl.when(i == 3)
        def _():
            for n in range(len(pre)):
                fc[n].wait_recv()
                passed[n].start()

        def pair(p, _):
            col = pl.multiple_of(p * 2 * HD, 2 * HD)
            qp = qT[i, pl.ds(col, 2 * HD), :]
            zero = jnp.zeros_like(qp)
            masked = (jnp.where(half, qp, zero), jnp.where(half, zero, qp))

            def block(m, carry, diag):
                kb = kn[m, :, pl.ds(col, 2 * HD)]
                vb = vT[m, pl.ds(col, 2 * HD), :]
                new = []
                for hh in range(2):
                    top, total, acc = carry[hh]
                    s = nn(kb, masked[hh])
                    if diag:
                        inside = (rowk >= at) & (rowk < at + PIC) & (colq >= at) & (colq < at + PIC)
                        s = jnp.where((rowk <= colq) | inside, s, NEG)
                    peak = jnp.maximum(top, jnp.max(s, axis=0, keepdims=True))
                    shrink = jnp.exp(top - peak)
                    e = jnp.exp(s - peak)
                    total = total * shrink + jnp.sum(e, axis=0, keepdims=True)
                    acc = acc * shrink + nn(vb[hh * HD : (hh + 1) * HD], e.astype(BF))
                    new.append((peak, total, acc))
                return tuple(new)

            blank = (
                jnp.full((1, rows), NEG, F32), jnp.zeros((1, rows), F32), jnp.zeros((HD, rows), F32)
            )
            c = block(i, (blank, blank), True)
            c = lax.fori_loop(0, i, lambda m, c: block(m, c, False), c)
            found = []
            for hh in range(2):
                top, total, acc = c[hh]
                found.append(acc * (1.0 / total))
                lsev[t ^ i, pl.ds(p * 2 + hh, 1), :] = top + jnp.log(total)
            att[i, :, pl.ds(col, 2 * HD)] = jnp.concatenate(found, axis=0).astype(BF).T
            return 0

        lax.fori_loop(0, head_width // (2 * HD), pair, 0)

        @pl.when(t != i)
        def _():
            mixed(i).start()

        return 0

    lax.fori_loop(0, 4, attend, 0)
    outs += [pltpu.make_async_copy(att.at[t ^ j], att_out.at[j], osem.at[4 + j]) for j in range(4)]
    outs.append(pltpu.make_async_copy(lsev, lse_out, osem.at[8]))
    outs.append(pltpu.make_async_copy(att.at[t], mix_out.at[t], osem.at[9]))
    for c in outs[7:]:
        c.start()
    shared[1].wait_recv()
    shared.append(go(remote(wo_out.at[t ^ 2], wo_out.at[t ^ 2], wos.at[3], wor.at[3], sib)))
    shared[0].wait_recv()
    shared[2].wait_recv()
    for j in range(1, 4):
        remote(att.at[0], mix_out.at[t ^ j], ats.at[0], atr.at[j], mates[j]).wait_recv()
    for i in range(4):

        @pl.when(t != i)
        def _(i=i):
            mixed(i).wait_send()

    for c in fc[len(pre) :] + [up] + more:
        c.wait_recv()
    for c in sends:
        c.wait_send()
    for c in local + outs:
        c.wait()


def head(shards, tokens, wq, wo, w1, w2, gain, bias, qv_bias, starts, cot):
    rows, width = tokens.shape
    head_width, per = wo.shape
    hid = w1.shape[1]
    lines = shards // 2
    chunks = 4
    heads = head_width // HD
    dma = pltpu.SemaphoreType.DMA
    vm = pl.BlockSpec(memory_space=VM)
    hbm = pl.BlockSpec(memory_space=HB)
    V = pltpu.VMEM
    full = (4, rows, width)
    three = (4, rows, 3 * head_width)
    return pl.pallas_call(
        functools.partial(head_kernel, shards, chunks),
        name="head",
        out_shape=[
            jax.ShapeDtypeStruct(full, BF),
            jax.ShapeDtypeStruct(three, BF),
            jax.ShapeDtypeStruct((shards, 3, per, head_width), BF),
            jax.ShapeDtypeStruct((4, head_width, width), BF),
            jax.ShapeDtypeStruct((shards, per, 2 * hid), BF),
            jax.ShapeDtypeStruct((rows, width), BF),
            jax.ShapeDtypeStruct((4, rows, head_width), BF),
            jax.ShapeDtypeStruct((4, heads, rows), F32),
            jax.ShapeDtypeStruct((4, rows, head_width), BF),
            jax.ShapeDtypeStruct((3 * head_width, width), BF),
            jax.ShapeDtypeStruct((4, head_width, rows), BF),
            jax.ShapeDtypeStruct((4, head_width, rows), BF),
        ],
        in_specs=[vm] * 8 + [pl.BlockSpec(memory_space=SM), hbm],
        out_specs=[hbm] * 12,
        scratch_shapes=[
            V(full, BF), V((shards, 3, per, head_width), BF), V((shards, head_width, per), BF),
            V((head_width, width), BF), V((per, 2 * hid), BF), V(three, BF),
            V((4, rows, head_width), BF), V((4, head_width, rows), BF), V((4, head_width, rows), BF),
            V((4, rows, head_width), BF), V((4, heads, rows), F32), V((3 * head_width, width), BF),
            V((4, head_width, rows), BF),
        ]
        + [dma((chunks,))] * 6
        + [dma((lines,))] * 8
        + [dma((max(lines, 4),))] * 6
        + [dma((1,))] * 2
        + [dma((4,))] * 4
        + [dma((1,)), dma((13,))],
        compiler_params=pltpu.CompilerParams(
            collective_id=0, has_side_effects=True, vmem_limit_bytes=56 << 20
        ),
        cost_estimate=pl.CostEstimate(flops=40 << 30, bytes_accessed=90 << 20, transcendentals=0),
    )(tokens, wq, wo, w1, w2, gain, bias, qv_bias, starts, cot)


def middle_kernel(
    shards, chunks,
    mix_in, wo_in, tok_in, cot, up_far, fc_in, gain, bias, out_bias, fc_bias,
    hid_out, ghid_out, back_out, do_out, g1_out, g2_out, part_far, vec,
    mix, wo, tok, wfc, wt, wot, upv, twov, actv, pgv, backv,
    s1, r1, a1, q1, near, hv, rx, sz, dov,
    dos, dor, c2s, c2r, y2s, y2r, f2s, f2r,
    s3s, s3r, y3s, y3r,
    s5s, s5r, ups, upr, lsem, xs, xr, osem, gxs, gxr, isem,
):
    first_in = [
        pltpu.make_async_copy(src, dst, isem.at[n])
        for n, (src, dst) in enumerate([(mix_in, mix), (wo_in, wo), (tok_in, tok)])
    ]
    for c in first_in:
        c.start()
    f = lax.axis_index("fsdp")
    t = lax.axis_index("tensor")
    rows, width = tok.shape
    per = fc_in.shape[1]
    hid = fc_in.shape[2] // 2
    pre = [d for d in PRE if d < shards // 2]
    step = rows // chunks
    lines = shards // 2
    far = {"fsdp": f, "tensor": t ^ 2}
    sib = {"fsdp": f, "tensor": t ^ 1}
    side = {"fsdp": f ^ 1, "tensor": t}
    direct = [d for d in range(1, lines) if d not in pre]
    mates = [{"fsdp": f, "tensor": t ^ j} for j in range(4)]
    greet(mates[1:] + [side])
    sends = []

    def go(copy):
        copy.start()
        sends.append(copy)
        return copy

    def part(c):
        return pl.ds(c * step, step)

    halves = (pl.ds(0, hid), pl.ds(hid, hid))
    late = [2 * d + 1 for d in direct]
    early = [e for e in range(shards) if e not in late]
    local = [
        pltpu.make_async_copy(fc_in.at[f ^ e], wfc.at[f ^ e], lsem.at[n])
        for n, e in enumerate(early)
    ]
    local.append(pltpu.make_async_copy(cot, upv.at[0], lsem.at[shards]))
    local.append(pltpu.make_async_copy(up_far, upv.at[2], lsem.at[shards + 1]))
    for c in local:
        c.start()
    xf = []
    for d in direct:
        block = f ^ (2 * d)
        xf.append(go(remote(fc_in.at[block], wfc.at[block], xs.at[d], xr.at[d], side)))
    up_copies = [
        go(remote(cot, upv.at[1], ups.at[0], upr.at[0], sib)),
        go(remote(up_far, upv.at[3], ups.at[1], upr.at[1], sib)),
    ]
    vec[...] = jnp.zeros_like(vec)
    for c in first_in:
        c.wait()
    ag_far, ag_sib = [], []
    for c in range(chunks):
        hidden = tok[part(c), :].astype(F32) + out_bias[...]
        for s in range(4):
            hidden = hidden + nn(mix[s, part(c), :], wo[s])
        hv[part(c), :] = hidden
        unit, _ = normalize(hidden)
        twov[0, part(c), :] = (unit * gain[...] + bias[...]).astype(BF)
        ag_far.append(go(remote(twov.at[0, part(c)], twov.at[2, part(c)], y2s.at[c], y2r.at[c], far)))
        ag_sib.append(go(remote(twov.at[0, part(c)], twov.at[1, part(c)], c2s.at[c], c2r.at[c], sib)))
    for s in range(4):
        wot[s] = wo[s].T
    outs = []
    for c in local:
        c.wait()

    def flip(slot):
        if per % 128 == 0:
            wt[:, pl.ds(pl.multiple_of(slot * per, per), per)] = wfc[slot].T

    def flip_early(e, _):
        flip(f ^ e)
        return 0

    if early == list(range(len(early))):
        lax.fori_loop(0, len(early), flip_early, 0)
    else:
        for e in early:
            flip(f ^ e)
    for c in xf:
        c.wait_recv()
    for e in late:
        flip(f ^ e)
    if per % 128:
        wt[...] = wfc[...].reshape(width, 2 * hid).T
    for c in up_copies:
        c.wait_recv()
    for c in ag_sib:
        c.wait_recv()
    start = pl.multiple_of(t * hid, hid)
    tile = hid // 2

    def feed(j, at):
        block = pl.ds(pl.multiple_of(at * step, step), step)
        two = twov[j, block, :]
        up = upv[j, block, :]
        total = None
        for n in range(2):
            cols = pl.ds(n * tile, tile)
            x = nn(two, wfc[:, :, cols].reshape(width, tile))
            x = x + fc_bias[:, pl.ds(pl.multiple_of(start + n * tile, tile), tile)]
            hg = nn(up, wfc[:, :, pl.ds(hid + n * tile, tile)].reshape(width, tile))
            sq = x * x
            th = jnp.tanh(GELU_SCALE * (x + GELU_CUBIC * (sq * x)))
            half = 0.5 * (1.0 + th)
            actv[j, block, cols] = (x * half).astype(BF)
            slope = half + (0.5 * GELU_SCALE) * x * (1.0 - th * th) * (1.0 + (3.0 * GELU_CUBIC) * sq)
            pg = (hg * slope).astype(BF)
            pgv[j, block, cols] = pg
            vec[0:1, cols] += jnp.sum(pg.astype(F32), axis=0, keepdims=True)
            term = nn(pg, wt[cols, :])
            total = term if total is None else total + term
        return total

    def copies(c):
        block = pl.ds(pl.multiple_of(c * step, step), step)
        return (
            remote(twov.at[0, block], twov.at[2, block], y2s.at[c], y2r.at[c], far),
            remote(twov.at[2, block], twov.at[3, block], f2s.at[c], f2r.at[c], sib),
            remote(a1.at[block], q1.at[block], y3s.at[c], y3r.at[c], far),
        )

    def core_copy(k, c):
        block = pl.ds(pl.multiple_of(c * step, step), step)
        return remote(s1.at[2 + k, block], r1.at[2 + k, block], s3s.at[k, c], s3r.at[k, c], sib)

    def rows_of(c, _):
        block = pl.ds(pl.multiple_of(c * step, step), step)
        got, fwd, send2 = copies(c)

        def one(i, _):
            total = feed(i ^ 1, c)

            @pl.when(i == 0)
            def _():
                s1[3, block, :] = total.astype(BF)
                core_copy(1, c).start()
                got.wait_recv()
                fwd.start()

            @pl.when(i == 1)
            def _():
                near[block, :] = total
                fwd.wait_recv()

            @pl.when(i == 2)
            def _():
                s1[2, block, :] = total.astype(BF)
                core_copy(0, c).start()

            @pl.when(i == 3)
            def _():
                core_copy(0, c).wait_recv()
                a1[block, :] = (total + r1[2, block, :].astype(F32)).astype(BF)
                send2.start()

            return 0

        lax.fori_loop(0, 4, one, 0)
        return 0

    lax.fori_loop(0, chunks, rows_of, 0)

    span = 256
    ratio = span // (2 * per)
    groups = width // span
    z = f // 2
    x = lax.rem(f, 2)

    def x_copy(d):
        return remote(wfc.at[(z ^ d) * 2 + (1 - x), :, halves[0]], rx.at[d], gxs.at[d], gxr.at[d], side)

    def weight_grad(left, right, h, send):
        def group_of(i, _):
            near_group = groups - 1 - i
            group = near_group ^ (z // ratio)
            cols = pl.ds(pl.multiple_of(group * span, span), span)
            acc = None
            for j in range(4):
                term = nn(left[j, :, cols].T, right[j])
                acc = term if acc is None else acc + term
            count = span // per
            slots = pl.ds(group * count, count)
            wfc[slots, :, halves[h]] = acc.astype(BF).reshape(count, per, hid)
            if send:

                def launch(e, _):
                    x_copy(near_group * ratio + e).start()
                    return 0

                lax.fori_loop(0, ratio, launch, 0)
            return 0

        lax.fori_loop(0, groups, group_of, 0)

    def give_part(k):
        for c in range(chunks):
            core_copy(k, c).wait_send()

        def give(c, _):
            block = pl.ds(pl.multiple_of(c * step, step), step)
            s1[k, block, :] = nn(actv[3 - 2 * k, block, :], wt[hid:, :]).astype(BF)
            return 0

        lax.fori_loop(0, chunks, give, 0)
        return go(remote(s1.at[k], r1.at[k], s5s.at[k], s5r.at[k], sib))

    def keep_part(k):
        def keep(c, _):
            block = pl.ds(pl.multiple_of(c * step, step), step)
            mine = nn(actv[2 - 2 * k, block, :], wt[hid:, :])
            if k:
                hv[block, :] += mine
            else:
                s1[2, block, :] = mine.astype(BF)
            return 0

        lax.fori_loop(0, chunks, keep, 0)

    def join_part(k, given):
        given.wait_recv()
        if k:
            hv[...] += r1[k].astype(F32)
            outs.append(pltpu.make_async_copy(hv, hid_out, osem.at[0]))
        else:
            s1[2] = (s1[2].astype(F32) + r1[k].astype(F32)).astype(BF)
            outs.append(pltpu.make_async_copy(s1.at[2], part_far, osem.at[2]))
        outs[-1].start()

    weight_grad(upv, actv, 0, True)
    given_do = []
    for c in range(chunks):
        _, _, send2 = copies(c)
        core_copy(1, c).wait_recv()
        send2.wait_recv()
        gn = near[part(c), :] + r1[3, part(c), :].astype(F32) + q1[part(c), :].astype(F32)
        unit, inv = normalize(hv[part(c), :])
        back, g_sum, b_sum = normalize_back(gn, unit, inv, gain[...])
        cots = upv[0, part(c), :].astype(F32)
        ghid = cots + back
        near[part(c), :] = ghid
        low = ghid.astype(BF)
        backv[part(c), :] = low
        for j in (2, 3, 1, 0):
            dov[j, part(c), :] = nn(low, wot[t ^ j]).astype(BF)
            if j > 0:
                given_do.append(
                    go(remote(dov.at[j, part(c)], do_out.at[j, part(c)], dos.at[j, c], dor.at[j, c], mates[j]))
                )
        vec[1:2, :] += g_sum[None]
        vec[2:3, :] += b_sum[None]
        vec[3:4, :] += jnp.sum(ghid, axis=0, keepdims=True)
        vec[4:5, :] += jnp.sum(cots, axis=0, keepdims=True)
        if c == 0:
            given = [give_part(0)]
            keep_part(0)
            given.append(give_part(1))
            join_part(0, given[0])
    keep_part(1)
    join_part(1, given[1])
    outs.append(pltpu.make_async_copy(near, ghid_out, osem.at[1]))
    outs[-1].start()

    weight_grad(twov, pgv, 1, False)
    outs.append(pltpu.make_async_copy(wfc.at[:, :, halves[1]], g1_out, osem.at[5]))
    outs[-1].start()
    outs.append(pltpu.make_async_copy(dov.at[0], do_out.at[0], osem.at[7]))
    outs[-1].start()
    outs.append(pltpu.make_async_copy(backv, back_out, osem.at[4]))
    outs[-1].start()

    def side_sum(i, _):
        d = lines - 1 - i
        x_copy(d).wait_recv()
        sz[d] = (wfc[(z ^ d) * 2 + x, :, halves[0]].astype(F32) + rx[d].astype(F32)).astype(BF)
        return 0

    lax.fori_loop(0, lines, side_sum, 0)
    outs.append(pltpu.make_async_copy(sz, g2_out, osem.at[6]))
    outs[-1].start()
    for c in given_do:
        c.wait_recv()
    for c in sends:
        c.wait_send()
    for c in range(chunks):
        _, fwd, send2 = copies(c)
        fwd.wait_send()
        send2.wait_send()

    def drain(d, _):
        x_copy(d).wait_send()
        return 0

    lax.fori_loop(0, lines, drain, 0)
    for c in outs:
        c.wait()


def middle(shards, mix, wo, tok, cot, up_far, fc_in, gain, bias, out_bias, fc_bias):
    rows, width = tok.shape
    per, hid2 = fc_in.shape[1:]
    hid = hid2 // 2
    head_width = wo.shape[1]
    lines = shards // 2
    chunks = 2
    step = rows // chunks
    dma = pltpu.SemaphoreType.DMA
    vm = pl.BlockSpec(memory_space=VM)
    hbm = pl.BlockSpec(memory_space=HB)
    full = (4, rows, width)
    one = (rows, width)
    block = (lines, per, hid)
    V = pltpu.VMEM
    sems = [
        (4, chunks), (4, chunks), (chunks,), (chunks,),
        (chunks,), (chunks,), (chunks,), (chunks,),
        (2, chunks), (2, chunks), (chunks,), (chunks,),
        (2,), (2,), (2,), (2,), (shards + 2,), (lines,), (lines,), (8,), (lines,), (lines,), (3,),
    ]
    return pl.pallas_call(
        functools.partial(middle_kernel, shards, chunks),
        name="middle",
        out_shape=[
            jax.ShapeDtypeStruct(one, F32),
            jax.ShapeDtypeStruct(one, F32),
            jax.ShapeDtypeStruct(one, BF),
            jax.ShapeDtypeStruct((4, rows, head_width), BF),
            jax.ShapeDtypeStruct((shards, per, hid), BF),
            jax.ShapeDtypeStruct(block, BF),
            jax.ShapeDtypeStruct(one, BF),
            jax.ShapeDtypeStruct((8, width), F32),
        ],
        in_specs=[hbm] * 6 + [vm] * 4,
        out_specs=[hbm] * 7 + [vm],
        scratch_shapes=[
            V(mix.shape, BF), V(wo.shape, BF), V(one, BF), V((shards, per, 2 * hid), BF), V((2 * hid, width), BF), V((4, width, head_width), BF),
            V(full, BF), V(full, BF), V((4, rows, hid), BF), V((4, rows, hid), BF), V(one, BF),
            V(full, BF), V(full, BF), V(one, BF), V(one, BF),
            V(one, F32), V(one, F32), V(block, BF), V(block, BF), V((4, rows, head_width), BF),
        ]
        + [dma(s) for s in sems],
        compiler_params=pltpu.CompilerParams(
            collective_id=1, has_side_effects=True, vmem_limit_bytes=60 << 20
        ),
        cost_estimate=pl.CostEstimate(flops=60 << 30, bytes_accessed=200 << 20, transcendentals=0),
    )(mix, wo, tok, cot, up_far, fc_in, gain, bias, out_bias, fc_bias)


def tail_kernel(
    shards, chunks,
    lse, starts, vec, gain, bias, fc2_bias,
    qs_in, dos_in, ats_in, weights_in, wt_in, qT_in, kT_in, one_in, back_in, tok_in, ghid_in, hid_in, pfar_in, g1_in, g2_in,
    out_out, tok_out, wq_out, wo_out, w1_out, w2_out, qv_out, fcb_out, g_a, g_b, g_c, g_d, g_e, g_f,
    qs, dos, ats, weights, qT, kT, doT, dk, dv, dl, dqkv,
    onev, backv, tokv, ghidv, hidv, pfarv, wt,
    s1, r1, a1, q1, near, gq, go_, rx, sz, rz, rxo, szo, rzo, rx1, sz1, rz1, rz2, sum1, sum2, wqs, wos,
    smat, lv, rv1, sv, rv2, gv,
    lsem, s1s, s1r, y1s, y1r, xs, xr, zs, zr, v1s, v1r, v2s, v2r, v3s, v3r, pfs, pfr, z2s, z2r, osem, isem,
):
    f = lax.axis_index("fsdp")
    t = lax.axis_index("tensor")
    _, rows, width = onev.shape
    head_width = ats.shape[2]
    first_in = [
        pltpu.make_async_copy(src, dst, isem.at[n])
        for n, (src, dst) in enumerate(
            [
                (dos_in, dos), (ats_in, ats), (qT_in, qT), (kT_in, kT), (qs_in, qs),
                (weights_in, weights), (wt_in, wt),
            ]
        )
    ]
    for c in first_in:
        c.start()
    per = width // shards
    lines = shards // 2
    step = rows // chunks
    z = f // 2
    x = lax.rem(f, 2)
    far = {"fsdp": f, "tensor": t ^ 2}
    sib = {"fsdp": f, "tensor": t ^ 1}
    side = {"fsdp": f ^ 1, "tensor": t}
    mates = [{"fsdp": f, "tensor": t ^ j} for j in range(1, 4)]
    others = [{"fsdp": f ^ e, "tensor": t} for e in range(1, shards)]
    greet(mates + others)
    sends = []

    def go(copy):
        copy.start()
        sends.append(copy)
        return copy

    def part(c):
        return pl.ds(c * step, step)

    def row(block):
        return pl.ds(pl.multiple_of(block * per, per), per)

    pairs = head_width // (2 * HD)
    sums = 2 + pairs
    sources = [lambda b: g1_in.at[b], lambda b: go_.at[row(b)]]
    lands = [(rx1, sz1, rz1), (rxo, szo, rzo)]
    for p in range(pairs):
        sources.append(lambda b, p=p: gq.at[p, row(b)])
        lands.append((rx.at[p], sz.at[p], rz.at[p]))

    def x_copy(k, d):
        return remote(
            sources[k]((z ^ d) * 2 + (1 - x)), lands[k][0].at[d], xs.at[k, d], xr.at[k, d], side
        )

    def z_copy(k, d):
        return remote(
            lands[k][1].at[d], lands[k][2].at[d], zs.at[k, d], zr.at[k, d],
            {"fsdp": f ^ (2 * d), "tensor": t},
        )

    def pass_on(k, d, own):
        x_copy(k, d).wait_recv()
        lands[k][1][d] = (own(d).astype(F32) + lands[k][0][d].astype(F32)).astype(BF)
        z_copy(k, d).start()

    def keep_of(d):
        return (z ^ d) * 2 + x

    def launch(i, _):
        x_copy(0, lines - 1 - i).start()
        return 0

    lax.fori_loop(0, lines, launch, 0)
    def z2_copy(d):
        return remote(
            g2_in.at[d], rz2.at[d], z2s.at[d], z2r.at[d], {"fsdp": f ^ (2 * d), "tensor": t}
        )

    def launch2(i, _):
        z2_copy(lines - 1 - i).start()
        return 0

    lax.fori_loop(0, lines - 1, launch2, 0)
    back_far = go(remote(back_in, backv.at[2], pfs.at[1], pfr.at[1], far))
    back_sib = go(remote(back_in, backv.at[1], pfs.at[2], pfr.at[2], sib))
    local = [
        pltpu.make_async_copy(src, dst, lsem.at[n])
        for n, (src, dst) in enumerate(
            [
                (back_in, backv.at[0]), (one_in, onev), (tok_in, tokv), (ghid_in, ghidv),
                (hid_in, hidv), (g2_in.at[0], rz2.at[0]),
            ]
        )
    ]
    for c in local:
        c.start()
    keeps = []

    def own_block(d, _):
        pltpu.make_async_copy(g1_in.at[keep_of(d)], sz1.at[d], lsem.at[8 + d]).start()
        return 0

    lax.fori_loop(0, lines, own_block, 0)

    def pass_fc1(d):
        pltpu.make_async_copy(g1_in.at[keep_of(d)], sz1.at[d], lsem.at[8 + d]).wait()
        pass_on(0, d, lambda d: sz1[d])

    first_in[0].wait()
    first_in[1].wait()
    for j in range(4):
        b = t ^ j
        do = dos[j]
        doT[b] = do.T
        prod = (do.astype(F32) * ats[j].astype(F32)).T
        for h in range(head_width // HD):
            dl[b, h : h + 1, :] = jnp.sum(prod[h * HD : (h + 1) * HD], axis=0, keepdims=True)
    dk[...] = jnp.zeros_like(dk)
    dv[...] = jnp.zeros_like(dv)
    for c in first_in[2:5]:
        c.wait()

    span = 256
    ratio = span // (2 * per)
    groups = width // span

    smat[...] = jnp.zeros_like(smat)

    def weight_grad(k, left, rights, target, p=None):
        def group_of(i, _):
            near_group = groups - 1 - i
            group = near_group ^ (z // ratio)
            cols = pl.ds(pl.multiple_of(group * span, span), span)
            turned = [left[j, :, cols].T for j in range(4)]
            count = span // per
            for n, (at, right) in enumerate(rights):
                acc = None
                for j in range(4):
                    term = nn(turned[j], right(j))
                    acc = term if acc is None else acc + term
                target[cols, at : at + acc.shape[1]] = acc.astype(BF)
                if p is not None:
                    block = weights[pl.ds(group * count, count), n, :, p * 2 * HD : (p + 1) * 2 * HD]
                    smat[cols, :] += acc * block.reshape(span, 2 * HD).astype(F32)

            def send(e, _):
                x_copy(k, near_group * ratio + e).start()
                return 0

            lax.fori_loop(0, ratio, send, 0)
            return 0

        lax.fori_loop(0, groups, group_of, 0)

    rowk = lax.broadcasted_iota(jnp.int32, (rows, rows), 0)
    colq = lax.broadcasted_iota(jnp.int32, (rows, rows), 1)
    hrow = lax.broadcasted_iota(jnp.int32, (2 * HD, rows), 0) < HD
    hcol = lax.broadcasted_iota(jnp.int32, (rows, 2 * HD), 1) < HD

    def two(v, m):
        zero = jnp.zeros_like(v)
        return (jnp.where(m, v, zero), jnp.where(m, zero, v))

    def attend(p, i):
        at = starts[0, i] - i * rows
        jj = t ^ i

        if True:
            col = pl.multiple_of(p * 2 * HD, 2 * HD)
            kcol = pl.multiple_of(head_width + p * 2 * HD, 2 * HD)
            vcol = pl.multiple_of(2 * head_width + p * 2 * HD, 2 * HD)
            qTz = two(qT[i, pl.ds(col, 2 * HD), :], hrow)
            doTz = two(doT[i, pl.ds(col, 2 * HD), :], hrow)
            qz = two(qs[jj, :, pl.ds(col, 2 * HD)], hcol)
            doz = two(dos[jj, :, pl.ds(col, 2 * HD)], hcol)
            ls = [lse[jj, pl.ds(p * 2 + hh, 1), :] for hh in range(2)]
            dlt = [dl[i, pl.ds(p * 2 + hh, 1), :] for hh in range(2)]

            def block(m, carry, diag):
                kb = qs[t ^ m, :, pl.ds(kcol, 2 * HD)]
                vb = qs[t ^ m, :, pl.ds(vcol, 2 * HD)]
                ktb = kT[m, pl.ds(col, 2 * HD), :]
                dvs, dks, new = 0.0, 0.0, []
                for hh in range(2):
                    s = nn(kb, qTz[hh])
                    if diag:
                        inside = (rowk >= at) & (rowk < at + PIC) & (colq >= at) & (colq < at + PIC)
                        s = jnp.where((rowk <= colq) | inside, s, NEG)
                    pr = jnp.exp(s - ls[hh])
                    dp = nn(vb, doTz[hh])
                    ds = (pr * (dp - dlt[hh])).astype(BF)
                    dvs = dvs + nn(pr.astype(BF), doz[hh])
                    dks = dks + nn(ds, qz[hh])
                    new.append(carry[hh] + nn(ktb[hh * HD : (hh + 1) * HD], ds))
                dv[m, :, pl.ds(col, 2 * HD)] += dvs
                dk[m, :, pl.ds(col, 2 * HD)] += dks
                return tuple(new)

            c = tuple(jnp.zeros((HD, rows), F32) for _ in range(2))
            c = block(i, c, True)
            c = lax.fori_loop(0, i, lambda m, c: block(m, c, False), c)
            dq = (jnp.concatenate(c, axis=0) * (HD**-0.5)).astype(BF)
            dqkv[jj, :, pl.ds(col, 2 * HD)] = dq.T

    back_fwd = remote(backv.at[2], backv.at[3], pfs.at[3], pfr.at[3], sib)
    pf = remote(pfar_in, pfarv, pfs.at[0], pfr.at[0], far)
    sends += [back_fwd, pf]

    def columns(p):
        return [
            (k * 2 * HD, lambda j, k=k: dqkv[j, :, k * head_width + p * 2 * HD : k * head_width + (p + 1) * 2 * HD])
            for k in range(3)
        ]

    def settle(p):
        kcol = pl.ds(pl.multiple_of(head_width + p * 2 * HD, 2 * HD), 2 * HD)
        vcol = pl.ds(pl.multiple_of(2 * head_width + p * 2 * HD, 2 * HD), 2 * HD)
        col = pl.ds(pl.multiple_of(p * 2 * HD, 2 * HD), 2 * HD)
        for j in range(4):
            dqkv[j, :, kcol] = (dk[t ^ j, :, col] * (HD**-0.5)).astype(BF)
            dqkv[j, :, vcol] = dv[t ^ j, :, col].astype(BF)

    def pass_pair(p):
        def one(i, _):
            pass_on(2 + p, lines - 1 - i, lambda d: gq[p, row(keep_of(d)), :])
            return 0

        lax.fori_loop(0, lines - 1, one, 0)

    def heads_of(p, _):
        def step_of(i, _):
            attend(p, i)

            @pl.when((p == 0) & (i == 1))
            def _():
                pass_fc1(lines - 1)
                if lines > 2:
                    pass_fc1(lines - 2)

            @pl.when((p == 0) & (i == 2))
            def _():
                if lines > 3:

                    def pass_more(n, _):
                        pass_fc1(lines - 3 - n)
                        return 0

                    lax.fori_loop(0, lines - 3, pass_more, 0)

            @pl.when((p == 1) & (i == 2))
            def _():
                pass_pair(0)

            return 0

        lax.fori_loop(0, 4, step_of, 0)
        settle(p)

        @pl.when(p == 0)
        def _():
            back_far.wait_recv()
            back_fwd.start()
            pf.start()
            local[1].wait()
            first_in[5].wait()
            weight_grad(2, onev, columns(0), gq.at[0], 0)

        return 0

    lax.fori_loop(0, pairs, heads_of, 0)
    for c in local[2:]:
        c.wait()

    def norm_grad(j, c):
        return nn(dqkv[j, part(c), :], wt[...])

    first, second, third = [], [], []
    def far_chunk(c):
        s1[0, part(c), :] = norm_grad(3, c).astype(BF)
        first.append(go(remote(s1.at[0, part(c)], r1.at[0, part(c)], s1s.at[0, c], s1r.at[0, c], sib)))
        mine = norm_grad(2, c)
        first[c].wait_recv()
        a1[part(c), :] = (mine + r1[0, part(c), :].astype(F32)).astype(BF)
        second.append(go(remote(a1.at[part(c)], q1.at[part(c)], y1s.at[c], y1r.at[c], far)))

    first_in[6].wait()
    far_chunk(0)
    local[0].wait()
    back_sib.wait_recv()
    back_fwd.wait_recv()
    weight_grad(1, backv, [(0, lambda j: ats[j])], go_)
    for p in range(1, pairs):
        weight_grad(2 + p, onev, columns(p), gq.at[p], p)
    column_sum = jnp.sum(dqkv[0].astype(F32), axis=0, keepdims=True)
    for j in range(1, 4):
        column_sum = column_sum + jnp.sum(dqkv[j].astype(F32), axis=0, keepdims=True)
    high = column_sum.astype(BF)
    low = (column_sum - high.astype(F32)).astype(BF)
    bias_sum = nn(high, wt[...]) + nn(low, wt[...])
    product = jnp.sum(smat[...].T, axis=0, keepdims=True)
    gain_sum = (product - bias[...] * bias_sum) / gain[...]

    slot = lax.broadcasted_iota(jnp.int32, (4, head_width), 0)
    lv[...] = jnp.zeros_like(lv)
    qsum = column_sum[:, :head_width]
    vsum = column_sum[:, 2 * head_width :]
    for u in range(4):
        cols = pl.ds(u * head_width, head_width)
        lv[u, 0:4, :] = jnp.where(slot == t, vec[0:1, cols], 0.0)
        here = (t == u).astype(F32)
        lv[u, 4:5, :] = qsum * here
        lv[u, 5:6, :] = vsum * here
        lv[u, 6:7, :] = vec[3:4, cols]
        lv[u, 7:8, :] = vec[4:5, cols]
        lv[u, 8:9, :] = vec[1:2, cols]
        lv[u, 9:10, :] = vec[2:3, cols]
        lv[u, 10:11, :] = gain_sum[:, u * head_width : (u + 1) * head_width]
        lv[u, 11:12, :] = bias_sum[:, u * head_width : (u + 1) * head_width]
    level1 = [
        go(remote(lv.at[t ^ j], rv1.at[j], v1s.at[j], v1r.at[j], mates[j - 1])) for j in range(1, 4)
    ]
    for c in range(1, chunks):
        far_chunk(c)

    def pass_out(i, _):
        pass_on(1, lines - 1 - i, lambda d: go_[row(keep_of(d)), :])
        return 0

    lax.fori_loop(0, lines - 1, pass_out, 0)
    for c in range(chunks):
        s1[1, part(c), :] = norm_grad(1, c).astype(BF)
        third.append(go(remote(s1.at[1, part(c)], r1.at[1, part(c)], s1s.at[1, c], s1r.at[1, c], sib)))
    for c in range(chunks):
        near[part(c), :] = norm_grad(0, c)

    def pass_qkv(i, _):
        for p in range(1, pairs):
            pass_on(2 + p, lines - 1 - i, lambda d, p=p: gq[p, row(keep_of(d)), :])
        return 0

    lax.fori_loop(0, (lines - 1) // 2, pass_qkv, 0)
    pf.wait_recv()
    hidv[...] = hidv[...] + pfarv[...].astype(F32) + fc2_bias[...]
    outs = [pltpu.make_async_copy(hidv, out_out, osem.at[0])]
    outs[0].start()
    for c in level1:
        c.wait_recv()
    sv[...] = lv[t] + rv1[1] + rv1[2] + rv1[3]
    level2 = [
        go(remote(sv, rv2.at[e], v2s.at[e], v2r.at[e], others[e - 1])) for e in range(1, shards)
    ]
    lax.fori_loop((lines - 1) // 2, max((lines - 1) // 2, lines - 2), pass_qkv, 0)
    for c in third:
        c.wait_recv()

    def finish(c):
        second[c].wait_recv()
        gn = near[part(c), :] + r1[1, part(c), :].astype(F32) + q1[part(c), :].astype(F32)
        unit, inv = normalize(tokv[part(c), :].astype(F32))
        scaled = gn * gain[...]
        inner = (
            scaled
            - jnp.mean(scaled, axis=1, keepdims=True)
            - unit * jnp.mean(scaled * unit, axis=1, keepdims=True)
        )
        ghidv[part(c), :] = ghidv[part(c), :] + inv * inner

    for c in range(chunks - 1):
        finish(c)
    lax.fori_loop(max((lines - 1) // 2, lines - 2), lines - 1, pass_qkv, 0)
    for c in level2:
        c.wait_recv()
    total = sv[...]
    for e in range(1, shards):
        total = total + rv2[e]
    gv[t] = total
    level3 = [
        go(remote(gv.at[t], gv.at[t], v3s.at[j], v3r.at[j], mates[j - 1])) for j in range(1, 4)
    ]

    def reduced(k, own):
        x_copy(k, 0).wait_recv()
        land = lands[k]
        result = own.astype(F32) + land[0][0].astype(F32)
        if lines <= 8:
            for d in range(lines - 1, 0, -1):
                z_copy(k, d).wait_recv()
                result = result + land[2][d].astype(F32)
            return result

        def collect(i, acc):
            d = lines - 1 - i
            z_copy(k, d).wait_recv()
            return acc + land[2][d].astype(F32)

        return lax.fori_loop(0, lines - 1, collect, result)

    pltpu.make_async_copy(g1_in.at[keep_of(0)], sz1.at[0], lsem.at[8]).wait()
    sum1[...] = reduced(0, sz1[0])
    outs.append(pltpu.make_async_copy(sum1, w1_out, osem.at[1]))
    outs[-1].start()
    total2 = rz2[0].astype(F32)
    for d in range(lines - 1, 0, -1):
        z2_copy(d).wait_recv()
        total2 = total2 + rz2[d].astype(F32)
    sum2[...] = total2.T
    outs.append(pltpu.make_async_copy(sum2, w2_out, osem.at[5]))
    outs[-1].start()
    wos[...] = reduced(1, go_[row(f), :]).T
    outs.append(pltpu.make_async_copy(wos, wo_out, osem.at[2]))
    outs[-1].start()
    finish(chunks - 1)
    outs.append(pltpu.make_async_copy(ghidv, tok_out, osem.at[3]))
    outs[-1].start()
    for p in range(pairs):
        mine = reduced(2 + p, gq[p, row(f), :])
        for k in range(3):
            wqs[k, :, p * 2 * HD : (p + 1) * 2 * HD] = mine[:, k * 2 * HD : (k + 1) * 2 * HD]
    outs.append(pltpu.make_async_copy(wqs, wq_out, osem.at[4]))
    outs[-1].start()
    for c in level3:
        c.wait_recv()
    for u in range(4):
        cols = slice(u * head_width, (u + 1) * head_width)
        for r in range(4):
            fcb_out[:, r * width + u * head_width : r * width + (u + 1) * head_width] = gv[u, r : r + 1, :]
        qv_out[:, cols] = gv[u, 4:6, :]
        for r, ref in enumerate((g_a, g_b, g_c, g_d, g_e, g_f)):
            ref[:, cols] = gv[u, 6 + r : 7 + r, :]
    for c in sends:
        c.wait_send()

    def drain(d, _):
        for k in range(sums):
            x_copy(k, d).wait_send()

        @pl.when(d > 0)
        def _():
            z2_copy(d).wait_send()
            for k in range(sums):
                z_copy(k, d).wait_send()

        return 0

    lax.fori_loop(0, lines, drain, 0)
    for c in outs:
        c.wait()


def tail(shards, lse, starts, vec, gain, bias, fc2_bias, qkv, grad_att, att, weights, wt, qT, kT, one, back, tok, ghid, hid, pfar, g1, g2):
    _, rows, width = one.shape
    head_width = att.shape[2]
    hidden = g1.shape[2]
    heads = head_width // HD
    pairs = heads // 2
    per = width // shards
    lines = shards // 2
    chunks = 2
    dma = pltpu.SemaphoreType.DMA
    vm = pl.BlockSpec(memory_space=VM)
    hbm = pl.BlockSpec(memory_space=HB)
    V = pltpu.VMEM
    small = (4, 16, head_width)
    sems = [
        (8 + lines,), (2, chunks), (2, chunks), (chunks,), (chunks,),
        (2 + pairs, lines), (2 + pairs, lines), (2 + pairs, lines), (2 + pairs, lines),
        (4,), (4,), (shards,), (shards,), (4,), (4,), (4,), (4,), (lines,), (lines,), (6,), (7,),
    ]
    turned = V((4, head_width, rows), BF)
    one_row = (rows, width)
    return pl.pallas_call(
        functools.partial(tail_kernel, shards, chunks),
        name="tail",
        out_shape=[
            jax.ShapeDtypeStruct(one_row, F32),
            jax.ShapeDtypeStruct(one_row, F32),
            jax.ShapeDtypeStruct((3, per, head_width), F32),
            jax.ShapeDtypeStruct((head_width, per), F32),
            jax.ShapeDtypeStruct((per, hidden), F32),
            jax.ShapeDtypeStruct((hidden, per), F32),
            jax.ShapeDtypeStruct((2, width), F32),
            jax.ShapeDtypeStruct((1, 4 * width), F32),
        ]
        + [jax.ShapeDtypeStruct((1, width), F32)] * 6,
        in_specs=[vm, pl.BlockSpec(memory_space=SM)] + [vm] * 4 + [hbm] * 15,
        out_specs=[hbm] * 6 + [vm] * 8,
        scratch_shapes=[
            V((4, rows, 3 * head_width), BF), V((4, rows, head_width), BF), V((4, rows, head_width), BF),
            V(weights.shape, BF), turned, turned, turned,
            V((4, rows, head_width), F32), V((4, rows, head_width), F32), V((4, heads, rows), F32),
            V((4, rows, 3 * head_width), BF),
            V((4, rows, width), BF), V((4, rows, width), BF), V(one_row, BF), V(one_row, F32),
            V(one_row, F32), V(one_row, BF), V((3 * head_width, width), BF),
            V((2, rows, width), BF), V((2, rows, width), BF), V(one_row, BF), V(one_row, BF),
            V(one_row, F32), V((pairs, width, 6 * HD), BF), V((width, head_width), BF),
        ]
        + [V((pairs, lines, per, 6 * HD), BF)] * 3
        + [V((lines, per, head_width), BF)] * 3
        + [V((lines, per, hidden), BF)] * 4
        + [
            V((per, hidden), F32), V((hidden, per), F32), V((3, per, head_width), F32), V((head_width, per), F32),
            V((width, 2 * HD), F32), V(small, F32), V(small, F32),
            V((16, head_width), F32), V((shards, 16, head_width), F32), V(small, F32),
        ]
        + [dma(s) for s in sems],
        compiler_params=pltpu.CompilerParams(
            collective_id=2, has_side_effects=True, vmem_limit_bytes=62 << 20
        ),
        cost_estimate=pl.CostEstimate(flops=60 << 30, bytes_accessed=100 << 20, transcendentals=0),
    )(lse, starts, vec, gain, bias, fc2_bias, qkv, grad_att, att, weights, wt, qT, kT, one, back, tok, ghid, hid, pfar, g1, g2)


def finish_kernel(parts, *refs):
    count = len(parts)
    held, sems = refs[2 * count : 3 * count], refs[-1]
    loads, stores = [], []
    for n, pieces in enumerate(parts):
        rows = held[n].shape[0] // pieces
        for i in range(pieces):
            block, k = pl.ds(i * rows, rows), len(loads)
            loads.append(
                pltpu.make_async_copy(refs[n].at[block], held[n].at[block], sems.at[0, k])
            )
            stores.append(
                pltpu.make_async_copy(held[n].at[block], refs[count + n].at[block], sems.at[1, k])
            )
    for c in loads:
        c.start()
    for load, store in zip(loads, stores):
        load.wait()
        store.start()
    for c in stores:
        c.wait()


def finish(arrays):
    parts = [4 if a.size >= 1 << 18 else 1 for a in arrays]
    hbm = pl.BlockSpec(memory_space=HB)
    return pl.pallas_call(
        functools.partial(finish_kernel, parts),
        name="finish",
        out_shape=[jax.ShapeDtypeStruct(a.shape, a.dtype) for a in arrays],
        in_specs=[hbm] * len(arrays),
        out_specs=[hbm] * len(arrays),
        scratch_shapes=[pltpu.VMEM(a.shape, a.dtype) for a in arrays]
        + [pltpu.SemaphoreType.DMA((2, sum(parts)))],
    )(*arrays)


def body(
    tokens,
    cotangent,
    pic_starts,
    w_qkv,
    qv_bias,
    w_out,
    out_bias,
    ln1_gain,
    ln1_bias,
    w_fc1,
    fc1_bias,
    w_fc2,
    fc2_bias,
    ln2_gain,
    ln2_bias,
):
    rows, width = tokens.shape
    shards = lax.axis_size("fsdp")
    one, qkv, wq_full, out_full, fc_in, up_far, att, lse, mix, wqt, qT, kT = head(
        shards, tokens, w_qkv.transpose(1, 0, 2), w_out, w_fc1, w_fc2,
        ln1_gain[None], ln1_bias[None], qv_bias, pic_starts, cotangent,
    )
    hidden_one, ghid, back, grad_att, fc1_part, fc2_part, part_far, vec = middle(
        shards, mix, out_full, tokens, cotangent, up_far, fc_in,
        ln2_gain[None], ln2_bias[None], out_bias[None], fc1_bias[None],
    )
    results = tail(
        shards, lse, pic_starts, vec, ln1_gain[None], ln1_bias[None], fc2_bias[None],
        qkv, grad_att, att, wq_full, wqt, qT, kT, one, back, tokens, ghid, hidden_one, part_far, fc1_part, fc2_part,
    )
    output, input_grad, wq_grad, wo_grad, fc1_grad, fc2_grad, qv_grad, fc1_b, *vecs = finish(results)
    out_b, fc2_b, gain_two, shift_two, gain_one, shift_one = [v[0] for v in vecs]
    return (
        output,
        input_grad,
        wq_grad.transpose(1, 0, 2),
        qv_grad,
        wo_grad,
        out_b,
        gain_one,
        shift_one,
        fc1_grad,
        fc1_b[0],
        fc2_grad,
        fc2_b,
        gain_two,
        shift_two,
    )


def solution(mesh):
    return jax.shard_map(
        body,
        mesh=mesh,
        in_specs=(
            P(("fsdp", "tensor"), None),
            P(("fsdp", "tensor"), None),
            P("fsdp", None),
            P("fsdp", None, "tensor"),
            P(),
            P("tensor", "fsdp"),
            P(),
            P(),
            P(),
            P("fsdp", "tensor"),
            P(),
            P("tensor", "fsdp"),
            P(),
            P(),
            P(),
        ),
        out_specs=(
            P(("fsdp", "tensor"), None),
            P(("fsdp", "tensor"), None),
            P("fsdp", None, "tensor"),
            P(),
            P("tensor", "fsdp"),
            P(),
            P(),
            P(),
            P("fsdp", "tensor"),
            P(),
            P("tensor", "fsdp"),
            P(),
            P(),
            P(),
        ),
        check_vma=False,
    )
```

```python
import functools
import math

import jax
import jax.numpy as jnp
from jax import lax
from jax.experimental import pallas as pl
from jax.experimental.pallas import tpu as pltpu
from jax.sharding import PartitionSpec as P

HD = 64
PIC = 256
F32 = jnp.float32
BF = jnp.bfloat16
NEG = -1e30
NORM_EPSILON = 1e-05
GELU_SCALE = math.sqrt(2.0 / math.pi)
GELU_CUBIC = 0.044715
VM = pltpu.MemorySpace.VMEM
SM = pltpu.MemorySpace.SMEM
HB = pltpu.MemorySpace.HBM
PRE = (1, 2)


def nn(a, b):
    return lax.dot_general(a, b, (((1,), (0,)), ((), ())), preferred_element_type=F32)


def nt(a, b):
    return lax.dot_general(a, b, (((1,), (1,)), ((), ())), preferred_element_type=F32)


def normalize(values):
    average = jnp.mean(values, axis=1, keepdims=True)
    centered = values - average
    inv_std = lax.rsqrt(jnp.mean(centered * centered, axis=1, keepdims=True) + NORM_EPSILON)
    return centered * inv_std, inv_std


def normalize_back(gradient, unit_rows, inv_std, gain_row):
    scaled = gradient * gain_row
    inner = (
        scaled
        - jnp.mean(scaled, axis=1, keepdims=True)
        - unit_rows * jnp.mean(scaled * unit_rows, axis=1, keepdims=True)
    )
    return inv_std * inner, jnp.sum(gradient * unit_rows, axis=0), jnp.sum(gradient, axis=0)


MESH = pl.DeviceIdType.MESH


def remote(src, dst, send, recv, where):
    return pltpu.make_async_remote_copy(
        src_ref=src, dst_ref=dst, send_sem=send, recv_sem=recv, device_id=where, device_id_type=MESH
    )


def greet(peers):
    barrier = pltpu.get_barrier_semaphore()
    for peer in peers:
        pl.semaphore_signal(barrier, inc=1, device_id=peer, device_id_type=MESH)
    pl.semaphore_wait(barrier, len(peers))


def head_kernel(
    shards, chunks,
    tok, wq, wo, w1, w2, gain, bias, qvb, starts, cot,
    n_out, qkv_out, wq_out, wo_out, fc_out, up_out, att_out, lse_out, mix_out, wqt_out, qT_out, kT_out,
    nv, wqv, wov, otv, fcv, qv, kn, qT, vT, att, lsev, wqt, kT,
    ysend, yrecv, csend, crecv, fsend, frecv, zqs, zqr, xqs, xqr, zos, zor, xos, xor,
    zfs, zfr, zds, zdr, xfs, xfr, ups, upr, wos, wor, ats, atr, lsem, osem,
):
    f = lax.axis_index("fsdp")
    t = lax.axis_index("tensor")
    rows, width = tok.shape
    head_width, per = wo.shape
    hid = w1.shape[1]
    step = rows // chunks
    lines = shards // 2
    far = {"fsdp": f, "tensor": t ^ 2}
    sib = {"fsdp": f, "tensor": t ^ 1}
    side = {"fsdp": f ^ 1, "tensor": t}
    alongs = [{"fsdp": f ^ (2 * d), "tensor": t} for d in range(1, lines)]
    mates = [{"fsdp": f, "tensor": t ^ j} for j in range(4)]
    greet(mates[1:] + [side] + alongs)
    sends = []

    def go(copy):
        copy.start()
        sends.append(copy)
        return copy

    zq, zo, xq, xo = [], [], [], []
    for d in range(1, lines):
        zq.append(go(remote(wq, wqv.at[f], zqs.at[d], zqr.at[d], alongs[d - 1])))
    xq.append(go(remote(wq, wqv.at[f], xqs.at[0], xqr.at[0], side)))
    ys, cs, fs = [], [], []
    for c in range(chunks):
        part = pl.ds(c * step, step)
        unit, _ = normalize(tok[part, :].astype(F32))
        nv[0, part, :] = (unit * gain[...] + bias[...]).astype(BF)
        ys.append(go(remote(nv.at[0, part], nv.at[2, part], ysend.at[c], yrecv.at[c], far)))
        cs.append(go(remote(nv.at[0, part], nv.at[1, part], csend.at[c], crecv.at[c], sib)))
    for d in range(1, lines):
        zo.append(go(remote(wo, wov.at[f], zos.at[d], zor.at[d], alongs[d - 1])))
    xo.append(go(remote(wo, wov.at[f], xos.at[0], xor.at[0], side)))
    wqv[f] = wq[...]
    wov[f] = wo[...]
    fcv[:, :hid] = w1[...]
    fcv[:, hid:] = w2[...].T
    local = [pltpu.make_async_copy(fcv, fc_out.at[f], lsem.at[0])]
    local[0].start()

    def forward_far(c):
        part = pl.ds(c * step, step)
        ys[c].wait_recv()
        fs.append(go(remote(nv.at[2, part], nv.at[3, part], fsend.at[c], frecv.at[c], sib)))

    todo = list(range(chunks))
    for d in range(1, lines):
        zq[d - 1].wait_recv()
        slot = f ^ (2 * d)
        xq.append(go(remote(wqv.at[slot], wqv.at[slot], xqs.at[d], xqr.at[d], side)))
        if len(todo) > 1:
            forward_far(todo.pop(0))
    for d in range(1, lines):
        zo[d - 1].wait_recv()
        slot = f ^ (2 * d)
        xo.append(go(remote(wov.at[slot], wov.at[slot], xos.at[d], xor.at[d], side)))
    fc = []
    for d in PRE:
        if d < lines:
            fc.append(go(remote(fcv, fc_out.at[f], zfs.at[d], zfr.at[d], alongs[d - 1])))
    while todo:
        forward_far(todo.pop(0))
    up = go(remote(cot, up_out, ups.at[0], upr.at[0], far))
    for c in cs:
        c.wait_recv()
    for d in range(lines):
        xq[d].wait_recv()
    start = pl.multiple_of(t * head_width, head_width)
    adds = (qvb[0:1, pl.ds(start, head_width)], None, qvb[1:2, pl.ds(start, head_width)])

    def project(j, _):
        b = t ^ j
        for k in range(3):
            value = nn(nv[j], wqv[:, k].reshape(width, head_width))
            if adds[k] is not None:
                value = value + adds[k]
            value = value.astype(BF)
            qv[j, :, k * head_width : (k + 1) * head_width] = value
            if k == 0:
                qT[b] = (value * jnp.asarray(HD**-0.5, BF)).T
            elif k == 1:
                kn[b] = value
                kT[b] = value.T
            else:
                vT[b] = value.T
        return 0

    lax.fori_loop(0, 2, project, 0)
    for c in fs:
        c.wait_recv()
    lax.fori_loop(2, 4, project, 0)
    for d in range(lines):
        xo[d].wait_recv()
    fc.append(go(remote(fcv, fc_out.at[f], zfs.at[0], zfr.at[0], side)))
    if per % 128 == 0:
        def place(s, _):
            otv[:, pl.ds(pl.multiple_of(s * per, per), per)] = wov[s]
            return 0

        lax.fori_loop(0, shards, place, 0)
    else:
        for s in range(shards):
            otv[:, s * per : (s + 1) * per] = wov[s]
    outs = [
        pltpu.make_async_copy(src, dst, osem.at[n])
        for n, (src, dst) in enumerate([(nv, n_out), (qv, qkv_out), (wqv, wq_out), (otv, wo_out.at[t])])
    ]
    for k in range(3):
        wqt[k * head_width : (k + 1) * head_width, :] = wqv[:, k].reshape(width, head_width).T
    outs += [
        pltpu.make_async_copy(src, dst, osem.at[10 + n])
        for n, (src, dst) in enumerate([(wqt, wqt_out), (qT, qT_out), (kT, kT_out)])
    ]
    for c in outs:
        c.start()
    shared = [
        go(remote(otv, wo_out.at[t], wos.at[1], wor.at[1], sib)),
        go(remote(otv, wo_out.at[t], wos.at[2], wor.at[2], far)),
    ]
    rowk = lax.broadcasted_iota(jnp.int32, (rows, rows), 0)
    colq = lax.broadcasted_iota(jnp.int32, (rows, rows), 1)
    half = lax.broadcasted_iota(jnp.int32, (2 * HD, rows), 0) < HD
    def mixed(i):
        return remote(
            att.at[i], mix_out.at[t], ats.at[i], atr.at[t ^ i], {"fsdp": f, "tensor": t * 0 + i}
        )

    pre = [d for d in PRE if d < lines]
    direct = [d for d in range(1, lines) if d not in pre]
    later = [remote(fcv, fc_out.at[f], zds.at[d], zdr.at[d], alongs[d - 1]) for d in direct]
    passed = []
    for d in pre:
        shard = fc_out.at[f ^ (2 * d)]
        passed.append(remote(shard, shard, xfs.at[d], xfr.at[d], side))
    more = later + passed
    sends += more

    def attend(i, _):
        at = starts[0, i] - i * rows

        @pl.when(i == 2)
        def _():
            for c in later:
                c.start()

        @pl.when(i == 3)
        def _():
            for n in range(len(pre)):
                fc[n].wait_recv()
                passed[n].start()

        def pair(p, _):
            col = pl.multiple_of(p * 2 * HD, 2 * HD)
            qp = qT[i, pl.ds(col, 2 * HD), :]
            zero = jnp.zeros_like(qp)
            masked = (jnp.where(half, qp, zero), jnp.where(half, zero, qp))

            def block(m, carry, diag):
                kb = kn[m, :, pl.ds(col, 2 * HD)]
                vb = vT[m, pl.ds(col, 2 * HD), :]
                new = []
                for hh in range(2):
                    top, total, acc = carry[hh]
                    s = nn(kb, masked[hh])
                    if diag:
                        inside = (rowk >= at) & (rowk < at + PIC) & (colq >= at) & (colq < at + PIC)
                        s = jnp.where((rowk <= colq) | inside, s, NEG)
                    peak = jnp.maximum(top, jnp.max(s, axis=0, keepdims=True))
                    shrink = jnp.exp(top - peak)
                    e = jnp.exp(s - peak)
                    total = total * shrink + jnp.sum(e, axis=0, keepdims=True)
                    acc = acc * shrink + nn(vb[hh * HD : (hh + 1) * HD], e.astype(BF))
                    new.append((peak, total, acc))
                return tuple(new)

            blank = (
                jnp.full((1, rows), NEG, F32), jnp.zeros((1, rows), F32), jnp.zeros((HD, rows), F32)
            )
            c = block(i, (blank, blank), True)
            c = lax.fori_loop(0, i, lambda m, c: block(m, c, False), c)
            found = []
            for hh in range(2):
                top, total, acc = c[hh]
                found.append(acc * (1.0 / total))
                lsev[t ^ i, pl.ds(p * 2 + hh, 1), :] = top + jnp.log(total)
            att[i, :, pl.ds(col, 2 * HD)] = jnp.concatenate(found, axis=0).astype(BF).T
            return 0

        lax.fori_loop(0, head_width // (2 * HD), pair, 0)

        @pl.when(t != i)
        def _():
            mixed(i).start()

        return 0

    lax.fori_loop(0, 4, attend, 0)
    outs += [pltpu.make_async_copy(att.at[t ^ j], att_out.at[j], osem.at[4 + j]) for j in range(4)]
    outs.append(pltpu.make_async_copy(lsev, lse_out, osem.at[8]))
    outs.append(pltpu.make_async_copy(att.at[t], mix_out.at[t], osem.at[9]))
    for c in outs[7:]:
        c.start()
    shared[1].wait_recv()
    shared.append(go(remote(wo_out.at[t ^ 2], wo_out.at[t ^ 2], wos.at[3], wor.at[3], sib)))
    shared[0].wait_recv()
    shared[2].wait_recv()
    for j in range(1, 4):
        remote(att.at[0], mix_out.at[t ^ j], ats.at[0], atr.at[j], mates[j]).wait_recv()
    for i in range(4):

        @pl.when(t != i)
        def _(i=i):
            mixed(i).wait_send()

    for c in fc[len(pre) :] + [up] + more:
        c.wait_recv()
    for c in sends:
        c.wait_send()
    for c in local + outs:
        c.wait()


def head(shards, tokens, wq, wo, w1, w2, gain, bias, qv_bias, starts, cot):
    rows, width = tokens.shape
    head_width, per = wo.shape
    hid = w1.shape[1]
    lines = shards // 2
    chunks = 4
    heads = head_width // HD
    dma = pltpu.SemaphoreType.DMA
    vm = pl.BlockSpec(memory_space=VM)
    hbm = pl.BlockSpec(memory_space=HB)
    V = pltpu.VMEM
    full = (4, rows, width)
    three = (4, rows, 3 * head_width)
    return pl.pallas_call(
        functools.partial(head_kernel, shards, chunks),
        name="head",
        out_shape=[
            jax.ShapeDtypeStruct(full, BF),
            jax.ShapeDtypeStruct(three, BF),
            jax.ShapeDtypeStruct((shards, 3, per, head_width), BF),
            jax.ShapeDtypeStruct((4, head_width, width), BF),
            jax.ShapeDtypeStruct((shards, per, 2 * hid), BF),
            jax.ShapeDtypeStruct((rows, width), BF),
            jax.ShapeDtypeStruct((4, rows, head_width), BF),
            jax.ShapeDtypeStruct((4, heads, rows), F32),
            jax.ShapeDtypeStruct((4, rows, head_width), BF),
            jax.ShapeDtypeStruct((3 * head_width, width), BF),
            jax.ShapeDtypeStruct((4, head_width, rows), BF),
            jax.ShapeDtypeStruct((4, head_width, rows), BF),
        ],
        in_specs=[vm] * 8 + [pl.BlockSpec(memory_space=SM), hbm],
        out_specs=[hbm] * 12,
        scratch_shapes=[
            V(full, BF), V((shards, 3, per, head_width), BF), V((shards, head_width, per), BF),
            V((head_width, width), BF), V((per, 2 * hid), BF), V(three, BF),
            V((4, rows, head_width), BF), V((4, head_width, rows), BF), V((4, head_width, rows), BF),
            V((4, rows, head_width), BF), V((4, heads, rows), F32), V((3 * head_width, width), BF),
            V((4, head_width, rows), BF),
        ]
        + [dma((chunks,))] * 6
        + [dma((lines,))] * 8
        + [dma((max(lines, 4),))] * 6
        + [dma((1,))] * 2
        + [dma((4,))] * 4
        + [dma((1,)), dma((13,))],
        compiler_params=pltpu.CompilerParams(
            collective_id=0, has_side_effects=True, vmem_limit_bytes=56 << 20
        ),
        cost_estimate=pl.CostEstimate(flops=40 << 30, bytes_accessed=90 << 20, transcendentals=0),
    )(tokens, wq, wo, w1, w2, gain, bias, qv_bias, starts, cot)


def middle_kernel(
    shards, chunks,
    mix_in, wo_in, tok_in, cot, up_far, fc_in, gain, bias, out_bias, fc_bias,
    hid_out, ghid_out, back_out, do_out, g1_out, g2_out, part_far, vec,
    mix, wo, tok, wfc, wt, wot, upv, twov, actv, pgv, backv,
    s1, r1, a1, q1, near, hv, rx, sz, dov,
    dos, dor, c2s, c2r, y2s, y2r, f2s, f2r,
    s3s, s3r, y3s, y3r,
    s5s, s5r, ups, upr, lsem, xs, xr, osem, gxs, gxr, isem,
):
    first_in = [
        pltpu.make_async_copy(src, dst, isem.at[n])
        for n, (src, dst) in enumerate([(mix_in, mix), (wo_in, wo), (tok_in, tok)])
    ]
    for c in first_in:
        c.start()
    f = lax.axis_index("fsdp")
    t = lax.axis_index("tensor")
    rows, width = tok.shape
    per = fc_in.shape[1]
    hid = fc_in.shape[2] // 2
    pre = [d for d in PRE if d < shards // 2]
    step = rows // chunks
    lines = shards // 2
    far = {"fsdp": f, "tensor": t ^ 2}
    sib = {"fsdp": f, "tensor": t ^ 1}
    side = {"fsdp": f ^ 1, "tensor": t}
    direct = [d for d in range(1, lines) if d not in pre]
    mates = [{"fsdp": f, "tensor": t ^ j} for j in range(4)]
    greet(mates[1:] + [side])
    sends = []

    def go(copy):
        copy.start()
        sends.append(copy)
        return copy

    def part(c):
        return pl.ds(c * step, step)

    halves = (pl.ds(0, hid), pl.ds(hid, hid))
    late = [2 * d + 1 for d in direct]
    early = [e for e in range(shards) if e not in late]
    local = [
        pltpu.make_async_copy(fc_in.at[f ^ e], wfc.at[f ^ e], lsem.at[n])
        for n, e in enumerate(early)
    ]
    local.append(pltpu.make_async_copy(cot, upv.at[0], lsem.at[shards]))
    local.append(pltpu.make_async_copy(up_far, upv.at[2], lsem.at[shards + 1]))
    for c in local:
        c.start()
    xf = []
    for d in direct:
        block = f ^ (2 * d)
        xf.append(go(remote(fc_in.at[block], wfc.at[block], xs.at[d], xr.at[d], side)))
    up_copies = [
        go(remote(cot, upv.at[1], ups.at[0], upr.at[0], sib)),
        go(remote(up_far, upv.at[3], ups.at[1], upr.at[1], sib)),
    ]
    vec[...] = jnp.zeros_like(vec)
    for c in first_in:
        c.wait()
    ag_far, ag_sib = [], []
    for c in range(chunks):
        hidden = tok[part(c), :].astype(F32) + out_bias[...]
        for s in range(4):
            hidden = hidden + nn(mix[s, part(c), :], wo[s])
        hv[part(c), :] = hidden
        unit, _ = normalize(hidden)
        twov[0, part(c), :] = (unit * gain[...] + bias[...]).astype(BF)
        ag_far.append(go(remote(twov.at[0, part(c)], twov.at[2, part(c)], y2s.at[c], y2r.at[c], far)))
        ag_sib.append(go(remote(twov.at[0, part(c)], twov.at[1, part(c)], c2s.at[c], c2r.at[c], sib)))
    for s in range(4):
        wot[s] = wo[s].T
    outs = []
    for c in local:
        c.wait()

    def flip(slot):
        if per % 128 == 0:
            wt[:, pl.ds(pl.multiple_of(slot * per, per), per)] = wfc[slot].T

    def flip_early(e, _):
        flip(f ^ e)
        return 0

    if early == list(range(len(early))):
        lax.fori_loop(0, len(early), flip_early, 0)
    else:
        for e in early:
            flip(f ^ e)
    for c in xf:
        c.wait_recv()
    for e in late:
        flip(f ^ e)
    if per % 128:
        wt[...] = wfc[...].reshape(width, 2 * hid).T
    for c in up_copies:
        c.wait_recv()
    for c in ag_sib:
        c.wait_recv()
    start = pl.multiple_of(t * hid, hid)
    tile = hid // 2

    def feed(j, at):
        block = pl.ds(pl.multiple_of(at * step, step), step)
        two = twov[j, block, :]
        up = upv[j, block, :]
        total = None
        for n in range(2):
            cols = pl.ds(n * tile, tile)
            x = nn(two, wfc[:, :, cols].reshape(width, tile))
            x = x + fc_bias[:, pl.ds(pl.multiple_of(start + n * tile, tile), tile)]
            hg = nn(up, wfc[:, :, pl.ds(hid + n * tile, tile)].reshape(width, tile))
            sq = x * x
            th = jnp.tanh(GELU_SCALE * (x + GELU_CUBIC * (sq * x)))
            half = 0.5 * (1.0 + th)
            actv[j, block, cols] = (x * half).astype(BF)
            slope = half + (0.5 * GELU_SCALE) * x * (1.0 - th * th) * (1.0 + (3.0 * GELU_CUBIC) * sq)
            pg = (hg * slope).astype(BF)
            pgv[j, block, cols] = pg
            vec[0:1, cols] += jnp.sum(pg.astype(F32), axis=0, keepdims=True)
            term = nn(pg, wt[cols, :])
            total = term if total is None else total + term
        return total

    def copies(c):
        block = pl.ds(pl.multiple_of(c * step, step), step)
        return (
            remote(twov.at[0, block], twov.at[2, block], y2s.at[c], y2r.at[c], far),
            remote(twov.at[2, block], twov.at[3, block], f2s.at[c], f2r.at[c], sib),
            remote(a1.at[block], q1.at[block], y3s.at[c], y3r.at[c], far),
        )

    def core_copy(k, c):
        block = pl.ds(pl.multiple_of(c * step, step), step)
        return remote(s1.at[2 + k, block], r1.at[2 + k, block], s3s.at[k, c], s3r.at[k, c], sib)

    def rows_of(c, _):
        block = pl.ds(pl.multiple_of(c * step, step), step)
        got, fwd, send2 = copies(c)

        def one(i, _):
            total = feed(i ^ 1, c)

            @pl.when(i == 0)
            def _():
                s1[3, block, :] = total.astype(BF)
                core_copy(1, c).start()
                got.wait_recv()
                fwd.start()

            @pl.when(i == 1)
            def _():
                near[block, :] = total
                fwd.wait_recv()

            @pl.when(i == 2)
            def _():
                s1[2, block, :] = total.astype(BF)
                core_copy(0, c).start()

            @pl.when(i == 3)
            def _():
                core_copy(0, c).wait_recv()
                a1[block, :] = (total + r1[2, block, :].astype(F32)).astype(BF)
                send2.start()

            return 0

        lax.fori_loop(0, 4, one, 0)
        return 0

    lax.fori_loop(0, chunks, rows_of, 0)

    span = 256
    ratio = span // (2 * per)
    groups = width // span
    z = f // 2
    x = lax.rem(f, 2)

    def x_copy(d):
        return remote(wfc.at[(z ^ d) * 2 + (1 - x), :, halves[0]], rx.at[d], gxs.at[d], gxr.at[d], side)

    def weight_grad(left, right, h, send):
        def group_of(i, _):
            near_group = groups - 1 - i
            group = near_group ^ (z // ratio)
            cols = pl.ds(pl.multiple_of(group * span, span), span)
            acc = None
            for j in range(4):
                term = nn(left[j, :, cols].T, right[j])
                acc = term if acc is None else acc + term
            count = span // per
            slots = pl.ds(group * count, count)
            wfc[slots, :, halves[h]] = acc.astype(BF).reshape(count, per, hid)
            if send:

                def launch(e, _):
                    x_copy(near_group * ratio + e).start()
                    return 0

                lax.fori_loop(0, ratio, launch, 0)
            return 0

        lax.fori_loop(0, groups, group_of, 0)

    def give_part(k):
        for c in range(chunks):
            core_copy(k, c).wait_send()

        def give(c, _):
            block = pl.ds(pl.multiple_of(c * step, step), step)
            s1[k, block, :] = nn(actv[3 - 2 * k, block, :], wt[hid:, :]).astype(BF)
            return 0

        lax.fori_loop(0, chunks, give, 0)
        return go(remote(s1.at[k], r1.at[k], s5s.at[k], s5r.at[k], sib))

    def keep_part(k):
        def keep(c, _):
            block = pl.ds(pl.multiple_of(c * step, step), step)
            mine = nn(actv[2 - 2 * k, block, :], wt[hid:, :])
            if k:
                hv[block, :] += mine
            else:
                s1[2, block, :] = mine.astype(BF)
            return 0

        lax.fori_loop(0, chunks, keep, 0)

    def join_part(k, given):
        given.wait_recv()
        if k:
            hv[...] += r1[k].astype(F32)
            outs.append(pltpu.make_async_copy(hv, hid_out, osem.at[0]))
        else:
            s1[2] = (s1[2].astype(F32) + r1[k].astype(F32)).astype(BF)
            outs.append(pltpu.make_async_copy(s1.at[2], part_far, osem.at[2]))
        outs[-1].start()

    weight_grad(upv, actv, 0, True)
    given_do = []
    for c in range(chunks):
        _, _, send2 = copies(c)
        core_copy(1, c).wait_recv()
        send2.wait_recv()
        gn = near[part(c), :] + r1[3, part(c), :].astype(F32) + q1[part(c), :].astype(F32)
        unit, inv = normalize(hv[part(c), :])
        back, g_sum, b_sum = normalize_back(gn, unit, inv, gain[...])
        cots = upv[0, part(c), :].astype(F32)
        ghid = cots + back
        near[part(c), :] = ghid
        low = ghid.astype(BF)
        backv[part(c), :] = low
        for j in (2, 3, 1, 0):
            dov[j, part(c), :] = nn(low, wot[t ^ j]).astype(BF)
            if j > 0:
                given_do.append(
                    go(remote(dov.at[j, part(c)], do_out.at[j, part(c)], dos.at[j, c], dor.at[j, c], mates[j]))
                )
        vec[1:2, :] += g_sum[None]
        vec[2:3, :] += b_sum[None]
        vec[3:4, :] += jnp.sum(ghid, axis=0, keepdims=True)
        vec[4:5, :] += jnp.sum(cots, axis=0, keepdims=True)
        if c == 0:
            given = [give_part(0)]
            keep_part(0)
            given.append(give_part(1))
            join_part(0, given[0])
    keep_part(1)
    join_part(1, given[1])
    outs.append(pltpu.make_async_copy(near, ghid_out, osem.at[1]))
    outs[-1].start()

    weight_grad(twov, pgv, 1, False)
    outs.append(pltpu.make_async_copy(wfc.at[:, :, halves[1]], g1_out, osem.at[5]))
    outs[-1].start()
    outs.append(pltpu.make_async_copy(dov.at[0], do_out.at[0], osem.at[7]))
    outs[-1].start()
    outs.append(pltpu.make_async_copy(backv, back_out, osem.at[4]))
    outs[-1].start()

    def side_sum(i, _):
        d = lines - 1 - i
        x_copy(d).wait_recv()
        sz[d] = (wfc[(z ^ d) * 2 + x, :, halves[0]].astype(F32) + rx[d].astype(F32)).astype(BF)
        return 0

    lax.fori_loop(0, lines, side_sum, 0)
    outs.append(pltpu.make_async_copy(sz, g2_out, osem.at[6]))
    outs[-1].start()
    for c in given_do:
        c.wait_recv()
    for c in sends:
        c.wait_send()
    for c in range(chunks):
        _, fwd, send2 = copies(c)
        fwd.wait_send()
        send2.wait_send()

    def drain(d, _):
        x_copy(d).wait_send()
        return 0

    lax.fori_loop(0, lines, drain, 0)
    for c in outs:
        c.wait()


def middle(shards, mix, wo, tok, cot, up_far, fc_in, gain, bias, out_bias, fc_bias):
    rows, width = tok.shape
    per, hid2 = fc_in.shape[1:]
    hid = hid2 // 2
    head_width = wo.shape[1]
    lines = shards // 2
    chunks = 2
    step = rows // chunks
    dma = pltpu.SemaphoreType.DMA
    vm = pl.BlockSpec(memory_space=VM)
    hbm = pl.BlockSpec(memory_space=HB)
    full = (4, rows, width)
    one = (rows, width)
    block = (lines, per, hid)
    V = pltpu.VMEM
    sems = [
        (4, chunks), (4, chunks), (chunks,), (chunks,),
        (chunks,), (chunks,), (chunks,), (chunks,),
        (2, chunks), (2, chunks), (chunks,), (chunks,),
        (2,), (2,), (2,), (2,), (shards + 2,), (lines,), (lines,), (8,), (lines,), (lines,), (3,),
    ]
    return pl.pallas_call(
        functools.partial(middle_kernel, shards, chunks),
        name="middle",
        out_shape=[
            jax.ShapeDtypeStruct(one, F32),
            jax.ShapeDtypeStruct(one, F32),
            jax.ShapeDtypeStruct(one, BF),
            jax.ShapeDtypeStruct((4, rows, head_width), BF),
            jax.ShapeDtypeStruct((shards, per, hid), BF),
            jax.ShapeDtypeStruct(block, BF),
            jax.ShapeDtypeStruct(one, BF),
            jax.ShapeDtypeStruct((8, width), F32),
        ],
        in_specs=[hbm] * 6 + [vm] * 4,
        out_specs=[hbm] * 7 + [vm],
        scratch_shapes=[
            V(mix.shape, BF), V(wo.shape, BF), V(one, BF), V((shards, per, 2 * hid), BF), V((2 * hid, width), BF), V((4, width, head_width), BF),
            V(full, BF), V(full, BF), V((4, rows, hid), BF), V((4, rows, hid), BF), V(one, BF),
            V(full, BF), V(full, BF), V(one, BF), V(one, BF),
            V(one, F32), V(one, F32), V(block, BF), V(block, BF), V((4, rows, head_width), BF),
        ]
        + [dma(s) for s in sems],
        compiler_params=pltpu.CompilerParams(
            collective_id=1, has_side_effects=True, vmem_limit_bytes=60 << 20
        ),
        cost_estimate=pl.CostEstimate(flops=60 << 30, bytes_accessed=200 << 20, transcendentals=0),
    )(mix, wo, tok, cot, up_far, fc_in, gain, bias, out_bias, fc_bias)


def tail_kernel(
    shards, chunks,
    lse, starts, vec, gain, bias, fc2_bias,
    qs_in, dos_in, ats_in, weights_in, wt_in, qT_in, kT_in, one_in, back_in, tok_in, ghid_in, hid_in, pfar_in, g1_in, g2_in,
    out_out, tok_out, wq_out, wo_out, w1_out, w2_out, qv_out, fcb_out, g_a, g_b, g_c, g_d, g_e, g_f,
    qs, dos, ats, weights, qT, kT, doT, dk, dv, dl, dqkv,
    onev, backv, tokv, ghidv, hidv, pfarv, wt,
    s1, r1, a1, q1, near, gq, go_, rx, sz, rz, rxo, szo, rzo, rx1, sz1, rz1, rz2, sum1, sum2, wqs, wos,
    smat, lv, rv1, sv, rv2, gv,
    lsem, s1s, s1r, y1s, y1r, xs, xr, zs, zr, v1s, v1r, v2s, v2r, v3s, v3r, pfs, pfr, z2s, z2r, osem, isem,
):
    f = lax.axis_index("fsdp")
    t = lax.axis_index("tensor")
    _, rows, width = onev.shape
    head_width = ats.shape[2]
    first_in = [
        pltpu.make_async_copy(src, dst, isem.at[n])
        for n, (src, dst) in enumerate(
            [
                (dos_in, dos), (ats_in, ats), (qT_in, qT), (kT_in, kT), (qs_in, qs),
                (weights_in, weights), (wt_in, wt),
            ]
        )
    ]
    for c in first_in:
        c.start()
    per = width // shards
    lines = shards // 2
    step = rows // chunks
    z = f // 2
    x = lax.rem(f, 2)
    far = {"fsdp": f, "tensor": t ^ 2}
    sib = {"fsdp": f, "tensor": t ^ 1}
    side = {"fsdp": f ^ 1, "tensor": t}
    mates = [{"fsdp": f, "tensor": t ^ j} for j in range(1, 4)]
    others = [{"fsdp": f ^ e, "tensor": t} for e in range(1, shards)]
    greet(mates + others)
    sends = []

    def go(copy):
        copy.start()
        sends.append(copy)
        return copy

    def part(c):
        return pl.ds(c * step, step)

    def row(block):
        return pl.ds(pl.multiple_of(block * per, per), per)

    pairs = head_width // (2 * HD)
    sums = 2 + pairs
    sources = [lambda b: g1_in.at[b], lambda b: go_.at[row(b)]]
    lands = [(rx1, sz1, rz1), (rxo, szo, rzo)]
    for p in range(pairs):
        sources.append(lambda b, p=p: gq.at[p, row(b)])
        lands.append((rx.at[p], sz.at[p], rz.at[p]))

    def x_copy(k, d):
        return remote(
            sources[k]((z ^ d) * 2 + (1 - x)), lands[k][0].at[d], xs.at[k, d], xr.at[k, d], side
        )

    def z_copy(k, d):
        return remote(
            lands[k][1].at[d], lands[k][2].at[d], zs.at[k, d], zr.at[k, d],
            {"fsdp": f ^ (2 * d), "tensor": t},
        )

    def pass_on(k, d, own):
        x_copy(k, d).wait_recv()
        lands[k][1][d] = (own(d).astype(F32) + lands[k][0][d].astype(F32)).astype(BF)
        z_copy(k, d).start()

    def keep_of(d):
        return (z ^ d) * 2 + x

    def launch(i, _):
        x_copy(0, lines - 1 - i).start()
        return 0

    lax.fori_loop(0, lines, launch, 0)
    def z2_copy(d):
        return remote(
            g2_in.at[d], rz2.at[d], z2s.at[d], z2r.at[d], {"fsdp": f ^ (2 * d), "tensor": t}
        )

    def launch2(i, _):
        z2_copy(lines - 1 - i).start()
        return 0

    lax.fori_loop(0, lines - 1, launch2, 0)
    back_far = go(remote(back_in, backv.at[2], pfs.at[1], pfr.at[1], far))
    back_sib = go(remote(back_in, backv.at[1], pfs.at[2], pfr.at[2], sib))
    local = [
        pltpu.make_async_copy(src, dst, lsem.at[n])
        for n, (src, dst) in enumerate(
            [
                (back_in, backv.at[0]), (one_in, onev), (tok_in, tokv), (ghid_in, ghidv),
                (hid_in, hidv), (g2_in.at[0], rz2.at[0]),
            ]
        )
    ]
    for c in local:
        c.start()
    keeps = []

    def own_block(d, _):
        pltpu.make_async_copy(g1_in.at[keep_of(d)], sz1.at[d], lsem.at[8 + d]).start()
        return 0

    lax.fori_loop(0, lines, own_block, 0)

    def pass_fc1(d):
        pltpu.make_async_copy(g1_in.at[keep_of(d)], sz1.at[d], lsem.at[8 + d]).wait()
        pass_on(0, d, lambda d: sz1[d])

    first_in[0].wait()
    first_in[1].wait()
    for j in range(4):
        b = t ^ j
        do = dos[j]
        doT[b] = do.T
        prod = (do.astype(F32) * ats[j].astype(F32)).T
        for h in range(head_width // HD):
            dl[b, h : h + 1, :] = jnp.sum(prod[h * HD : (h + 1) * HD], axis=0, keepdims=True)
    dk[...] = jnp.zeros_like(dk)
    dv[...] = jnp.zeros_like(dv)
    for c in first_in[2:5]:
        c.wait()

    span = 256
    ratio = span // (2 * per)
    groups = width // span

    smat[...] = jnp.zeros_like(smat)

    def weight_grad(k, left, rights, target, p=None):
        def group_of(i, _):
            near_group = groups - 1 - i
            group = near_group ^ (z // ratio)
            cols = pl.ds(pl.multiple_of(group * span, span), span)
            turned = [left[j, :, cols].T for j in range(4)]
            count = span // per
            for n, (at, right) in enumerate(rights):
                acc = None
                for j in range(4):
                    term = nn(turned[j], right(j))
                    acc = term if acc is None else acc + term
                target[cols, at : at + acc.shape[1]] = acc.astype(BF)
                if p is not None:
                    block = weights[pl.ds(group * count, count), n, :, p * 2 * HD : (p + 1) * 2 * HD]
                    smat[cols, :] += acc * block.reshape(span, 2 * HD).astype(F32)

            def send(e, _):
                x_copy(k, near_group * ratio + e).start()
                return 0

            lax.fori_loop(0, ratio, send, 0)
            return 0

        lax.fori_loop(0, groups, group_of, 0)

    rowk = lax.broadcasted_iota(jnp.int32, (rows, rows), 0)
    colq = lax.broadcasted_iota(jnp.int32, (rows, rows), 1)
    hrow = lax.broadcasted_iota(jnp.int32, (2 * HD, rows), 0) < HD
    hcol = lax.broadcasted_iota(jnp.int32, (rows, 2 * HD), 1) < HD

    def two(v, m):
        zero = jnp.zeros_like(v)
        return (jnp.where(m, v, zero), jnp.where(m, zero, v))

    def attend(p, i):
        at = starts[0, i] - i * rows
        jj = t ^ i

        if True:
            col = pl.multiple_of(p * 2 * HD, 2 * HD)
            kcol = pl.multiple_of(head_width + p * 2 * HD, 2 * HD)
            vcol = pl.multiple_of(2 * head_width + p * 2 * HD, 2 * HD)
            qTz = two(qT[i, pl.ds(col, 2 * HD), :], hrow)
            doTz = two(doT[i, pl.ds(col, 2 * HD), :], hrow)
            qz = two(qs[jj, :, pl.ds(col, 2 * HD)], hcol)
            doz = two(dos[jj, :, pl.ds(col, 2 * HD)], hcol)
            ls = [lse[jj, pl.ds(p * 2 + hh, 1), :] for hh in range(2)]
            dlt = [dl[i, pl.ds(p * 2 + hh, 1), :] for hh in range(2)]

            def block(m, carry, diag):
                kb = qs[t ^ m, :, pl.ds(kcol, 2 * HD)]
                vb = qs[t ^ m, :, pl.ds(vcol, 2 * HD)]
                ktb = kT[m, pl.ds(col, 2 * HD), :]
                dvs, dks, new = 0.0, 0.0, []
                for hh in range(2):
                    s = nn(kb, qTz[hh])
                    if diag:
                        inside = (rowk >= at) & (rowk < at + PIC) & (colq >= at) & (colq < at + PIC)
                        s = jnp.where((rowk <= colq) | inside, s, NEG)
                    pr = jnp.exp(s - ls[hh])
                    dp = nn(vb, doTz[hh])
                    ds = (pr * (dp - dlt[hh])).astype(BF)
                    dvs = dvs + nn(pr.astype(BF), doz[hh])
                    dks = dks + nn(ds, qz[hh])
                    new.append(carry[hh] + nn(ktb[hh * HD : (hh + 1) * HD], ds))
                dv[m, :, pl.ds(col, 2 * HD)] += dvs
                dk[m, :, pl.ds(col, 2 * HD)] += dks
                return tuple(new)

            c = tuple(jnp.zeros((HD, rows), F32) for _ in range(2))
            c = block(i, c, True)
            c = lax.fori_loop(0, i, lambda m, c: block(m, c, False), c)
            dq = (jnp.concatenate(c, axis=0) * (HD**-0.5)).astype(BF)
            dqkv[jj, :, pl.ds(col, 2 * HD)] = dq.T

    back_fwd = remote(backv.at[2], backv.at[3], pfs.at[3], pfr.at[3], sib)
    pf = remote(pfar_in, pfarv, pfs.at[0], pfr.at[0], far)
    sends += [back_fwd, pf]

    def columns(p):
        return [
            (k * 2 * HD, lambda j, k=k: dqkv[j, :, k * head_width + p * 2 * HD : k * head_width + (p + 1) * 2 * HD])
            for k in range(3)
        ]

    def settle(p):
        kcol = pl.ds(pl.multiple_of(head_width + p * 2 * HD, 2 * HD), 2 * HD)
        vcol = pl.ds(pl.multiple_of(2 * head_width + p * 2 * HD, 2 * HD), 2 * HD)
        col = pl.ds(pl.multiple_of(p * 2 * HD, 2 * HD), 2 * HD)
        for j in range(4):
            dqkv[j, :, kcol] = (dk[t ^ j, :, col] * (HD**-0.5)).astype(BF)
            dqkv[j, :, vcol] = dv[t ^ j, :, col].astype(BF)

    def pass_pair(p):
        def one(i, _):
            pass_on(2 + p, lines - 1 - i, lambda d: gq[p, row(keep_of(d)), :])
            return 0

        lax.fori_loop(0, lines - 1, one, 0)

    def heads_of(p, _):
        def step_of(i, _):
            attend(p, i)

            @pl.when((p == 0) & (i == 1))
            def _():
                pass_fc1(lines - 1)
                if lines > 2:
                    pass_fc1(lines - 2)

            @pl.when((p == 0) & (i == 2))
            def _():
                if lines > 3:

                    def pass_more(n, _):
                        pass_fc1(lines - 3 - n)
                        return 0

                    lax.fori_loop(0, lines - 3, pass_more, 0)

            @pl.when((p == 1) & (i == 2))
            def _():
                pass_pair(0)

            return 0

        lax.fori_loop(0, 4, step_of, 0)
        settle(p)

        @pl.when(p == 0)
        def _():
            back_far.wait_recv()
            back_fwd.start()
            pf.start()
            local[1].wait()
            first_in[5].wait()
            weight_grad(2, onev, columns(0), gq.at[0], 0)

        return 0

    lax.fori_loop(0, pairs, heads_of, 0)
    for c in local[2:]:
        c.wait()

    def norm_grad(j, c):
        return nn(dqkv[j, part(c), :], wt[...])

    first, second, third = [], [], []
    def far_chunk(c):
        s1[0, part(c), :] = norm_grad(3, c).astype(BF)
        first.append(go(remote(s1.at[0, part(c)], r1.at[0, part(c)], s1s.at[0, c], s1r.at[0, c], sib)))
        mine = norm_grad(2, c)
        first[c].wait_recv()
        a1[part(c), :] = (mine + r1[0, part(c), :].astype(F32)).astype(BF)
        second.append(go(remote(a1.at[part(c)], q1.at[part(c)], y1s.at[c], y1r.at[c], far)))

    first_in[6].wait()
    far_chunk(0)
    local[0].wait()
    back_sib.wait_recv()
    back_fwd.wait_recv()
    weight_grad(1, backv, [(0, lambda j: ats[j])], go_)
    for p in range(1, pairs):
        weight_grad(2 + p, onev, columns(p), gq.at[p], p)
    column_sum = jnp.sum(dqkv[0].astype(F32), axis=0, keepdims=True)
    for j in range(1, 4):
        column_sum = column_sum + jnp.sum(dqkv[j].astype(F32), axis=0, keepdims=True)
    high = column_sum.astype(BF)
    low = (column_sum - high.astype(F32)).astype(BF)
    bias_sum = nn(high, wt[...]) + nn(low, wt[...])
    product = jnp.sum(smat[...].T, axis=0, keepdims=True)
    gain_sum = (product - bias[...] * bias_sum) / gain[...]

    slot = lax.broadcasted_iota(jnp.int32, (4, head_width), 0)
    lv[...] = jnp.zeros_like(lv)
    qsum = column_sum[:, :head_width]
    vsum = column_sum[:, 2 * head_width :]
    for u in range(4):
        cols = pl.ds(u * head_width, head_width)
        lv[u, 0:4, :] = jnp.where(slot == t, vec[0:1, cols], 0.0)
        here = (t == u).astype(F32)
        lv[u, 4:5, :] = qsum * here
        lv[u, 5:6, :] = vsum * here
        lv[u, 6:7, :] = vec[3:4, cols]
        lv[u, 7:8, :] = vec[4:5, cols]
        lv[u, 8:9, :] = vec[1:2, cols]
        lv[u, 9:10, :] = vec[2:3, cols]
        lv[u, 10:11, :] = gain_sum[:, u * head_width : (u + 1) * head_width]
        lv[u, 11:12, :] = bias_sum[:, u * head_width : (u + 1) * head_width]
    level1 = [
        go(remote(lv.at[t ^ j], rv1.at[j], v1s.at[j], v1r.at[j], mates[j - 1])) for j in range(1, 4)
    ]
    for c in range(1, chunks):
        far_chunk(c)

    def pass_out(i, _):
        pass_on(1, lines - 1 - i, lambda d: go_[row(keep_of(d)), :])
        return 0

    lax.fori_loop(0, lines - 1, pass_out, 0)
    for c in range(chunks):
        s1[1, part(c), :] = norm_grad(1, c).astype(BF)
        third.append(go(remote(s1.at[1, part(c)], r1.at[1, part(c)], s1s.at[1, c], s1r.at[1, c], sib)))
    for c in range(chunks):
        near[part(c), :] = norm_grad(0, c)

    def pass_qkv(i, _):
        for p in range(1, pairs):
            pass_on(2 + p, lines - 1 - i, lambda d, p=p: gq[p, row(keep_of(d)), :])
        return 0

    lax.fori_loop(0, (lines - 1) // 2, pass_qkv, 0)
    pf.wait_recv()
    hidv[...] = hidv[...] + pfarv[...].astype(F32) + fc2_bias[...]
    outs = [pltpu.make_async_copy(hidv, out_out, osem.at[0])]
    outs[0].start()
    for c in level1:
        c.wait_recv()
    sv[...] = lv[t] + rv1[1] + rv1[2] + rv1[3]
    level2 = [
        go(remote(sv, rv2.at[e], v2s.at[e], v2r.at[e], others[e - 1])) for e in range(1, shards)
    ]
    lax.fori_loop((lines - 1) // 2, max((lines - 1) // 2, lines - 2), pass_qkv, 0)
    for c in third:
        c.wait_recv()

    def finish(c):
        second[c].wait_recv()
        gn = near[part(c), :] + r1[1, part(c), :].astype(F32) + q1[part(c), :].astype(F32)
        unit, inv = normalize(tokv[part(c), :].astype(F32))
        scaled = gn * gain[...]
        inner = (
            scaled
            - jnp.mean(scaled, axis=1, keepdims=True)
            - unit * jnp.mean(scaled * unit, axis=1, keepdims=True)
        )
        ghidv[part(c), :] = ghidv[part(c), :] + inv * inner

    for c in range(chunks - 1):
        finish(c)
    lax.fori_loop(max((lines - 1) // 2, lines - 2), lines - 1, pass_qkv, 0)
    for c in level2:
        c.wait_recv()
    total = sv[...]
    for e in range(1, shards):
        total = total + rv2[e]
    gv[t] = total
    level3 = [
        go(remote(gv.at[t], gv.at[t], v3s.at[j], v3r.at[j], mates[j - 1])) for j in range(1, 4)
    ]

    def reduced(k, own):
        x_copy(k, 0).wait_recv()
        land = lands[k]
        result = own.astype(F32) + land[0][0].astype(F32)
        if lines <= 8:
            for d in range(lines - 1, 0, -1):
                z_copy(k, d).wait_recv()
                result = result + land[2][d].astype(F32)
            return result

        def collect(i, acc):
            d = lines - 1 - i
            z_copy(k, d).wait_recv()
            return acc + land[2][d].astype(F32)

        return lax.fori_loop(0, lines - 1, collect, result)

    pltpu.make_async_copy(g1_in.at[keep_of(0)], sz1.at[0], lsem.at[8]).wait()
    sum1[...] = reduced(0, sz1[0])
    outs.append(pltpu.make_async_copy(sum1, w1_out, osem.at[1]))
    outs[-1].start()
    total2 = rz2[0].astype(F32)
    for d in range(lines - 1, 0, -1):
        z2_copy(d).wait_recv()
        total2 = total2 + rz2[d].astype(F32)
    sum2[...] = total2.T
    outs.append(pltpu.make_async_copy(sum2, w2_out, osem.at[5]))
    outs[-1].start()
    wos[...] = reduced(1, go_[row(f), :]).T
    outs.append(pltpu.make_async_copy(wos, wo_out, osem.at[2]))
    outs[-1].start()
    finish(chunks - 1)
    outs.append(pltpu.make_async_copy(ghidv, tok_out, osem.at[3]))
    outs[-1].start()
    for p in range(pairs):
        mine = reduced(2 + p, gq[p, row(f), :])
        for k in range(3):
            wqs[k, :, p * 2 * HD : (p + 1) * 2 * HD] = mine[:, k * 2 * HD : (k + 1) * 2 * HD]
    outs.append(pltpu.make_async_copy(wqs, wq_out, osem.at[4]))
    outs[-1].start()
    for c in level3:
        c.wait_recv()
    for u in range(4):
        cols = slice(u * head_width, (u + 1) * head_width)
        for r in range(4):
            fcb_out[:, r * width + u * head_width : r * width + (u + 1) * head_width] = gv[u, r : r + 1, :]
        qv_out[:, cols] = gv[u, 4:6, :]
        for r, ref in enumerate((g_a, g_b, g_c, g_d, g_e, g_f)):
            ref[:, cols] = gv[u, 6 + r : 7 + r, :]
    for c in sends:
        c.wait_send()

    def drain(d, _):
        for k in range(sums):
            x_copy(k, d).wait_send()

        @pl.when(d > 0)
        def _():
            z2_copy(d).wait_send()
            for k in range(sums):
                z_copy(k, d).wait_send()

        return 0

    lax.fori_loop(0, lines, drain, 0)
    for c in outs:
        c.wait()


def tail(shards, lse, starts, vec, gain, bias, fc2_bias, qkv, grad_att, att, weights, wt, qT, kT, one, back, tok, ghid, hid, pfar, g1, g2):
    _, rows, width = one.shape
    head_width = att.shape[2]
    hidden = g1.shape[2]
    heads = head_width // HD
    pairs = heads // 2
    per = width // shards
    lines = shards // 2
    chunks = 2
    dma = pltpu.SemaphoreType.DMA
    vm = pl.BlockSpec(memory_space=VM)
    hbm = pl.BlockSpec(memory_space=HB)
    V = pltpu.VMEM
    small = (4, 16, head_width)
    sems = [
        (8 + lines,), (2, chunks), (2, chunks), (chunks,), (chunks,),
        (2 + pairs, lines), (2 + pairs, lines), (2 + pairs, lines), (2 + pairs, lines),
        (4,), (4,), (shards,), (shards,), (4,), (4,), (4,), (4,), (lines,), (lines,), (6,), (7,),
    ]
    turned = V((4, head_width, rows), BF)
    one_row = (rows, width)
    return pl.pallas_call(
        functools.partial(tail_kernel, shards, chunks),
        name="tail",
        out_shape=[
            jax.ShapeDtypeStruct(one_row, F32),
            jax.ShapeDtypeStruct(one_row, F32),
            jax.ShapeDtypeStruct((3, per, head_width), F32),
            jax.ShapeDtypeStruct((head_width, per), F32),
            jax.ShapeDtypeStruct((per, hidden), F32),
            jax.ShapeDtypeStruct((hidden, per), F32),
            jax.ShapeDtypeStruct((2, width), F32),
            jax.ShapeDtypeStruct((1, 4 * width), F32),
        ]
        + [jax.ShapeDtypeStruct((1, width), F32)] * 6,
        in_specs=[vm, pl.BlockSpec(memory_space=SM)] + [vm] * 4 + [hbm] * 15,
        out_specs=[hbm] * 6 + [vm] * 8,
        scratch_shapes=[
            V((4, rows, 3 * head_width), BF), V((4, rows, head_width), BF), V((4, rows, head_width), BF),
            V(weights.shape, BF), turned, turned, turned,
            V((4, rows, head_width), F32), V((4, rows, head_width), F32), V((4, heads, rows), F32),
            V((4, rows, 3 * head_width), BF),
            V((4, rows, width), BF), V((4, rows, width), BF), V(one_row, BF), V(one_row, F32),
            V(one_row, F32), V(one_row, BF), V((3 * head_width, width), BF),
            V((2, rows, width), BF), V((2, rows, width), BF), V(one_row, BF), V(one_row, BF),
            V(one_row, F32), V((pairs, width, 6 * HD), BF), V((width, head_width), BF),
        ]
        + [V((pairs, lines, per, 6 * HD), BF)] * 3
        + [V((lines, per, head_width), BF)] * 3
        + [V((lines, per, hidden), BF)] * 4
        + [
            V((per, hidden), F32), V((hidden, per), F32), V((3, per, head_width), F32), V((head_width, per), F32),
            V((width, 2 * HD), F32), V(small, F32), V(small, F32),
            V((16, head_width), F32), V((shards, 16, head_width), F32), V(small, F32),
        ]
        + [dma(s) for s in sems],
        compiler_params=pltpu.CompilerParams(
            collective_id=2, has_side_effects=True, vmem_limit_bytes=62 << 20
        ),
        cost_estimate=pl.CostEstimate(flops=60 << 30, bytes_accessed=100 << 20, transcendentals=0),
    )(lse, starts, vec, gain, bias, fc2_bias, qkv, grad_att, att, weights, wt, qT, kT, one, back, tok, ghid, hid, pfar, g1, g2)


def finish_kernel(parts, *refs):
    count = len(parts)
    held, sems = refs[2 * count : 3 * count], refs[-1]
    loads, stores = [], []
    for n, pieces in enumerate(parts):
        rows = held[n].shape[0] // pieces
        for i in range(pieces):
            block, k = pl.ds(i * rows, rows), len(loads)
            loads.append(
                pltpu.make_async_copy(refs[n].at[block], held[n].at[block], sems.at[0, k])
            )
            stores.append(
                pltpu.make_async_copy(held[n].at[block], refs[count + n].at[block], sems.at[1, k])
            )
    for c in loads:
        c.start()
    for load, store in zip(loads, stores):
        load.wait()
        store.start()
    for c in stores:
        c.wait()


def finish(arrays):
    parts = [8 if a.size >= 1 << 18 else 2 if a.size >= 1 << 17 else 1 for a in arrays]
    hbm = pl.BlockSpec(memory_space=HB)
    return pl.pallas_call(
        functools.partial(finish_kernel, parts),
        name="finish",
        out_shape=[jax.ShapeDtypeStruct(a.shape, a.dtype) for a in arrays],
        in_specs=[hbm] * len(arrays),
        out_specs=[hbm] * len(arrays),
        scratch_shapes=[pltpu.VMEM(a.shape, a.dtype) for a in arrays]
        + [pltpu.SemaphoreType.DMA((2, sum(parts)))],
    )(*arrays)


def body(
    tokens,
    cotangent,
    pic_starts,
    w_qkv,
    qv_bias,
    w_out,
    out_bias,
    ln1_gain,
    ln1_bias,
    w_fc1,
    fc1_bias,
    w_fc2,
    fc2_bias,
    ln2_gain,
    ln2_bias,
):
    rows, width = tokens.shape
    shards = lax.axis_size("fsdp")
    one, qkv, wq_full, out_full, fc_in, up_far, att, lse, mix, wqt, qT, kT = head(
        shards, tokens, w_qkv.transpose(1, 0, 2), w_out, w_fc1, w_fc2,
        ln1_gain[None], ln1_bias[None], qv_bias, pic_starts, cotangent,
    )
    hidden_one, ghid, back, grad_att, fc1_part, fc2_part, part_far, vec = middle(
        shards, mix, out_full, tokens, cotangent, up_far, fc_in,
        ln2_gain[None], ln2_bias[None], out_bias[None], fc1_bias[None],
    )
    results = tail(
        shards, lse, pic_starts, vec, ln1_gain[None], ln1_bias[None], fc2_bias[None],
        qkv, grad_att, att, wq_full, wqt, qT, kT, one, back, tokens, ghid, hidden_one, part_far, fc1_part, fc2_part,
    )
    output, input_grad, wq_grad, wo_grad, fc1_grad, fc2_grad, qv_grad, fc1_b, *vecs = finish(results)
    out_b, fc2_b, gain_two, shift_two, gain_one, shift_one = [v[0] for v in vecs]
    return (
        output,
        input_grad,
        wq_grad.transpose(1, 0, 2),
        qv_grad,
        wo_grad,
        out_b,
        gain_one,
        shift_one,
        fc1_grad,
        fc1_b[0],
        fc2_grad,
        fc2_b,
        gain_two,
        shift_two,
    )


def solution(mesh):
    return jax.shard_map(
        body,
        mesh=mesh,
        in_specs=(
            P(("fsdp", "tensor"), None),
            P(("fsdp", "tensor"), None),
            P("fsdp", None),
            P("fsdp", None, "tensor"),
            P(),
            P("tensor", "fsdp"),
            P(),
            P(),
            P(),
            P("fsdp", "tensor"),
            P(),
            P("tensor", "fsdp"),
            P(),
            P(),
            P(),
        ),
        out_specs=(
            P(("fsdp", "tensor"), None),
            P(("fsdp", "tensor"), None),
            P("fsdp", None, "tensor"),
            P(),
            P("tensor", "fsdp"),
            P(),
            P(),
            P(),
            P("fsdp", "tensor"),
            P(),
            P("tensor", "fsdp"),
            P(),
            P(),
            P(),
        ),
        check_vma=False,
    )
```
